32 devices in a mesh: parts: 2 (over x), fibre: 16 (over z, y, core).
Axes of the slice: x: 2, y: 2, z: 4, core: 2. Of those that a mesh axis runs over, the one named last changes fastest.
Arguments:
- signal: bfloat16 [64, 16, 8192], P('parts', None, 'fibre'), parts along dimension 0, may hold values from -6 to 6
- conv_taps: bfloat16 [5, 5, 64, 32], replicated, may hold values from -0.21875 to 0.21875
- response: float32 [2, 64, 4096], P(None, 'fibre'), may hold values from -4 to 4
- cotangent: bfloat16 [128, 8, 4096], P('parts', None, 'fibre'), parts along dimension 0, may hold values from -6 to 6
Outputs:
- input_grad: bfloat16 [64, 16, 8192], P('parts', None, 'fibre'), parts along dimension 0
- tap_grad: float32 [10, 5, 64, 32], P('parts'), parts along dimension 0
- filter_grad: float32 [4, 64, 4096], P('parts', 'fibre'), parts along dimension 0
The draws below stay inside these ranges and needn't reach their ends.
There are 2 independent parts, one for each index of `parts`. The reference program is written for one: setup_inputs(seed, part) draws one part's arguments, and reference() takes and returns one part's arrays. A program takes and returns all parts, laid end to end along the dimension named above; an argument that names none is the same for every part. Nothing has to cross between parts.
All inputs are finite; a program needn't handle non-finite values.
Results may differ from the reference program's by a relative error of at most 0.012.
Values may be sent and summed in bfloat16 or wider, within the bound.
No kernel may reach another device: no remote copies, remote signals or barrier semaphores. Data moves between devices by JAX's collectives and lax.ppermute only.
A program may use at most 64 MiB of HBM per device.

```python
import math
import jax
import jax.numpy as jnp
from jax import lax

CIN = 32
COUT = 64
KS = 5
TW = 16
TH = 8
FIB = 8192
KH = 4096


def block_scale(stream_key, dims, cuts, least, largest):
    loudness = 1.0
    for axis_at, shards_of in cuts:
        steps = jax.random.uniform(jax.random.fold_in(jax.random.fold_in(stream_key, 6), axis_at), (shards_of,), jnp.float32, least / len(cuts), largest / len(cuts))
        loudness = loudness * jnp.repeat(jnp.exp(steps), dims[axis_at] // shards_of).reshape((-1,) + (1,) * (len(dims) - 1 - axis_at))
    return loudness


def bell_draw(own_key, extent, width, most, shards=(), held_as=jnp.bfloat16):
    array = width * jax.random.normal(own_key, extent, jnp.float32)
    if shards:
        array = array * block_scale(own_key, extent, shards, -0.22, 0.18)
    return jnp.clip(array, -most, most).astype(held_as)


def setup_inputs(seed: int = 0, part: int = 0) -> dict:
    key_list = jax.random.split(jax.random.key(seed), 5)
    part_keys = jax.random.split(jax.random.fold_in(key_list[4], part), 5)
    return {
        "signal": bell_draw(part_keys[0], (CIN, TW, FIB), 1.0, 6.0, ((2, 16),)),
        "conv_taps": bell_draw(key_list[1], (KS, KS, COUT, CIN), (CIN * KS * KS) ** -0.5, 0.21875),
        "response": bell_draw(key_list[2], (2, COUT, KH), 0.8, 4.0, ((1, 16),), jnp.float32),
        "cotangent": bell_draw(part_keys[3], (COUT, TH, KH), 1.0, 6.0, ((2, 16),)),
    }


inv_root_two = 1.0 / math.sqrt(2.0)
inv_root_tau = 1.0 / math.sqrt(2.0 * math.pi)

def gelu_slope(values):
    return 0.5 * (1.0 + jax.scipy.special.erf(values * inv_root_two)) + values * jnp.exp(-0.5 * values * values) * inv_root_tau

def reference(signal, conv_taps, response, cotangent):
    margin = KS // 2
    padded = jnp.pad(signal, ((0, 0), (margin, margin), (margin, margin)))
    conv_sum = jnp.zeros((COUT, TH * KH), jnp.float32)
    for tap_row in range(KS):
        for tap_col in range(KS):
            patches = padded[:, tap_row:tap_row + 2 * TH:2, tap_col:tap_col + 2 * KH:2].reshape(CIN, TH * KH)
            conv_sum = conv_sum + jnp.dot(conv_taps[tap_row, tap_col], patches, preferred_element_type=jnp.float32)
    conv_out = conv_sum.astype(jnp.bfloat16).reshape(COUT, TH, KH)
    spectra = jnp.fft.fft(conv_out.astype(jnp.float32), axis=-1)
    filter_resp = (response[0] + 1j * response[1])[:, None, :]
    filtered = jnp.real(jnp.fft.ifft(filter_resp * spectra, axis=-1))
    slope_grad = cotangent.astype(jnp.float32) * gelu_slope(filtered)
    grad_spec = jnp.fft.fft(slope_grad, axis=-1)
    cross_spec = spectra * jnp.conj(grad_spec)
    filter_grad = jnp.stack([lax.optimization_barrier(jnp.sum(jnp.real(cross_spec), axis=1)), -lax.optimization_barrier(jnp.sum(jnp.imag(cross_spec), axis=1))]) / KH
    conv_grad = jnp.real(jnp.fft.ifft(jnp.conj(filter_resp) * grad_spec, axis=-1)).astype(jnp.bfloat16)
    grad_flat = conv_grad.reshape(COUT, TH * KH)
    grad_pad = jnp.zeros((CIN, TW + 2 * margin, FIB + 2 * margin), jnp.float32)
    tap_list = []
    for tap_row in range(KS):
        for tap_col in range(KS):
            patches = padded[:, tap_row:tap_row + 2 * TH:2, tap_col:tap_col + 2 * KH:2].reshape(CIN, TH * KH)
            back_term = jnp.dot(conv_taps[tap_row, tap_col].T, grad_flat, preferred_element_type=jnp.float32)
            grad_pad = grad_pad.at[:, tap_row:tap_row + 2 * TH:2, tap_col:tap_col + 2 * KH:2].add(back_term.reshape(CIN, TH, KH))
            tap_list.append(jnp.dot(grad_flat, patches.T, preferred_element_type=jnp.float32))
    input_grad = grad_pad[:, margin:margin + TW, margin:margin + FIB].astype(jnp.bfloat16)
    tap_grad = jnp.stack(tap_list).reshape(KS, KS, COUT, CIN) * (1.0 / math.sqrt(TH * KH))
    return (input_grad, tap_grad, filter_grad)
```

```python
import functools
import math

import jax
import jax.numpy as jnp
import numpy as np
from jax import lax
from jax.experimental import pallas as pl
from jax.experimental.pallas import tpu as pltpu
from jax.sharding import PartitionSpec as P

bf16 = jnp.bfloat16
f32 = jnp.float32
inv_root_two = 1.0 / math.sqrt(2.0)
inv_root_tau = 1.0 / math.sqrt(2.0 * math.pi)
lanes = 128
edge_rows = 8
tap_rows = 416


def dot(a, b):
    return jnp.dot(a, b, preferred_element_type=f32)


def dot_nt(a, b):
    return lax.dot_general(a, b, (((1,), (1,)), ((), ())), preferred_element_type=f32)


def dot_tn(a, b):
    return lax.dot_general(a, b, (((0,), (0,)), ((), ())), preferred_element_type=f32)


def iota(shape, dim):
    return lax.broadcasted_iota(jnp.int32, shape, dim)


def one_hot(shape, column_of_row):
    return (iota(shape, 1) == column_of_row(iota(shape, 0))).astype(f32).astype(bf16)


def one_hot_columns(shape, row_of_column):
    return (iota(shape, 0) == row_of_column(iota(shape, 1))).astype(f32).astype(bf16)


def call(kernel, outs, scratch, flops, args):
    moved = sum(a.size * a.dtype.itemsize for a in list(args) + list(outs))
    return pl.pallas_call(
        kernel,
        out_shape=outs,
        in_specs=[pl.BlockSpec(memory_space=pltpu.VMEM)] * len(args),
        out_specs=[pl.BlockSpec(memory_space=pltpu.VMEM)] * len(outs),
        scratch_shapes=scratch,
        compiler_params=pltpu.CompilerParams(vmem_limit_bytes=48 << 20),
        cost_estimate=pl.CostEstimate(flops=int(flops), bytes_accessed=moved, transcendentals=0),
    )(*args)


def conv_kernel(dims, sig_ref, taps_ref, out_ref, z_ref, w_ref):
    cin, tin, cout, tout, ks, count, rows = dims
    k_in, k_out = cin * tin, cout * tout
    half = sig_ref.shape[1] // 2
    split = one_hot_columns((2 * lanes, 2 * lanes), lambda q: 2 * (q % lanes) + q // lanes)
    parts = [dot(sig_ref[:, b : b + 2 * lanes], split) for b in range(0, 2 * half, 2 * lanes)]
    apart = jnp.concatenate([p[:, :lanes] for p in parts] + [p[:, lanes:] for p in parts], axis=1)
    to_time = one_hot((k_in, k_in), lambda r: (r % cin) * tin + r // cin)
    z = dot(to_time, apart.astype(bf16)).astype(bf16)
    z_ref[...] = z
    blank = jnp.zeros((2 * cin, cout), bf16)
    stacked = []
    for j in range(ks):
        column = jnp.concatenate([blank] + [taps_ref[i, j] for i in range(ks)] + [blank, blank], axis=0)
        for v in range(4):
            stacked.append(column[2 * cin * v : 2 * cin * v + lanes])
    eye = one_hot((cout, cout), lambda r: r)
    tiles = dot_nt(eye, jnp.concatenate(stacked, axis=0)).astype(bf16)
    empty = jnp.zeros((cout, lanes), bf16)
    for j in range(ks):
        for t in range(tout):
            for q in range(k_in // lanes):
                v = 2 * q - t + 2
                at = (j * 4 + v) * lanes
                tile = tiles[:, at : at + lanes] if 0 <= v < 4 else empty
                w_ref[j, cout * t : cout * (t + 1), lanes * q : lanes * (q + 1)] = tile
    even, odd = z[:, :half], z[:, half:]
    left = dot(w_ref[0], even) + dot(w_ref[1], odd)
    right = dot(w_ref[4], even)
    lane = iota((k_out, half), 1)
    own = (
        dot(w_ref[2], even)
        + dot(w_ref[3], odd)
        + jnp.where(lane == 0, 0.0, pltpu.roll(left, 1, 1))
        + jnp.where(lane == half - 1, 0.0, pltpu.roll(right, half - 1, 1))
    )
    high = own.astype(bf16)
    rest = (own - high.astype(f32)).astype(bf16)
    left_edge, right_edge = left[:, half - lanes :], right[:, :lanes]
    left_high, right_high = left_edge.astype(bf16), right_edge.astype(bf16)
    left_rest = (left_edge - left_high.astype(f32)).astype(bf16)
    right_rest = (right_edge - right_high.astype(f32)).astype(bf16)

    def pick(row, column, tile):
        at = (iota((edge_rows, lanes), 0) == row) & (iota((edge_rows, lanes), 1) == column)
        return dot_nt(at.astype(f32).astype(bf16), tile)

    edges = (
        pick(0, 0, rest[:, :lanes])
        + pick(1, lanes - 1, rest[:, half - lanes :])
        + pick(2, lanes - 1, left_high)
        + pick(3, lanes - 1, left_rest)
        + pick(4, 0, right_high)
        + pick(5, 0, right_rest)
    ).astype(bf16)
    to_channel = one_hot((k_out, k_out), lambda r: (r % tout) * cout + r // tout)
    edges = dot_nt(edges, to_channel)
    main = dot(to_channel, high).astype(bf16)
    for d in range(count):
        out_ref[d, :rows] = main[rows * d : rows * (d + 1)]
        out_ref[d, rows:] = jnp.zeros((edge_rows, half), bf16)
        out_ref[d, rows:, :rows] = edges[:, rows * d : rows * (d + 1)].astype(bf16)


def transform(real, imag, sign):
    size = len(real)
    if size == 1:
        return (list(real), [None] if imag is None else list(imag))
    even_re, even_im = transform(real[0::2], None if imag is None else imag[0::2], sign)
    odd_re, odd_im = transform(real[1::2], None if imag is None else imag[1::2], sign)
    out_re, out_im = [None] * size, [None] * size

    def plus(a, b):
        return b if a is None else (a if b is None else a + b)

    def minus(a, b):
        return a if b is None else (-b if a is None else a - b)

    for k in range(size // 2):
        re, im = odd_re[k], odd_im[k]
        if k == 0:
            tr, ti = re, im
        elif 4 * k == size:
            tr = None if im is None else (im if sign < 0 else -im)
            ti = -re if sign < 0 else re
        else:
            c, s = math.cos(2 * math.pi * k / size), sign * math.sin(2 * math.pi * k / size)
            if im is None:
                tr, ti = c * re, s * re
            elif 8 * k == size:
                tr, ti = (c * (re - im), c * (re + im)) if sign > 0 else (c * (re + im), c * (im - re))
            elif 8 * k == 3 * size:
                tr, ti = (c * (re + im), c * (im - re)) if sign > 0 else (c * (re - im), c * (re + im))
            else:
                tr, ti = c * re - s * im, s * re + c * im
        out_re[k], out_im[k] = plus(even_re[k], tr), plus(even_im[k], ti)
        out_re[k + size // 2], out_im[k + size // 2] = minus(even_re[k], tr), minus(even_im[k], ti)
    return out_re, out_im


def gelu_slope(v):
    return 0.5 * (1.0 + lax.erf(v * inv_root_two)) + v * jnp.exp(-0.5 * v * v) * inv_root_tau


def filter_kernel(
    dims, conv_ref, cot_ref, resp_ref, twist_ref, high_ref, rest_ref,
    out_ref, fgrad_ref, x_ref, y_ref, spec_ref, grad_ref,
):
    count, channels, tout, width = dims
    rows = channels * tout
    scale = 1.0 / (count * width)
    edge_row, edge_col = iota((edge_rows, width), 0), iota((edge_rows, width), 1)
    to_low = (edge_col == 0) & ((edge_row == 0) | (edge_row == 2) | (edge_row == 3))
    to_high = (edge_col == width - 1) & ((edge_row == 1) | (edge_row == 4) | (edge_row == 5))
    spread = (to_low | to_high).astype(f32).astype(bf16)
    edges = [conv_ref[d, rows:, :rows].astype(f32) for d in range(count)]
    none = jnp.zeros((edge_rows, rows), f32)
    kind = iota((edge_rows, rows), 0)
    for d in range(count):
        before = edges[d - 1] if d > 0 else none
        after = edges[d + 1] if d < count - 1 else none
        joined = jnp.where(kind < 2, edges[d], jnp.where(kind < 4, before, after))
        whole = conv_ref[d, :rows].astype(f32) + dot_tn(joined.astype(bf16), spread)
        x_ref[d] = whole.astype(bf16).astype(f32)

    def forward_planes(planes, r, h):
        re, im = transform(planes, None, -1)
        for k in range(count):
            c = twist_ref[0, k : k + 1, h : h + lanes]
            s = twist_ref[1, k : k + 1, h : h + lanes]
            at = pl.ds(k * rows + r, tout)
            if k == 0:
                y_ref[at, h : h + lanes] = re[k]
                y_ref[at, width + h : width + h + lanes] = jnp.zeros_like(re[k]) if im[k] is None else im[k]
            elif im[k] is None:
                y_ref[at, h : h + lanes] = re[k] * c
                y_ref[at, width + h : width + h + lanes] = -(re[k] * s)
            else:
                y_ref[at, h : h + lanes] = re[k] * c + im[k] * s
                y_ref[at, width + h : width + h + lanes] = im[k] * c - re[k] * s

    def backward_planes(r, h):
        re, im = [], []
        for k in range(count):
            c = twist_ref[0, k : k + 1, h : h + lanes]
            s = twist_ref[1, k : k + 1, h : h + lanes]
            at = pl.ds(k * rows + r, tout)
            a, b = y_ref[at, h : h + lanes], y_ref[at, width + h : width + h + lanes]
            re.append(a * c - b * s if k else a)
            im.append(b * c + a * s if k else b)
        return transform(re, im, 1)[0]

    def halves(v):
        high = v.astype(bf16)
        return high, (v - high.astype(f32)).astype(bf16)

    def inner(product):
        high, rest = halves(y_ref[...])
        return (
            product(high, high_ref[...]) + product(rest, high_ref[...]) + product(high, rest_ref[...])
        )

    chunks = [(r * tout, h) for r in range(channels) for h in range(0, width, lanes)]
    for r, h in chunks:
        forward_planes([x_ref[d, r : r + tout, h : h + lanes] for d in range(count)], r, h)
    spec_ref[...] = inner(dot)
    for k in range(count):
        for ch in range(channels):
            at = pl.ds(k * rows + ch * tout, tout)
            sr, si = spec_ref[at, :width], spec_ref[at, width:]
            rr, ri = resp_ref[0, ch, k : k + 1], resp_ref[1, ch, k : k + 1]
            y_ref[at, :width] = rr * sr - ri * si
            y_ref[at, width:] = rr * si + ri * sr
    y_ref[...] = inner(dot_nt)
    for r, h in chunks:
        planes = backward_planes(r, h)
        slopes = [
            cot_ref[d, r : r + tout, h : h + lanes].astype(f32) * gelu_slope(planes[d])
            for d in range(count)
        ]
        forward_planes(slopes, r, h)
    grad_ref[...] = inner(dot)
    for k in range(count):
        for ch in range(channels):
            at = pl.ds(k * rows + ch * tout, tout)
            sr, si = spec_ref[at, :width], spec_ref[at, width:]
            gr, gi = grad_ref[at, :width], grad_ref[at, width:]
            rr, ri = resp_ref[0, ch, k : k + 1], resp_ref[1, ch, k : k + 1]
            fgrad_ref[0, ch, k : k + 1] = jnp.sum(sr * gr + si * gi, axis=0, keepdims=True) * scale
            fgrad_ref[1, ch, k : k + 1] = jnp.sum(sr * gi - si * gr, axis=0, keepdims=True) * scale
            y_ref[at, :width] = rr * gr + ri * gi
            y_ref[at, width:] = rr * gi - ri * gr
    y_ref[...] = inner(dot_nt)
    for r, h in chunks:
        planes = backward_planes(r, h)
        for d in range(count):
            x_ref[d, r : r + tout, h : h + lanes] = planes[d]
    last = ((iota((edge_rows, lanes), 0) == 0) & (iota((edge_rows, lanes), 1) == lanes - 1)).astype(f32).astype(bf16)
    first = ((iota((edge_rows, lanes), 0) == 1) & (iota((edge_rows, lanes), 1) == 0)).astype(f32).astype(bf16)
    for d in range(count):
        out_ref[d, :rows] = x_ref[d].astype(bf16)
        out_ref[d, rows:] = jnp.zeros((edge_rows, width), bf16)
        edge = none
        if d > 0:
            edge = edge + dot_nt(last, x_ref[d - 1, :, width - lanes :].astype(bf16))
        if d < count - 1:
            edge = edge + dot_nt(first, x_ref[d + 1, :, :lanes].astype(bf16))
        out_ref[d, rows:, :rows] = edge.astype(bf16)


def tap_kernel(dims, grad_ref, z_ref, tap_ref, shifted_ref, g_ref, zp_ref):
    cin, tin, cout, tout, ks, count, rows = dims
    half = grad_ref.shape[2]
    k_out = cout * tout
    row, col = iota((edge_rows, lanes), 0), iota((edge_rows, lanes), 1)
    spread = (((row == 1) & (col == 0)) | ((row == 0) & (col == 1))).astype(f32).astype(bf16)
    for d in range(count):
        at = slice(rows * d, rows * (d + 1))
        g_ref[at, :half] = grad_ref[d, :rows].astype(f32)
        g_ref[at, half:] = dot_tn(grad_ref[d, rows:, :rows], spread)
    to_time = one_hot((k_out, k_out), lambda r: (r % cout) * tout + r // cout)
    g = dot(to_time, g_ref[...].astype(bf16)).astype(bf16)
    wide = half + lanes
    later = one_hot_columns((wide, half), lambda n: n + 1)
    sooner = one_hot_columns((wide, half), lambda n: jnp.where(n == 0, half + 1, n - 1))
    shifted_ref[0] = dot(g, later).astype(bf16)
    shifted_ref[1] = g[:, :half]
    shifted_ref[2] = dot(g, sooner).astype(bf16)
    k_in = cin * tin
    pad = 2 * cin
    zp_ref[:pad] = jnp.zeros((pad, 2 * half), bf16)
    zp_ref[pad + k_in :] = jnp.zeros((zp_ref.shape[0] - pad - k_in, 2 * half), bf16)
    zp_ref[pad : pad + k_in] = z_ref[...]
    both, lone = None, None
    for t in range(tout):
        at = slice(cout * t, cout * (t + 1))
        band = zp_ref[2 * cin * t : 2 * cin * t + ks * cin]
        pair = jnp.concatenate([shifted_ref[0, at], shifted_ref[1, at]], axis=0)
        even, odd = band[:, :half], band[:, half:]
        term = jnp.concatenate([dot_nt(even, pair), dot_nt(odd, pair)], axis=0)
        both = term if both is None else both + term
        blank = jnp.zeros((cout, half), bf16)
        mid = ks * cin // 2
        term = dot_nt(even[:mid], jnp.concatenate([shifted_ref[2, at], blank], axis=0)) + dot_nt(
            even[mid:], jnp.concatenate([blank, shifted_ref[2, at]], axis=0)
        )
        lone = term if lone is None else lone + term
    top = both.shape[0]
    tap_ref[:top] = both
    tap_ref[top : top + lone.shape[0]] = lone
    tap_ref[top + lone.shape[0] :] = jnp.zeros((tap_ref.shape[0] - top - lone.shape[0], lanes), f32)


def input_kernel(dims, shifted_ref, taps_ref, out_ref, w_ref):
    cin, tin, cout, tout, ks, count, rows = dims
    k_in = cin * tin
    half = shifted_ref.shape[2]
    blank = jnp.zeros((cin, cout), bf16)
    firsts, seconds = [], []
    for j in range(ks):
        for i in range(ks + 2):
            firsts.append(taps_ref[i, j] if i < ks else blank)
            seconds.append(taps_ref[i - 2, j] if i >= 2 else blank)
    to_first = one_hot((cout, lanes), lambda r: r)
    to_second = one_hot((cout, lanes), lambda r: r + cout)
    tiles = (
        dot(jnp.concatenate(firsts, axis=0), to_first) + dot(jnp.concatenate(seconds, axis=0), to_second)
    ).astype(bf16)
    empty = jnp.zeros((cin, lanes), bf16)
    for j in range(ks):
        for s in range(tin):
            for q in range(cout * tout // lanes):
                i = s - 4 * q + 2
                at = (j * (ks + 2) + i) * cin
                tile = tiles[at : at + cin] if 0 <= i < ks + 2 else empty
                w_ref[j, cin * s : cin * (s + 1), lanes * q : lanes * (q + 1)] = tile
    later, same, sooner = shifted_ref[0], shifted_ref[1], shifted_ref[2]
    even = dot(w_ref[0], later) + dot(w_ref[2], same) + dot(w_ref[4], sooner)
    odd = dot(w_ref[1], later) + dot(w_ref[3], same)
    both = jnp.concatenate([even.astype(bf16), odd.astype(bf16)], axis=1)
    to_channel = one_hot((k_in, k_in), lambda r: (r % tin) * cin + r // tin)
    both = dot(to_channel, both).astype(bf16)
    merge = one_hot((2 * lanes, 2 * lanes), lambda r: 2 * (r % lanes) + r // lanes)
    for b in range(half // lanes):
        part = jnp.concatenate(
            [both[:, lanes * b : lanes * (b + 1)], both[:, half + lanes * b : half + lanes * (b + 1)]], axis=1
        )
        out_ref[:, 2 * lanes * b : 2 * lanes * (b + 1)] = dot(part, merge).astype(bf16)


def unpack_kernel(dims, scale, tap_ref, out_ref):
    cin, tin, cout, tout, ks, count, rows = dims
    band = ks * cin
    for i in range(ks):
        at = slice(cin * i, cin * (i + 1))
        even, odd = tap_ref[at] * scale, tap_ref[band + cin * i : band + cin * (i + 1)] * scale
        out_ref[i, 0] = even[:, :cout]
        out_ref[i, 2] = even[:, cout:]
        out_ref[i, 1] = odd[:, :cout]
        out_ref[i, 3] = odd[:, cout:]
        for c in range(0, cin, 8):
            at = cin * i + c
            low = at < band // 2
            packed = tap_ref[2 * band + at % (band // 2) : 2 * band + at % (band // 2) + 8] * scale
            out_ref[i, 4, c : c + 8] = packed[:, :cout] if low else packed[:, cout:]


def summed_over(rows, axis):
    count = lax.axis_size(axis)
    index = lax.axis_index(axis)
    pairs = lambda step: [(i, i ^ step) for i in range(count)]
    halved = [step for step in (1, 2) if step < count]
    for step in halved:
        size = rows.shape[0] // 2
        bit = (index // step) % 2
        kept = lax.dynamic_slice_in_dim(rows, bit * size, size)
        sent = lax.dynamic_slice_in_dim(rows, (1 - bit) * size, size)
        rows = kept + lax.ppermute(sent, axis, pairs(step))
    step = 2 * halved[-1] if halved else 1
    while step < count:
        rows = rows + lax.ppermute(rows, axis, pairs(step))
        step *= 2
    for step in reversed(halved):
        bit = (index // step) % 2
        other = lax.ppermute(rows, axis, pairs(step))
        rows = jnp.where(bit == 0, jnp.concatenate([rows, other]), jnp.concatenate([other, rows]))
    return rows


def tables(count, width):
    inner = np.outer(np.arange(width), np.arange(width)) % width * (2.0 * np.pi / width)
    c, s = np.cos(inner), np.sin(inner)
    table = np.block([[c, -s], [s, c]]).astype(np.float32)
    high = table.astype(bf16)
    rest = (table - high.astype(np.float32)).astype(bf16)
    outer = np.outer(np.arange(count), np.arange(width)) * (2.0 * np.pi / (count * width))
    twist = np.stack([np.cos(outer), np.sin(outer)]).astype(np.float32)
    return twist, high, rest


def per_device(signal, conv_taps, response, cotangent):
    cin, tin, fibre_in = signal.shape
    cout, tout, width = cotangent.shape
    ks = conv_taps.shape[0]
    count = lax.axis_size("fibre")
    channels = cout // count
    rows = channels * tout
    waves = count * width
    dims = (cin, tin, cout, tout, ks, count, rows)
    k_in, k_out = cin * tin, cout * tout
    taps = jnp.swapaxes(conv_taps, 2, 3)
    shape = jax.ShapeDtypeStruct
    cot_cols = lax.all_to_all(
        cotangent.reshape(count, rows, width), "fibre", split_axis=0, concat_axis=0, tiled=True
    )
    conv_part, z = call(
        functools.partial(conv_kernel, dims),
        [shape((count, rows + edge_rows, width), bf16), shape((k_in, fibre_in), bf16)],
        [pltpu.VMEM((ks, k_out, k_in), bf16)],
        2e9,
        (signal.reshape(k_in, fibre_in), taps),
    )
    conv_cols = lax.all_to_all(conv_part, "fibre", split_axis=0, concat_axis=0, tiled=True)
    arranged = (response * (1.0 / waves)).reshape(2, channels, width, count).transpose(0, 1, 3, 2)
    twist, high, rest = tables(count, width)
    big = count * rows
    grad_part, fgrad = call(
        functools.partial(filter_kernel, (count, channels, tout, width)),
        [shape((count, rows + edge_rows, width), bf16), shape((2, channels, count, width), f32)],
        [
            pltpu.VMEM((count, rows, width), f32),
            pltpu.VMEM((big, 2 * width), f32),
            pltpu.VMEM((big, 2 * width), f32),
            pltpu.VMEM((big, 2 * width), f32),
        ],
        6e9,
        (conv_cols, cot_cols, arranged, jnp.asarray(twist), jnp.asarray(high), jnp.asarray(rest)),
    )
    filter_grad = fgrad.transpose(0, 1, 3, 2).reshape(2, channels, waves)
    grad_cols = lax.all_to_all(grad_part, "fibre", split_axis=0, concat_axis=0, tiled=True)
    taps_part, shifted = call(
        functools.partial(tap_kernel, dims),
        [shape((tap_rows, lanes), f32), shape((3, k_out, width), bf16)],
        [pltpu.VMEM((k_out, width + lanes), f32), pltpu.VMEM((k_in + 4 * cin, fibre_in), bf16)],
        1e9,
        (grad_cols, z),
    )
    total = summed_over(taps_part, "fibre")
    (input_grad,) = call(
        functools.partial(input_kernel, dims),
        [shape((k_in, fibre_in), bf16)],
        [pltpu.VMEM((ks, k_in, k_out), bf16)],
        2e9,
        (shifted, taps),
    )
    (tap_grad,) = call(
        functools.partial(unpack_kernel, dims, 1.0 / math.sqrt(tout * waves)),
        [shape((ks, ks, cin, cout), f32)],
        [],
        1e6,
        (total,),
    )
    return (input_grad.reshape(signal.shape), jnp.swapaxes(tap_grad, 2, 3), filter_grad)


def solution(mesh):
    in_specs = (P("parts", None, "fibre"), P(), P(None, "fibre", None), P("parts", None, "fibre"))
    out_specs = (P("parts", None, "fibre"), P("parts", None, None, None), P("parts", "fibre", None))
    return jax.shard_map(
        per_device, mesh=mesh, in_specs=in_specs, out_specs=out_specs, check_vma=False
    )
```

```python
import functools
import math

import jax
import jax.numpy as jnp
import numpy as np
from jax import lax
from jax.experimental import pallas as pl
from jax.experimental.pallas import tpu as pltpu
from jax.sharding import PartitionSpec as P

bf16 = jnp.bfloat16
f32 = jnp.float32
inv_root_two = 1.0 / math.sqrt(2.0)
inv_root_tau = 1.0 / math.sqrt(2.0 * math.pi)
lanes = 128
edge_rows = 8
tap_rows = 416


def dot(a, b):
    return jnp.dot(a, b, preferred_element_type=f32)


def dot_nt(a, b):
    return lax.dot_general(a, b, (((1,), (1,)), ((), ())), preferred_element_type=f32)


def dot_tn(a, b):
    return lax.dot_general(a, b, (((0,), (0,)), ((), ())), preferred_element_type=f32)


def iota(shape, dim):
    return lax.broadcasted_iota(jnp.int32, shape, dim)


def one_hot(shape, column_of_row):
    return (iota(shape, 1) == column_of_row(iota(shape, 0))).astype(f32).astype(bf16)


def one_hot_columns(shape, row_of_column):
    return (iota(shape, 0) == row_of_column(iota(shape, 1))).astype(f32).astype(bf16)


def call(kernel, outs, scratch, flops, args, left=(), room=48):
    moved = sum(a.size * a.dtype.itemsize for a in list(args) + list(outs))
    return pl.pallas_call(
        kernel,
        out_shape=outs,
        in_specs=[
            pl.BlockSpec(memory_space=pltpu.HBM if a in left else pltpu.VMEM) for a in range(len(args))
        ],
        out_specs=[pl.BlockSpec(memory_space=pltpu.VMEM)] * len(outs),
        scratch_shapes=scratch,
        compiler_params=pltpu.CompilerParams(vmem_limit_bytes=room << 20),
        cost_estimate=pl.CostEstimate(flops=int(flops), bytes_accessed=moved, transcendentals=0),
    )(*args)


def conv_kernel(dims, sig_hbm, cot_hbm, taps_ref, out_ref, z_ref, w_ref, sig_ref, cot_ref, sem):
    cin, tin, cout, tout, ks, count, rows = dims
    k_in, k_out = cin * tin, cout * tout
    half = sig_ref.shape[1] // 2
    sig_copy = pltpu.make_async_copy(sig_hbm, sig_ref, sem.at[0])
    cot_copy = pltpu.make_async_copy(cot_hbm, cot_ref, sem.at[1])
    sig_copy.start()
    cot_copy.start()
    blank = jnp.zeros((2 * cin, cout), bf16)
    stacked = []
    for j in range(ks):
        column = jnp.concatenate([blank] + [taps_ref[i, j] for i in range(ks)] + [blank, blank], axis=0)
        for v in range(4):
            stacked.append(column[2 * cin * v : 2 * cin * v + lanes])
    eye = one_hot((cout, cout), lambda r: r)
    tiles = dot_nt(eye, jnp.concatenate(stacked, axis=0)).astype(bf16)
    empty = jnp.zeros((cout, lanes), bf16)
    for j in range(ks):
        for t in range(tout):
            for q in range(k_in // lanes):
                v = 2 * q - t + 2
                at = (j * 4 + v) * lanes
                tile = tiles[:, at : at + lanes] if 0 <= v < 4 else empty
                w_ref[j, cout * t : cout * (t + 1), lanes * q : lanes * (q + 1)] = tile
    sig_copy.wait()
    split = one_hot_columns((2 * lanes, 2 * lanes), lambda q: 2 * (q % lanes) + q // lanes)
    parts = [dot(sig_ref[:, b : b + 2 * lanes], split) for b in range(0, 2 * half, 2 * lanes)]
    apart = jnp.concatenate([p[:, :lanes] for p in parts] + [p[:, lanes:] for p in parts], axis=1)
    to_time = one_hot((k_in, k_in), lambda r: (r % cin) * tin + r // cin)
    z = dot(to_time, apart.astype(bf16)).astype(bf16)
    z_ref[...] = z
    even, odd = z[:, :half], z[:, half:]
    left = dot(w_ref[0], even) + dot(w_ref[1], odd)
    right = dot(w_ref[4], even)
    lane = iota((k_out, half), 1)
    own = (
        dot(w_ref[2], even)
        + dot(w_ref[3], odd)
        + jnp.where(lane == 0, 0.0, pltpu.roll(left, 1, 1))
        + jnp.where(lane == half - 1, 0.0, pltpu.roll(right, half - 1, 1))
    )
    high = own.astype(bf16)
    rest = (own - high.astype(f32)).astype(bf16)
    left_edge, right_edge = left[:, half - lanes :], right[:, :lanes]
    left_high, right_high = left_edge.astype(bf16), right_edge.astype(bf16)
    left_rest = (left_edge - left_high.astype(f32)).astype(bf16)
    right_rest = (right_edge - right_high.astype(f32)).astype(bf16)

    def pick(row, column, tile):
        at = (iota((edge_rows, lanes), 0) == row) & (iota((edge_rows, lanes), 1) == column)
        return dot_nt(at.astype(f32).astype(bf16), tile)

    edges = (
        pick(0, 0, rest[:, :lanes])
        + pick(1, lanes - 1, rest[:, half - lanes :])
        + pick(2, lanes - 1, left_high)
        + pick(3, lanes - 1, left_rest)
        + pick(4, 0, right_high)
        + pick(5, 0, right_rest)
    ).astype(bf16)
    to_channel = one_hot((k_out, k_out), lambda r: (r % tout) * cout + r // tout)
    edges = dot_nt(edges, to_channel)
    main = dot(to_channel, high).astype(bf16)
    cot_copy.wait()
    for d in range(count):
        for b in range(half // lanes):
            at = slice(lanes * b, lanes * (b + 1))
            out_ref[d, rows * b : rows * (b + 1)] = main[rows * d : rows * (d + 1), at]
            low = rows * (half // lanes + b)
            out_ref[d, low : low + rows] = cot_ref[d, :, at]
        low = 2 * rows * (half // lanes)
        out_ref[d, low:] = jnp.zeros((edge_rows, lanes), bf16)
        out_ref[d, low:, :rows] = edges[:, rows * d : rows * (d + 1)].astype(bf16)


def transform(real, imag, sign):
    size = len(real)
    if size == 1:
        return (list(real), [None] if imag is None else list(imag))
    even_re, even_im = transform(real[0::2], None if imag is None else imag[0::2], sign)
    odd_re, odd_im = transform(real[1::2], None if imag is None else imag[1::2], sign)
    out_re, out_im = [None] * size, [None] * size

    def plus(a, b):
        return b if a is None else (a if b is None else a + b)

    def minus(a, b):
        return a if b is None else (-b if a is None else a - b)

    for k in range(size // 2):
        re, im = odd_re[k], odd_im[k]
        if k == 0:
            tr, ti = re, im
        elif 4 * k == size:
            tr = None if im is None else (im if sign < 0 else -im)
            ti = -re if sign < 0 else re
        else:
            c, s = math.cos(2 * math.pi * k / size), sign * math.sin(2 * math.pi * k / size)
            if im is None:
                tr, ti = c * re, s * re
            elif 8 * k == size:
                tr, ti = (c * (re - im), c * (re + im)) if sign > 0 else (c * (re + im), c * (im - re))
            elif 8 * k == 3 * size:
                tr, ti = (c * (re + im), c * (im - re)) if sign > 0 else (c * (re - im), c * (re + im))
            else:
                tr, ti = c * re - s * im, s * re + c * im
        out_re[k], out_im[k] = plus(even_re[k], tr), plus(even_im[k], ti)
        out_re[k + size // 2], out_im[k + size // 2] = minus(even_re[k], tr), minus(even_im[k], ti)
    return out_re, out_im


def gelu_slope(v):
    return 0.5 * (1.0 + lax.erf(v * inv_root_two)) + v * jnp.exp(-0.5 * v * v) * inv_root_tau


def filter_kernel(
    dims, cols_ref, resp_ref, twist_ref, high_ref, rest_ref,
    out_ref, fgrad_ref, x_ref, y_ref, spec_ref, grad_ref,
):
    count, channels, tout, width = dims
    rows = channels * tout
    scale = 1.0 / (count * width)
    edge_row, edge_col = iota((edge_rows, width), 0), iota((edge_rows, width), 1)
    to_low = (edge_col == 0) & ((edge_row == 0) | (edge_row == 2) | (edge_row == 3))
    to_high = (edge_col == width - 1) & ((edge_row == 1) | (edge_row == 4) | (edge_row == 5))
    spread = (to_low | to_high).astype(f32).astype(bf16)
    low = 2 * rows * (width // lanes)
    edges = [cols_ref[d, low:, :rows].astype(f32) for d in range(count)]
    none = jnp.zeros((edge_rows, rows), f32)
    kind = iota((edge_rows, rows), 0)
    for d in range(count):
        before = edges[d - 1] if d > 0 else none
        after = edges[d + 1] if d < count - 1 else none
        joined = jnp.where(kind < 2, edges[d], jnp.where(kind < 4, before, after))
        blocks = [cols_ref[d, rows * b : rows * (b + 1)] for b in range(width // lanes)]
        whole = jnp.concatenate(blocks, axis=1).astype(f32) + dot_tn(joined.astype(bf16), spread)
        x_ref[d] = whole.astype(bf16).astype(f32)

    def forward_planes(planes, r, h):
        re, im = transform(planes, None, -1)
        for k in range(count):
            c = twist_ref[0, k : k + 1, h : h + lanes]
            s = twist_ref[1, k : k + 1, h : h + lanes]
            at = pl.ds(k * rows + r, tout)
            if k == 0:
                y_ref[at, h : h + lanes] = re[k]
                y_ref[at, width + h : width + h + lanes] = jnp.zeros_like(re[k]) if im[k] is None else im[k]
            elif im[k] is None:
                y_ref[at, h : h + lanes] = re[k] * c
                y_ref[at, width + h : width + h + lanes] = -(re[k] * s)
            else:
                y_ref[at, h : h + lanes] = re[k] * c + im[k] * s
                y_ref[at, width + h : width + h + lanes] = im[k] * c - re[k] * s

    def backward_planes(r, h):
        re, im = [], []
        for k in range(count):
            c = twist_ref[0, k : k + 1, h : h + lanes]
            s = twist_ref[1, k : k + 1, h : h + lanes]
            at = pl.ds(k * rows + r, tout)
            a, b = y_ref[at, h : h + lanes], y_ref[at, width + h : width + h + lanes]
            re.append(a * c - b * s if k else a)
            im.append(b * c + a * s if k else b)
        return transform(re, im, 1)[0]

    def halves(v):
        high = v.astype(bf16)
        return high, (v - high.astype(f32)).astype(bf16)

    def inner(product):
        high, rest = halves(y_ref[...])
        return (
            product(high, high_ref[...]) + product(rest, high_ref[...]) + product(high, rest_ref[...])
        )

    chunks = [(r * tout, h) for r in range(channels) for h in range(0, width, lanes)]
    for r, h in chunks:
        forward_planes([x_ref[d, r : r + tout, h : h + lanes] for d in range(count)], r, h)
    spec_ref[...] = inner(dot)
    for k in range(count):
        for ch in range(channels):
            at = pl.ds(k * rows + ch * tout, tout)
            sr, si = spec_ref[at, :width], spec_ref[at, width:]
            rr, ri = resp_ref[0, ch, k : k + 1], resp_ref[1, ch, k : k + 1]
            y_ref[at, :width] = rr * sr - ri * si
            y_ref[at, width:] = rr * si + ri * sr
    y_ref[...] = inner(dot_nt)
    for r, h in chunks:
        planes = backward_planes(r, h)
        at = rows * (width + h) // lanes + r
        slopes = [
            cols_ref[d, at : at + tout].astype(f32) * gelu_slope(planes[d]) for d in range(count)
        ]
        forward_planes(slopes, r, h)
    grad_ref[...] = inner(dot)
    for k in range(count):
        for ch in range(channels):
            at = pl.ds(k * rows + ch * tout, tout)
            sr, si = spec_ref[at, :width], spec_ref[at, width:]
            gr, gi = grad_ref[at, :width], grad_ref[at, width:]
            rr, ri = resp_ref[0, ch, k : k + 1], resp_ref[1, ch, k : k + 1]
            fgrad_ref[0, ch, k : k + 1] = jnp.sum(sr * gr + si * gi, axis=0, keepdims=True) * scale
            fgrad_ref[1, ch, k : k + 1] = jnp.sum(sr * gi - si * gr, axis=0, keepdims=True) * scale
            y_ref[at, :width] = rr * gr + ri * gi
            y_ref[at, width:] = rr * gi - ri * gr
    y_ref[...] = inner(dot_nt)
    for r, h in chunks:
        planes = backward_planes(r, h)
        for d in range(count):
            x_ref[d, r : r + tout, h : h + lanes] = planes[d]
    last = ((iota((edge_rows, lanes), 0) == 0) & (iota((edge_rows, lanes), 1) == lanes - 1)).astype(f32).astype(bf16)
    first = ((iota((edge_rows, lanes), 0) == 1) & (iota((edge_rows, lanes), 1) == 0)).astype(f32).astype(bf16)
    for d in range(count):
        for b in range(width // lanes):
            out_ref[d, rows * b : rows * (b + 1)] = x_ref[d, :, lanes * b : lanes * (b + 1)].astype(bf16)
        low = rows * (width // lanes)
        out_ref[d, low:] = jnp.zeros((edge_rows, lanes), bf16)
        edge = none
        if d > 0:
            edge = edge + dot_nt(last, x_ref[d - 1, :, width - lanes :].astype(bf16))
        if d < count - 1:
            edge = edge + dot_nt(first, x_ref[d + 1, :, :lanes].astype(bf16))
        out_ref[d, low:, :rows] = edge.astype(bf16)


def tap_kernel(dims, grad_ref, z_ref, tap_ref, shifted_ref, g_ref, zp_ref):
    cin, tin, cout, tout, ks, count, rows = dims
    half = zp_ref.shape[1] // 2
    k_out = cout * tout
    row, col = iota((edge_rows, lanes), 0), iota((edge_rows, lanes), 1)
    spread = (((row == 1) & (col == 0)) | ((row == 0) & (col == 1))).astype(f32).astype(bf16)
    for d in range(count):
        at = slice(rows * d, rows * (d + 1))
        for b in range(half // lanes):
            g_ref[at, lanes * b : lanes * (b + 1)] = grad_ref[d, rows * b : rows * (b + 1)].astype(f32)
        g_ref[at, half:] = dot_tn(grad_ref[d, rows * (half // lanes) :, :rows], spread)
    to_time = one_hot((k_out, k_out), lambda r: (r % cout) * tout + r // cout)
    g = dot(to_time, g_ref[...].astype(bf16)).astype(bf16)
    wide = half + lanes
    later = one_hot_columns((wide, half), lambda n: n + 1)
    sooner = one_hot_columns((wide, half), lambda n: jnp.where(n == 0, half + 1, n - 1))
    shifted_ref[0] = dot(g, later).astype(bf16)
    shifted_ref[1] = g[:, :half]
    shifted_ref[2] = dot(g, sooner).astype(bf16)
    k_in = cin * tin
    pad = 2 * cin
    zp_ref[:pad] = jnp.zeros((pad, 2 * half), bf16)
    zp_ref[pad + k_in :] = jnp.zeros((zp_ref.shape[0] - pad - k_in, 2 * half), bf16)
    zp_ref[pad : pad + k_in] = z_ref[...]
    both, lone = None, None
    for t in range(tout):
        at = slice(cout * t, cout * (t + 1))
        band = zp_ref[2 * cin * t : 2 * cin * t + ks * cin]
        pair = jnp.concatenate([shifted_ref[0, at], shifted_ref[1, at]], axis=0)
        even, odd = band[:, :half], band[:, half:]
        term = jnp.concatenate([dot_nt(even, pair), dot_nt(odd, pair)], axis=0)
        both = term if both is None else both + term
        blank = jnp.zeros((cout, half), bf16)
        mid = ks * cin // 2
        term = dot_nt(even[:mid], jnp.concatenate([shifted_ref[2, at], blank], axis=0)) + dot_nt(
            even[mid:], jnp.concatenate([blank, shifted_ref[2, at]], axis=0)
        )
        lone = term if lone is None else lone + term
    top = both.shape[0]
    tap_ref[:top] = both
    tap_ref[top : top + lone.shape[0]] = lone
    tap_ref[top + lone.shape[0] :] = jnp.zeros((tap_ref.shape[0] - top - lone.shape[0], lanes), f32)


def input_kernel(dims, shifted_ref, taps_ref, out_ref, w_ref):
    cin, tin, cout, tout, ks, count, rows = dims
    k_in = cin * tin
    half = shifted_ref.shape[2]
    blank = jnp.zeros((cin, cout), bf16)
    firsts, seconds = [], []
    for j in range(ks):
        for i in range(ks + 2):
            firsts.append(taps_ref[i, j] if i < ks else blank)
            seconds.append(taps_ref[i - 2, j] if i >= 2 else blank)
    to_first = one_hot((cout, lanes), lambda r: r)
    to_second = one_hot((cout, lanes), lambda r: r + cout)
    tiles = (
        dot(jnp.concatenate(firsts, axis=0), to_first) + dot(jnp.concatenate(seconds, axis=0), to_second)
    ).astype(bf16)
    empty = jnp.zeros((cin, lanes), bf16)
    for j in range(ks):
        for s in range(tin):
            for q in range(cout * tout // lanes):
                i = s - 4 * q + 2
                at = (j * (ks + 2) + i) * cin
                tile = tiles[at : at + cin] if 0 <= i < ks + 2 else empty
                w_ref[j, cin * s : cin * (s + 1), lanes * q : lanes * (q + 1)] = tile
    later, same, sooner = shifted_ref[0], shifted_ref[1], shifted_ref[2]
    even = dot(w_ref[0], later) + dot(w_ref[2], same) + dot(w_ref[4], sooner)
    odd = dot(w_ref[1], later) + dot(w_ref[3], same)
    both = jnp.concatenate([even.astype(bf16), odd.astype(bf16)], axis=1)
    to_channel = one_hot((k_in, k_in), lambda r: (r % tin) * cin + r // tin)
    both = dot(to_channel, both).astype(bf16)
    merge = one_hot((2 * lanes, 2 * lanes), lambda r: 2 * (r % lanes) + r // lanes)
    for b in range(half // lanes):
        part = jnp.concatenate(
            [both[:, lanes * b : lanes * (b + 1)], both[:, half + lanes * b : half + lanes * (b + 1)]], axis=1
        )
        out_ref[:, 2 * lanes * b : 2 * lanes * (b + 1)] = dot(part, merge).astype(bf16)


def unpack_kernel(dims, scale, tap_ref, out_ref):
    cin, tin, cout, tout, ks, count, rows = dims
    band = ks * cin
    for i in range(ks):
        at = slice(cin * i, cin * (i + 1))
        even, odd = tap_ref[at] * scale, tap_ref[band + cin * i : band + cin * (i + 1)] * scale
        out_ref[i, 0] = even[:, :cout]
        out_ref[i, 2] = even[:, cout:]
        out_ref[i, 1] = odd[:, :cout]
        out_ref[i, 3] = odd[:, cout:]
        for c in range(0, cin, 8):
            at = cin * i + c
            low = at < band // 2
            packed = tap_ref[2 * band + at % (band // 2) : 2 * band + at % (band // 2) + 8] * scale
            out_ref[i, 4, c : c + 8] = packed[:, :cout] if low else packed[:, cout:]


def summed_over(rows, axis, beside):
    count = lax.axis_size(axis)
    index = lax.axis_index(axis)
    pairs = lambda step: [(i, i ^ step) for i in range(count)]
    halved = [step for step in (1, 2) if step < count]
    for step in halved:
        size = rows.shape[0] // 2
        bit = (index // step) % 2
        kept = lax.dynamic_slice_in_dim(rows, bit * size, size)
        sent = lax.dynamic_slice_in_dim(rows, (1 - bit) * size, size)
        rows = kept + lax.ppermute(sent, axis, pairs(step))
    rows, beside = lax.optimization_barrier((rows, beside))
    step = 2 * halved[-1] if halved else 1
    while step < count:
        rows = rows + lax.ppermute(rows, axis, pairs(step))
        step *= 2
    for step in reversed(halved):
        bit = (index // step) % 2
        other = lax.ppermute(rows, axis, pairs(step))
        rows = jnp.where(bit == 0, jnp.concatenate([rows, other]), jnp.concatenate([other, rows]))
    return rows, beside


def tables(count, width):
    inner = np.outer(np.arange(width), np.arange(width)) % width * (2.0 * np.pi / width)
    c, s = np.cos(inner), np.sin(inner)
    table = np.block([[c, -s], [s, c]]).astype(np.float32)
    high = table.astype(bf16)
    rest = (table - high.astype(np.float32)).astype(bf16)
    outer = np.outer(np.arange(count), np.arange(width)) * (2.0 * np.pi / (count * width))
    twist = np.stack([np.cos(outer), np.sin(outer)]).astype(np.float32)
    return twist, high, rest


def per_device(signal, conv_taps, response, cotangent):
    cin, tin, fibre_in = signal.shape
    cout, tout, width = cotangent.shape
    ks = conv_taps.shape[0]
    count = lax.axis_size("fibre")
    channels = cout // count
    rows = channels * tout
    waves = count * width
    tiles = width // lanes
    dims = (cin, tin, cout, tout, ks, count, rows)
    k_in, k_out = cin * tin, cout * tout
    taps = jnp.swapaxes(conv_taps, 2, 3)
    shape = jax.ShapeDtypeStruct
    conv_part, z = call(
        functools.partial(conv_kernel, dims),
        [
            shape((count, 2 * rows * tiles + edge_rows, lanes), bf16),
            shape((k_in, fibre_in), bf16),
        ],
        [
            pltpu.VMEM((ks, k_out, k_in), bf16),
            pltpu.VMEM((k_in, fibre_in), bf16),
            pltpu.VMEM((count, rows, width), bf16),
            pltpu.SemaphoreType.DMA((2,)),
        ],
        2e9,
        (signal.reshape(k_in, fibre_in), cotangent.reshape(count, rows, width), taps),
        left=(0, 1),
        room=60,
    )
    cols = lax.all_to_all(conv_part, "fibre", split_axis=0, concat_axis=0, tiled=True)
    arranged = (response * (1.0 / waves)).reshape(2, channels, width, count).transpose(0, 1, 3, 2)
    twist, high, rest = tables(count, width)
    big = count * rows
    grad_part, fgrad = call(
        functools.partial(filter_kernel, (count, channels, tout, width)),
        [
            shape((count, rows * tiles + edge_rows, lanes), bf16),
            shape((2, channels, count, width), f32),
        ],
        [
            pltpu.VMEM((count, rows, width), f32),
            pltpu.VMEM((big, 2 * width), f32),
            pltpu.VMEM((big, 2 * width), f32),
            pltpu.VMEM((big, 2 * width), f32),
        ],
        6e9,
        (cols, arranged, jnp.asarray(twist), jnp.asarray(high), jnp.asarray(rest)),
    )
    filter_grad = fgrad.transpose(0, 1, 3, 2).reshape(2, channels, waves)
    grad_cols = lax.all_to_all(grad_part, "fibre", split_axis=0, concat_axis=0, tiled=True)
    grad_cols, filter_grad = lax.optimization_barrier((grad_cols, filter_grad))
    taps_part, shifted = call(
        functools.partial(tap_kernel, dims),
        [shape((tap_rows, lanes), f32), shape((3, k_out, width), bf16)],
        [pltpu.VMEM((k_out, width + lanes), f32), pltpu.VMEM((k_in + 4 * cin, fibre_in), bf16)],
        1e9,
        (grad_cols, z),
    )
    (input_grad,) = call(
        functools.partial(input_kernel, dims),
        [shape((k_in, fibre_in), bf16)],
        [pltpu.VMEM((ks, k_in, k_out), bf16)],
        2e9,
        (shifted, taps),
    )
    total, input_grad = summed_over(taps_part, "fibre", input_grad)
    (tap_grad,) = call(
        functools.partial(unpack_kernel, dims, 1.0 / math.sqrt(tout * waves)),
        [shape((ks, ks, cin, cout), f32)],
        [],
        1e6,
        (total,),
    )
    return (input_grad.reshape(signal.shape), jnp.swapaxes(tap_grad, 2, 3), filter_grad)


def solution(mesh):
    in_specs = (P("parts", None, "fibre"), P(), P(None, "fibre", None), P("parts", None, "fibre"))
    out_specs = (P("parts", None, "fibre"), P("parts", None, None, None), P("parts", "fibre", None))
    return jax.shard_map(
        per_device, mesh=mesh, in_specs=in_specs, out_specs=out_specs, check_vma=False
    )
```

```python
import functools
import math

import jax
import jax.numpy as jnp
import numpy as np
from jax import lax
from jax.experimental import pallas as pl
from jax.experimental.pallas import tpu as pltpu
from jax.sharding import PartitionSpec as P

bf16 = jnp.bfloat16
f32 = jnp.float32
inv_root_two = 1.0 / math.sqrt(2.0)
inv_root_tau = 1.0 / math.sqrt(2.0 * math.pi)
lanes = 128
edge_rows = 8
tap_rows = 416


def dot(a, b):
    return jnp.dot(a, b, preferred_element_type=f32)


def dot_nt(a, b):
    return lax.dot_general(a, b, (((1,), (1,)), ((), ())), preferred_element_type=f32)


def dot_tn(a, b):
    return lax.dot_general(a, b, (((0,), (0,)), ((), ())), preferred_element_type=f32)


def iota(shape, dim):
    return lax.broadcasted_iota(jnp.int32, shape, dim)


def split_index(x, size):
    if size & (size - 1):
        return x // size, x % size
    return lax.shift_right_logical(x, jnp.full_like(x, size.bit_length() - 1)), x & (size - 1)


def swapped(x, outer, inner):
    a, b = split_index(x, inner)
    return b * outer + a


def one_hot(shape, column_of_row):
    return (iota(shape, 1) == column_of_row(iota((shape[0], 1), 0))).astype(f32).astype(bf16)


def one_hot_columns(shape, row_of_column):
    return (iota(shape, 0) == row_of_column(iota((1, shape[1]), 1))).astype(f32).astype(bf16)


def call(kernel, outs, scratch, flops, args, left=(), room=48):
    moved = sum(a.size * a.dtype.itemsize for a in list(args) + list(outs))
    return pl.pallas_call(
        kernel,
        out_shape=outs,
        in_specs=[
            pl.BlockSpec(memory_space=pltpu.HBM if a in left else pltpu.VMEM) for a in range(len(args))
        ],
        out_specs=[pl.BlockSpec(memory_space=pltpu.VMEM)] * len(outs),
        scratch_shapes=scratch,
        compiler_params=pltpu.CompilerParams(vmem_limit_bytes=room << 20),
        cost_estimate=pl.CostEstimate(flops=int(flops), bytes_accessed=moved, transcendentals=0),
    )(*args)


def conv_kernel(dims, sig_hbm, cot_hbm, taps_ref, out_ref, z_ref, w_ref, sig_ref, cot_ref, sem):
    cin, tin, cout, tout, ks, count, rows = dims
    k_in, k_out = cin * tin, cout * tout
    half = sig_ref.shape[1] // 2
    sig_copy = pltpu.make_async_copy(sig_hbm, sig_ref, sem.at[0])
    cot_copy = pltpu.make_async_copy(cot_hbm, cot_ref, sem.at[1])
    sig_copy.start()
    cot_copy.start()
    blank = jnp.zeros((2 * cin, cout), bf16)
    stacked = []
    for j in range(ks):
        column = jnp.concatenate([blank] + [taps_ref[i, j] for i in range(ks)] + [blank, blank], axis=0)
        for v in range(4):
            stacked.append(column[2 * cin * v : 2 * cin * v + lanes])
    eye = one_hot((cout, cout), lambda r: r)
    tiles = dot_nt(eye, jnp.concatenate(stacked, axis=0)).astype(bf16)
    empty = jnp.zeros((cout, lanes), bf16)
    for j in range(ks):
        for t in range(tout):
            for q in range(k_in // lanes):
                v = 2 * q - t + 2
                at = (j * 4 + v) * lanes
                tile = tiles[:, at : at + lanes] if 0 <= v < 4 else empty
                w_ref[j, cout * t : cout * (t + 1), lanes * q : lanes * (q + 1)] = tile
    sig_copy.wait()
    split = one_hot_columns((2 * lanes, 2 * lanes), lambda q: swapped(q, 2, lanes))
    parts = [dot(sig_ref[:, b : b + 2 * lanes], split) for b in range(0, 2 * half, 2 * lanes)]
    apart = jnp.concatenate([p[:, :lanes] for p in parts] + [p[:, lanes:] for p in parts], axis=1)
    to_time = one_hot((k_in, k_in), lambda r: swapped(r, tin, cin))
    z = dot(to_time, apart.astype(bf16)).astype(bf16)
    z_ref[...] = z
    even, odd = z[:, :half], z[:, half:]
    left = dot(w_ref[0], even) + dot(w_ref[1], odd)
    right = dot(w_ref[4], even)
    lane = iota((k_out, half), 1)
    own = (
        dot(w_ref[2], even)
        + dot(w_ref[3], odd)
        + jnp.where(lane == 0, 0.0, pltpu.roll(left, 1, 1))
        + jnp.where(lane == half - 1, 0.0, pltpu.roll(right, half - 1, 1))
    )
    high = own.astype(bf16)
    rest = (own - high.astype(f32)).astype(bf16)
    left_edge, right_edge = left[:, half - lanes :], right[:, :lanes]
    left_high, right_high = left_edge.astype(bf16), right_edge.astype(bf16)
    left_rest = (left_edge - left_high.astype(f32)).astype(bf16)
    right_rest = (right_edge - right_high.astype(f32)).astype(bf16)

    def pick(row, column, tile):
        at = (iota((edge_rows, lanes), 0) == row) & (iota((edge_rows, lanes), 1) == column)
        return dot_nt(at.astype(f32).astype(bf16), tile)

    edges = (
        pick(0, 0, rest[:, :lanes])
        + pick(1, lanes - 1, rest[:, half - lanes :])
        + pick(2, lanes - 1, left_high)
        + pick(3, lanes - 1, left_rest)
        + pick(4, 0, right_high)
        + pick(5, 0, right_rest)
    ).astype(bf16)
    to_channel = one_hot((k_out, k_out), lambda r: swapped(r, cout, tout))
    edges = dot_nt(edges, to_channel)
    main = dot(to_channel, high).astype(bf16)
    cot_copy.wait()
    for d in range(count):
        for b in range(half // lanes):
            at = slice(lanes * b, lanes * (b + 1))
            out_ref[d, rows * b : rows * (b + 1)] = main[rows * d : rows * (d + 1), at]
            low = rows * (half // lanes + b)
            out_ref[d, low : low + rows] = cot_ref[d, :, at]
        low = 2 * rows * (half // lanes)
        out_ref[d, low:] = jnp.zeros((edge_rows, lanes), bf16)
        out_ref[d, low:, :rows] = edges[:, rows * d : rows * (d + 1)].astype(bf16)


def transform(real, imag, sign):
    size = len(real)
    if size == 1:
        return (list(real), [None] if imag is None else list(imag))
    even_re, even_im = transform(real[0::2], None if imag is None else imag[0::2], sign)
    odd_re, odd_im = transform(real[1::2], None if imag is None else imag[1::2], sign)
    out_re, out_im = [None] * size, [None] * size

    def plus(a, b):
        return b if a is None else (a if b is None else a + b)

    def minus(a, b):
        return a if b is None else (-b if a is None else a - b)

    for k in range(size // 2):
        re, im = odd_re[k], odd_im[k]
        if k == 0:
            tr, ti = re, im
        elif 4 * k == size:
            tr = None if im is None else (im if sign < 0 else -im)
            ti = -re if sign < 0 else re
        else:
            c, s = math.cos(2 * math.pi * k / size), sign * math.sin(2 * math.pi * k / size)
            if im is None:
                tr, ti = c * re, s * re
            elif 8 * k == size:
                tr, ti = (c * (re - im), c * (re + im)) if sign > 0 else (c * (re + im), c * (im - re))
            elif 8 * k == 3 * size:
                tr, ti = (c * (re + im), c * (im - re)) if sign > 0 else (c * (re - im), c * (re + im))
            else:
                tr, ti = c * re - s * im, s * re + c * im
        out_re[k], out_im[k] = plus(even_re[k], tr), plus(even_im[k], ti)
        out_re[k + size // 2], out_im[k + size // 2] = minus(even_re[k], tr), minus(even_im[k], ti)
    return out_re, out_im


def gelu_slope(v):
    return 0.5 * (1.0 + lax.erf(v * inv_root_two)) + v * jnp.exp(-0.5 * v * v) * inv_root_tau


def filter_kernel(
    dims, cols_ref, resp_ref, twist_ref, high_ref, rest_ref,
    out_ref, fgrad_ref, x_ref, y_ref, spec_ref, grad_ref,
):
    count, channels, tout, width = dims
    rows = channels * tout
    scale = 1.0 / (count * width)
    edge_row, edge_col = iota((edge_rows, width), 0), iota((edge_rows, width), 1)
    to_low = (edge_col == 0) & ((edge_row == 0) | (edge_row == 2) | (edge_row == 3))
    to_high = (edge_col == width - 1) & ((edge_row == 1) | (edge_row == 4) | (edge_row == 5))
    spread = (to_low | to_high).astype(f32).astype(bf16)
    low = 2 * rows * (width // lanes)
    edges = [cols_ref[d, low:, :rows].astype(f32) for d in range(count)]
    none = jnp.zeros((edge_rows, rows), f32)
    kind = iota((edge_rows, rows), 0)
    for d in range(count):
        before = edges[d - 1] if d > 0 else none
        after = edges[d + 1] if d < count - 1 else none
        joined = jnp.where(kind < 2, edges[d], jnp.where(kind < 4, before, after))
        blocks = [cols_ref[d, rows * b : rows * (b + 1)] for b in range(width // lanes)]
        whole = jnp.concatenate(blocks, axis=1).astype(f32) + dot_tn(joined.astype(bf16), spread)
        x_ref[d] = whole.astype(bf16).astype(f32)

    def forward_planes(planes, r, h):
        re, im = transform(planes, None, -1)
        for k in range(count):
            c = twist_ref[0, k : k + 1, h : h + lanes]
            s = twist_ref[1, k : k + 1, h : h + lanes]
            at = pl.ds(k * rows + r, tout)
            if k == 0:
                y_ref[at, h : h + lanes] = re[k]
                y_ref[at, width + h : width + h + lanes] = jnp.zeros_like(re[k]) if im[k] is None else im[k]
            elif im[k] is None:
                y_ref[at, h : h + lanes] = re[k] * c
                y_ref[at, width + h : width + h + lanes] = -(re[k] * s)
            else:
                y_ref[at, h : h + lanes] = re[k] * c + im[k] * s
                y_ref[at, width + h : width + h + lanes] = im[k] * c - re[k] * s

    def backward_planes(r, h):
        re, im = [], []
        for k in range(count):
            c = twist_ref[0, k : k + 1, h : h + lanes]
            s = twist_ref[1, k : k + 1, h : h + lanes]
            at = pl.ds(k * rows + r, tout)
            a, b = y_ref[at, h : h + lanes], y_ref[at, width + h : width + h + lanes]
            re.append(a * c - b * s if k else a)
            im.append(b * c + a * s if k else b)
        return transform(re, im, 1)[0]

    def halves(v):
        high = v.astype(bf16)
        return high, (v - high.astype(f32)).astype(bf16)

    def inner(product):
        high, rest = halves(y_ref[...])
        return (
            product(high, high_ref[...]) + product(rest, high_ref[...]) + product(high, rest_ref[...])
        )

    chunks = [(r * tout, h) for r in range(channels) for h in range(0, width, lanes)]
    for r, h in chunks:
        forward_planes([x_ref[d, r : r + tout, h : h + lanes] for d in range(count)], r, h)
    spec_ref[...] = inner(dot)
    for k in range(count):
        for ch in range(channels):
            at = pl.ds(k * rows + ch * tout, tout)
            sr, si = spec_ref[at, :width], spec_ref[at, width:]
            rr, ri = resp_ref[0, ch, k : k + 1], resp_ref[1, ch, k : k + 1]
            y_ref[at, :width] = rr * sr - ri * si
            y_ref[at, width:] = rr * si + ri * sr
    y_ref[...] = inner(dot_nt)
    for r, h in chunks:
        planes = backward_planes(r, h)
        at = rows * (width + h) // lanes + r
        slopes = [
            cols_ref[d, at : at + tout].astype(f32) * gelu_slope(planes[d]) for d in range(count)
        ]
        forward_planes(slopes, r, h)
    grad_ref[...] = inner(dot)
    for k in range(count):
        for ch in range(channels):
            at = pl.ds(k * rows + ch * tout, tout)
            sr, si = spec_ref[at, :width], spec_ref[at, width:]
            gr, gi = grad_ref[at, :width], grad_ref[at, width:]
            rr, ri = resp_ref[0, ch, k : k + 1], resp_ref[1, ch, k : k + 1]
            fgrad_ref[0, ch, k : k + 1] = jnp.sum(sr * gr + si * gi, axis=0, keepdims=True) * scale
            fgrad_ref[1, ch, k : k + 1] = jnp.sum(sr * gi - si * gr, axis=0, keepdims=True) * scale
            y_ref[at, :width] = rr * gr + ri * gi
            y_ref[at, width:] = rr * gi - ri * gr
    y_ref[...] = inner(dot_nt)
    for r, h in chunks:
        planes = backward_planes(r, h)
        for d in range(count):
            x_ref[d, r : r + tout, h : h + lanes] = planes[d]
    last = ((iota((edge_rows, lanes), 0) == 0) & (iota((edge_rows, lanes), 1) == lanes - 1)).astype(f32).astype(bf16)
    first = ((iota((edge_rows, lanes), 0) == 1) & (iota((edge_rows, lanes), 1) == 0)).astype(f32).astype(bf16)
    for d in range(count):
        for b in range(width // lanes):
            out_ref[d, rows * b : rows * (b + 1)] = x_ref[d, :, lanes * b : lanes * (b + 1)].astype(bf16)
        low = rows * (width // lanes)
        out_ref[d, low:] = jnp.zeros((edge_rows, lanes), bf16)
        edge = none
        if d > 0:
            edge = edge + dot_nt(last, x_ref[d - 1, :, width - lanes :].astype(bf16))
        if d < count - 1:
            edge = edge + dot_nt(first, x_ref[d + 1, :, :lanes].astype(bf16))
        out_ref[d, low:, :rows] = edge.astype(bf16)


def tap_kernel(dims, grad_ref, z_ref, tap_ref, shifted_ref, g_ref, zp_ref):
    cin, tin, cout, tout, ks, count, rows = dims
    half = zp_ref.shape[1] // 2
    k_out = cout * tout
    row, col = iota((edge_rows, lanes), 0), iota((edge_rows, lanes), 1)
    spread = (((row == 1) & (col == 0)) | ((row == 0) & (col == 1))).astype(f32).astype(bf16)
    for d in range(count):
        at = slice(rows * d, rows * (d + 1))
        for b in range(half // lanes):
            g_ref[at, lanes * b : lanes * (b + 1)] = grad_ref[d, rows * b : rows * (b + 1)].astype(f32)
        g_ref[at, half:] = dot_tn(grad_ref[d, rows * (half // lanes) :, :rows], spread)
    to_time = one_hot((k_out, k_out), lambda r: swapped(r, tout, cout))
    g = dot(to_time, g_ref[...].astype(bf16)).astype(bf16)
    wide = half + lanes
    later = one_hot_columns((wide, half), lambda n: n + 1)
    sooner = one_hot_columns((wide, half), lambda n: jnp.where(n == 0, half + 1, n - 1))
    shifted_ref[0] = dot(g, later).astype(bf16)
    shifted_ref[1] = g[:, :half]
    shifted_ref[2] = dot(g, sooner).astype(bf16)
    k_in = cin * tin
    pad = 2 * cin
    zp_ref[:pad] = jnp.zeros((pad, 2 * half), bf16)
    zp_ref[pad + k_in :] = jnp.zeros((zp_ref.shape[0] - pad - k_in, 2 * half), bf16)
    zp_ref[pad : pad + k_in] = z_ref[...]
    both, lone = None, None
    for t in range(tout):
        at = slice(cout * t, cout * (t + 1))
        band = zp_ref[2 * cin * t : 2 * cin * t + ks * cin]
        pair = jnp.concatenate([shifted_ref[0, at], shifted_ref[1, at]], axis=0)
        even, odd = band[:, :half], band[:, half:]
        term = jnp.concatenate([dot_nt(even, pair), dot_nt(odd, pair)], axis=0)
        both = term if both is None else both + term
        blank = jnp.zeros((cout, half), bf16)
        mid = ks * cin // 2
        term = dot_nt(even[:mid], jnp.concatenate([shifted_ref[2, at], blank], axis=0)) + dot_nt(
            even[mid:], jnp.concatenate([blank, shifted_ref[2, at]], axis=0)
        )
        lone = term if lone is None else lone + term
    top = both.shape[0]
    tap_ref[:top] = both
    tap_ref[top : top + lone.shape[0]] = lone
    tap_ref[top + lone.shape[0] :] = jnp.zeros((tap_ref.shape[0] - top - lone.shape[0], lanes), f32)


def input_kernel(dims, shifted_ref, taps_ref, out_ref, w_ref):
    cin, tin, cout, tout, ks, count, rows = dims
    k_in = cin * tin
    half = shifted_ref.shape[2]
    blank = jnp.zeros((cin, cout), bf16)
    firsts, seconds = [], []
    for j in range(ks):
        for i in range(ks + 2):
            firsts.append(taps_ref[i, j] if i < ks else blank)
            seconds.append(taps_ref[i - 2, j] if i >= 2 else blank)
    to_first = one_hot((cout, lanes), lambda r: r)
    to_second = one_hot((cout, lanes), lambda r: r + cout)
    tiles = (
        dot(jnp.concatenate(firsts, axis=0), to_first) + dot(jnp.concatenate(seconds, axis=0), to_second)
    ).astype(bf16)
    empty = jnp.zeros((cin, lanes), bf16)
    for j in range(ks):
        for s in range(tin):
            for q in range(cout * tout // lanes):
                i = s - 4 * q + 2
                at = (j * (ks + 2) + i) * cin
                tile = tiles[at : at + cin] if 0 <= i < ks + 2 else empty
                w_ref[j, cin * s : cin * (s + 1), lanes * q : lanes * (q + 1)] = tile
    later, same, sooner = shifted_ref[0], shifted_ref[1], shifted_ref[2]
    even = dot(w_ref[0], later) + dot(w_ref[2], same) + dot(w_ref[4], sooner)
    odd = dot(w_ref[1], later) + dot(w_ref[3], same)
    both = jnp.concatenate([even.astype(bf16), odd.astype(bf16)], axis=1)
    to_channel = one_hot((k_in, k_in), lambda r: swapped(r, cin, tin))
    both = dot(to_channel, both).astype(bf16)
    merge = one_hot((2 * lanes, 2 * lanes), lambda r: swapped(r, 2, lanes))
    for b in range(half // lanes):
        part = jnp.concatenate(
            [both[:, lanes * b : lanes * (b + 1)], both[:, half + lanes * b : half + lanes * (b + 1)]], axis=1
        )
        out_ref[:, 2 * lanes * b : 2 * lanes * (b + 1)] = dot(part, merge).astype(bf16)


def unpack_kernel(dims, scale, tap_ref, out_ref):
    cin, tin, cout, tout, ks, count, rows = dims
    band = ks * cin
    for i in range(ks):
        at = slice(cin * i, cin * (i + 1))
        even, odd = tap_ref[at] * scale, tap_ref[band + cin * i : band + cin * (i + 1)] * scale
        out_ref[i, 0] = even[:, :cout]
        out_ref[i, 2] = even[:, cout:]
        out_ref[i, 1] = odd[:, :cout]
        out_ref[i, 3] = odd[:, cout:]
        for c in range(0, cin, 8):
            at = cin * i + c
            low = at < band // 2
            packed = tap_ref[2 * band + at % (band // 2) : 2 * band + at % (band // 2) + 8] * scale
            out_ref[i, 4, c : c + 8] = packed[:, :cout] if low else packed[:, cout:]


def summed_over(rows, axis, beside):
    count = lax.axis_size(axis)
    bit = lax.axis_index(axis) % 2
    pairs = lambda step: [(i, i ^ step) for i in range(count)]
    size = rows.shape[0] // 2
    kept = lax.dynamic_slice_in_dim(rows, bit * size, size)
    sent = lax.dynamic_slice_in_dim(rows, (1 - bit) * size, size)
    rows = kept + lax.ppermute(sent, axis, pairs(1))
    step = 2
    while step < count:
        rounded = rows.astype(bf16)
        rows = rounded.astype(f32) + lax.ppermute(rounded, axis, pairs(step)).astype(f32)
        if step == 2:
            rows, beside = lax.optimization_barrier((rows, beside))
        step *= 2
    other = lax.ppermute(rows, axis, pairs(1))
    rows = jnp.where(bit == 0, jnp.concatenate([rows, other]), jnp.concatenate([other, rows]))
    return rows, beside


def tables(count, width):
    inner = np.outer(np.arange(width), np.arange(width)) % width * (2.0 * np.pi / width)
    c, s = np.cos(inner), np.sin(inner)
    table = np.block([[c, -s], [s, c]]).astype(np.float32)
    high = table.astype(bf16)
    rest = (table - high.astype(np.float32)).astype(bf16)
    outer = np.outer(np.arange(count), np.arange(width)) * (2.0 * np.pi / (count * width))
    twist = np.stack([np.cos(outer), np.sin(outer)]).astype(np.float32)
    return twist, high, rest


def per_device(signal, conv_taps, response, cotangent):
    cin, tin, fibre_in = signal.shape
    cout, tout, width = cotangent.shape
    ks = conv_taps.shape[0]
    count = lax.axis_size("fibre")
    channels = cout // count
    rows = channels * tout
    waves = count * width
    tiles = width // lanes
    dims = (cin, tin, cout, tout, ks, count, rows)
    k_in, k_out = cin * tin, cout * tout
    taps = jnp.swapaxes(conv_taps, 2, 3)
    shape = jax.ShapeDtypeStruct
    conv_part, z = call(
        functools.partial(conv_kernel, dims),
        [
            shape((count, 2 * rows * tiles + edge_rows, lanes), bf16),
            shape((k_in, fibre_in), bf16),
        ],
        [
            pltpu.VMEM((ks, k_out, k_in), bf16),
            pltpu.VMEM((k_in, fibre_in), bf16),
            pltpu.VMEM((count, rows, width), bf16),
            pltpu.SemaphoreType.DMA((2,)),
        ],
        2e9,
        (signal.reshape(k_in, fibre_in), cotangent.reshape(count, rows, width), taps),
        left=(0, 1),
        room=60,
    )
    cols = lax.all_to_all(conv_part, "fibre", split_axis=0, concat_axis=0, tiled=True)
    arranged = (response * (1.0 / waves)).reshape(2, channels, width, count).transpose(0, 1, 3, 2)
    twist, high, rest = tables(count, width)
    big = count * rows
    grad_part, fgrad = call(
        functools.partial(filter_kernel, (count, channels, tout, width)),
        [
            shape((count, rows * tiles + edge_rows, lanes), bf16),
            shape((2, channels, count, width), f32),
        ],
        [
            pltpu.VMEM((count, rows, width), f32),
            pltpu.VMEM((big, 2 * width), f32),
            pltpu.VMEM((big, 2 * width), f32),
            pltpu.VMEM((big, 2 * width), f32),
        ],
        6e9,
        (cols, arranged, jnp.asarray(twist), jnp.asarray(high), jnp.asarray(rest)),
    )
    filter_grad = fgrad.transpose(0, 1, 3, 2).reshape(2, channels, waves)
    grad_cols = lax.all_to_all(grad_part, "fibre", split_axis=0, concat_axis=0, tiled=True)
    grad_cols, filter_grad = lax.optimization_barrier((grad_cols, filter_grad))
    taps_part, shifted = call(
        functools.partial(tap_kernel, dims),
        [shape((tap_rows, lanes), f32), shape((3, k_out, width), bf16)],
        [pltpu.VMEM((k_out, width + lanes), f32), pltpu.VMEM((k_in + 4 * cin, fibre_in), bf16)],
        1e9,
        (grad_cols, z),
    )
    (input_grad,) = call(
        functools.partial(input_kernel, dims),
        [shape((k_in, fibre_in), bf16)],
        [pltpu.VMEM((ks, k_in, k_out), bf16)],
        2e9,
        (shifted, taps),
    )
    total, input_grad = summed_over(taps_part, "fibre", input_grad)
    (tap_grad,) = call(
        functools.partial(unpack_kernel, dims, 1.0 / math.sqrt(tout * waves)),
        [shape((ks, ks, cin, cout), f32)],
        [],
        1e6,
        (total,),
    )
    return (input_grad.reshape(signal.shape), jnp.swapaxes(tap_grad, 2, 3), filter_grad)


def solution(mesh):
    in_specs = (P("parts", None, "fibre"), P(), P(None, "fibre", None), P("parts", None, "fibre"))
    out_specs = (P("parts", None, "fibre"), P("parts", None, None, None), P("parts", "fibre", None))
    return jax.shard_map(
        per_device, mesh=mesh, in_specs=in_specs, out_specs=out_specs, check_vma=False
    )
```

```python
import functools
import math

import jax
import jax.numpy as jnp
import numpy as np
from jax import lax
from jax.experimental import pallas as pl
from jax.experimental.pallas import tpu as pltpu
from jax.sharding import PartitionSpec as P

bf16 = jnp.bfloat16
f32 = jnp.float32
inv_root_two = 1.0 / math.sqrt(2.0)
inv_root_tau = 1.0 / math.sqrt(2.0 * math.pi)
lanes = 128
edge_rows = 8
tap_rows = 416


def dot(a, b):
    return jnp.dot(a, b, preferred_element_type=f32)


def dot_nt(a, b):
    return lax.dot_general(a, b, (((1,), (1,)), ((), ())), preferred_element_type=f32)


def dot_tn(a, b):
    return lax.dot_general(a, b, (((0,), (0,)), ((), ())), preferred_element_type=f32)


def iota(shape, dim):
    return lax.broadcasted_iota(jnp.int32, shape, dim)


def split_index(x, size):
    if size & (size - 1):
        return x // size, x % size
    return lax.shift_right_logical(x, jnp.full_like(x, size.bit_length() - 1)), x & (size - 1)


def swapped(x, outer, inner):
    a, b = split_index(x, inner)
    return b * outer + a


def packed_of(r, cout, tout):
    def place(count):
        channels, pair = cout // count, tout // 2
        t, o = split_index(r, cout)
        owner, channel = split_index(o, channels)
        late, step = split_index(t, pair)
        return ((owner * 2 + late) * channels + channel) * pair + step

    return place


def one_hot(shape, column_of_row):
    return (iota(shape, 1) == column_of_row(iota((shape[0], 1), 0))).astype(f32).astype(bf16)


def one_hot_columns(shape, row_of_column):
    return (iota(shape, 0) == row_of_column(iota((1, shape[1]), 1))).astype(f32).astype(bf16)


def call(kernel, outs, scratch, flops, args, left=(), left_out=(), room=48):
    moved = sum(a.size * a.dtype.itemsize for a in list(args) + list(outs))
    return pl.pallas_call(
        kernel,
        out_shape=outs,
        in_specs=[
            pl.BlockSpec(memory_space=pltpu.HBM if a in left else pltpu.VMEM) for a in range(len(args))
        ],
        out_specs=[
            pl.BlockSpec(memory_space=pltpu.HBM if a in left_out else pltpu.VMEM) for a in range(len(outs))
        ],
        scratch_shapes=scratch,
        compiler_params=pltpu.CompilerParams(vmem_limit_bytes=room << 20),
        cost_estimate=pl.CostEstimate(flops=int(flops), bytes_accessed=moved, transcendentals=0),
    )(*args)


def conv_kernel(
    dims, sig_hbm, cot_hbm, taps_hbm, out_hbm, z_hbm,
    w_ref, sig_ref, cot_ref, taps_ref, out_ref, z_ref, sem,
):
    cin, tin, cout, tout, ks, count, rows = dims
    k_in, k_out = cin * tin, cout * tout
    half = sig_ref.shape[1] // 2
    tiles_wide = half // lanes
    conv_rows = rows * tiles_wide
    taps_copy = pltpu.make_async_copy(taps_hbm, taps_ref, sem.at[0])
    cot_copy = pltpu.make_async_copy(cot_hbm, cot_ref, sem.at[1])
    sig_copy = pltpu.make_async_copy(sig_hbm, sig_ref, sem.at[2])
    at_cot, at_conv = pl.ds(conv_rows, conv_rows), pl.ds(0, conv_rows)
    at_edge = pl.ds(2 * conv_rows, edge_rows)
    cot_out = pltpu.make_async_copy(out_ref.at[:, at_cot], out_hbm.at[:, at_cot], sem.at[3])
    z_out = pltpu.make_async_copy(z_ref, z_hbm, sem.at[4])
    conv_out = pltpu.make_async_copy(out_ref.at[:, at_conv], out_hbm.at[:, at_conv], sem.at[5])
    edge_out = pltpu.make_async_copy(out_ref.at[:, at_edge], out_hbm.at[:, at_edge], sem.at[6])
    taps_copy.start()
    cot_copy.start()
    sig_copy.start()
    packed = packed_of(iota((1, k_out), 1), cout, tout)(count)
    from_time = (iota((k_out, k_out), 0) == packed).astype(f32).astype(bf16)
    natural = packed_of(swapped(iota((1, k_out), 1), cout, tout), cout, tout)(count)
    from_channel = (iota((k_out, k_out), 0) == natural).astype(f32).astype(bf16)
    cot_copy.wait()
    cot = dot(from_channel, cot_ref[...]).astype(bf16)
    for d in range(count):
        for b in range(tiles_wide):
            at = conv_rows + rows * b
            out_ref[d, at : at + rows] = cot[rows * d : rows * (d + 1), lanes * b : lanes * (b + 1)]
    cot_out.start()
    taps_copy.wait()
    blank = jnp.zeros((2 * cin, cout), bf16)
    stacked = []
    for j in range(ks):
        column = jnp.concatenate([blank] + [taps_ref[i, j] for i in range(ks)] + [blank, blank], axis=0)
        for v in range(4):
            stacked.append(column[2 * cin * v : 2 * cin * v + lanes])
    eye = one_hot((cout, cout), lambda r: r)
    tiles = dot_nt(eye, jnp.concatenate(stacked, axis=0)).astype(bf16)
    empty = jnp.zeros((cout, lanes), bf16)
    for j in range(ks):
        for t in range(tout):
            for q in range(k_in // lanes):
                v = 2 * q - t + 2
                at = (j * 4 + v) * lanes
                tile = tiles[:, at : at + lanes] if 0 <= v < 4 else empty
                w_ref[j, cout * t : cout * (t + 1), lanes * q : lanes * (q + 1)] = tile
    sig_copy.wait()
    split = one_hot_columns((2 * lanes, 2 * lanes), lambda q: swapped(q, 2, lanes))
    parts = [dot(sig_ref[:, b : b + 2 * lanes], split) for b in range(0, 2 * half, 2 * lanes)]
    apart = jnp.concatenate([p[:, :lanes] for p in parts] + [p[:, lanes:] for p in parts], axis=1)
    to_time = one_hot((k_in, k_in), lambda r: swapped(r, tin, cin))
    z = dot(to_time, apart.astype(bf16)).astype(bf16)
    z_ref[...] = z
    z_out.start()
    even, odd = z[:, :half], z[:, half:]
    left = dot(w_ref[0], even) + dot(w_ref[1], odd)
    right = dot(w_ref[4], even)
    lane = iota((k_out, half), 1)
    own = (
        dot(w_ref[2], even)
        + dot(w_ref[3], odd)
        + jnp.where(lane == 0, 0.0, pltpu.roll(left, 1, 1))
        + jnp.where(lane == half - 1, 0.0, pltpu.roll(right, half - 1, 1))
    )
    high = own.astype(bf16)
    rest = (own - high.astype(f32)).astype(bf16)
    left_edge, right_edge = left[:, half - lanes :], right[:, :lanes]
    left_high, right_high = left_edge.astype(bf16), right_edge.astype(bf16)
    left_rest = (left_edge - left_high.astype(f32)).astype(bf16)
    right_rest = (right_edge - right_high.astype(f32)).astype(bf16)

    def pick(row, column, tile):
        at = (iota((edge_rows, lanes), 0) == row) & (iota((edge_rows, lanes), 1) == column)
        return dot_nt(at.astype(f32).astype(bf16), tile)

    edges = (
        pick(0, 0, rest[:, :lanes])
        + pick(1, lanes - 1, rest[:, half - lanes :])
        + pick(2, lanes - 1, left_high)
        + pick(3, lanes - 1, left_rest)
        + pick(4, 0, right_high)
        + pick(5, 0, right_rest)
    ).astype(bf16)
    edges = dot_nt(edges, from_time)
    main = dot(from_time, high).astype(bf16)
    for d in range(count):
        for b in range(tiles_wide):
            at = slice(lanes * b, lanes * (b + 1))
            out_ref[d, rows * b : rows * (b + 1)] = main[rows * d : rows * (d + 1), at]
        out_ref[d, 2 * conv_rows :] = jnp.zeros((edge_rows, lanes), bf16)
        out_ref[d, 2 * conv_rows :, :rows] = edges[:, rows * d : rows * (d + 1)].astype(bf16)
    conv_out.start()
    edge_out.start()
    cot_out.wait()
    z_out.wait()
    conv_out.wait()
    edge_out.wait()


def transform(real, imag, sign):
    size = len(real)
    if size == 1:
        return (list(real), [None] if imag is None else list(imag))
    even_re, even_im = transform(real[0::2], None if imag is None else imag[0::2], sign)
    odd_re, odd_im = transform(real[1::2], None if imag is None else imag[1::2], sign)
    out_re, out_im = [None] * size, [None] * size

    def plus(a, b):
        return b if a is None else (a if b is None else a + b)

    def minus(a, b):
        return a if b is None else (-b if a is None else a - b)

    for k in range(size // 2):
        re, im = odd_re[k], odd_im[k]
        if k == 0:
            tr, ti = re, im
        elif 4 * k == size:
            tr = None if im is None else (im if sign < 0 else -im)
            ti = -re if sign < 0 else re
        else:
            c, s = math.cos(2 * math.pi * k / size), sign * math.sin(2 * math.pi * k / size)
            if im is None:
                tr, ti = c * re, s * re
            elif 8 * k == size:
                tr, ti = (c * (re - im), c * (re + im)) if sign > 0 else (c * (re + im), c * (im - re))
            elif 8 * k == 3 * size:
                tr, ti = (c * (re + im), c * (im - re)) if sign > 0 else (c * (re - im), c * (re + im))
            else:
                tr, ti = c * re - s * im, s * re + c * im
        out_re[k], out_im[k] = plus(even_re[k], tr), plus(even_im[k], ti)
        out_re[k + size // 2], out_im[k + size // 2] = minus(even_re[k], tr), minus(even_im[k], ti)
    return out_re, out_im


def gelu_slope(v):
    return 0.5 * (1.0 + lax.erf(v * inv_root_two)) + v * jnp.exp(-0.5 * v * v) * inv_root_tau


def filter_kernel(
    dims, cols_ref, resp_ref, twist_ref, high_ref, rest_ref,
    out_ref, cross_ref, x_ref, y_ref, spec_ref, grad_ref,
):
    count, channels, tout, width = dims
    rows, pair = channels * tout, tout // 2
    packed = rows // 2
    chunk = min(8, packed)
    edge_row, edge_col = iota((edge_rows, width), 0), iota((edge_rows, width), 1)
    to_low = (edge_col == 0) & ((edge_row == 0) | (edge_row == 2) | (edge_row == 3))
    to_high = (edge_col == width - 1) & ((edge_row == 1) | (edge_row == 4) | (edge_row == 5))
    spread = (to_low | to_high).astype(f32).astype(bf16)
    low = 2 * rows * (width // lanes)
    edges = [cols_ref[d, low:, :rows].astype(f32) for d in range(count)]
    none = jnp.zeros((edge_rows, rows), f32)
    kind = iota((edge_rows, rows), 0)
    for d in range(count):
        before = edges[d - 1] if d > 0 else none
        after = edges[d + 1] if d < count - 1 else none
        joined = jnp.where(kind < 2, edges[d], jnp.where(kind < 4, before, after))
        blocks = [cols_ref[d, rows * b : rows * (b + 1)] for b in range(width // lanes)]
        whole = jnp.concatenate(blocks, axis=1).astype(f32) + dot_tn(joined.astype(bf16), spread)
        x_ref[d] = whole.astype(bf16).astype(f32)

    def forward_planes(real, imag, r, h):
        re, im = transform(real, imag, -1)
        for k in range(count):
            c = twist_ref[0, k : k + 1, h : h + lanes]
            s = twist_ref[1, k : k + 1, h : h + lanes]
            at = slice(k * packed + r, k * packed + r + chunk)
            y_ref[at, h : h + lanes] = re[k] * c + im[k] * s if k else re[k]
            y_ref[at, width + h : width + h + lanes] = im[k] * c - re[k] * s if k else im[k]

    def backward_planes(r, h):
        re, im = [], []
        for k in range(count):
            c = twist_ref[0, k : k + 1, h : h + lanes]
            s = twist_ref[1, k : k + 1, h : h + lanes]
            at = slice(k * packed + r, k * packed + r + chunk)
            a, b = y_ref[at, h : h + lanes], y_ref[at, width + h : width + h + lanes]
            re.append(a * c - b * s if k else a)
            im.append(b * c + a * s if k else b)
        return transform(re, im, 1)

    def inner(product):
        v = y_ref[...]
        high = v.astype(bf16)
        rest = (v - high.astype(f32)).astype(bf16)
        both = product(jnp.concatenate([high, rest], axis=0), high_ref[...])
        size = v.shape[0]
        return both[:size] + both[size:] + product(high, rest_ref[...])

    chunks = [(r, h) for r in range(0, packed, chunk) for h in range(0, width, lanes)]
    for r, h in chunks:
        at, to = slice(r, r + chunk), slice(packed + r, packed + r + chunk)
        forward_planes(
            [x_ref[d, at, h : h + lanes] for d in range(count)],
            [x_ref[d, to, h : h + lanes] for d in range(count)],
            r, h,
        )
    spec_ref[...] = inner(dot)
    sr, si = spec_ref[:, :width], spec_ref[:, width:]
    rr, ri = resp_ref[0], resp_ref[1]
    y_ref[:, :width] = rr * sr - ri * si
    y_ref[:, width:] = rr * si + ri * sr
    y_ref[...] = inner(dot_nt)
    for r, h in chunks:
        real, imag = backward_planes(r, h)
        at = rows * (width + h) // lanes + r
        cot = [cols_ref[d, at : at + chunk].astype(f32) for d in range(count)]
        real = [cot[d] * gelu_slope(real[d]) for d in range(count)]
        at += packed
        cot = [cols_ref[d, at : at + chunk].astype(f32) for d in range(count)]
        imag = [cot[d] * gelu_slope(imag[d]) for d in range(count)]
        forward_planes(real, imag, r, h)
    grad_ref[...] = inner(dot)
    sr, si = spec_ref[:, :width], spec_ref[:, width:]
    gr, gi = grad_ref[:, :width], grad_ref[:, width:]
    rr, ri = resp_ref[0], resp_ref[1]
    y_ref[:, :width] = rr * gr + ri * gi
    y_ref[:, width:] = rr * gi - ri * gr
    scale = 1.0 / (count * width)
    spec_ref[:, :width], spec_ref[:, width:] = (sr * gr + si * gi) * scale, (sr * gi - si * gr) * scale
    for k in range(count):
        for ch in range(channels):
            at = k * packed + ch * pair
            cross_ref[k, ch : ch + 1] = jnp.sum(spec_ref[at : at + pair], axis=0, keepdims=True)
    y_ref[...] = inner(dot_nt)
    for r, h in chunks:
        real, imag = backward_planes(r, h)
        for d in range(count):
            x_ref[d, r : r + chunk, h : h + lanes] = real[d]
            x_ref[d, packed + r : packed + r + chunk, h : h + lanes] = imag[d]
    last = ((iota((edge_rows, lanes), 0) == 0) & (iota((edge_rows, lanes), 1) == lanes - 1)).astype(f32).astype(bf16)
    first = ((iota((edge_rows, lanes), 0) == 1) & (iota((edge_rows, lanes), 1) == 0)).astype(f32).astype(bf16)
    for d in range(count):
        for b in range(width // lanes):
            out_ref[d, rows * b : rows * (b + 1)] = x_ref[d, :, lanes * b : lanes * (b + 1)].astype(bf16)
        low = rows * (width // lanes)
        out_ref[d, low:] = jnp.zeros((edge_rows, lanes), bf16)
        edge = none
        if d > 0:
            edge = edge + dot_nt(last, x_ref[d - 1, :, width - lanes :].astype(bf16))
        if d < count - 1:
            edge = edge + dot_nt(first, x_ref[d + 1, :, :lanes].astype(bf16))
        out_ref[d, low:, :rows] = edge.astype(bf16)


def tap_kernel(dims, grad_ref, z_ref, tap_ref, shifted_ref, g_ref, zp_ref):
    cin, tin, cout, tout, ks, count, rows = dims
    half = zp_ref.shape[1] // 2
    k_out = cout * tout
    row, col = iota((edge_rows, lanes), 0), iota((edge_rows, lanes), 1)
    spread = (((row == 1) & (col == 0)) | ((row == 0) & (col == 1))).astype(f32).astype(bf16)
    for d in range(count):
        at = slice(rows * d, rows * (d + 1))
        for b in range(half // lanes):
            g_ref[at, lanes * b : lanes * (b + 1)] = grad_ref[d, rows * b : rows * (b + 1)].astype(f32)
        g_ref[at, half:] = dot_tn(grad_ref[d, rows * (half // lanes) :, :rows], spread)
    to_time = one_hot((k_out, k_out), lambda r: packed_of(r, cout, tout)(count))
    g = dot(to_time, g_ref[...].astype(bf16)).astype(bf16)
    wide = half + lanes
    later = one_hot_columns((wide, half), lambda n: n + 1)
    sooner = one_hot_columns((wide, half), lambda n: jnp.where(n == 0, half + 1, n - 1))
    shifted_ref[0] = dot(g, later).astype(bf16)
    shifted_ref[1] = g[:, :half]
    shifted_ref[2] = dot(g, sooner).astype(bf16)
    k_in = cin * tin
    pad = 2 * cin
    zp_ref[:pad] = jnp.zeros((pad, 2 * half), bf16)
    zp_ref[pad + k_in :] = jnp.zeros((zp_ref.shape[0] - pad - k_in, 2 * half), bf16)
    zp_ref[pad : pad + k_in] = z_ref[...]
    both, lone = None, None
    for t in range(tout):
        at = slice(cout * t, cout * (t + 1))
        band = zp_ref[2 * cin * t : 2 * cin * t + ks * cin]
        pair = jnp.concatenate([shifted_ref[0, at], shifted_ref[1, at]], axis=0)
        even, odd = band[:, :half], band[:, half:]
        term = jnp.concatenate([dot_nt(even, pair), dot_nt(odd, pair)], axis=0)
        both = term if both is None else both + term
        blank = jnp.zeros((cout, half), bf16)
        mid = ks * cin // 2
        term = dot_nt(even[:mid], jnp.concatenate([shifted_ref[2, at], blank], axis=0)) + dot_nt(
            even[mid:], jnp.concatenate([blank, shifted_ref[2, at]], axis=0)
        )
        lone = term if lone is None else lone + term
    top = both.shape[0]
    tap_ref[:top] = both
    tap_ref[top : top + lone.shape[0]] = lone
    tap_ref[top + lone.shape[0] :] = jnp.zeros((tap_ref.shape[0] - top - lone.shape[0], lanes), f32)


def input_kernel(dims, shifted_ref, taps_ref, out_ref, w_ref):
    cin, tin, cout, tout, ks, count, rows = dims
    k_in = cin * tin
    half = shifted_ref.shape[2]
    blank = jnp.zeros((cin, cout), bf16)
    firsts, seconds = [], []
    for j in range(ks):
        for i in range(ks + 2):
            firsts.append(taps_ref[i, j] if i < ks else blank)
            seconds.append(taps_ref[i - 2, j] if i >= 2 else blank)
    to_first = one_hot((cout, lanes), lambda r: r)
    to_second = one_hot((cout, lanes), lambda r: r + cout)
    tiles = (
        dot(jnp.concatenate(firsts, axis=0), to_first) + dot(jnp.concatenate(seconds, axis=0), to_second)
    ).astype(bf16)
    empty = jnp.zeros((cin, lanes), bf16)
    for j in range(ks):
        for s in range(tin):
            for q in range(cout * tout // lanes):
                i = s - 4 * q + 2
                at = (j * (ks + 2) + i) * cin
                tile = tiles[at : at + cin] if 0 <= i < ks + 2 else empty
                w_ref[j, cin * s : cin * (s + 1), lanes * q : lanes * (q + 1)] = tile
    later, same, sooner = shifted_ref[0], shifted_ref[1], shifted_ref[2]
    even = dot(w_ref[0], later) + dot(w_ref[2], same) + dot(w_ref[4], sooner)
    odd = dot(w_ref[1], later) + dot(w_ref[3], same)
    both = jnp.concatenate([even.astype(bf16), odd.astype(bf16)], axis=1)
    to_channel = one_hot((k_in, k_in), lambda r: swapped(r, cin, tin))
    both = dot(to_channel, both).astype(bf16)
    merge = one_hot((2 * lanes, 2 * lanes), lambda r: swapped(r, 2, lanes))
    for b in range(half // lanes):
        part = jnp.concatenate(
            [both[:, lanes * b : lanes * (b + 1)], both[:, half + lanes * b : half + lanes * (b + 1)]], axis=1
        )
        out_ref[:, 2 * lanes * b : 2 * lanes * (b + 1)] = dot(part, merge).astype(bf16)


def unpack_kernel(dims, scale, tap_ref, out_ref):
    cin, tin, cout, tout, ks, count, rows = dims
    band = ks * cin
    for i in range(ks):
        at = slice(cin * i, cin * (i + 1))
        even, odd = tap_ref[at] * scale, tap_ref[band + cin * i : band + cin * (i + 1)] * scale
        out_ref[i, 0] = even[:, :cout]
        out_ref[i, 2] = even[:, cout:]
        out_ref[i, 1] = odd[:, :cout]
        out_ref[i, 3] = odd[:, cout:]
        for c in range(0, cin, 8):
            at = cin * i + c
            low = at < band // 2
            packed = tap_ref[2 * band + at % (band // 2) : 2 * band + at % (band // 2) + 8] * scale
            out_ref[i, 4, c : c + 8] = packed[:, :cout] if low else packed[:, cout:]


def summed_over(rows, axis, beside):
    count = lax.axis_size(axis)
    bit = lax.axis_index(axis) % 2
    pairs = lambda step: [(i, i ^ step) for i in range(count)]
    size = rows.shape[0] // 2
    kept = lax.dynamic_slice_in_dim(rows, bit * size, size)
    sent = lax.dynamic_slice_in_dim(rows, (1 - bit) * size, size)
    rows = kept + lax.ppermute(sent, axis, pairs(1))
    step = 2
    while step < count:
        rounded = rows.astype(bf16)
        theirs = lambda step: lax.ppermute(rounded, axis, pairs(step)).astype(f32)
        if step == 2 and 4 * step <= count:
            rows = (rounded.astype(f32) + theirs(step)) + (theirs(2 * step) + theirs(3 * step))
            rows, beside = lax.optimization_barrier((rows, beside))
            step *= 4
        else:
            rows = rounded.astype(f32) + theirs(step)
            step *= 2
    other = lax.ppermute(rows, axis, pairs(1))
    rows = jnp.where(bit == 0, jnp.concatenate([rows, other]), jnp.concatenate([other, rows]))
    return rows, beside


def mirrored(spectrum):
    return jnp.roll(jnp.flip(spectrum, -1), 1, -1)


def tables(count, width):
    inner = np.outer(np.arange(width), np.arange(width)) % width * (2.0 * np.pi / width)
    c, s = np.cos(inner), np.sin(inner)
    table = np.block([[c, -s], [s, c]]).astype(np.float32)
    high = table.astype(bf16)
    rest = (table - high.astype(np.float32)).astype(bf16)
    outer = np.outer(np.arange(count), np.arange(width)) * (2.0 * np.pi / (count * width))
    twist = np.stack([np.cos(outer), np.sin(outer)]).astype(np.float32)
    return twist, high, rest


def per_device(signal, conv_taps, response, cotangent):
    cin, tin, fibre_in = signal.shape
    cout, tout, width = cotangent.shape
    ks = conv_taps.shape[0]
    count = lax.axis_size("fibre")
    channels = cout // count
    rows = channels * tout
    waves = count * width
    tiles = width // lanes
    dims = (cin, tin, cout, tout, ks, count, rows)
    k_in, k_out = cin * tin, cout * tout
    taps = jnp.swapaxes(conv_taps, 2, 3)
    shape = jax.ShapeDtypeStruct
    conv_part, z = call(
        functools.partial(conv_kernel, dims),
        [
            shape((count, 2 * rows * tiles + edge_rows, lanes), bf16),
            shape((k_in, fibre_in), bf16),
        ],
        [
            pltpu.VMEM((ks, k_out, k_in), bf16),
            pltpu.VMEM((k_in, fibre_in), bf16),
            pltpu.VMEM((k_out, width), bf16),
            pltpu.VMEM(taps.shape, bf16),
            pltpu.VMEM((count, 2 * rows * tiles + edge_rows, lanes), bf16),
            pltpu.VMEM((k_in, fibre_in), bf16),
            pltpu.SemaphoreType.DMA((7,)),
        ],
        2e9,
        (signal.reshape(k_in, fibre_in), cotangent.reshape(k_out, width), taps),
        left=(0, 1, 2),
        left_out=(0, 1),
        room=60,
    )
    cols = lax.all_to_all(conv_part, "fibre", split_axis=0, concat_axis=0, tiled=True)
    pair = tout // 2
    back = mirrored(response)
    real = jnp.stack([response[0] + back[0], response[1] - back[1]]) * (0.5 / waves)
    real = real.reshape(2, channels, 1, width, count).transpose(0, 4, 1, 2, 3)
    real = jnp.broadcast_to(real, (2, count, channels, pair, width)).reshape(2, count * rows // 2, width)
    twist, high, rest = tables(count, width)
    big = count * rows // 2
    grad_part, cross = call(
        functools.partial(filter_kernel, (count, channels, tout, width)),
        [
            shape((count, rows * tiles + edge_rows, lanes), bf16),
            shape((count, channels, 2 * width), f32),
        ],
        [
            pltpu.VMEM((count, rows, width), f32),
            pltpu.VMEM((big, 2 * width), f32),
            pltpu.VMEM((big, 2 * width), f32),
            pltpu.VMEM((big, 2 * width), f32),
        ],
        6e9,
        (cols, real, jnp.asarray(twist), jnp.asarray(high), jnp.asarray(rest)),
    )
    cross = cross.reshape(count, channels, 2, width).transpose(2, 1, 3, 0).reshape(2, channels, waves)
    back = mirrored(cross)
    filter_grad = 0.5 * jnp.stack([cross[0] + back[0], cross[1] - back[1]])
    grad_cols = lax.all_to_all(grad_part, "fibre", split_axis=0, concat_axis=0, tiled=True)
    grad_cols, filter_grad = lax.optimization_barrier((grad_cols, filter_grad))
    taps_part, shifted = call(
        functools.partial(tap_kernel, dims),
        [shape((tap_rows, lanes), f32), shape((3, k_out, width), bf16)],
        [pltpu.VMEM((k_out, width + lanes), f32), pltpu.VMEM((k_in + 4 * cin, fibre_in), bf16)],
        1e9,
        (grad_cols, z),
    )
    (input_grad,) = call(
        functools.partial(input_kernel, dims),
        [shape((k_in, fibre_in), bf16)],
        [pltpu.VMEM((ks, k_in, k_out), bf16)],
        2e9,
        (shifted, taps),
    )
    total, input_grad = summed_over(taps_part, "fibre", input_grad)
    (tap_grad,) = call(
        functools.partial(unpack_kernel, dims, 1.0 / math.sqrt(tout * waves)),
        [shape((ks, ks, cin, cout), f32)],
        [],
        1e6,
        (total,),
    )
    return (input_grad.reshape(signal.shape), jnp.swapaxes(tap_grad, 2, 3), filter_grad)


def solution(mesh):
    in_specs = (P("parts", None, "fibre"), P(), P(None, "fibre", None), P("parts", None, "fibre"))
    out_specs = (P("parts", None, "fibre"), P("parts", None, None, None), P("parts", "fibre", None))
    return jax.shard_map(
        per_device, mesh=mesh, in_specs=in_specs, out_specs=out_specs, check_vma=False
    )
```

```python
import functools
import math

import jax
import jax.numpy as jnp
import numpy as np
from jax import lax
from jax.experimental import pallas as pl
from jax.experimental.pallas import tpu as pltpu
from jax.sharding import PartitionSpec as P

bf16 = jnp.bfloat16
f32 = jnp.float32
inv_root_two = 1.0 / math.sqrt(2.0)
inv_root_tau = 1.0 / math.sqrt(2.0 * math.pi)
lanes = 128
edge_rows = 8
tap_rows = 416


def dot(a, b):
    return jnp.dot(a, b, preferred_element_type=f32)


def dot_nt(a, b):
    return lax.dot_general(a, b, (((1,), (1,)), ((), ())), preferred_element_type=f32)


def dot_tn(a, b):
    return lax.dot_general(a, b, (((0,), (0,)), ((), ())), preferred_element_type=f32)


def iota(shape, dim):
    return lax.broadcasted_iota(jnp.int32, shape, dim)


def split_index(x, size):
    if size & (size - 1):
        return x // size, x % size
    return lax.shift_right_logical(x, jnp.full_like(x, size.bit_length() - 1)), x & (size - 1)


def swapped(x, outer, inner):
    a, b = split_index(x, inner)
    return b * outer + a


def one_hot(shape, column_of_row):
    return (iota(shape, 1) == column_of_row(iota((shape[0], 1), 0))).astype(f32).astype(bf16)


def one_hot_columns(shape, row_of_column):
    return (iota(shape, 0) == row_of_column(iota((1, shape[1]), 1))).astype(f32).astype(bf16)


def call(kernel, outs, scratch, flops, args, left=(), left_out=(), room=48):
    moved = sum(a.size * a.dtype.itemsize for a in list(args) + list(outs))
    return pl.pallas_call(
        kernel,
        out_shape=outs,
        in_specs=[
            pl.BlockSpec(memory_space=pltpu.HBM if a in left else pltpu.VMEM) for a in range(len(args))
        ],
        out_specs=[
            pl.BlockSpec(memory_space=pltpu.HBM if a in left_out else pltpu.VMEM) for a in range(len(outs))
        ],
        scratch_shapes=scratch,
        compiler_params=pltpu.CompilerParams(vmem_limit_bytes=room << 20),
        cost_estimate=pl.CostEstimate(flops=int(flops), bytes_accessed=moved, transcendentals=0),
    )(*args)


def conv_kernel(
    dims, sig_hbm, cot_hbm, taps_hbm, out_hbm, z_hbm,
    w_ref, sig_ref, taps_ref, out_ref, z_ref, sem,
):
    cin, tin, cout, tout, ks, count, rows = dims
    k_in, k_out = cin * tin, cout * tout
    half = sig_ref.shape[1] // 2
    tiles_wide = half // lanes
    conv_rows = rows * tiles_wide
    taps_copy = pltpu.make_async_copy(taps_hbm, taps_ref, sem.at[0])
    sig_copy = pltpu.make_async_copy(sig_hbm, sig_ref, sem.at[1])
    cot_copies = [
        pltpu.make_async_copy(
            cot_hbm.at[:, :, pl.ds(lanes * b, lanes)],
            out_hbm.at[:, pl.ds(conv_rows + rows * b, rows)],
            sem.at[5 + b],
        )
        for b in range(tiles_wide)
    ]
    at_conv, at_edge = pl.ds(0, conv_rows), pl.ds(2 * conv_rows, edge_rows)
    z_out = pltpu.make_async_copy(z_ref, z_hbm, sem.at[2])
    conv_out = pltpu.make_async_copy(out_ref.at[:, at_conv], out_hbm.at[:, at_conv], sem.at[3])
    edge_out = pltpu.make_async_copy(out_ref.at[:, at_edge], out_hbm.at[:, at_edge], sem.at[4])
    taps_copy.start()
    sig_copy.start()
    for copy in cot_copies:
        copy.start()
    taps_copy.wait()
    blank = jnp.zeros((2 * cin, cout), bf16)
    stacked = []
    for j in range(ks):
        column = jnp.concatenate([blank] + [taps_ref[i, j] for i in range(ks)] + [blank, blank], axis=0)
        for v in range(4):
            stacked.append(column[2 * cin * v : 2 * cin * v + lanes])
    eye = one_hot((cout, cout), lambda r: r)
    tiles = dot_nt(eye, jnp.concatenate(stacked, axis=0)).astype(bf16)
    empty = jnp.zeros((cout, lanes), bf16)
    for j in range(ks):
        for t in range(tout):
            for q in range(k_in // lanes):
                v = 2 * q - t + 2
                at = (j * 4 + v) * lanes
                tile = tiles[:, at : at + lanes] if 0 <= v < 4 else empty
                w_ref[j, cout * t : cout * (t + 1), lanes * q : lanes * (q + 1)] = tile
    sig_copy.wait()
    split = one_hot_columns((2 * lanes, 2 * lanes), lambda q: swapped(q, 2, lanes))
    parts = [dot(sig_ref[:, b : b + 2 * lanes], split) for b in range(0, 2 * half, 2 * lanes)]
    apart = jnp.concatenate([p[:, :lanes] for p in parts] + [p[:, lanes:] for p in parts], axis=1)
    to_time = one_hot((k_in, k_in), lambda r: swapped(r, tin, cin))
    z = dot(to_time, apart.astype(bf16)).astype(bf16)
    z_ref[...] = z
    z_out.start()
    even, odd = z[:, :half], z[:, half:]
    left = dot(w_ref[0], even) + dot(w_ref[1], odd)
    right = dot(w_ref[4], even)
    lane = iota((k_out, half), 1)
    own = (
        dot(w_ref[2], even)
        + dot(w_ref[3], odd)
        + jnp.where(lane == 0, 0.0, pltpu.roll(left, 1, 1))
        + jnp.where(lane == half - 1, 0.0, pltpu.roll(right, half - 1, 1))
    )
    high = own.astype(bf16)
    first = iota((k_out, lanes), 1) == 0

    def parts_of(v):
        top = v.astype(bf16)
        return top, (v - top.astype(f32)).astype(bf16)

    _, own_rest = parts_of(jnp.where(first, own[:, :lanes], own[:, half - lanes :]))
    next_high, next_rest = parts_of(jnp.where(first, right[:, :lanes], left[:, half - lanes :]))
    row, col = iota((edge_rows, 3 * lanes), 0), iota((edge_rows, 3 * lanes), 1)
    pick = jnp.zeros((edge_rows, 3 * lanes), f32)
    for at, column in enumerate((0, lanes - 1, 2 * lanes - 1, 3 * lanes - 1, lanes, 2 * lanes)):
        pick = jnp.where((row == at) & (col == column), 1.0, pick)
    edges = dot_nt(pick.astype(bf16), jnp.concatenate([own_rest, next_high, next_rest], axis=1))
    from_time = one_hot((k_out, k_out), lambda r: swapped(r, cout, tout))
    edges = dot_nt(edges.astype(bf16), from_time)
    main = dot(from_time, high).astype(bf16)
    for d in range(count):
        for b in range(tiles_wide):
            at = slice(lanes * b, lanes * (b + 1))
            out_ref[d, rows * b : rows * (b + 1)] = main[rows * d : rows * (d + 1), at]
        out_ref[d, 2 * conv_rows :] = jnp.zeros((edge_rows, lanes), bf16)
        out_ref[d, 2 * conv_rows :, :rows] = edges[:, rows * d : rows * (d + 1)].astype(bf16)
    conv_out.start()
    edge_out.start()
    for copy in cot_copies:
        copy.wait()
    z_out.wait()
    conv_out.wait()
    edge_out.wait()


def transform(real, imag, sign):
    size = len(real)
    if size == 1:
        return (list(real), [None] if imag is None else list(imag))
    even_re, even_im = transform(real[0::2], None if imag is None else imag[0::2], sign)
    odd_re, odd_im = transform(real[1::2], None if imag is None else imag[1::2], sign)
    out_re, out_im = [None] * size, [None] * size

    def plus(a, b):
        return b if a is None else (a if b is None else a + b)

    def minus(a, b):
        return a if b is None else (-b if a is None else a - b)

    for k in range(size // 2):
        re, im = odd_re[k], odd_im[k]
        if k == 0:
            tr, ti = re, im
        elif 4 * k == size:
            tr = None if im is None else (im if sign < 0 else -im)
            ti = -re if sign < 0 else re
        else:
            c, s = math.cos(2 * math.pi * k / size), sign * math.sin(2 * math.pi * k / size)
            if im is None:
                tr, ti = c * re, s * re
            elif 8 * k == size:
                tr, ti = (c * (re - im), c * (re + im)) if sign > 0 else (c * (re + im), c * (im - re))
            elif 8 * k == 3 * size:
                tr, ti = (c * (re + im), c * (im - re)) if sign > 0 else (c * (re - im), c * (re + im))
            else:
                tr, ti = c * re - s * im, s * re + c * im
        out_re[k], out_im[k] = plus(even_re[k], tr), plus(even_im[k], ti)
        out_re[k + size // 2], out_im[k + size // 2] = minus(even_re[k], tr), minus(even_im[k], ti)
    return out_re, out_im


def gelu_slope(v):
    return 0.5 * (1.0 + lax.erf(v * inv_root_two)) + v * jnp.exp(-0.5 * v * v) * inv_root_tau


def filter_kernel(
    dims, cols_ref, resp_ref, twist_ref, high_ref, rest_ref,
    out_ref, cross_ref, x_ref, y_ref, spec_ref, grad_ref,
):
    count, channels, tout, width = dims
    rows, pair = channels * tout, tout // 2
    packed = rows // 2
    group = min(2, channels)
    chunk = group * pair
    edge_row, edge_col = iota((edge_rows, width), 0), iota((edge_rows, width), 1)
    to_low = (edge_col == 0) & ((edge_row == 0) | (edge_row == 2) | (edge_row == 3))
    to_high = (edge_col == width - 1) & ((edge_row == 1) | (edge_row == 4) | (edge_row == 5))
    spread = (to_low | to_high).astype(f32).astype(bf16)
    low = 2 * rows * (width // lanes)
    edges = [cols_ref[d, low:, :rows].astype(f32) for d in range(count)]
    none = jnp.zeros((edge_rows, rows), f32)
    kind = iota((edge_rows, rows), 0)
    for d in range(count):
        before = edges[d - 1] if d > 0 else none
        after = edges[d + 1] if d < count - 1 else none
        joined = jnp.where(kind < 2, edges[d], jnp.where(kind < 4, before, after))
        blocks = [cols_ref[d, rows * b : rows * (b + 1)] for b in range(width // lanes)]
        whole = jnp.concatenate(blocks, axis=1).astype(f32) + dot_tn(joined.astype(bf16), spread)
        x_ref[d] = whole.astype(bf16).astype(f32)

    def forward_planes(real, imag, r, h):
        re, im = transform(real, imag, -1)
        for k in range(count):
            c = twist_ref[0, k : k + 1, h : h + lanes]
            s = twist_ref[1, k : k + 1, h : h + lanes]
            at = slice(k * packed + r, k * packed + r + chunk)
            y_ref[at, h : h + lanes] = re[k] * c + im[k] * s if k else re[k]
            y_ref[at, width + h : width + h + lanes] = im[k] * c - re[k] * s if k else im[k]

    def backward_planes(r, h):
        re, im = [], []
        for k in range(count):
            c = twist_ref[0, k : k + 1, h : h + lanes]
            s = twist_ref[1, k : k + 1, h : h + lanes]
            at = slice(k * packed + r, k * packed + r + chunk)
            a, b = y_ref[at, h : h + lanes], y_ref[at, width + h : width + h + lanes]
            re.append(a * c - b * s if k else a)
            im.append(b * c + a * s if k else b)
        return transform(re, im, 1)

    def inner(product):
        v = y_ref[...]
        high = v.astype(bf16)
        rest = (v - high.astype(f32)).astype(bf16)
        both = product(jnp.concatenate([high, rest], axis=0), high_ref[...])
        size = v.shape[0]
        return both[:size] + both[size:] + product(high, rest_ref[...])

    def paired(tiles):
        return (
            jnp.concatenate([tile[:pair] for tile in tiles], axis=0),
            jnp.concatenate([tile[pair:] for tile in tiles], axis=0),
        )

    chunks = [(r, h) for r in range(0, packed, chunk) for h in range(0, width, lanes)]
    for r, h in chunks:
        planes = [
            paired([x_ref[d, 2 * r + tout * g : 2 * r + tout * (g + 1), h : h + lanes] for g in range(group)])
            for d in range(count)
        ]
        forward_planes([re for re, im in planes], [im for re, im in planes], r, h)
    spec_ref[...] = inner(dot)
    sr, si = spec_ref[:, :width], spec_ref[:, width:]
    rr, ri = resp_ref[0], resp_ref[1]
    y_ref[:, :width] = rr * sr - ri * si
    y_ref[:, width:] = rr * si + ri * sr
    y_ref[...] = inner(dot_nt)
    for r, h in chunks:
        real, imag = backward_planes(r, h)
        at = rows * (width + h) // lanes + 2 * r
        for d in range(count):
            cot = cols_ref[d, at : at + tout * group].astype(f32)
            re, im = paired([cot[tout * g : tout * (g + 1)] for g in range(group)])
            real[d], imag[d] = re * gelu_slope(real[d]), im * gelu_slope(imag[d])
        forward_planes(real, imag, r, h)
    grad_ref[...] = inner(dot)
    sr, si = spec_ref[:, :width], spec_ref[:, width:]
    gr, gi = grad_ref[:, :width], grad_ref[:, width:]
    rr, ri = resp_ref[0], resp_ref[1]
    y_ref[:, :width] = rr * gr + ri * gi
    y_ref[:, width:] = rr * gi - ri * gr
    scale = 1.0 / (count * width)
    spec_ref[:, :width], spec_ref[:, width:] = (sr * gr + si * gi) * scale, (sr * gi - si * gr) * scale
    for k in range(count):
        for ch in range(channels):
            at = k * packed + ch * pair
            cross_ref[k, ch : ch + 1] = jnp.sum(spec_ref[at : at + pair], axis=0, keepdims=True)
    y_ref[...] = inner(dot_nt)
    for r, h in chunks:
        real, imag = backward_planes(r, h)
        for d in range(count):
            for g in range(group):
                at = slice(pair * g, pair * (g + 1))
                tile = jnp.concatenate([real[d][at], imag[d][at]], axis=0)
                x_ref[d, 2 * r + tout * g : 2 * r + tout * (g + 1), h : h + lanes] = tile
    last = ((iota((edge_rows, lanes), 0) == 0) & (iota((edge_rows, lanes), 1) == lanes - 1)).astype(f32).astype(bf16)
    first = ((iota((edge_rows, lanes), 0) == 1) & (iota((edge_rows, lanes), 1) == 0)).astype(f32).astype(bf16)
    for d in range(count):
        for b in range(width // lanes):
            out_ref[d, rows * b : rows * (b + 1)] = x_ref[d, :, lanes * b : lanes * (b + 1)].astype(bf16)
        low = rows * (width // lanes)
        out_ref[d, low:] = jnp.zeros((edge_rows, lanes), bf16)
        edge = none
        if d > 0:
            edge = edge + dot_nt(last, x_ref[d - 1, :, width - lanes :].astype(bf16))
        if d < count - 1:
            edge = edge + dot_nt(first, x_ref[d + 1, :, :lanes].astype(bf16))
        out_ref[d, low:, :rows] = edge.astype(bf16)


def hermitian_kernel(cross_ref, out_ref):
    count, channels, wide = cross_ref.shape
    width = wide // 2
    row, col = iota((width, width), 0), iota((width, width), 1)
    flip = (row + col == width - 1).astype(f32).astype(bf16)
    flip_first = ((row + col == width) | ((row == 0) & (col == 0))).astype(f32).astype(bf16)

    def moved(v, by):
        total = None
        for _ in range(3):
            part = v.astype(bf16)
            v = v - part.astype(f32)
            term = dot(part, by)
            total = term if total is None else total + term
        return total

    for k in range(count):
        own, other = cross_ref[k], cross_ref[(count - k) % count]
        by = flip if k else flip_first
        out_ref[0, :, k] = 0.5 * (own[:, :width] + moved(other[:, :width], by))
        out_ref[1, :, k] = 0.5 * (own[:, width:] - moved(other[:, width:], by))


def tap_kernel(dims, grad_ref, z_ref, tap_ref, shifted_ref, g_ref, zp_ref):
    cin, tin, cout, tout, ks, count, rows = dims
    half = zp_ref.shape[1] // 2
    k_out = cout * tout
    row, col = iota((edge_rows, lanes), 0), iota((edge_rows, lanes), 1)
    spread = (((row == 1) & (col == 0)) | ((row == 0) & (col == 1))).astype(f32).astype(bf16)
    for d in range(count):
        at = slice(rows * d, rows * (d + 1))
        for b in range(half // lanes):
            g_ref[at, lanes * b : lanes * (b + 1)] = grad_ref[d, rows * b : rows * (b + 1)].astype(f32)
        g_ref[at, half:] = dot_tn(grad_ref[d, rows * (half // lanes) :, :rows], spread)
    to_time = one_hot((k_out, k_out), lambda r: swapped(r, tout, cout))
    g = dot(to_time, g_ref[...].astype(bf16)).astype(bf16)
    wide = half + lanes
    later = one_hot_columns((wide, half), lambda n: n + 1)
    sooner = one_hot_columns((wide, half), lambda n: jnp.where(n == 0, half + 1, n - 1))
    shifted_ref[0] = dot(g, later).astype(bf16)
    shifted_ref[1] = g[:, :half]
    shifted_ref[2] = dot(g, sooner).astype(bf16)
    k_in = cin * tin
    pad = 2 * cin
    zp_ref[:pad] = jnp.zeros((pad, 2 * half), bf16)
    zp_ref[pad + k_in :] = jnp.zeros((zp_ref.shape[0] - pad - k_in, 2 * half), bf16)
    zp_ref[pad : pad + k_in] = z_ref[...]
    both, lone = None, None
    for t in range(tout):
        at = slice(cout * t, cout * (t + 1))
        band = zp_ref[2 * cin * t : 2 * cin * t + ks * cin]
        pair = jnp.concatenate([shifted_ref[0, at], shifted_ref[1, at]], axis=0)
        even, odd = band[:, :half], band[:, half:]
        term = jnp.concatenate([dot_nt(even, pair), dot_nt(odd, pair)], axis=0)
        both = term if both is None else both + term
        blank = jnp.zeros((cout, half), bf16)
        mid = ks * cin // 2
        term = dot_nt(even[:mid], jnp.concatenate([shifted_ref[2, at], blank], axis=0)) + dot_nt(
            even[mid:], jnp.concatenate([blank, shifted_ref[2, at]], axis=0)
        )
        lone = term if lone is None else lone + term
    top = both.shape[0]
    tap_ref[:top] = both
    tap_ref[top : top + lone.shape[0]] = lone
    tap_ref[top + lone.shape[0] :] = jnp.zeros((tap_ref.shape[0] - top - lone.shape[0], lanes), f32)


def input_kernel(dims, shifted_ref, taps_ref, out_ref, w_ref):
    cin, tin, cout, tout, ks, count, rows = dims
    k_in = cin * tin
    half = shifted_ref.shape[2]
    blank = jnp.zeros((cin, cout), bf16)
    firsts, seconds = [], []
    for j in range(ks):
        for i in range(ks + 2):
            firsts.append(taps_ref[i, j] if i < ks else blank)
            seconds.append(taps_ref[i - 2, j] if i >= 2 else blank)
    to_first = one_hot((cout, lanes), lambda r: r)
    to_second = one_hot((cout, lanes), lambda r: r + cout)
    tiles = (
        dot(jnp.concatenate(firsts, axis=0), to_first) + dot(jnp.concatenate(seconds, axis=0), to_second)
    ).astype(bf16)
    empty = jnp.zeros((cin, lanes), bf16)
    for j in range(ks):
        for s in range(tin):
            for q in range(cout * tout // lanes):
                i = s - 4 * q + 2
                at = (j * (ks + 2) + i) * cin
                tile = tiles[at : at + cin] if 0 <= i < ks + 2 else empty
                w_ref[j, cin * s : cin * (s + 1), lanes * q : lanes * (q + 1)] = tile
    later, same, sooner = shifted_ref[0], shifted_ref[1], shifted_ref[2]
    even = dot(w_ref[0], later) + dot(w_ref[2], same) + dot(w_ref[4], sooner)
    odd = dot(w_ref[1], later) + dot(w_ref[3], same)
    both = jnp.concatenate([even.astype(bf16), odd.astype(bf16)], axis=1)
    to_channel = one_hot((k_in, k_in), lambda r: swapped(r, cin, tin))
    both = dot(to_channel, both).astype(bf16)
    merge = one_hot((2 * lanes, 2 * lanes), lambda r: swapped(r, 2, lanes))
    for b in range(half // lanes):
        part = jnp.concatenate(
            [both[:, lanes * b : lanes * (b + 1)], both[:, half + lanes * b : half + lanes * (b + 1)]], axis=1
        )
        out_ref[:, 2 * lanes * b : 2 * lanes * (b + 1)] = dot(part, merge).astype(bf16)


def unpack_kernel(dims, scale, tap_ref, out_ref):
    cin, tin, cout, tout, ks, count, rows = dims
    band = ks * cin
    for i in range(ks):
        at = slice(cin * i, cin * (i + 1))
        even, odd = tap_ref[at] * scale, tap_ref[band + cin * i : band + cin * (i + 1)] * scale
        out_ref[i, 0] = even[:, :cout]
        out_ref[i, 2] = even[:, cout:]
        out_ref[i, 1] = odd[:, :cout]
        out_ref[i, 3] = odd[:, cout:]
        for c in range(0, cin, 8):
            at = cin * i + c
            low = at < band // 2
            packed = tap_ref[2 * band + at % (band // 2) : 2 * band + at % (band // 2) + 8] * scale
            out_ref[i, 4, c : c + 8] = packed[:, :cout] if low else packed[:, cout:]


def summed_over(rows, axis, beside):
    count = lax.axis_size(axis)
    bit = lax.axis_index(axis) % 2
    pairs = lambda step: [(i, i ^ step) for i in range(count)]
    size = rows.shape[0] // 2
    kept = lax.dynamic_slice_in_dim(rows, bit * size, size)
    sent = lax.dynamic_slice_in_dim(rows, (1 - bit) * size, size)
    rows = kept + lax.ppermute(sent, axis, pairs(1))
    step = 2
    while step < count:
        rounded = rows.astype(bf16)
        theirs = lambda step: lax.ppermute(rounded, axis, pairs(step)).astype(f32)
        if step == 2 and 4 * step <= count:
            rows = (rounded.astype(f32) + theirs(step)) + (theirs(2 * step) + theirs(3 * step))
            rows, beside = lax.optimization_barrier((rows, beside))
            step *= 4
        else:
            rows = rounded.astype(f32) + theirs(step)
            step *= 2
    other = lax.ppermute(rows, axis, pairs(1))
    rows = jnp.where(bit == 0, jnp.concatenate([rows, other]), jnp.concatenate([other, rows]))
    return rows, beside


def mirrored(spectrum):
    return jnp.roll(jnp.flip(spectrum, -1), 1, -1)


def tables(count, width):
    inner = np.outer(np.arange(width), np.arange(width)) % width * (2.0 * np.pi / width)
    c, s = np.cos(inner), np.sin(inner)
    table = np.block([[c, -s], [s, c]]).astype(np.float32)
    high = table.astype(bf16)
    rest = (table - high.astype(np.float32)).astype(bf16)
    outer = np.outer(np.arange(count), np.arange(width)) * (2.0 * np.pi / (count * width))
    twist = np.stack([np.cos(outer), np.sin(outer)]).astype(np.float32)
    return twist, high, rest


def per_device(signal, conv_taps, response, cotangent):
    cin, tin, fibre_in = signal.shape
    cout, tout, width = cotangent.shape
    ks = conv_taps.shape[0]
    count = lax.axis_size("fibre")
    channels = cout // count
    rows = channels * tout
    waves = count * width
    tiles = width // lanes
    dims = (cin, tin, cout, tout, ks, count, rows)
    k_in, k_out = cin * tin, cout * tout
    taps = jnp.swapaxes(conv_taps, 2, 3)
    shape = jax.ShapeDtypeStruct
    conv_part, z = call(
        functools.partial(conv_kernel, dims),
        [
            shape((count, 2 * rows * tiles + edge_rows, lanes), bf16),
            shape((k_in, fibre_in), bf16),
        ],
        [
            pltpu.VMEM((ks, k_out, k_in), bf16),
            pltpu.VMEM((k_in, fibre_in), bf16),
            pltpu.VMEM(taps.shape, bf16),
            pltpu.VMEM((count, 2 * rows * tiles + edge_rows, lanes), bf16),
            pltpu.VMEM((k_in, fibre_in), bf16),
            pltpu.SemaphoreType.DMA((5 + tiles,)),
        ],
        2e9,
        (signal.reshape(k_in, fibre_in), cotangent.reshape(count, rows, width), taps),
        left=(0, 1, 2),
        left_out=(0, 1),
        room=60,
    )
    cols = lax.all_to_all(conv_part, "fibre", split_axis=0, concat_axis=0, tiled=True)
    pair = tout // 2
    back = mirrored(response)
    real = jnp.stack([response[0] + back[0], response[1] - back[1]]) * (0.5 / waves)
    real = real.reshape(2, channels, 1, width, count).transpose(0, 4, 1, 2, 3)
    real = jnp.broadcast_to(real, (2, count, channels, pair, width)).reshape(2, count * rows // 2, width)
    twist, high, rest = tables(count, width)
    big = count * rows // 2
    grad_part, cross = call(
        functools.partial(filter_kernel, (count, channels, tout, width)),
        [
            shape((count, rows * tiles + edge_rows, lanes), bf16),
            shape((count, channels, 2 * width), f32),
        ],
        [
            pltpu.VMEM((count, rows, width), f32),
            pltpu.VMEM((big, 2 * width), f32),
            pltpu.VMEM((big, 2 * width), f32),
            pltpu.VMEM((big, 2 * width), f32),
        ],
        6e9,
        (cols, real, jnp.asarray(twist), jnp.asarray(high), jnp.asarray(rest)),
    )
    (cross,) = call(hermitian_kernel, [shape((2, channels, count, width), f32)], [], 1e6, (cross,))
    filter_grad = cross.transpose(0, 1, 3, 2).reshape(2, channels, waves)
    grad_cols = lax.all_to_all(grad_part, "fibre", split_axis=0, concat_axis=0, tiled=True)
    grad_cols, filter_grad = lax.optimization_barrier((grad_cols, filter_grad))
    taps_part, shifted = call(
        functools.partial(tap_kernel, dims),
        [shape((tap_rows, lanes), f32), shape((3, k_out, width), bf16)],
        [pltpu.VMEM((k_out, width + lanes), f32), pltpu.VMEM((k_in + 4 * cin, fibre_in), bf16)],
        1e9,
        (grad_cols, z),
    )
    (input_grad,) = call(
        functools.partial(input_kernel, dims),
        [shape((k_in, fibre_in), bf16)],
        [pltpu.VMEM((ks, k_in, k_out), bf16)],
        2e9,
        (shifted, taps),
    )
    total, input_grad = summed_over(taps_part, "fibre", input_grad)
    (tap_grad,) = call(
        functools.partial(unpack_kernel, dims, 1.0 / math.sqrt(tout * waves)),
        [shape((ks, ks, cin, cout), f32)],
        [],
        1e6,
        (total,),
    )
    return (input_grad.reshape(signal.shape), jnp.swapaxes(tap_grad, 2, 3), filter_grad)


def solution(mesh):
    in_specs = (P("parts", None, "fibre"), P(), P(None, "fibre", None), P("parts", None, "fibre"))
    out_specs = (P("parts", None, "fibre"), P("parts", None, None, None), P("parts", "fibre", None))
    return jax.shard_map(
        per_device, mesh=mesh, in_specs=in_specs, out_specs=out_specs, check_vma=False
    )
```

```python
import functools
import math

import jax
import jax.numpy as jnp
import numpy as np
from jax import lax
from jax.experimental import pallas as pl
from jax.experimental.pallas import tpu as pltpu
from jax.sharding import PartitionSpec as P

bf16 = jnp.bfloat16
f32 = jnp.float32
inv_root_two = 1.0 / math.sqrt(2.0)
inv_root_tau = 1.0 / math.sqrt(2.0 * math.pi)
lanes = 128
edge_rows = 8
tap_rows = 416


def dot(a, b):
    return jnp.dot(a, b, preferred_element_type=f32)


def dot_nt(a, b):
    return lax.dot_general(a, b, (((1,), (1,)), ((), ())), preferred_element_type=f32)


def dot_tn(a, b):
    return lax.dot_general(a, b, (((0,), (0,)), ((), ())), preferred_element_type=f32)


def iota(shape, dim):
    return lax.broadcasted_iota(jnp.int32, shape, dim)


def split_index(x, size):
    if size & (size - 1):
        return x // size, x % size
    return lax.shift_right_logical(x, jnp.full_like(x, size.bit_length() - 1)), x & (size - 1)


def swapped(x, outer, inner):
    a, b = split_index(x, inner)
    return b * outer + a


def one_hot(shape, column_of_row):
    return (iota(shape, 1) == column_of_row(iota((shape[0], 1), 0))).astype(f32).astype(bf16)


def one_hot_columns(shape, row_of_column):
    return (iota(shape, 0) == row_of_column(iota((1, shape[1]), 1))).astype(f32).astype(bf16)


def call(kernel, outs, scratch, flops, args, left=(), left_out=(), room=48):
    moved = sum(a.size * a.dtype.itemsize for a in list(args) + list(outs))
    return pl.pallas_call(
        kernel,
        out_shape=outs,
        in_specs=[
            pl.BlockSpec(memory_space=pltpu.HBM if a in left else pltpu.VMEM) for a in range(len(args))
        ],
        out_specs=[
            pl.BlockSpec(memory_space=pltpu.HBM if a in left_out else pltpu.VMEM) for a in range(len(outs))
        ],
        scratch_shapes=scratch,
        compiler_params=pltpu.CompilerParams(vmem_limit_bytes=room << 20),
        cost_estimate=pl.CostEstimate(flops=int(flops), bytes_accessed=moved, transcendentals=0),
    )(*args)


def conv_kernel(
    dims, sig_hbm, cot_hbm, taps_hbm, out_hbm, z_hbm,
    w_ref, sig_ref, taps_ref, out_ref, z_ref, sem,
):
    cin, tin, cout, tout, ks, count, rows = dims
    k_in, k_out = cin * tin, cout * tout
    half = sig_ref.shape[1] // 2
    tiles_wide = half // lanes
    conv_rows = rows * tiles_wide
    taps_copy = pltpu.make_async_copy(taps_hbm, taps_ref, sem.at[0])
    sig_copy = pltpu.make_async_copy(sig_hbm, sig_ref, sem.at[1])
    cot_copies = [
        pltpu.make_async_copy(
            cot_hbm.at[:, :, pl.ds(lanes * b, lanes)],
            out_ref.at[:, pl.ds(conv_rows + rows * b, rows)],
            sem.at[6 + b],
        )
        for b in range(tiles_wide)
    ]
    at_conv, at_edge = pl.ds(0, conv_rows), pl.ds(2 * conv_rows, edge_rows)
    at_cot = pl.ds(conv_rows, conv_rows)
    cot_out = pltpu.make_async_copy(out_ref.at[:, at_cot], out_hbm.at[:, at_cot], sem.at[5])
    z_out = pltpu.make_async_copy(z_ref, z_hbm, sem.at[2])
    conv_out = pltpu.make_async_copy(out_ref.at[:, at_conv], out_hbm.at[:, at_conv], sem.at[3])
    edge_out = pltpu.make_async_copy(out_ref.at[:, at_edge], out_hbm.at[:, at_edge], sem.at[4])
    taps_copy.start()
    sig_copy.start()
    for copy in cot_copies:
        copy.start()
    taps_copy.wait()
    blank = jnp.zeros((2 * cin, cout), bf16)
    stacked = []
    for j in range(ks):
        column = jnp.concatenate([blank] + [taps_ref[i, j] for i in range(ks)] + [blank, blank], axis=0)
        for v in range(4):
            stacked.append(column[2 * cin * v : 2 * cin * v + lanes])
    eye = one_hot((cout, cout), lambda r: r)
    tiles = dot_nt(eye, jnp.concatenate(stacked, axis=0)).astype(bf16)
    empty = jnp.zeros((cout, lanes), bf16)
    for j in range(ks):
        for t in range(tout):
            for q in range(k_in // lanes):
                v = 2 * q - t + 2
                at = (j * 4 + v) * lanes
                tile = tiles[:, at : at + lanes] if 0 <= v < 4 else empty
                w_ref[j, cout * t : cout * (t + 1), lanes * q : lanes * (q + 1)] = tile
    sig_copy.wait()
    split = one_hot_columns((2 * lanes, 2 * lanes), lambda q: swapped(q, 2, lanes))
    parts = [dot(sig_ref[:, b : b + 2 * lanes], split) for b in range(0, 2 * half, 2 * lanes)]
    apart = jnp.concatenate([p[:, :lanes] for p in parts] + [p[:, lanes:] for p in parts], axis=1)
    to_time = one_hot((k_in, k_in), lambda r: swapped(r, tin, cin))
    z = dot(to_time, apart.astype(bf16)).astype(bf16)
    z_ref[...] = z
    z_out.start()
    for copy in cot_copies:
        copy.wait()
    cot_out.start()
    even, odd = z[:, :half], z[:, half:]
    left = dot(w_ref[0], even) + dot(w_ref[1], odd)
    right = dot(w_ref[4], even)
    lane = iota((k_out, half), 1)
    own = (
        dot(w_ref[2], even)
        + dot(w_ref[3], odd)
        + jnp.where(lane == 0, 0.0, pltpu.roll(left, 1, 1))
        + jnp.where(lane == half - 1, 0.0, pltpu.roll(right, half - 1, 1))
    )
    high = own.astype(bf16)
    first = iota((k_out, lanes), 1) == 0

    def parts_of(v):
        top = v.astype(bf16)
        return top, (v - top.astype(f32)).astype(bf16)

    _, own_rest = parts_of(jnp.where(first, own[:, :lanes], own[:, half - lanes :]))
    next_high, next_rest = parts_of(jnp.where(first, right[:, :lanes], left[:, half - lanes :]))
    row, col = iota((edge_rows, 3 * lanes), 0), iota((edge_rows, 3 * lanes), 1)
    pick = jnp.zeros((edge_rows, 3 * lanes), f32)
    for at, column in enumerate((0, lanes - 1, 2 * lanes - 1, 3 * lanes - 1, lanes, 2 * lanes)):
        pick = jnp.where((row == at) & (col == column), 1.0, pick)
    edges = dot_nt(pick.astype(bf16), jnp.concatenate([own_rest, next_high, next_rest], axis=1))
    from_time = one_hot((k_out, k_out), lambda r: swapped(r, cout, tout))
    edges = dot_nt(edges.astype(bf16), from_time)
    main = dot(from_time, high).astype(bf16)
    for d in range(count):
        for b in range(tiles_wide):
            at = slice(lanes * b, lanes * (b + 1))
            out_ref[d, rows * b : rows * (b + 1)] = main[rows * d : rows * (d + 1), at]
        out_ref[d, 2 * conv_rows :] = jnp.zeros((edge_rows, lanes), bf16)
        out_ref[d, 2 * conv_rows :, :rows] = edges[:, rows * d : rows * (d + 1)].astype(bf16)
    conv_out.start()
    edge_out.start()
    cot_out.wait()
    z_out.wait()
    conv_out.wait()
    edge_out.wait()


def transform(real, imag, sign):
    size = len(real)
    if size == 1:
        return (list(real), [None] if imag is None else list(imag))
    even_re, even_im = transform(real[0::2], None if imag is None else imag[0::2], sign)
    odd_re, odd_im = transform(real[1::2], None if imag is None else imag[1::2], sign)
    out_re, out_im = [None] * size, [None] * size

    def plus(a, b):
        return b if a is None else (a if b is None else a + b)

    def minus(a, b):
        return a if b is None else (-b if a is None else a - b)

    for k in range(size // 2):
        re, im = odd_re[k], odd_im[k]
        if k == 0:
            tr, ti = re, im
        elif 4 * k == size:
            tr = None if im is None else (im if sign < 0 else -im)
            ti = -re if sign < 0 else re
        else:
            c, s = math.cos(2 * math.pi * k / size), sign * math.sin(2 * math.pi * k / size)
            if im is None:
                tr, ti = c * re, s * re
            elif 8 * k == size:
                tr, ti = (c * (re - im), c * (re + im)) if sign > 0 else (c * (re + im), c * (im - re))
            elif 8 * k == 3 * size:
                tr, ti = (c * (re + im), c * (im - re)) if sign > 0 else (c * (re - im), c * (re + im))
            else:
                tr, ti = c * re - s * im, s * re + c * im
        out_re[k], out_im[k] = plus(even_re[k], tr), plus(even_im[k], ti)
        out_re[k + size // 2], out_im[k + size // 2] = minus(even_re[k], tr), minus(even_im[k], ti)
    return out_re, out_im


def gelu_slope(v):
    return 0.5 * (1.0 + lax.erf(v * inv_root_two)) + v * jnp.exp(-0.5 * v * v) * inv_root_tau


def filter_kernel(
    dims, cols_ref, resp_ref, twist_ref, high_ref, rest_ref,
    out_ref, cross_ref, x_ref, y_ref, spec_ref, grad_ref,
):
    count, channels, tout, width = dims
    rows, pair = channels * tout, tout // 2
    packed = rows // 2
    group = min(2, channels)
    chunk = group * pair
    edge_row, edge_col = iota((edge_rows, width), 0), iota((edge_rows, width), 1)
    to_low = (edge_col == 0) & ((edge_row == 0) | (edge_row == 2) | (edge_row == 3))
    to_high = (edge_col == width - 1) & ((edge_row == 1) | (edge_row == 4) | (edge_row == 5))
    spread = (to_low | to_high).astype(f32).astype(bf16)
    low = 2 * rows * (width // lanes)
    edges = [cols_ref[d, low:, :rows].astype(f32) for d in range(count)]
    none = jnp.zeros((edge_rows, rows), f32)
    kind = iota((edge_rows, rows), 0)
    for d in range(count):
        before = edges[d - 1] if d > 0 else none
        after = edges[d + 1] if d < count - 1 else none
        joined = jnp.where(kind < 2, edges[d], jnp.where(kind < 4, before, after))
        blocks = [cols_ref[d, rows * b : rows * (b + 1)] for b in range(width // lanes)]
        whole = jnp.concatenate(blocks, axis=1).astype(f32) + dot_tn(joined.astype(bf16), spread)
        x_ref[d] = whole.astype(bf16).astype(f32)

    def forward_planes(real, imag, r, h):
        re, im = transform(real, imag, -1)
        for k in range(count):
            c = twist_ref[0, k : k + 1, h : h + lanes]
            s = twist_ref[1, k : k + 1, h : h + lanes]
            at = slice(k * packed + r, k * packed + r + chunk)
            y_ref[at, h : h + lanes] = re[k] * c + im[k] * s if k else re[k]
            y_ref[at, width + h : width + h + lanes] = im[k] * c - re[k] * s if k else im[k]

    def backward_planes(r, h):
        re, im = [], []
        for k in range(count):
            c = twist_ref[0, k : k + 1, h : h + lanes]
            s = twist_ref[1, k : k + 1, h : h + lanes]
            at = slice(k * packed + r, k * packed + r + chunk)
            a, b = y_ref[at, h : h + lanes], y_ref[at, width + h : width + h + lanes]
            re.append(a * c - b * s if k else a)
            im.append(b * c + a * s if k else b)
        return transform(re, im, 1)

    def inner(product):
        v = y_ref[...]
        high = v.astype(bf16)
        rest = (v - high.astype(f32)).astype(bf16)
        both = product(jnp.concatenate([high, rest], axis=0), high_ref[...])
        size = v.shape[0]
        return both[:size] + both[size:] + product(high, rest_ref[...])

    def paired(tiles):
        return (
            jnp.concatenate([tile[:pair] for tile in tiles], axis=0),
            jnp.concatenate([tile[pair:] for tile in tiles], axis=0),
        )

    chunks = [(r, h) for r in range(0, packed, chunk) for h in range(0, width, lanes)]
    for r, h in chunks:
        planes = [
            paired([x_ref[d, 2 * r + tout * g : 2 * r + tout * (g + 1), h : h + lanes] for g in range(group)])
            for d in range(count)
        ]
        forward_planes([re for re, im in planes], [im for re, im in planes], r, h)
    spec_ref[...] = inner(dot)
    sr, si = spec_ref[:, :width], spec_ref[:, width:]
    rr, ri = resp_ref[0], resp_ref[1]
    y_ref[:, :width] = rr * sr - ri * si
    y_ref[:, width:] = rr * si + ri * sr
    y_ref[...] = inner(dot_nt)
    for r, h in chunks:
        real, imag = backward_planes(r, h)
        at = rows * (width + h) // lanes + 2 * r
        for d in range(count):
            cot = cols_ref[d, at : at + tout * group].astype(f32)
            re, im = paired([cot[tout * g : tout * (g + 1)] for g in range(group)])
            real[d], imag[d] = re * gelu_slope(real[d]), im * gelu_slope(imag[d])
        forward_planes(real, imag, r, h)
    grad_ref[...] = inner(dot)
    sr, si = spec_ref[:, :width], spec_ref[:, width:]
    gr, gi = grad_ref[:, :width], grad_ref[:, width:]
    rr, ri = resp_ref[0], resp_ref[1]
    y_ref[:, :width] = rr * gr + ri * gi
    y_ref[:, width:] = rr * gi - ri * gr
    scale = 1.0 / (count * width)
    spec_ref[:, :width], spec_ref[:, width:] = (sr * gr + si * gi) * scale, (sr * gi - si * gr) * scale
    for k in range(count):
        for ch in range(channels):
            at = k * packed + ch * pair
            cross_ref[k, ch : ch + 1] = jnp.sum(spec_ref[at : at + pair], axis=0, keepdims=True)
    y_ref[...] = inner(dot_nt)
    for r, h in chunks:
        real, imag = backward_planes(r, h)
        for d in range(count):
            for g in range(group):
                at = slice(pair * g, pair * (g + 1))
                tile = jnp.concatenate([real[d][at], imag[d][at]], axis=0)
                x_ref[d, 2 * r + tout * g : 2 * r + tout * (g + 1), h : h + lanes] = tile
    last = ((iota((edge_rows, lanes), 0) == 0) & (iota((edge_rows, lanes), 1) == lanes - 1)).astype(f32).astype(bf16)
    first = ((iota((edge_rows, lanes), 0) == 1) & (iota((edge_rows, lanes), 1) == 0)).astype(f32).astype(bf16)
    for d in range(count):
        for b in range(width // lanes):
            out_ref[d, rows * b : rows * (b + 1)] = x_ref[d, :, lanes * b : lanes * (b + 1)].astype(bf16)
        low = rows * (width // lanes)
        out_ref[d, low:] = jnp.zeros((edge_rows, lanes), bf16)
        edge = none
        if d > 0:
            edge = edge + dot_nt(last, x_ref[d - 1, :, width - lanes :].astype(bf16))
        if d < count - 1:
            edge = edge + dot_nt(first, x_ref[d + 1, :, :lanes].astype(bf16))
        out_ref[d, low:, :rows] = edge.astype(bf16)


def hermitian_kernel(cross_ref, out_ref):
    count, channels, wide = cross_ref.shape
    width = wide // 2
    row, col = iota((width, width), 0), iota((width, width), 1)
    flip = (row + col == width - 1).astype(f32).astype(bf16)
    flip_first = ((row + col == width) | ((row == 0) & (col == 0))).astype(f32).astype(bf16)

    def moved(v, by):
        total = None
        for _ in range(3):
            part = v.astype(bf16)
            v = v - part.astype(f32)
            term = dot(part, by)
            total = term if total is None else total + term
        return total

    for k in range(count):
        own, other = cross_ref[k], cross_ref[(count - k) % count]
        by = flip if k else flip_first
        out_ref[0, :, k] = 0.5 * (own[:, :width] + moved(other[:, :width], by))
        out_ref[1, :, k] = 0.5 * (own[:, width:] - moved(other[:, width:], by))


def tap_kernel(dims, grad_ref, z_ref, tap_ref, shifted_ref, g_ref, zp_ref):
    cin, tin, cout, tout, ks, count, rows = dims
    half = zp_ref.shape[1] // 2
    k_out = cout * tout
    row, col = iota((edge_rows, lanes), 0), iota((edge_rows, lanes), 1)
    spread = (((row == 1) & (col == 0)) | ((row == 0) & (col == 1))).astype(f32).astype(bf16)
    for d in range(count):
        at = slice(rows * d, rows * (d + 1))
        for b in range(half // lanes):
            g_ref[at, lanes * b : lanes * (b + 1)] = grad_ref[d, rows * b : rows * (b + 1)].astype(f32)
        g_ref[at, half:] = dot_tn(grad_ref[d, rows * (half // lanes) :, :rows], spread)
    to_time = one_hot((k_out, k_out), lambda r: swapped(r, tout, cout))
    g = dot(to_time, g_ref[...].astype(bf16)).astype(bf16)
    wide = half + lanes
    later = one_hot_columns((wide, half), lambda n: n + 1)
    sooner = one_hot_columns((wide, half), lambda n: jnp.where(n == 0, half + 1, n - 1))
    shifted_ref[0] = dot(g, later).astype(bf16)
    shifted_ref[1] = g[:, :half]
    shifted_ref[2] = dot(g, sooner).astype(bf16)
    k_in = cin * tin
    pad = 2 * cin
    zp_ref[:pad] = jnp.zeros((pad, 2 * half), bf16)
    zp_ref[pad + k_in :] = jnp.zeros((zp_ref.shape[0] - pad - k_in, 2 * half), bf16)
    zp_ref[pad : pad + k_in] = z_ref[...]
    both, lone = None, None
    for t in range(tout):
        at = slice(cout * t, cout * (t + 1))
        band = zp_ref[2 * cin * t : 2 * cin * t + ks * cin]
        pair = jnp.concatenate([shifted_ref[0, at], shifted_ref[1, at]], axis=0)
        even, odd = band[:, :half], band[:, half:]
        term = jnp.concatenate([dot_nt(even, pair), dot_nt(odd, pair)], axis=0)
        both = term if both is None else both + term
        blank = jnp.zeros((cout, half), bf16)
        mid = ks * cin // 2
        term = dot_nt(even[:mid], jnp.concatenate([shifted_ref[2, at], blank], axis=0)) + dot_nt(
            even[mid:], jnp.concatenate([blank, shifted_ref[2, at]], axis=0)
        )
        lone = term if lone is None else lone + term
    top = both.shape[0]
    tap_ref[:top] = both
    tap_ref[top : top + lone.shape[0]] = lone
    tap_ref[top + lone.shape[0] :] = jnp.zeros((tap_ref.shape[0] - top - lone.shape[0], lanes), f32)


def input_kernel(dims, shifted_ref, taps_ref, out_ref, w_ref):
    cin, tin, cout, tout, ks, count, rows = dims
    k_in = cin * tin
    half = shifted_ref.shape[2]
    blank = jnp.zeros((cin, cout), bf16)
    firsts, seconds = [], []
    for j in range(ks):
        for i in range(ks + 2):
            firsts.append(taps_ref[i, j] if i < ks else blank)
            seconds.append(taps_ref[i - 2, j] if i >= 2 else blank)
    to_first = one_hot((cout, lanes), lambda r: r)
    to_second = one_hot((cout, lanes), lambda r: r + cout)
    tiles = (
        dot(jnp.concatenate(firsts, axis=0), to_first) + dot(jnp.concatenate(seconds, axis=0), to_second)
    ).astype(bf16)
    empty = jnp.zeros((cin, lanes), bf16)
    for j in range(ks):
        for s in range(tin):
            for q in range(cout * tout // lanes):
                i = s - 4 * q + 2
                at = (j * (ks + 2) + i) * cin
                tile = tiles[at : at + cin] if 0 <= i < ks + 2 else empty
                w_ref[j, cin * s : cin * (s + 1), lanes * q : lanes * (q + 1)] = tile
    later, same, sooner = shifted_ref[0], shifted_ref[1], shifted_ref[2]
    even = dot(w_ref[0], later) + dot(w_ref[2], same) + dot(w_ref[4], sooner)
    odd = dot(w_ref[1], later) + dot(w_ref[3], same)
    both = jnp.concatenate([even.astype(bf16), odd.astype(bf16)], axis=1)
    to_channel = one_hot((k_in, k_in), lambda r: swapped(r, cin, tin))
    both = dot(to_channel, both).astype(bf16)
    merge = one_hot((2 * lanes, 2 * lanes), lambda r: swapped(r, 2, lanes))
    for b in range(half // lanes):
        part = jnp.concatenate(
            [both[:, lanes * b : lanes * (b + 1)], both[:, half + lanes * b : half + lanes * (b + 1)]], axis=1
        )
        out_ref[:, 2 * lanes * b : 2 * lanes * (b + 1)] = dot(part, merge).astype(bf16)


def unpack_kernel(dims, scale, tap_ref, out_ref):
    cin, tin, cout, tout, ks, count, rows = dims
    band = ks * cin
    for i in range(ks):
        at = slice(cin * i, cin * (i + 1))
        even, odd = tap_ref[at] * scale, tap_ref[band + cin * i : band + cin * (i + 1)] * scale
        out_ref[i, 0] = even[:, :cout]
        out_ref[i, 2] = even[:, cout:]
        out_ref[i, 1] = odd[:, :cout]
        out_ref[i, 3] = odd[:, cout:]
        for c in range(0, cin, 8):
            at = cin * i + c
            low = at < band // 2
            packed = tap_ref[2 * band + at % (band // 2) : 2 * band + at % (band // 2) + 8] * scale
            out_ref[i, 4, c : c + 8] = packed[:, :cout] if low else packed[:, cout:]


def summed_over(rows, axis, beside):
    count = lax.axis_size(axis)
    bit = lax.axis_index(axis) % 2
    pairs = lambda step: [(i, i ^ step) for i in range(count)]
    size = rows.shape[0] // 2
    kept = lax.dynamic_slice_in_dim(rows, bit * size, size)
    sent = lax.dynamic_slice_in_dim(rows, (1 - bit) * size, size)
    rows = kept + lax.ppermute(sent, axis, pairs(1))
    step = 2
    while step < count:
        rounded = rows.astype(bf16)
        theirs = lambda step: lax.ppermute(rounded, axis, pairs(step)).astype(f32)
        if step == 2 and 4 * step <= count:
            rows = (rounded.astype(f32) + theirs(step)) + (theirs(2 * step) + theirs(3 * step))
            rows, beside = lax.optimization_barrier((rows, beside))
            step *= 4
        else:
            rows = rounded.astype(f32) + theirs(step)
            step *= 2
    other = lax.ppermute(rows, axis, pairs(1))
    rows = jnp.where(bit == 0, jnp.concatenate([rows, other]), jnp.concatenate([other, rows]))
    return rows, beside


def mirrored(spectrum):
    return jnp.roll(jnp.flip(spectrum, -1), 1, -1)


def tables(count, width):
    inner = np.outer(np.arange(width), np.arange(width)) % width * (2.0 * np.pi / width)
    c, s = np.cos(inner), np.sin(inner)
    table = np.block([[c, -s], [s, c]]).astype(np.float32)
    high = table.astype(bf16)
    rest = (table - high.astype(np.float32)).astype(bf16)
    outer = np.outer(np.arange(count), np.arange(width)) * (2.0 * np.pi / (count * width))
    twist = np.stack([np.cos(outer), np.sin(outer)]).astype(np.float32)
    return twist, high, rest


def per_device(signal, conv_taps, response, cotangent):
    cin, tin, fibre_in = signal.shape
    cout, tout, width = cotangent.shape
    ks = conv_taps.shape[0]
    count = lax.axis_size("fibre")
    channels = cout // count
    rows = channels * tout
    waves = count * width
    tiles = width // lanes
    dims = (cin, tin, cout, tout, ks, count, rows)
    k_in, k_out = cin * tin, cout * tout
    taps = jnp.swapaxes(conv_taps, 2, 3)
    shape = jax.ShapeDtypeStruct
    conv_part, z = call(
        functools.partial(conv_kernel, dims),
        [
            shape((count, 2 * rows * tiles + edge_rows, lanes), bf16),
            shape((k_in, fibre_in), bf16),
        ],
        [
            pltpu.VMEM((ks, k_out, k_in), bf16),
            pltpu.VMEM((k_in, fibre_in), bf16),
            pltpu.VMEM(taps.shape, bf16),
            pltpu.VMEM((count, 2 * rows * tiles + edge_rows, lanes), bf16),
            pltpu.VMEM((k_in, fibre_in), bf16),
            pltpu.SemaphoreType.DMA((6 + tiles,)),
        ],
        2e9,
        (signal.reshape(k_in, fibre_in), cotangent.reshape(count, rows, width), taps),
        left=(0, 1, 2),
        left_out=(0, 1),
        room=60,
    )
    cols = lax.all_to_all(conv_part, "fibre", split_axis=0, concat_axis=0, tiled=True)
    pair = tout // 2
    back = mirrored(response)
    real = jnp.stack([response[0] + back[0], response[1] - back[1]]) * (0.5 / waves)
    real = real.reshape(2, channels, 1, width, count).transpose(0, 4, 1, 2, 3)
    real = jnp.broadcast_to(real, (2, count, channels, pair, width)).reshape(2, count * rows // 2, width)
    twist, high, rest = tables(count, width)
    big = count * rows // 2
    grad_part, cross = call(
        functools.partial(filter_kernel, (count, channels, tout, width)),
        [
            shape((count, rows * tiles + edge_rows, lanes), bf16),
            shape((count, channels, 2 * width), f32),
        ],
        [
            pltpu.VMEM((count, rows, width), f32),
            pltpu.VMEM((big, 2 * width), f32),
            pltpu.VMEM((big, 2 * width), f32),
            pltpu.VMEM((big, 2 * width), f32),
        ],
        6e9,
        (cols, real, jnp.asarray(twist), jnp.asarray(high), jnp.asarray(rest)),
    )
    (cross,) = call(hermitian_kernel, [shape((2, channels, count, width), f32)], [], 1e6, (cross,))
    filter_grad = cross.transpose(0, 1, 3, 2).reshape(2, channels, waves)
    grad_cols = lax.all_to_all(grad_part, "fibre", split_axis=0, concat_axis=0, tiled=True)
    grad_cols, filter_grad = lax.optimization_barrier((grad_cols, filter_grad))
    taps_part, shifted = call(
        functools.partial(tap_kernel, dims),
        [shape((tap_rows, lanes), f32), shape((3, k_out, width), bf16)],
        [pltpu.VMEM((k_out, width + lanes), f32), pltpu.VMEM((k_in + 4 * cin, fibre_in), bf16)],
        1e9,
        (grad_cols, z),
    )
    (input_grad,) = call(
        functools.partial(input_kernel, dims),
        [shape((k_in, fibre_in), bf16)],
        [pltpu.VMEM((ks, k_in, k_out), bf16)],
        2e9,
        (shifted, taps),
    )
    total, input_grad = summed_over(taps_part, "fibre", input_grad)
    (tap_grad,) = call(
        functools.partial(unpack_kernel, dims, 1.0 / math.sqrt(tout * waves)),
        [shape((ks, ks, cin, cout), f32)],
        [],
        1e6,
        (total,),
    )
    return (input_grad.reshape(signal.shape), jnp.swapaxes(tap_grad, 2, 3), filter_grad)


def solution(mesh):
    in_specs = (P("parts", None, "fibre"), P(), P(None, "fibre", None), P("parts", None, "fibre"))
    out_specs = (P("parts", None, "fibre"), P("parts", None, None, None), P("parts", "fibre", None))
    return jax.shard_map(
        per_device, mesh=mesh, in_specs=in_specs, out_specs=out_specs, check_vma=False
    )
```

```python
import functools
import math

import jax
import jax.numpy as jnp
import numpy as np
from jax import lax
from jax.experimental import pallas as pl
from jax.experimental.pallas import tpu as pltpu
from jax.sharding import PartitionSpec as P

bf16 = jnp.bfloat16
f32 = jnp.float32
inv_root_two = 1.0 / math.sqrt(2.0)
inv_root_tau = 1.0 / math.sqrt(2.0 * math.pi)
lanes = 128
edge_rows = 8
cores = 2


def dot(a, b):
    return jnp.dot(a, b, preferred_element_type=f32)


def dot_nt(a, b):
    return lax.dot_general(a, b, (((1,), (1,)), ((), ())), preferred_element_type=f32)


def dot_tn(a, b):
    return lax.dot_general(a, b, (((0,), (0,)), ((), ())), preferred_element_type=f32)


def iota(shape, dim):
    return lax.broadcasted_iota(jnp.int32, shape, dim)


def split_index(x, size):
    if size & (size - 1):
        return x // size, x % size
    return lax.shift_right_logical(x, jnp.full_like(x, size.bit_length() - 1)), x & (size - 1)


def swapped(x, outer, inner):
    a, b = split_index(x, inner)
    return b * outer + a


def one_hot(shape, column_of_row):
    return (iota(shape, 1) == column_of_row(iota((shape[0], 1), 0))).astype(f32).astype(bf16)


def one_hot_columns(shape, row_of_column):
    return (iota(shape, 0) == row_of_column(iota((1, shape[1]), 1))).astype(f32).astype(bf16)


def call(kernel, outs, scratch, flops, args, left=(), left_out=(), small=(), room=48):
    moved = sum(a.size * a.dtype.itemsize for a in list(args) + list(outs))
    return pl.pallas_call(
        kernel,
        out_shape=outs,
        in_specs=[
            pl.BlockSpec(
                memory_space=pltpu.HBM if a in left else pltpu.SMEM if a in small else pltpu.VMEM
            )
            for a in range(len(args))
        ],
        out_specs=[
            pl.BlockSpec(memory_space=pltpu.HBM if a in left_out else pltpu.VMEM) for a in range(len(outs))
        ],
        scratch_shapes=scratch,
        compiler_params=pltpu.CompilerParams(vmem_limit_bytes=room << 20),
        cost_estimate=pl.CostEstimate(flops=int(flops), bytes_accessed=moved, transcendentals=0),
    )(*args)


def conv_kernel(
    dims, sig_hbm, cot_hbm, taps_hbm, out_hbm, z_hbm,
    w_ref, sig_ref, taps_ref, out_ref, z_ref, sem,
):
    cin, tin, cout, tout, ks, count, rows = dims
    k_in, k_out = cin * tin, cout * tout
    half = sig_ref.shape[1] // 2
    tiles_wide = half // lanes
    conv_rows = rows * tiles_wide
    taps_copy = pltpu.make_async_copy(taps_hbm, taps_ref, sem.at[0])
    sig_copy = pltpu.make_async_copy(sig_hbm, sig_ref, sem.at[1])
    cot_copies = [
        pltpu.make_async_copy(
            cot_hbm.at[:, :, pl.ds(lanes * b, lanes)],
            out_ref.at[:, pl.ds(conv_rows + rows * b, rows)],
            sem.at[6 + b],
        )
        for b in range(tiles_wide)
    ]
    at_conv, at_edge = pl.ds(0, conv_rows), pl.ds(2 * conv_rows, edge_rows)
    at_cot = pl.ds(conv_rows, conv_rows)
    cot_out = pltpu.make_async_copy(out_ref.at[:, at_cot], out_hbm.at[:, at_cot], sem.at[5])
    z_out = pltpu.make_async_copy(z_ref, z_hbm, sem.at[2])
    conv_out = pltpu.make_async_copy(out_ref.at[:, at_conv], out_hbm.at[:, at_conv], sem.at[3])
    edge_out = pltpu.make_async_copy(out_ref.at[:, at_edge], out_hbm.at[:, at_edge], sem.at[4])
    taps_copy.start()
    sig_copy.start()
    for copy in cot_copies:
        copy.start()
    taps_copy.wait()
    blank = jnp.zeros((2 * cin, cout), bf16)
    stacked = []
    for j in range(ks):
        column = jnp.concatenate([blank] + [taps_ref[i, j] for i in range(ks)] + [blank, blank], axis=0)
        for v in range(4):
            stacked.append(column[2 * cin * v : 2 * cin * v + lanes])
    eye = one_hot((cout, cout), lambda r: r)
    tiles = dot_nt(eye, jnp.concatenate(stacked, axis=0)).astype(bf16)
    empty = jnp.zeros((cout, lanes), bf16)
    for j in range(ks):
        for t in range(tout):
            for q in range(k_in // lanes):
                v = 2 * q - t + 2
                at = (j * 4 + v) * lanes
                tile = tiles[:, at : at + lanes] if 0 <= v < 4 else empty
                w_ref[j, cout * t : cout * (t + 1), lanes * q : lanes * (q + 1)] = tile
    sig_copy.wait()
    split = one_hot_columns((2 * lanes, 2 * lanes), lambda q: swapped(q, 2, lanes))
    parts = [dot(sig_ref[:, b : b + 2 * lanes], split) for b in range(0, 2 * half, 2 * lanes)]
    apart = jnp.concatenate([p[:, :lanes] for p in parts] + [p[:, lanes:] for p in parts], axis=1)
    to_time = one_hot((k_in, k_in), lambda r: swapped(r, tin, cin))
    z = dot(to_time, apart.astype(bf16)).astype(bf16)
    z_ref[...] = z
    z_out.start()
    for copy in cot_copies:
        copy.wait()
    cot_out.start()
    even, odd = z[:, :half], z[:, half:]
    left = dot(w_ref[0], even) + dot(w_ref[1], odd)
    right = dot(w_ref[4], even)
    lane = iota((k_out, half), 1)
    own = (
        dot(w_ref[2], even)
        + dot(w_ref[3], odd)
        + jnp.where(lane == 0, 0.0, pltpu.roll(left, 1, 1))
        + jnp.where(lane == half - 1, 0.0, pltpu.roll(right, half - 1, 1))
    )
    high = own.astype(bf16)
    first = iota((k_out, lanes), 1) == 0

    def parts_of(v):
        top = v.astype(bf16)
        return top, (v - top.astype(f32)).astype(bf16)

    _, own_rest = parts_of(jnp.where(first, own[:, :lanes], own[:, half - lanes :]))
    next_high, next_rest = parts_of(jnp.where(first, right[:, :lanes], left[:, half - lanes :]))
    row, col = iota((edge_rows, 3 * lanes), 0), iota((edge_rows, 3 * lanes), 1)
    pick = jnp.zeros((edge_rows, 3 * lanes), f32)
    for at, column in enumerate((0, lanes - 1, 2 * lanes - 1, 3 * lanes - 1, lanes, 2 * lanes)):
        pick = jnp.where((row == at) & (col == column), 1.0, pick)
    edges = dot_nt(pick.astype(bf16), jnp.concatenate([own_rest, next_high, next_rest], axis=1))
    from_time = one_hot((k_out, k_out), lambda r: swapped(r, cout, tout))
    edges = dot_nt(edges.astype(bf16), from_time)
    main = dot(from_time, high).astype(bf16)
    for d in range(count):
        for b in range(tiles_wide):
            at = slice(lanes * b, lanes * (b + 1))
            out_ref[d, rows * b : rows * (b + 1)] = main[rows * d : rows * (d + 1), at]
        out_ref[d, 2 * conv_rows :] = jnp.zeros((edge_rows, lanes), bf16)
        out_ref[d, 2 * conv_rows :, :rows] = edges[:, rows * d : rows * (d + 1)].astype(bf16)
    conv_out.start()
    edge_out.start()
    cot_out.wait()
    z_out.wait()
    conv_out.wait()
    edge_out.wait()


def transform(real, imag, sign):
    size = len(real)
    if size == 1:
        return (list(real), [None] if imag is None else list(imag))
    even_re, even_im = transform(real[0::2], None if imag is None else imag[0::2], sign)
    odd_re, odd_im = transform(real[1::2], None if imag is None else imag[1::2], sign)
    out_re, out_im = [None] * size, [None] * size

    def plus(a, b):
        return b if a is None else (a if b is None else a + b)

    def minus(a, b):
        return a if b is None else (-b if a is None else a - b)

    for k in range(size // 2):
        re, im = odd_re[k], odd_im[k]
        if k == 0:
            tr, ti = re, im
        elif 4 * k == size:
            tr = None if im is None else (im if sign < 0 else -im)
            ti = -re if sign < 0 else re
        else:
            c, s = math.cos(2 * math.pi * k / size), sign * math.sin(2 * math.pi * k / size)
            if im is None:
                tr, ti = c * re, s * re
            elif 8 * k == size:
                tr, ti = (c * (re - im), c * (re + im)) if sign > 0 else (c * (re + im), c * (im - re))
            elif 8 * k == 3 * size:
                tr, ti = (c * (re + im), c * (im - re)) if sign > 0 else (c * (re - im), c * (re + im))
            else:
                tr, ti = c * re - s * im, s * re + c * im
        out_re[k], out_im[k] = plus(even_re[k], tr), plus(even_im[k], ti)
        out_re[k + size // 2], out_im[k + size // 2] = minus(even_re[k], tr), minus(even_im[k], ti)
    return out_re, out_im


def gelu_slope(v):
    return 0.5 * (1.0 + lax.erf(v * inv_root_two)) + v * jnp.exp(-0.5 * v * v) * inv_root_tau


def filter_kernel(
    dims, cols_ref, resp_ref, twist_ref, high_ref, rest_ref,
    out_ref, cross_ref, x_ref, y_ref, spec_ref, grad_ref,
):
    count, channels, tout, width = dims
    rows, pair = channels * tout, tout // 2
    packed = rows // 2
    group = min(2, channels)
    chunk = group * pair
    edge_row, edge_col = iota((edge_rows, width), 0), iota((edge_rows, width), 1)
    to_low = (edge_col == 0) & ((edge_row == 0) | (edge_row == 2) | (edge_row == 3))
    to_high = (edge_col == width - 1) & ((edge_row == 1) | (edge_row == 4) | (edge_row == 5))
    spread = (to_low | to_high).astype(f32).astype(bf16)
    low = 2 * rows * (width // lanes)
    edges = [cols_ref[d, low:, :rows].astype(f32) for d in range(count)]
    none = jnp.zeros((edge_rows, rows), f32)
    kind = iota((edge_rows, rows), 0)
    for d in range(count):
        before = edges[d - 1] if d > 0 else none
        after = edges[d + 1] if d < count - 1 else none
        joined = jnp.where(kind < 2, edges[d], jnp.where(kind < 4, before, after))
        blocks = [cols_ref[d, rows * b : rows * (b + 1)] for b in range(width // lanes)]
        whole = jnp.concatenate(blocks, axis=1).astype(f32) + dot_tn(joined.astype(bf16), spread)
        x_ref[d] = whole.astype(bf16).astype(f32)

    def forward_planes(real, imag, r, h):
        re, im = transform(real, imag, -1)
        for k in range(count):
            c = twist_ref[0, k : k + 1, h : h + lanes]
            s = twist_ref[1, k : k + 1, h : h + lanes]
            at = slice(k * packed + r, k * packed + r + chunk)
            y_ref[at, h : h + lanes] = re[k] * c + im[k] * s if k else re[k]
            y_ref[at, width + h : width + h + lanes] = im[k] * c - re[k] * s if k else im[k]

    def backward_planes(r, h):
        re, im = [], []
        for k in range(count):
            c = twist_ref[0, k : k + 1, h : h + lanes]
            s = twist_ref[1, k : k + 1, h : h + lanes]
            at = slice(k * packed + r, k * packed + r + chunk)
            a, b = y_ref[at, h : h + lanes], y_ref[at, width + h : width + h + lanes]
            re.append(a * c - b * s if k else a)
            im.append(b * c + a * s if k else b)
        return transform(re, im, 1)

    def inner(product):
        v = y_ref[...]
        high = v.astype(bf16)
        rest = (v - high.astype(f32)).astype(bf16)
        both = product(jnp.concatenate([high, rest], axis=0), high_ref[...])
        size = v.shape[0]
        return both[:size] + both[size:] + product(high, rest_ref[...])

    def paired(tiles):
        return (
            jnp.concatenate([tile[:pair] for tile in tiles], axis=0),
            jnp.concatenate([tile[pair:] for tile in tiles], axis=0),
        )

    chunks = [(r, h) for r in range(0, packed, chunk) for h in range(0, width, lanes)]
    for r, h in chunks:
        planes = [
            paired([x_ref[d, 2 * r + tout * g : 2 * r + tout * (g + 1), h : h + lanes] for g in range(group)])
            for d in range(count)
        ]
        forward_planes([re for re, im in planes], [im for re, im in planes], r, h)
    spec_ref[...] = inner(dot)
    sr, si = spec_ref[:, :width], spec_ref[:, width:]
    rr, ri = resp_ref[0], resp_ref[1]
    y_ref[:, :width] = rr * sr - ri * si
    y_ref[:, width:] = rr * si + ri * sr
    y_ref[...] = inner(dot_nt)
    for r, h in chunks:
        real, imag = backward_planes(r, h)
        at = rows * (width + h) // lanes + 2 * r
        for d in range(count):
            cot = cols_ref[d, at : at + tout * group].astype(f32)
            re, im = paired([cot[tout * g : tout * (g + 1)] for g in range(group)])
            real[d], imag[d] = re * gelu_slope(real[d]), im * gelu_slope(imag[d])
        forward_planes(real, imag, r, h)
    grad_ref[...] = inner(dot)
    sr, si = spec_ref[:, :width], spec_ref[:, width:]
    gr, gi = grad_ref[:, :width], grad_ref[:, width:]
    rr, ri = resp_ref[0], resp_ref[1]
    y_ref[:, :width] = rr * gr + ri * gi
    y_ref[:, width:] = rr * gi - ri * gr
    scale = 1.0 / (count * width)
    spec_ref[:, :width], spec_ref[:, width:] = (sr * gr + si * gi) * scale, (sr * gi - si * gr) * scale
    for k in range(count):
        for ch in range(channels):
            at = k * packed + ch * pair
            cross_ref[k, ch : ch + 1] = jnp.sum(spec_ref[at : at + pair], axis=0, keepdims=True)
    y_ref[...] = inner(dot_nt)
    for r, h in chunks:
        real, imag = backward_planes(r, h)
        for d in range(count):
            for g in range(group):
                at = slice(pair * g, pair * (g + 1))
                tile = jnp.concatenate([real[d][at], imag[d][at]], axis=0)
                x_ref[d, 2 * r + tout * g : 2 * r + tout * (g + 1), h : h + lanes] = tile
    last = ((iota((edge_rows, lanes), 0) == 0) & (iota((edge_rows, lanes), 1) == lanes - 1)).astype(f32).astype(bf16)
    first = ((iota((edge_rows, lanes), 0) == 1) & (iota((edge_rows, lanes), 1) == 0)).astype(f32).astype(bf16)
    for chip in range(count // cores):
        at = 0
        for d in range(cores * chip, cores * (chip + 1)):
            for b in range(0, width, lanes):
                out_ref[chip, at : at + rows] = x_ref[d, :, b : b + lanes].astype(bf16)
                at += rows
        out_ref[chip, at:] = jnp.zeros((edge_rows, lanes), bf16)
        edge = none
        if chip > 0:
            edge = edge + dot_nt(last, x_ref[cores * chip - 1, :, width - lanes :].astype(bf16))
        if chip < count // cores - 1:
            edge = edge + dot_nt(first, x_ref[cores * (chip + 1), :, :lanes].astype(bf16))
        out_ref[chip, at:, :rows] = edge.astype(bf16)


def hermitian_kernel(cross_ref, out_ref):
    count, channels, wide = cross_ref.shape
    width = wide // 2
    row, col = iota((width, width), 0), iota((width, width), 1)
    flip = (row + col == width - 1).astype(f32).astype(bf16)
    flip_first = ((row + col == width) | ((row == 0) & (col == 0))).astype(f32).astype(bf16)

    def moved(v, by):
        total = None
        for _ in range(3):
            part = v.astype(bf16)
            v = v - part.astype(f32)
            term = dot(part, by)
            total = term if total is None else total + term
        return total

    for k in range(count):
        own, other = cross_ref[k], cross_ref[(count - k) % count]
        by = flip if k else flip_first
        out_ref[0, :, k] = 0.5 * (own[:, :width] + moved(other[:, :width], by))
        out_ref[1, :, k] = 0.5 * (own[:, width:] - moved(other[:, width:], by))


def gather_kernel(core_ref, own_ref, other_ref, out_ref):
    k_in, wide = own_ref.shape
    width = wide // 2
    pad = (out_ref.shape[0] - k_in) // 2
    core = core_ref[0]
    out_ref[:pad] = jnp.zeros((pad, cores * wide), bf16)
    out_ref[pad + k_in :] = jnp.zeros((pad, cores * wide), bf16)
    for phase in range(2):
        at = slice(width * phase, width * (phase + 1))
        own_at = pl.multiple_of(wide * phase + width * core, lanes)
        other_at = pl.multiple_of(wide * phase + width * (1 - core), lanes)
        out_ref[pad : pad + k_in, pl.ds(own_at, width)] = own_ref[:, at]
        out_ref[pad : pad + k_in, pl.ds(other_at, width)] = other_ref[:, at]


def tap_kernel(dims, core_ref, grad_ref, z_ref, tap_ref, keep_ref, send_ref, g_ref, shifted_ref):
    cin, tin, cout, tout, ks, count, rows = dims
    some = cout // cores
    width = keep_ref.shape[2]
    wide = cores * width
    core = core_ref[0]
    row, col = iota((edge_rows, 2 * lanes), 0), iota((edge_rows, 2 * lanes), 1)
    spread = (((row == 0) & (col == lanes - 1)) | ((row == 1) & (col == lanes))).astype(f32).astype(bf16)
    for chip in range(count // cores):
        at = slice(rows * chip, rows * (chip + 1))
        low = 0
        for b in range(0, wide, lanes):
            g_ref[at, lanes + b : 2 * lanes + b] = grad_ref[chip, low : low + rows].astype(f32)
            low += rows
        edge = dot_tn(grad_ref[chip, low:, :rows], spread)
        g_ref[at, :lanes] = edge[:, :lanes]
        g_ref[at, lanes + wide :] = edge[:, lanes:]
    to_time = one_hot((some * tout, some * tout), lambda r: swapped(r, tout, some))
    g = dot(to_time, g_ref[...].astype(bf16))
    inside = slice(lanes, lanes + wide)
    shifted_ref[0] = pltpu.roll(g, wide + 2 * lanes - 1, 1)[:, inside].astype(bf16)
    shifted_ref[1] = g[:, inside].astype(bf16)
    shifted_ref[2] = pltpu.roll(g, 1, 1)[:, inside].astype(bf16)
    for shift in range(3):
        keep_ref[shift] = shifted_ref[shift, :, pl.ds(pl.multiple_of(width * core, lanes), width)]
        send_ref[shift] = shifted_ref[shift, :, pl.ds(pl.multiple_of(width * (1 - core), lanes), width)]
    blank = jnp.zeros((lanes - 3 * some, wide), bf16)
    total = None
    for t in range(tout):
        at = slice(some * t, some * (t + 1))
        band = slice(2 * cin * t, 2 * cin * t + ks * cin)
        taken = jnp.concatenate([shifted_ref[shift, at] for shift in range(3)] + [blank], axis=0)
        samples = jnp.concatenate([z_ref[band, :wide], z_ref[band, wide:]], axis=0)
        term = dot_nt(samples, taken)
        total = term if total is None else total + term
    size = ks * cin
    even, odd = total[:size], total[size:]
    tap_ref[:size] = jnp.where(iota((size, lanes), 1) < 3 * some, even, pltpu.roll(odd, 3 * some, 1))
    fold = size * some // lanes
    folded = jnp.zeros((fold, lanes), f32)
    for part in range(lanes // some):
        moved = pltpu.roll(odd[fold * part : fold * (part + 1)], (some * (part - 1)) % lanes, 1)
        here = split_index(iota((fold, lanes), 1), some)[0] == part
        folded = jnp.where(here, moved, folded)
    tap_ref[size:] = folded


def input_kernel(dims, core_ref, own_ref, other_ref, taps_ref, out_ref, w_ref):
    cin, tin, cout, tout, ks, count, rows = dims
    k_in = cin * tin
    half = own_ref.shape[2]
    some, channels = cout // cores, cout // count
    steps = lanes // some
    kinds = ks + 2 * (steps - 1)
    blank = jnp.zeros((cin, cout), bf16)
    core = core_ref[0]
    o, lane = iota((cout, lanes), 0), iota((cout, lanes), 1)
    device, channel = split_index(o, channels)
    chip, core_of = split_index(device, cores)
    for part in range(cores):
        wanted = core if part == 0 else 1 - core
        tiles = None
        for step in range(steps):
            picked = [taps_ref[i - 2 * step, j] if 0 <= i - 2 * step < ks else blank
                      for j in range(ks) for i in range(kinds)]
            place = (core_of == wanted) & (lane == some * step + chip * channels + channel)
            term = dot(jnp.concatenate(picked, axis=0), place.astype(f32).astype(bf16))
            tiles = term if tiles is None else tiles + term
        tiles = tiles.astype(bf16)
        empty = jnp.zeros((cin, lanes), bf16)
        for j in range(ks):
            for s in range(tin):
                for q in range(some * tout // lanes):
                    i = s - 2 * steps * q + 2
                    at = (j * kinds + i) * cin
                    tile = tiles[at : at + cin] if 0 <= i < kinds else empty
                    low = some * tout * part + lanes * q
                    w_ref[j, cin * s : cin * (s + 1), low : low + lanes] = tile
    later, same, sooner = (jnp.concatenate([own_ref[k], other_ref[k]], axis=0) for k in range(3))
    even = dot(w_ref[0], later) + dot(w_ref[2], same) + dot(w_ref[4], sooner)
    odd = dot(w_ref[1], later) + dot(w_ref[3], same)
    both = jnp.concatenate([even.astype(bf16), odd.astype(bf16)], axis=1)
    to_channel = one_hot((k_in, k_in), lambda r: swapped(r, cin, tin))
    both = dot(to_channel, both).astype(bf16)
    merge = one_hot((2 * lanes, 2 * lanes), lambda r: swapped(r, 2, lanes))
    for b in range(half // lanes):
        part = jnp.concatenate(
            [both[:, lanes * b : lanes * (b + 1)], both[:, half + lanes * b : half + lanes * (b + 1)]], axis=1
        )
        out_ref[:, 2 * lanes * b : 2 * lanes * (b + 1)] = dot(part, merge).astype(bf16)


def unpack_kernel(dims, scale, tap_ref, out_ref):
    cin, tin, cout, tout, ks, count, rows = dims
    some, channels = cout // cores, cout // count
    size, folds = ks * cin, lanes // some
    fold = size // folds
    packed = size + fold
    both = jnp.concatenate([tap_ref[:packed], tap_ref[packed:]], axis=1)

    wide = cores * lanes
    source, target = iota((wide, folds * cout), 0), iota((wide, folds * cout), 1)
    slot, o = split_index(target, cout)
    device, channel = split_index(o, channels)
    chip, core_of = split_index(device, cores)
    place = (source == core_of * lanes + slot * some + chip * channels + channel).astype(f32).astype(bf16)
    total, rest = None, both
    for _ in range(3):
        part = rest.astype(bf16)
        rest = rest - part.astype(f32)
        term = dot(part, place)
        total = term if total is None else total + term
    total = total * scale
    for slot, j in enumerate((0, 2, 4, 1)):
        for i in range(ks):
            out_ref[i, j] = total[cin * i : cin * (i + 1), cout * slot : cout * (slot + 1)]
    for at in range(0, size, 8):
        slot, low = at // fold, size + at % fold
        out_ref[at // cin, 3, at % cin : at % cin + 8] = total[low : low + 8, cout * slot : cout * (slot + 1)]


def summed_over_chips(rows, axis, steps):
    count = lax.axis_size(axis)
    rounded = rows.astype(bf16)
    theirs = [lax.ppermute(rounded, axis, partners(count, step)).astype(f32) for step in steps]
    if len(steps) == 1:
        return rounded.astype(f32) + theirs[0]
    return (rounded.astype(f32) + theirs[0]) + (theirs[1] + theirs[2])


def partners(count, step):
    return [(i, i ^ step) for i in range(count)]


def mirrored(spectrum):
    return jnp.roll(jnp.flip(spectrum, -1), 1, -1)


def tables(count, width):
    inner = np.outer(np.arange(width), np.arange(width)) % width * (2.0 * np.pi / width)
    c, s = np.cos(inner), np.sin(inner)
    table = np.block([[c, -s], [s, c]]).astype(np.float32)
    high = table.astype(bf16)
    rest = (table - high.astype(np.float32)).astype(bf16)
    outer = np.outer(np.arange(count), np.arange(width)) * (2.0 * np.pi / (count * width))
    twist = np.stack([np.cos(outer), np.sin(outer)]).astype(np.float32)
    return twist, high, rest


def per_device(signal, conv_taps, response, cotangent):
    cin, tin, fibre_in = signal.shape
    cout, tout, width = cotangent.shape
    ks = conv_taps.shape[0]
    count = lax.axis_size("fibre")
    channels = cout // count
    rows = channels * tout
    waves = count * width
    tiles = width // lanes
    dims = (cin, tin, cout, tout, ks, count, rows)
    k_in, k_out = cin * tin, cout * tout
    taps = jnp.swapaxes(conv_taps, 2, 3)
    shape = jax.ShapeDtypeStruct
    conv_part, z = call(
        functools.partial(conv_kernel, dims),
        [
            shape((count, 2 * rows * tiles + edge_rows, lanes), bf16),
            shape((k_in, fibre_in), bf16),
        ],
        [
            pltpu.VMEM((ks, k_out, k_in), bf16),
            pltpu.VMEM((k_in, fibre_in), bf16),
            pltpu.VMEM(taps.shape, bf16),
            pltpu.VMEM((count, 2 * rows * tiles + edge_rows, lanes), bf16),
            pltpu.VMEM((k_in, fibre_in), bf16),
            pltpu.SemaphoreType.DMA((6 + tiles,)),
        ],
        2e9,
        (signal.reshape(k_in, fibre_in), cotangent.reshape(count, rows, width), taps),
        left=(0, 1, 2),
        left_out=(0, 1),
        room=60,
    )
    other_z = lax.ppermute(z, "fibre", partners(count, 1))
    cols = lax.all_to_all(conv_part, "fibre", split_axis=0, concat_axis=0, tiled=True)
    pair = tout // 2
    back = mirrored(response)
    real = jnp.stack([response[0] + back[0], response[1] - back[1]]) * (0.5 / waves)
    real = real.reshape(2, channels, 1, width, count).transpose(0, 4, 1, 2, 3)
    real = jnp.broadcast_to(real, (2, count, channels, pair, width)).reshape(2, count * rows // 2, width)
    twist, high, rest = tables(count, width)
    big = count * rows // 2
    grad_part, cross = call(
        functools.partial(filter_kernel, (count, channels, tout, width)),
        [
            shape((count // cores, cores * rows * tiles + edge_rows, lanes), bf16),
            shape((count, channels, 2 * width), f32),
        ],
        [
            pltpu.VMEM((count, rows, width), f32),
            pltpu.VMEM((big, 2 * width), f32),
            pltpu.VMEM((big, 2 * width), f32),
            pltpu.VMEM((big, 2 * width), f32),
        ],
        6e9,
        (cols, real, jnp.asarray(twist), jnp.asarray(high), jnp.asarray(rest)),
    )
    (cross,) = call(hermitian_kernel, [shape((2, channels, count, width), f32)], [], 1e6, (cross,))
    filter_grad = cross.transpose(0, 1, 3, 2).reshape(2, channels, waves)
    chips = [[core + cores * chip for chip in range(count // cores)] for core in range(cores)]
    grad_cols = lax.all_to_all(
        grad_part, "fibre", split_axis=0, concat_axis=0, tiled=True, axis_index_groups=chips
    )
    core = (lax.axis_index("fibre") % cores).astype(jnp.int32).reshape(1)
    (samples,) = call(
        gather_kernel,
        [shape((k_in + 4 * cin, cores * fibre_in), bf16)],
        [],
        1e6,
        (core, z, other_z),
        small=(0,),
    )
    grad_cols, filter_grad, samples = lax.optimization_barrier((grad_cols, filter_grad, samples))
    some = k_out // cores
    taps_part, keep, send = call(
        functools.partial(tap_kernel, dims),
        [
            shape((ks * cin + ks * cin * (cout // cores) // lanes, lanes), f32),
            shape((3, some, width), bf16),
            shape((3, some, width), bf16),
        ],
        [
            pltpu.VMEM((some, cores * width + 2 * lanes), f32),
            pltpu.VMEM((3, some, cores * width), bf16),
        ],
        1e9,
        (core, grad_cols, samples),
        small=(0,),
    )
    got = lax.ppermute(send, "fibre", partners(count, 1))
    chips = count // cores
    step = 4 if chips % 4 == 0 else 1
    total = taps_part
    if step == 4:
        total = summed_over_chips(total, "fibre", (cores, 2 * cores, 3 * cores))
    total, keep, got = lax.optimization_barrier((total, keep, got))
    (input_grad,) = call(
        functools.partial(input_kernel, dims),
        [shape((k_in, fibre_in), bf16)],
        [pltpu.VMEM((ks, k_in, k_out), bf16)],
        2e9,
        (core, keep, got, taps),
        small=(0,),
    )
    while step < chips:
        total = summed_over_chips(total, "fibre", (cores * step,))
        step *= 2
    total, input_grad = lax.optimization_barrier((total, input_grad))
    other = lax.ppermute(total, "fibre", partners(count, 1))
    total = jnp.where(core[0] == 0, jnp.concatenate([total, other]), jnp.concatenate([other, total]))
    (tap_grad,) = call(
        functools.partial(unpack_kernel, dims, 1.0 / math.sqrt(tout * waves)),
        [shape((ks, ks, cin, cout), f32)],
        [],
        1e6,
        (total,),
    )
    return (input_grad.reshape(signal.shape), jnp.swapaxes(tap_grad, 2, 3), filter_grad)


def solution(mesh):
    in_specs = (P("parts", None, "fibre"), P(), P(None, "fibre", None), P("parts", None, "fibre"))
    out_specs = (P("parts", None, "fibre"), P("parts", None, None, None), P("parts", "fibre", None))
    return jax.shard_map(
        per_device, mesh=mesh, in_specs=in_specs, out_specs=out_specs, check_vma=False
    )
```

```python
import functools
import math

import jax
import jax.numpy as jnp
import numpy as np
from jax import lax
from jax.experimental import pallas as pl
from jax.experimental.pallas import tpu as pltpu
from jax.sharding import PartitionSpec as P

bf16 = jnp.bfloat16
f32 = jnp.float32
inv_root_two = 1.0 / math.sqrt(2.0)
inv_root_tau = 1.0 / math.sqrt(2.0 * math.pi)
lanes = 128
edge_rows = 8
cores = 2


def dot(a, b):
    return jnp.dot(a, b, preferred_element_type=f32)


def dot_nt(a, b):
    return lax.dot_general(a, b, (((1,), (1,)), ((), ())), preferred_element_type=f32)


def dot_tn(a, b):
    return lax.dot_general(a, b, (((0,), (0,)), ((), ())), preferred_element_type=f32)


def iota(shape, dim):
    return lax.broadcasted_iota(jnp.int32, shape, dim)


def split_index(x, size):
    if size & (size - 1):
        return x // size, x % size
    return lax.shift_right_logical(x, jnp.full_like(x, size.bit_length() - 1)), x & (size - 1)


def swapped(x, outer, inner):
    a, b = split_index(x, inner)
    return b * outer + a


def one_hot(shape, column_of_row):
    return (iota(shape, 1) == column_of_row(iota((shape[0], 1), 0))).astype(f32).astype(bf16)


def one_hot_columns(shape, row_of_column):
    return (iota(shape, 0) == row_of_column(iota((1, shape[1]), 1))).astype(f32).astype(bf16)


def call(kernel, outs, scratch, flops, args, left=(), left_out=(), small=(), room=24):
    moved = sum(a.size * a.dtype.itemsize for a in list(args) + list(outs))
    return pl.pallas_call(
        kernel,
        out_shape=outs,
        in_specs=[
            pl.BlockSpec(
                memory_space=pltpu.HBM if a in left else pltpu.SMEM if a in small else pltpu.VMEM
            )
            for a in range(len(args))
        ],
        out_specs=[
            pl.BlockSpec(memory_space=pltpu.HBM if a in left_out else pltpu.VMEM) for a in range(len(outs))
        ],
        scratch_shapes=scratch,
        compiler_params=pltpu.CompilerParams(vmem_limit_bytes=room << 20),
        cost_estimate=pl.CostEstimate(flops=int(flops), bytes_accessed=moved, transcendentals=0),
    )(*args)


def conv_kernel(
    dims, sig_hbm, cot_hbm, taps_hbm, out_hbm, z_hbm,
    w_ref, sig_ref, taps_ref, out_ref, z_ref, sem,
):
    cin, tin, cout, tout, ks, count, rows = dims
    k_in, k_out = cin * tin, cout * tout
    half = sig_ref.shape[1] // 2
    tiles_wide = half // lanes
    conv_rows = rows * tiles_wide
    taps_copy = pltpu.make_async_copy(taps_hbm, taps_ref, sem.at[0])
    sig_copy = pltpu.make_async_copy(sig_hbm, sig_ref, sem.at[1])
    cot_copies = [
        pltpu.make_async_copy(
            cot_hbm.at[:, :, pl.ds(lanes * b, lanes)],
            out_ref.at[:, pl.ds(conv_rows + rows * b, rows)],
            sem.at[6 + b],
        )
        for b in range(tiles_wide)
    ]
    at_conv, at_edge = pl.ds(0, conv_rows), pl.ds(2 * conv_rows, edge_rows)
    at_cot = pl.ds(conv_rows, conv_rows)
    cot_out = pltpu.make_async_copy(out_ref.at[:, at_cot], out_hbm.at[:, at_cot], sem.at[5])
    z_out = pltpu.make_async_copy(z_ref, z_hbm, sem.at[2])
    conv_out = pltpu.make_async_copy(out_ref.at[:, at_conv], out_hbm.at[:, at_conv], sem.at[3])
    edge_out = pltpu.make_async_copy(out_ref.at[:, at_edge], out_hbm.at[:, at_edge], sem.at[4])
    taps_copy.start()
    sig_copy.start()
    for copy in cot_copies:
        copy.start()
    taps_copy.wait()
    blank = jnp.zeros((2 * cin, cout), bf16)
    stacked = []
    for j in range(ks):
        column = jnp.concatenate([blank] + [taps_ref[i, j] for i in range(ks)] + [blank, blank], axis=0)
        for v in range(4):
            stacked.append(column[2 * cin * v : 2 * cin * v + lanes])
    eye = one_hot((cout, cout), lambda r: r)
    tiles = dot_nt(eye, jnp.concatenate(stacked, axis=0)).astype(bf16)
    empty = jnp.zeros((cout, lanes), bf16)
    for j in range(ks):
        for t in range(tout):
            for q in range(k_in // lanes):
                v = 2 * q - t + 2
                at = (j * 4 + v) * lanes
                tile = tiles[:, at : at + lanes] if 0 <= v < 4 else empty
                w_ref[j, cout * t : cout * (t + 1), lanes * q : lanes * (q + 1)] = tile
    sig_copy.wait()
    split = one_hot_columns((2 * lanes, 2 * lanes), lambda q: swapped(q, 2, lanes))
    parts = [dot(sig_ref[:, b : b + 2 * lanes], split) for b in range(0, 2 * half, 2 * lanes)]
    apart = jnp.concatenate([p[:, :lanes] for p in parts] + [p[:, lanes:] for p in parts], axis=1)
    to_time = one_hot((k_in, k_in), lambda r: swapped(r, tin, cin))
    z = dot(to_time, apart.astype(bf16)).astype(bf16)
    z_ref[...] = z
    z_out.start()
    for copy in cot_copies:
        copy.wait()
    cot_out.start()
    even, odd = z[:, :half], z[:, half:]
    left = dot(w_ref[0], even) + dot(w_ref[1], odd)
    right = dot(w_ref[4], even)
    lane = iota((k_out, half), 1)
    own = (
        dot(w_ref[2], even)
        + dot(w_ref[3], odd)
        + jnp.where(lane == 0, 0.0, pltpu.roll(left, 1, 1))
        + jnp.where(lane == half - 1, 0.0, pltpu.roll(right, half - 1, 1))
    )
    high = own.astype(bf16)
    first = iota((k_out, lanes), 1) == 0

    def parts_of(v):
        top = v.astype(bf16)
        return top, (v - top.astype(f32)).astype(bf16)

    _, own_rest = parts_of(jnp.where(first, own[:, :lanes], own[:, half - lanes :]))
    next_high, next_rest = parts_of(jnp.where(first, right[:, :lanes], left[:, half - lanes :]))
    row, col = iota((edge_rows, 3 * lanes), 0), iota((edge_rows, 3 * lanes), 1)
    pick = jnp.zeros((edge_rows, 3 * lanes), f32)
    for at, column in enumerate((0, lanes - 1, 2 * lanes - 1, 3 * lanes - 1, lanes, 2 * lanes)):
        pick = jnp.where((row == at) & (col == column), 1.0, pick)
    edges = dot_nt(pick.astype(bf16), jnp.concatenate([own_rest, next_high, next_rest], axis=1))
    from_time = one_hot((k_out, k_out), lambda r: swapped(r, cout, tout))
    edges = dot_nt(edges.astype(bf16), from_time)
    main = dot(from_time, high).astype(bf16)
    for d in range(count):
        for b in range(tiles_wide):
            at = slice(lanes * b, lanes * (b + 1))
            out_ref[d, rows * b : rows * (b + 1)] = main[rows * d : rows * (d + 1), at]
        out_ref[d, 2 * conv_rows :] = jnp.zeros((edge_rows, lanes), bf16)
        out_ref[d, 2 * conv_rows :, :rows] = edges[:, rows * d : rows * (d + 1)].astype(bf16)
    conv_out.start()
    edge_out.start()
    cot_out.wait()
    z_out.wait()
    conv_out.wait()
    edge_out.wait()


def transform(real, imag, sign):
    size = len(real)
    if size == 1:
        return (list(real), [None] if imag is None else list(imag))
    even_re, even_im = transform(real[0::2], None if imag is None else imag[0::2], sign)
    odd_re, odd_im = transform(real[1::2], None if imag is None else imag[1::2], sign)
    out_re, out_im = [None] * size, [None] * size

    def plus(a, b):
        return b if a is None else (a if b is None else a + b)

    def minus(a, b):
        return a if b is None else (-b if a is None else a - b)

    for k in range(size // 2):
        re, im = odd_re[k], odd_im[k]
        if k == 0:
            tr, ti = re, im
        elif 4 * k == size:
            tr = None if im is None else (im if sign < 0 else -im)
            ti = -re if sign < 0 else re
        else:
            c, s = math.cos(2 * math.pi * k / size), sign * math.sin(2 * math.pi * k / size)
            if im is None:
                tr, ti = c * re, s * re
            elif 8 * k == size:
                tr, ti = (c * (re - im), c * (re + im)) if sign > 0 else (c * (re + im), c * (im - re))
            elif 8 * k == 3 * size:
                tr, ti = (c * (re + im), c * (im - re)) if sign > 0 else (c * (re - im), c * (re + im))
            else:
                tr, ti = c * re - s * im, s * re + c * im
        out_re[k], out_im[k] = plus(even_re[k], tr), plus(even_im[k], ti)
        out_re[k + size // 2], out_im[k + size // 2] = minus(even_re[k], tr), minus(even_im[k], ti)
    return out_re, out_im


def gelu_slope(v):
    return 0.5 * (1.0 + lax.erf(v * inv_root_two)) + v * jnp.exp(-0.5 * v * v) * inv_root_tau


def filter_kernel(
    dims, cols_ref, resp_ref, twist_ref, high_ref, rest_ref,
    out_ref, cross_ref, x_ref, y_ref, spec_ref, grad_ref, prod_ref,
):
    count, channels, tout, width = dims
    rows, pair = channels * tout, tout // 2
    packed = rows // 2
    group = min(2, channels)
    chunk = group * pair
    edge_row, edge_col = iota((edge_rows, width), 0), iota((edge_rows, width), 1)
    to_low = (edge_col == 0) & ((edge_row == 0) | (edge_row == 2) | (edge_row == 3))
    to_high = (edge_col == width - 1) & ((edge_row == 1) | (edge_row == 4) | (edge_row == 5))
    spread = (to_low | to_high).astype(f32).astype(bf16)
    low = 2 * rows * (width // lanes)
    edges = [cols_ref[d, low:, :rows].astype(f32) for d in range(count)]
    none = jnp.zeros((edge_rows, rows), f32)
    kind = iota((edge_rows, rows), 0)
    for d in range(count):
        before = edges[d - 1] if d > 0 else none
        after = edges[d + 1] if d < count - 1 else none
        joined = jnp.where(kind < 2, edges[d], jnp.where(kind < 4, before, after))
        blocks = [cols_ref[d, rows * b : rows * (b + 1)] for b in range(width // lanes)]
        whole = jnp.concatenate(blocks, axis=1).astype(f32) + dot_tn(joined.astype(bf16), spread)
        x_ref[d] = whole.astype(bf16).astype(f32)

    def forward_planes(real, imag, r, h):
        re, im = transform(real, imag, -1)
        for k in range(count):
            c = twist_ref[0, k : k + 1, h : h + lanes]
            s = twist_ref[1, k : k + 1, h : h + lanes]
            at = slice(k * packed + r, k * packed + r + chunk)
            y_ref[at, h : h + lanes] = re[k] * c + im[k] * s if k else re[k]
            y_ref[at, width + h : width + h + lanes] = im[k] * c - re[k] * s if k else im[k]

    def backward_planes(r, h):
        re, im = [], []
        for k in range(count):
            c = twist_ref[0, k : k + 1, h : h + lanes]
            s = twist_ref[1, k : k + 1, h : h + lanes]
            at = slice(k * packed + r, k * packed + r + chunk)
            a, b = y_ref[at, h : h + lanes], y_ref[at, width + h : width + h + lanes]
            re.append(a * c - b * s if k else a)
            im.append(b * c + a * s if k else b)
        return transform(re, im, 1)

    def inner(product):
        v = y_ref[...]
        high = v.astype(bf16)
        rest = (v - high.astype(f32)).astype(bf16)
        both = product(jnp.concatenate([high, rest], axis=0), high_ref[...])
        size = v.shape[0]
        return both[:size] + both[size:] + product(high, rest_ref[...])

    def paired(tiles):
        return (
            jnp.concatenate([tile[:pair] for tile in tiles], axis=0),
            jnp.concatenate([tile[pair:] for tile in tiles], axis=0),
        )

    chunks = [(r, h) for r in range(0, packed, chunk) for h in range(0, width, lanes)]
    for r, h in chunks:
        planes = [
            paired([x_ref[d, 2 * r + tout * g : 2 * r + tout * (g + 1), h : h + lanes] for g in range(group)])
            for d in range(count)
        ]
        forward_planes([re for re, im in planes], [im for re, im in planes], r, h)
    spec_ref[...] = inner(dot)
    sr, si = spec_ref[:, :width], spec_ref[:, width:]
    rr, ri = resp_ref[0], resp_ref[1]
    y_ref[:, :width] = rr * sr - ri * si
    y_ref[:, width:] = rr * si + ri * sr
    y_ref[...] = inner(dot_nt)
    for r, h in chunks:
        real, imag = backward_planes(r, h)
        at = rows * (width + h) // lanes + 2 * r
        for d in range(count):
            cot = cols_ref[d, at : at + tout * group].astype(f32)
            re, im = paired([cot[tout * g : tout * (g + 1)] for g in range(group)])
            real[d], imag[d] = re * gelu_slope(real[d]), im * gelu_slope(imag[d])
        forward_planes(real, imag, r, h)
    grad_ref[...] = inner(dot)
    sr, si = spec_ref[:, :width], spec_ref[:, width:]
    gr, gi = grad_ref[:, :width], grad_ref[:, width:]
    rr, ri = resp_ref[0], resp_ref[1]
    y_ref[:, :width] = rr * gr + ri * gi
    y_ref[:, width:] = rr * gi - ri * gr
    scale = 1.0 / (count * width)
    crossed = ((sr * gr + si * gi) * scale, (sr * gi - si * gr) * scale)
    wide = width // lanes
    for b in range(2 * wide):
        prod_ref[b] = crossed[b // wide][:, lanes * (b % wide) : lanes * (b % wide + 1)]
    groups = count * channels
    for b in range(2 * wide):
        summed = prod_ref[b, pl.ds(0, groups, stride=pair), :]
        for step in range(1, pair):
            summed = summed + prod_ref[b, pl.ds(step, groups, stride=pair), :]
        cross_ref[:, lanes * b : lanes * (b + 1)] = summed
    y_ref[...] = inner(dot_nt)
    for r, h in chunks:
        real, imag = backward_planes(r, h)
        for d in range(count):
            for g in range(group):
                at = slice(pair * g, pair * (g + 1))
                tile = jnp.concatenate([real[d][at], imag[d][at]], axis=0)
                x_ref[d, 2 * r + tout * g : 2 * r + tout * (g + 1), h : h + lanes] = tile
    last = ((iota((edge_rows, lanes), 0) == 0) & (iota((edge_rows, lanes), 1) == lanes - 1)).astype(f32).astype(bf16)
    first = ((iota((edge_rows, lanes), 0) == 1) & (iota((edge_rows, lanes), 1) == 0)).astype(f32).astype(bf16)
    for chip in range(count // cores):
        at = 0
        for d in range(cores * chip, cores * (chip + 1)):
            for b in range(0, width, lanes):
                out_ref[chip, at : at + rows] = x_ref[d, :, b : b + lanes].astype(bf16)
                at += rows
        out_ref[chip, at:] = jnp.zeros((edge_rows, lanes), bf16)
        edge = none
        if chip > 0:
            edge = edge + dot_nt(last, x_ref[cores * chip - 1, :, width - lanes :].astype(bf16))
        if chip < count // cores - 1:
            edge = edge + dot_nt(first, x_ref[cores * (chip + 1), :, :lanes].astype(bf16))
        out_ref[chip, at:, :rows] = edge.astype(bf16)


def hermitian_kernel(cross_ref, out_ref):
    _, channels, count, width = out_ref.shape
    row, col = iota((width, width), 0), iota((width, width), 1)
    flip = (row + col == width - 1).astype(f32).astype(bf16)
    flip_first = ((row + col == width) | ((row == 0) & (col == 0))).astype(f32).astype(bf16)

    def moved(v, by):
        total = None
        for _ in range(3):
            part = v.astype(bf16)
            v = v - part.astype(f32)
            term = dot(part, by)
            total = term if total is None else total + term
        return total

    for k in range(count):
        from_k = channels * ((count - k) % count)
        own = cross_ref[channels * k : channels * (k + 1)]
        other = cross_ref[from_k : from_k + channels]
        by = flip if k else flip_first
        out_ref[0, :, k] = 0.5 * (own[:, :width] + moved(other[:, :width], by))
        out_ref[1, :, k] = 0.5 * (own[:, width:] - moved(other[:, width:], by))


def gather_kernel(core_ref, own_ref, other_ref, wave_ref, out_ref, high_ref, rest_ref):
    k_in, wide = own_ref.shape
    width = wide // 2
    pad = (out_ref.shape[0] - k_in) // 2
    core = core_ref[0]
    out_ref[:pad] = jnp.zeros((pad, cores * wide), bf16)
    out_ref[pad + k_in :] = jnp.zeros((pad, cores * wide), bf16)
    for phase in range(2):
        at = slice(width * phase, width * (phase + 1))
        own_at = pl.multiple_of(wide * phase + width * core, lanes)
        other_at = pl.multiple_of(wide * phase + width * (1 - core), lanes)
        out_ref[pad : pad + k_in, pl.ds(own_at, width)] = own_ref[:, at]
        out_ref[pad : pad + k_in, pl.ds(other_at, width)] = other_ref[:, at]
    for at, table_ref in ((0, high_ref), (width, rest_ref)):
        cosine, sine = wave_ref[at : at + width, :width], wave_ref[at : at + width, width:]
        table_ref[:width, :width], table_ref[:width, width:] = cosine, -sine
        table_ref[width:, :width], table_ref[width:, width:] = sine, cosine


def tap_kernel(dims, core_ref, grad_ref, z_ref, tap_ref, keep_ref, send_ref, g_ref, shifted_ref):
    cin, tin, cout, tout, ks, count, rows = dims
    some = cout // cores
    width = keep_ref.shape[2]
    wide = cores * width
    core = core_ref[0]
    row, col = iota((edge_rows, 2 * lanes), 0), iota((edge_rows, 2 * lanes), 1)
    spread = (((row == 0) & (col == lanes - 1)) | ((row == 1) & (col == lanes))).astype(f32).astype(bf16)
    for chip in range(count // cores):
        at = slice(rows * chip, rows * (chip + 1))
        low = 0
        for b in range(0, wide, lanes):
            g_ref[at, lanes + b : 2 * lanes + b] = grad_ref[chip, low : low + rows].astype(f32)
            low += rows
        edge = dot_tn(grad_ref[chip, low:, :rows], spread)
        g_ref[at, :lanes] = edge[:, :lanes]
        g_ref[at, lanes + wide :] = edge[:, lanes:]
    to_time = one_hot((some * tout, some * tout), lambda r: swapped(r, tout, some))
    g = dot(to_time, g_ref[...].astype(bf16))
    inside = slice(lanes, lanes + wide)
    shifted_ref[0] = pltpu.roll(g, wide + 2 * lanes - 1, 1)[:, inside].astype(bf16)
    shifted_ref[1] = g[:, inside].astype(bf16)
    shifted_ref[2] = pltpu.roll(g, 1, 1)[:, inside].astype(bf16)
    for shift in range(3):
        keep_ref[shift] = shifted_ref[shift, :, pl.ds(pl.multiple_of(width * core, lanes), width)]
        send_ref[shift] = shifted_ref[shift, :, pl.ds(pl.multiple_of(width * (1 - core), lanes), width)]
    blank = jnp.zeros((lanes - 3 * some, wide), bf16)
    total = None
    for t in range(tout):
        at = slice(some * t, some * (t + 1))
        band = slice(2 * cin * t, 2 * cin * t + ks * cin)
        taken = jnp.concatenate([shifted_ref[shift, at] for shift in range(3)] + [blank], axis=0)
        samples = jnp.concatenate([z_ref[band, :wide], z_ref[band, wide:]], axis=0)
        term = dot_nt(samples, taken)
        total = term if total is None else total + term
    size = ks * cin
    even, odd = total[:size], total[size:]
    tap_ref[:size] = jnp.where(iota((size, lanes), 1) < 3 * some, even, pltpu.roll(odd, 3 * some, 1))
    fold = size * some // lanes
    folded = jnp.zeros((fold, lanes), f32)
    for part in range(lanes // some):
        moved = pltpu.roll(odd[fold * part : fold * (part + 1)], (some * (part - 1)) % lanes, 1)
        here = split_index(iota((fold, lanes), 1), some)[0] == part
        folded = jnp.where(here, moved, folded)
    tap_ref[size:] = folded


def input_kernel(dims, core_ref, own_ref, other_ref, taps_ref, out_ref, w_ref):
    cin, tin, cout, tout, ks, count, rows = dims
    k_in = cin * tin
    half = own_ref.shape[2]
    some, channels = cout // cores, cout // count
    steps = lanes // some
    kinds = ks + 2 * (steps - 1)
    blank = jnp.zeros((cin, cout), bf16)
    core = core_ref[0]
    o, lane = iota((cout, lanes), 0), iota((cout, lanes), 1)
    device, channel = split_index(o, channels)
    chip, core_of = split_index(device, cores)
    for part in range(cores):
        wanted = core if part == 0 else 1 - core
        tiles = None
        for step in range(steps):
            picked = [taps_ref[i - 2 * step, j] if 0 <= i - 2 * step < ks else blank
                      for j in range(ks) for i in range(kinds)]
            place = (core_of == wanted) & (lane == some * step + chip * channels + channel)
            term = dot(jnp.concatenate(picked, axis=0), place.astype(f32).astype(bf16))
            tiles = term if tiles is None else tiles + term
        tiles = tiles.astype(bf16)
        empty = jnp.zeros((cin, lanes), bf16)
        for j in range(ks):
            for s in range(tin):
                for q in range(some * tout // lanes):
                    i = s - 2 * steps * q + 2
                    at = (j * kinds + i) * cin
                    tile = tiles[at : at + cin] if 0 <= i < kinds else empty
                    low = some * tout * part + lanes * q
                    w_ref[j, cin * s : cin * (s + 1), low : low + lanes] = tile
    later, same, sooner = (jnp.concatenate([own_ref[k], other_ref[k]], axis=0) for k in range(3))
    even = dot(w_ref[0], later) + dot(w_ref[2], same) + dot(w_ref[4], sooner)
    odd = dot(w_ref[1], later) + dot(w_ref[3], same)
    both = jnp.concatenate([even.astype(bf16), odd.astype(bf16)], axis=1)
    to_channel = one_hot((k_in, k_in), lambda r: swapped(r, cin, tin))
    both = dot(to_channel, both).astype(bf16)
    merge = one_hot((2 * lanes, 2 * lanes), lambda r: swapped(r, 2, lanes))
    for b in range(half // lanes):
        part = jnp.concatenate(
            [both[:, lanes * b : lanes * (b + 1)], both[:, half + lanes * b : half + lanes * (b + 1)]], axis=1
        )
        out_ref[:, 2 * lanes * b : 2 * lanes * (b + 1)] = dot(part, merge).astype(bf16)


def unpack_kernel(dims, scale, tap_ref, out_ref):
    cin, tin, cout, tout, ks, count, rows = dims
    some, channels = cout // cores, cout // count
    size, folds = ks * cin, lanes // some
    fold = size // folds
    packed = size + fold
    both = jnp.concatenate([tap_ref[:packed], tap_ref[packed:]], axis=1)

    wide = cores * lanes
    source, target = iota((wide, folds * cout), 0), iota((wide, folds * cout), 1)
    slot, o = split_index(target, cout)
    device, channel = split_index(o, channels)
    chip, core_of = split_index(device, cores)
    place = (source == core_of * lanes + slot * some + chip * channels + channel).astype(f32).astype(bf16)
    total, rest = None, both
    for _ in range(3):
        part = rest.astype(bf16)
        rest = rest - part.astype(f32)
        term = dot(part, place)
        total = term if total is None else total + term
    total = total * scale
    for slot, j in enumerate((0, 2, 4, 1)):
        for i in range(ks):
            out_ref[i, j] = total[cin * i : cin * (i + 1), cout * slot : cout * (slot + 1)]
    for at in range(0, size, 8):
        slot, low = at // fold, size + at % fold
        out_ref[at // cin, 3, at % cin : at % cin + 8] = total[low : low + 8, cout * slot : cout * (slot + 1)]


def summed_over_chips(rows, axis, steps):
    count = lax.axis_size(axis)
    rounded = rows.astype(bf16)
    theirs = [lax.ppermute(rounded, axis, partners(count, step)).astype(f32) for step in steps]
    if len(steps) == 1:
        return rounded.astype(f32) + theirs[0]
    return (rounded.astype(f32) + theirs[0]) + (theirs[1] + theirs[2])


def partners(count, step):
    return [(i, i ^ step) for i in range(count)]


def mirrored(spectrum):
    return jnp.roll(jnp.flip(spectrum, -1), 1, -1)


def tables(count, width):
    inner = np.outer(np.arange(width), np.arange(width)) % width * (2.0 * np.pi / width)
    table = np.concatenate([np.cos(inner), np.sin(inner)], axis=1).astype(np.float32)
    high = table.astype(bf16)
    rest = (table - high.astype(np.float32)).astype(bf16)
    outer = np.outer(np.arange(count), np.arange(width)) * (2.0 * np.pi / (count * width))
    twist = np.stack([np.cos(outer), np.sin(outer)]).astype(np.float32)
    return twist, np.concatenate([high, rest])


def per_device(signal, conv_taps, response, cotangent):
    cin, tin, fibre_in = signal.shape
    cout, tout, width = cotangent.shape
    ks = conv_taps.shape[0]
    count = lax.axis_size("fibre")
    channels = cout // count
    rows = channels * tout
    waves = count * width
    tiles = width // lanes
    dims = (cin, tin, cout, tout, ks, count, rows)
    k_in, k_out = cin * tin, cout * tout
    taps = jnp.swapaxes(conv_taps, 2, 3)
    shape = jax.ShapeDtypeStruct
    conv_part, z = call(
        functools.partial(conv_kernel, dims),
        [
            shape((count, 2 * rows * tiles + edge_rows, lanes), bf16),
            shape((k_in, fibre_in), bf16),
        ],
        [
            pltpu.VMEM((ks, k_out, k_in), bf16),
            pltpu.VMEM((k_in, fibre_in), bf16),
            pltpu.VMEM(taps.shape, bf16),
            pltpu.VMEM((count, 2 * rows * tiles + edge_rows, lanes), bf16),
            pltpu.VMEM((k_in, fibre_in), bf16),
            pltpu.SemaphoreType.DMA((6 + tiles,)),
        ],
        2e9,
        (signal.reshape(k_in, fibre_in), cotangent.reshape(count, rows, width), taps),
        left=(0, 1, 2),
        left_out=(0, 1),
        room=60,
    )
    other_z = lax.ppermute(z, "fibre", partners(count, 1))
    cols = lax.all_to_all(conv_part, "fibre", split_axis=0, concat_axis=0, tiled=True)
    core = (lax.axis_index("fibre") % cores).astype(jnp.int32).reshape(1)
    twist, waves_table = tables(count, width)
    matrix = shape((2 * width, 2 * width), bf16)
    samples, high, rest = call(
        gather_kernel,
        [shape((k_in + 4 * cin, cores * fibre_in), bf16), matrix, matrix],
        [],
        1e6,
        (core, z, other_z, jnp.asarray(waves_table)),
        small=(0,),
    )
    cols, samples, high, rest = lax.optimization_barrier((cols, samples, high, rest))
    pair = tout // 2
    back = mirrored(response)
    real = jnp.stack([response[0] + back[0], response[1] - back[1]]) * (0.5 / waves)
    real = real.reshape(2, channels, 1, width, count).transpose(0, 4, 1, 2, 3)
    real = jnp.broadcast_to(real, (2, count, channels, pair, width)).reshape(2, count * rows // 2, width)
    big = count * rows // 2
    grad_part, cross = call(
        functools.partial(filter_kernel, (count, channels, tout, width)),
        [
            shape((count // cores, cores * rows * tiles + edge_rows, lanes), bf16),
            shape((count * channels, 2 * width), f32),
        ],
        [
            pltpu.VMEM((count, rows, width), f32),
            pltpu.VMEM((big, 2 * width), f32),
            pltpu.VMEM((big, 2 * width), f32),
            pltpu.VMEM((big, 2 * width), f32),
            pltpu.VMEM((2 * tiles, big, lanes), f32),
        ],
        6e9,
        (cols, real, jnp.asarray(twist), high, rest),
    )
    (cross,) = call(hermitian_kernel, [shape((2, channels, count, width), f32)], [], 1e6, (cross,))
    filter_grad = cross.transpose(0, 1, 3, 2).reshape(2, channels, waves)
    chips = [[core + cores * chip for chip in range(count // cores)] for core in range(cores)]
    grad_cols = lax.all_to_all(
        grad_part, "fibre", split_axis=0, concat_axis=0, tiled=True, axis_index_groups=chips
    )
    grad_cols, filter_grad = lax.optimization_barrier((grad_cols, filter_grad))
    some = k_out // cores
    taps_part, keep, send = call(
        functools.partial(tap_kernel, dims),
        [
            shape((ks * cin + ks * cin * (cout // cores) // lanes, lanes), f32),
            shape((3, some, width), bf16),
            shape((3, some, width), bf16),
        ],
        [
            pltpu.VMEM((some, cores * width + 2 * lanes), f32),
            pltpu.VMEM((3, some, cores * width), bf16),
        ],
        1e9,
        (core, grad_cols, samples),
        small=(0,),
    )
    got = lax.ppermute(send, "fibre", partners(count, 1))
    chips = count // cores
    step = 4 if chips % 4 == 0 else 1
    total = taps_part
    if step == 4:
        total = summed_over_chips(total, "fibre", (cores, 2 * cores, 3 * cores))
    total, keep, got = lax.optimization_barrier((total, keep, got))
    (input_grad,) = call(
        functools.partial(input_kernel, dims),
        [shape((k_in, fibre_in), bf16)],
        [pltpu.VMEM((ks, k_in, k_out), bf16)],
        2e9,
        (core, keep, got, taps),
        small=(0,),
    )
    while step < chips:
        total = summed_over_chips(total, "fibre", (cores * step,))
        step *= 2
    total, input_grad = lax.optimization_barrier((total, input_grad))
    other = lax.ppermute(total, "fibre", partners(count, 1))
    total = jnp.where(core[0] == 0, jnp.concatenate([total, other]), jnp.concatenate([other, total]))
    (tap_grad,) = call(
        functools.partial(unpack_kernel, dims, 1.0 / math.sqrt(tout * waves)),
        [shape((ks, ks, cin, cout), f32)],
        [],
        1e6,
        (total,),
    )
    return (input_grad.reshape(signal.shape), jnp.swapaxes(tap_grad, 2, 3), filter_grad)


def solution(mesh):
    in_specs = (P("parts", None, "fibre"), P(), P(None, "fibre", None), P("parts", None, "fibre"))
    out_specs = (P("parts", None, "fibre"), P("parts", None, None, None), P("parts", "fibre", None))
    return jax.shard_map(
        per_device, mesh=mesh, in_specs=in_specs, out_specs=out_specs, check_vma=False
    )
```

```python
import functools
import math

import jax
import jax.numpy as jnp
import numpy as np
from jax import lax
from jax.experimental import pallas as pl
from jax.experimental.pallas import tpu as pltpu
from jax.sharding import PartitionSpec as P

bf16 = jnp.bfloat16
f32 = jnp.float32
inv_root_two = 1.0 / math.sqrt(2.0)
inv_root_tau = 1.0 / math.sqrt(2.0 * math.pi)
lanes = 128
edge_rows = 8
cores = 2


def dot(a, b):
    return jnp.dot(a, b, preferred_element_type=f32)


def dot_nt(a, b):
    return lax.dot_general(a, b, (((1,), (1,)), ((), ())), preferred_element_type=f32)


def dot_tn(a, b):
    return lax.dot_general(a, b, (((0,), (0,)), ((), ())), preferred_element_type=f32)


def iota(shape, dim):
    return lax.broadcasted_iota(jnp.int32, shape, dim)


def split_index(x, size):
    if size & (size - 1):
        return x // size, x % size
    return lax.shift_right_logical(x, jnp.full_like(x, size.bit_length() - 1)), x & (size - 1)


def swapped(x, outer, inner):
    a, b = split_index(x, inner)
    return b * outer + a


def one_hot(shape, column_of_row):
    return (iota(shape, 1) == column_of_row(iota((shape[0], 1), 0))).astype(f32).astype(bf16)


def one_hot_columns(shape, row_of_column):
    return (iota(shape, 0) == row_of_column(iota((1, shape[1]), 1))).astype(f32).astype(bf16)


def call(kernel, outs, scratch, flops, args, left=(), left_out=(), small=(), room=24):
    moved = sum(a.size * a.dtype.itemsize for a in list(args) + list(outs))
    return pl.pallas_call(
        kernel,
        out_shape=outs,
        in_specs=[
            pl.BlockSpec(
                memory_space=pltpu.HBM if a in left else pltpu.SMEM if a in small else pltpu.VMEM
            )
            for a in range(len(args))
        ],
        out_specs=[
            pl.BlockSpec(memory_space=pltpu.HBM if a in left_out else pltpu.VMEM) for a in range(len(outs))
        ],
        scratch_shapes=scratch,
        compiler_params=pltpu.CompilerParams(vmem_limit_bytes=room << 20),
        cost_estimate=pl.CostEstimate(flops=int(flops), bytes_accessed=moved, transcendentals=0),
    )(*args)


def conv_kernel(
    dims, sig_hbm, cot_hbm, taps_hbm, out_hbm, z_hbm,
    w_ref, sig_ref, taps_ref, out_ref, z_ref, sem,
):
    cin, tin, cout, tout, ks, count, rows = dims
    k_in, k_out = cin * tin, cout * tout
    half = sig_ref.shape[1] // 2
    tiles_wide = half // lanes
    conv_rows = rows * tiles_wide
    taps_copy = pltpu.make_async_copy(taps_hbm, taps_ref, sem.at[0])
    sig_copy = pltpu.make_async_copy(sig_hbm, sig_ref, sem.at[1])
    cot_copies = [
        pltpu.make_async_copy(
            cot_hbm.at[:, :, pl.ds(lanes * b, lanes)],
            out_ref.at[:, pl.ds(conv_rows + rows * b, rows)],
            sem.at[6 + b],
        )
        for b in range(tiles_wide)
    ]
    at_conv, at_edge = pl.ds(0, conv_rows), pl.ds(2 * conv_rows, edge_rows)
    at_cot = pl.ds(conv_rows, conv_rows)
    cot_out = pltpu.make_async_copy(out_ref.at[:, at_cot], out_hbm.at[:, at_cot], sem.at[5])
    z_out = pltpu.make_async_copy(z_ref, z_hbm, sem.at[2])
    conv_out = pltpu.make_async_copy(out_ref.at[:, at_conv], out_hbm.at[:, at_conv], sem.at[3])
    edge_out = pltpu.make_async_copy(out_ref.at[:, at_edge], out_hbm.at[:, at_edge], sem.at[4])
    taps_copy.start()
    sig_copy.start()
    for copy in cot_copies:
        copy.start()
    taps_copy.wait()
    blank = jnp.zeros((2 * cin, cout), bf16)
    stacked = []
    for j in range(ks):
        column = jnp.concatenate([blank] + [taps_ref[i, j] for i in range(ks)] + [blank, blank], axis=0)
        for v in range(4):
            stacked.append(column[2 * cin * v : 2 * cin * v + lanes])
    eye = one_hot((cout, cout), lambda r: r)
    tiles = dot_nt(eye, jnp.concatenate(stacked, axis=0)).astype(bf16)
    empty = jnp.zeros((cout, lanes), bf16)
    for j in range(ks):
        for t in range(tout):
            for q in range(k_in // lanes):
                v = 2 * q - t + 2
                at = (j * 4 + v) * lanes
                tile = tiles[:, at : at + lanes] if 0 <= v < 4 else empty
                w_ref[j, cout * t : cout * (t + 1), lanes * q : lanes * (q + 1)] = tile
    sig_copy.wait()
    split = one_hot_columns((2 * lanes, 2 * lanes), lambda q: swapped(q, 2, lanes))
    parts = [dot(sig_ref[:, b : b + 2 * lanes], split) for b in range(0, 2 * half, 2 * lanes)]
    apart = jnp.concatenate([p[:, :lanes] for p in parts] + [p[:, lanes:] for p in parts], axis=1)
    to_time = one_hot((k_in, k_in), lambda r: swapped(r, tin, cin))
    z = dot(to_time, apart.astype(bf16)).astype(bf16)
    z_ref[...] = z
    z_out.start()
    for copy in cot_copies:
        copy.wait()
    cot_out.start()
    even, odd = z[:, :half], z[:, half:]
    left = dot(w_ref[0], even) + dot(w_ref[1], odd)
    right = dot(w_ref[4], even)
    lane = iota((k_out, half), 1)
    own = (
        dot(w_ref[2], even)
        + dot(w_ref[3], odd)
        + jnp.where(lane == 0, 0.0, pltpu.roll(left, 1, 1))
        + jnp.where(lane == half - 1, 0.0, pltpu.roll(right, half - 1, 1))
    )
    high = own.astype(bf16)
    first = iota((k_out, lanes), 1) == 0

    def parts_of(v):
        top = v.astype(bf16)
        return top, (v - top.astype(f32)).astype(bf16)

    _, own_rest = parts_of(jnp.where(first, own[:, :lanes], own[:, half - lanes :]))
    next_high, next_rest = parts_of(jnp.where(first, right[:, :lanes], left[:, half - lanes :]))
    row, col = iota((edge_rows, 3 * lanes), 0), iota((edge_rows, 3 * lanes), 1)
    pick = jnp.zeros((edge_rows, 3 * lanes), f32)
    for at, column in enumerate((0, lanes - 1, 2 * lanes - 1, 3 * lanes - 1, lanes, 2 * lanes)):
        pick = jnp.where((row == at) & (col == column), 1.0, pick)
    edges = dot_nt(pick.astype(bf16), jnp.concatenate([own_rest, next_high, next_rest], axis=1))
    from_time = one_hot((k_out, k_out), lambda r: swapped(r, cout, tout))
    edges = dot_nt(edges.astype(bf16), from_time)
    main = dot(from_time, high).astype(bf16)
    for d in range(count):
        for b in range(tiles_wide):
            at = slice(lanes * b, lanes * (b + 1))
            out_ref[d, rows * b : rows * (b + 1)] = main[rows * d : rows * (d + 1), at]
        out_ref[d, 2 * conv_rows :] = jnp.zeros((edge_rows, lanes), bf16)
        out_ref[d, 2 * conv_rows :, :rows] = edges[:, rows * d : rows * (d + 1)].astype(bf16)
    conv_out.start()
    edge_out.start()
    cot_out.wait()
    z_out.wait()
    conv_out.wait()
    edge_out.wait()


def transform(real, imag, sign):
    size = len(real)
    if size == 1:
        return (list(real), [None] if imag is None else list(imag))
    even_re, even_im = transform(real[0::2], None if imag is None else imag[0::2], sign)
    odd_re, odd_im = transform(real[1::2], None if imag is None else imag[1::2], sign)
    out_re, out_im = [None] * size, [None] * size

    def plus(a, b):
        return b if a is None else (a if b is None else a + b)

    def minus(a, b):
        return a if b is None else (-b if a is None else a - b)

    for k in range(size // 2):
        re, im = odd_re[k], odd_im[k]
        if k == 0:
            tr, ti = re, im
        elif 4 * k == size:
            tr = None if im is None else (im if sign < 0 else -im)
            ti = -re if sign < 0 else re
        else:
            c, s = math.cos(2 * math.pi * k / size), sign * math.sin(2 * math.pi * k / size)
            if im is None:
                tr, ti = c * re, s * re
            elif 8 * k == size:
                tr, ti = (c * (re - im), c * (re + im)) if sign > 0 else (c * (re + im), c * (im - re))
            elif 8 * k == 3 * size:
                tr, ti = (c * (re + im), c * (im - re)) if sign > 0 else (c * (re - im), c * (re + im))
            else:
                tr, ti = c * re - s * im, s * re + c * im
        out_re[k], out_im[k] = plus(even_re[k], tr), plus(even_im[k], ti)
        out_re[k + size // 2], out_im[k + size // 2] = minus(even_re[k], tr), minus(even_im[k], ti)
    return out_re, out_im


def gelu_slope(v):
    return 0.5 * (1.0 + lax.erf(v * inv_root_two)) + v * jnp.exp(-0.5 * v * v) * inv_root_tau


def filter_kernel(
    dims, cols_ref, own_ref, twist_ref, wave_ref,
    out_ref, cross_ref, x_ref, y_ref, spec_ref, grad_ref, prod_ref, resp_ref, high_ref, rest_ref,
):
    count, channels, tout, width = dims
    rows, pair = channels * tout, tout // 2
    wide, groups = width // lanes, count * channels
    for at, table_ref in ((0, high_ref), (width, rest_ref)):
        cosine, sine = wave_ref[at : at + width, :width], wave_ref[at : at + width, width:]
        table_ref[:width, :width], table_ref[:width, width:] = cosine, -sine
        table_ref[width:, :width], table_ref[width:, width:] = sine, cosine
    for b in range(2 * wide):
        own = own_ref[b // wide, :, lanes * (b % wide) : lanes * (b % wide + 1)]
        for step in range(pair):
            resp_ref[b, pl.ds(step, groups, stride=pair), :] = own
    packed = rows // 2
    group = min(2, channels)
    chunk = group * pair
    edge_row, edge_col = iota((edge_rows, width), 0), iota((edge_rows, width), 1)
    to_low = (edge_col == 0) & ((edge_row == 0) | (edge_row == 2) | (edge_row == 3))
    to_high = (edge_col == width - 1) & ((edge_row == 1) | (edge_row == 4) | (edge_row == 5))
    spread = (to_low | to_high).astype(f32).astype(bf16)
    low = 2 * rows * (width // lanes)
    edges = [cols_ref[d, low:, :rows].astype(f32) for d in range(count)]
    none = jnp.zeros((edge_rows, rows), f32)
    kind = iota((edge_rows, rows), 0)
    for d in range(count):
        before = edges[d - 1] if d > 0 else none
        after = edges[d + 1] if d < count - 1 else none
        joined = jnp.where(kind < 2, edges[d], jnp.where(kind < 4, before, after))
        blocks = [cols_ref[d, rows * b : rows * (b + 1)] for b in range(width // lanes)]
        whole = jnp.concatenate(blocks, axis=1).astype(f32) + dot_tn(joined.astype(bf16), spread)
        x_ref[d] = whole.astype(bf16).astype(f32)

    def forward_planes(real, imag, r, h):
        re, im = transform(real, imag, -1)
        for k in range(count):
            c = twist_ref[0, k : k + 1, h : h + lanes]
            s = twist_ref[1, k : k + 1, h : h + lanes]
            at = slice(k * packed + r, k * packed + r + chunk)
            y_ref[at, h : h + lanes] = re[k] * c + im[k] * s if k else re[k]
            y_ref[at, width + h : width + h + lanes] = im[k] * c - re[k] * s if k else im[k]

    def backward_planes(r, h):
        re, im = [], []
        for k in range(count):
            c = twist_ref[0, k : k + 1, h : h + lanes]
            s = twist_ref[1, k : k + 1, h : h + lanes]
            at = slice(k * packed + r, k * packed + r + chunk)
            a, b = y_ref[at, h : h + lanes], y_ref[at, width + h : width + h + lanes]
            re.append(a * c - b * s if k else a)
            im.append(b * c + a * s if k else b)
        return transform(re, im, 1)

    def inner(product):
        v = y_ref[...]
        high = v.astype(bf16)
        rest = (v - high.astype(f32)).astype(bf16)
        both = product(jnp.concatenate([high, rest], axis=0), high_ref[...])
        size = v.shape[0]
        return both[:size] + both[size:] + product(high, rest_ref[...])

    def paired(tiles):
        return (
            jnp.concatenate([tile[:pair] for tile in tiles], axis=0),
            jnp.concatenate([tile[pair:] for tile in tiles], axis=0),
        )

    chunks = [(r, h) for r in range(0, packed, chunk) for h in range(0, width, lanes)]
    for r, h in chunks:
        planes = [
            paired([x_ref[d, 2 * r + tout * g : 2 * r + tout * (g + 1), h : h + lanes] for g in range(group)])
            for d in range(count)
        ]
        forward_planes([re for re, im in planes], [im for re, im in planes], r, h)
    spec_ref[...] = inner(dot)
    sr, si = spec_ref[:, :width], spec_ref[:, width:]
    rr, ri = (jnp.concatenate([resp_ref[p * wide + b] for b in range(wide)], axis=1) for p in range(2))
    y_ref[:, :width] = rr * sr - ri * si
    y_ref[:, width:] = rr * si + ri * sr
    y_ref[...] = inner(dot_nt)
    for r, h in chunks:
        real, imag = backward_planes(r, h)
        at = rows * (width + h) // lanes + 2 * r
        for d in range(count):
            cot = cols_ref[d, at : at + tout * group].astype(f32)
            re, im = paired([cot[tout * g : tout * (g + 1)] for g in range(group)])
            real[d], imag[d] = re * gelu_slope(real[d]), im * gelu_slope(imag[d])
        forward_planes(real, imag, r, h)
    grad_ref[...] = inner(dot)
    sr, si = spec_ref[:, :width], spec_ref[:, width:]
    gr, gi = grad_ref[:, :width], grad_ref[:, width:]
    rr, ri = (jnp.concatenate([resp_ref[p * wide + b] for b in range(wide)], axis=1) for p in range(2))
    y_ref[:, :width] = rr * gr + ri * gi
    y_ref[:, width:] = rr * gi - ri * gr
    scale = 1.0 / (count * width)
    crossed = ((sr * gr + si * gi) * scale, (sr * gi - si * gr) * scale)
    for b in range(2 * wide):
        prod_ref[b] = crossed[b // wide][:, lanes * (b % wide) : lanes * (b % wide + 1)]
    for b in range(2 * wide):
        summed = prod_ref[b, pl.ds(0, groups, stride=pair), :]
        for step in range(1, pair):
            summed = summed + prod_ref[b, pl.ds(step, groups, stride=pair), :]
        cross_ref[:, lanes * b : lanes * (b + 1)] = summed
    y_ref[...] = inner(dot_nt)
    for r, h in chunks:
        real, imag = backward_planes(r, h)
        for d in range(count):
            for g in range(group):
                at = slice(pair * g, pair * (g + 1))
                tile = jnp.concatenate([real[d][at], imag[d][at]], axis=0)
                x_ref[d, 2 * r + tout * g : 2 * r + tout * (g + 1), h : h + lanes] = tile
    last = ((iota((edge_rows, lanes), 0) == 0) & (iota((edge_rows, lanes), 1) == lanes - 1)).astype(f32).astype(bf16)
    first = ((iota((edge_rows, lanes), 0) == 1) & (iota((edge_rows, lanes), 1) == 0)).astype(f32).astype(bf16)
    for chip in range(count // cores):
        at = 0
        for d in range(cores * chip, cores * (chip + 1)):
            for b in range(0, width, lanes):
                out_ref[chip, at : at + rows] = x_ref[d, :, b : b + lanes].astype(bf16)
                at += rows
        out_ref[chip, at:] = jnp.zeros((edge_rows, lanes), bf16)
        edge = none
        if chip > 0:
            edge = edge + dot_nt(last, x_ref[cores * chip - 1, :, width - lanes :].astype(bf16))
        if chip < count // cores - 1:
            edge = edge + dot_nt(first, x_ref[cores * (chip + 1), :, :lanes].astype(bf16))
        out_ref[chip, at:, :rows] = edge.astype(bf16)


def hermitian_kernel(cross_ref, out_ref):
    _, channels, count, width = out_ref.shape
    row, col = iota((width, width), 0), iota((width, width), 1)
    flip = (row + col == width - 1).astype(f32).astype(bf16)
    flip_first = ((row + col == width) | ((row == 0) & (col == 0))).astype(f32).astype(bf16)

    def moved(v, by):
        total = None
        for _ in range(3):
            part = v.astype(bf16)
            v = v - part.astype(f32)
            term = dot(part, by)
            total = term if total is None else total + term
        return total

    for k in range(count):
        from_k = channels * ((count - k) % count)
        own = cross_ref[channels * k : channels * (k + 1)]
        other = cross_ref[from_k : from_k + channels]
        by = flip if k else flip_first
        out_ref[0, :, k] = 0.5 * (own[:, :width] + moved(other[:, :width], by))
        out_ref[1, :, k] = 0.5 * (own[:, width:] - moved(other[:, width:], by))


def gather_kernel(core_ref, own_ref, other_ref, out_ref):
    k_in, wide = own_ref.shape
    width = wide // 2
    pad = (out_ref.shape[0] - k_in) // 2
    core = core_ref[0]
    out_ref[:pad] = jnp.zeros((pad, cores * wide), bf16)
    out_ref[pad + k_in :] = jnp.zeros((pad, cores * wide), bf16)
    for phase in range(2):
        at = slice(width * phase, width * (phase + 1))
        own_at = pl.multiple_of(wide * phase + width * core, lanes)
        other_at = pl.multiple_of(wide * phase + width * (1 - core), lanes)
        out_ref[pad : pad + k_in, pl.ds(own_at, width)] = own_ref[:, at]
        out_ref[pad : pad + k_in, pl.ds(other_at, width)] = other_ref[:, at]


def tap_kernel(dims, core_ref, grad_ref, z_ref, tap_ref, keep_ref, send_ref, g_ref, shifted_ref):
    cin, tin, cout, tout, ks, count, rows = dims
    some = cout // cores
    width = keep_ref.shape[2]
    wide = cores * width
    core = core_ref[0]
    row, col = iota((edge_rows, 2 * lanes), 0), iota((edge_rows, 2 * lanes), 1)
    spread = (((row == 0) & (col == lanes - 1)) | ((row == 1) & (col == lanes))).astype(f32).astype(bf16)
    for chip in range(count // cores):
        at = slice(rows * chip, rows * (chip + 1))
        low = 0
        for b in range(0, wide, lanes):
            g_ref[at, lanes + b : 2 * lanes + b] = grad_ref[chip, low : low + rows].astype(f32)
            low += rows
        edge = dot_tn(grad_ref[chip, low:, :rows], spread)
        g_ref[at, :lanes] = edge[:, :lanes]
        g_ref[at, lanes + wide :] = edge[:, lanes:]
    to_time = one_hot((some * tout, some * tout), lambda r: swapped(r, tout, some))
    g = dot(to_time, g_ref[...].astype(bf16))
    inside = slice(lanes, lanes + wide)
    shifted_ref[0] = pltpu.roll(g, wide + 2 * lanes - 1, 1)[:, inside].astype(bf16)
    shifted_ref[1] = g[:, inside].astype(bf16)
    shifted_ref[2] = pltpu.roll(g, 1, 1)[:, inside].astype(bf16)
    for shift in range(3):
        keep_ref[shift] = shifted_ref[shift, :, pl.ds(pl.multiple_of(width * core, lanes), width)]
        send_ref[shift] = shifted_ref[shift, :, pl.ds(pl.multiple_of(width * (1 - core), lanes), width)]
    blank = jnp.zeros((lanes - 3 * some, wide), bf16)
    total = None
    for t in range(tout):
        at = slice(some * t, some * (t + 1))
        band = slice(2 * cin * t, 2 * cin * t + ks * cin)
        taken = jnp.concatenate([shifted_ref[shift, at] for shift in range(3)] + [blank], axis=0)
        samples = jnp.concatenate([z_ref[band, :wide], z_ref[band, wide:]], axis=0)
        term = dot_nt(samples, taken)
        total = term if total is None else total + term
    size = ks * cin
    even, odd = total[:size], total[size:]
    tap_ref[:size] = jnp.where(iota((size, lanes), 1) < 3 * some, even, pltpu.roll(odd, 3 * some, 1))
    fold = size * some // lanes
    folded = jnp.zeros((fold, lanes), f32)
    for part in range(lanes // some):
        moved = pltpu.roll(odd[fold * part : fold * (part + 1)], (some * (part - 1)) % lanes, 1)
        here = split_index(iota((fold, lanes), 1), some)[0] == part
        folded = jnp.where(here, moved, folded)
    tap_ref[size:] = folded


def input_kernel(dims, core_ref, own_ref, other_ref, taps_ref, out_ref, w_ref):
    cin, tin, cout, tout, ks, count, rows = dims
    k_in = cin * tin
    half = own_ref.shape[2]
    some, channels = cout // cores, cout // count
    steps = lanes // some
    kinds = ks + 2 * (steps - 1)
    blank = jnp.zeros((cin, cout), bf16)
    core = core_ref[0]
    o, lane = iota((cout, lanes), 0), iota((cout, lanes), 1)
    device, channel = split_index(o, channels)
    chip, core_of = split_index(device, cores)
    for part in range(cores):
        wanted = core if part == 0 else 1 - core
        tiles = None
        for step in range(steps):
            picked = [taps_ref[i - 2 * step, j] if 0 <= i - 2 * step < ks else blank
                      for j in range(ks) for i in range(kinds)]
            place = (core_of == wanted) & (lane == some * step + chip * channels + channel)
            term = dot(jnp.concatenate(picked, axis=0), place.astype(f32).astype(bf16))
            tiles = term if tiles is None else tiles + term
        tiles = tiles.astype(bf16)
        empty = jnp.zeros((cin, lanes), bf16)
        for j in range(ks):
            for s in range(tin):
                for q in range(some * tout // lanes):
                    i = s - 2 * steps * q + 2
                    at = (j * kinds + i) * cin
                    tile = tiles[at : at + cin] if 0 <= i < kinds else empty
                    low = some * tout * part + lanes * q
                    w_ref[j, cin * s : cin * (s + 1), low : low + lanes] = tile
    later, same, sooner = (jnp.concatenate([own_ref[k], other_ref[k]], axis=0) for k in range(3))
    even = dot(w_ref[0], later) + dot(w_ref[2], same) + dot(w_ref[4], sooner)
    odd = dot(w_ref[1], later) + dot(w_ref[3], same)
    both = jnp.concatenate([even.astype(bf16), odd.astype(bf16)], axis=1)
    to_channel = one_hot((k_in, k_in), lambda r: swapped(r, cin, tin))
    both = dot(to_channel, both).astype(bf16)
    merge = one_hot((2 * lanes, 2 * lanes), lambda r: swapped(r, 2, lanes))
    for b in range(half // lanes):
        part = jnp.concatenate(
            [both[:, lanes * b : lanes * (b + 1)], both[:, half + lanes * b : half + lanes * (b + 1)]], axis=1
        )
        out_ref[:, 2 * lanes * b : 2 * lanes * (b + 1)] = dot(part, merge).astype(bf16)


def unpack_kernel(dims, scale, tap_ref, out_ref):
    cin, tin, cout, tout, ks, count, rows = dims
    some, channels = cout // cores, cout // count
    size, folds = ks * cin, lanes // some
    fold = size // folds
    packed = size + fold
    both = jnp.concatenate([tap_ref[:packed], tap_ref[packed:]], axis=1)

    wide = cores * lanes
    source, target = iota((wide, folds * cout), 0), iota((wide, folds * cout), 1)
    slot, o = split_index(target, cout)
    device, channel = split_index(o, channels)
    chip, core_of = split_index(device, cores)
    place = (source == core_of * lanes + slot * some + chip * channels + channel).astype(f32).astype(bf16)
    total, rest = None, both
    for _ in range(3):
        part = rest.astype(bf16)
        rest = rest - part.astype(f32)
        term = dot(part, place)
        total = term if total is None else total + term
    total = total * scale
    for slot, j in enumerate((0, 2, 4, 1)):
        for i in range(ks):
            out_ref[i, j] = total[cin * i : cin * (i + 1), cout * slot : cout * (slot + 1)]
    for at in range(0, size, 8):
        slot, low = at // fold, size + at % fold
        out_ref[at // cin, 3, at % cin : at % cin + 8] = total[low : low + 8, cout * slot : cout * (slot + 1)]


def summed_over_chips(rows, axis, steps):
    count = lax.axis_size(axis)
    rounded = rows.astype(bf16)
    theirs = [lax.ppermute(rounded, axis, partners(count, step)).astype(f32) for step in steps]
    if len(steps) == 1:
        return rounded.astype(f32) + theirs[0]
    return (rounded.astype(f32) + theirs[0]) + (theirs[1] + theirs[2])


def partners(count, step):
    return [(i, i ^ step) for i in range(count)]


def mirrored(spectrum):
    return jnp.roll(jnp.flip(spectrum, -1), 1, -1)


def tables(count, width):
    inner = np.outer(np.arange(width), np.arange(width)) % width * (2.0 * np.pi / width)
    table = np.concatenate([np.cos(inner), np.sin(inner)], axis=1).astype(np.float32)
    high = table.astype(bf16)
    rest = (table - high.astype(np.float32)).astype(bf16)
    outer = np.outer(np.arange(count), np.arange(width)) * (2.0 * np.pi / (count * width))
    twist = np.stack([np.cos(outer), np.sin(outer)]).astype(np.float32)
    return twist, np.concatenate([high, rest])


def per_device(signal, conv_taps, response, cotangent):
    cin, tin, fibre_in = signal.shape
    cout, tout, width = cotangent.shape
    ks = conv_taps.shape[0]
    count = lax.axis_size("fibre")
    channels = cout // count
    rows = channels * tout
    waves = count * width
    tiles = width // lanes
    dims = (cin, tin, cout, tout, ks, count, rows)
    k_in, k_out = cin * tin, cout * tout
    taps = jnp.swapaxes(conv_taps, 2, 3)
    shape = jax.ShapeDtypeStruct
    conv_part, z = call(
        functools.partial(conv_kernel, dims),
        [
            shape((count, 2 * rows * tiles + edge_rows, lanes), bf16),
            shape((k_in, fibre_in), bf16),
        ],
        [
            pltpu.VMEM((ks, k_out, k_in), bf16),
            pltpu.VMEM((k_in, fibre_in), bf16),
            pltpu.VMEM(taps.shape, bf16),
            pltpu.VMEM((count, 2 * rows * tiles + edge_rows, lanes), bf16),
            pltpu.VMEM((k_in, fibre_in), bf16),
            pltpu.SemaphoreType.DMA((6 + tiles,)),
        ],
        2e9,
        (signal.reshape(k_in, fibre_in), cotangent.reshape(count, rows, width), taps),
        left=(0, 1, 2),
        left_out=(0, 1),
        room=60,
    )
    other_z = lax.ppermute(z, "fibre", partners(count, 1))
    cols = lax.all_to_all(conv_part, "fibre", split_axis=0, concat_axis=0, tiled=True)
    back = mirrored(response)
    real = jnp.stack([response[0] + back[0], response[1] - back[1]]) * (0.5 / waves)
    real = real.reshape(2, channels, width, count).transpose(0, 3, 1, 2)
    real = real.reshape(2, count * channels, width)
    twist, waves_table = tables(count, width)
    big = count * rows // 2
    grad_part, cross = call(
        functools.partial(filter_kernel, (count, channels, tout, width)),
        [
            shape((count // cores, cores * rows * tiles + edge_rows, lanes), bf16),
            shape((count * channels, 2 * width), f32),
        ],
        [
            pltpu.VMEM((count, rows, width), f32),
            pltpu.VMEM((big, 2 * width), f32),
            pltpu.VMEM((big, 2 * width), f32),
            pltpu.VMEM((big, 2 * width), f32),
            pltpu.VMEM((2 * tiles, big, lanes), f32),
            pltpu.VMEM((2 * tiles, big, lanes), f32),
            pltpu.VMEM((2 * width, 2 * width), bf16),
            pltpu.VMEM((2 * width, 2 * width), bf16),
        ],
        6e9,
        (cols, real, jnp.asarray(twist), jnp.asarray(waves_table)),
    )
    (cross,) = call(hermitian_kernel, [shape((2, channels, count, width), f32)], [], 1e6, (cross,))
    filter_grad = cross.transpose(0, 1, 3, 2).reshape(2, channels, waves)
    chips = [[core + cores * chip for chip in range(count // cores)] for core in range(cores)]
    grad_cols = lax.all_to_all(
        grad_part, "fibre", split_axis=0, concat_axis=0, tiled=True, axis_index_groups=chips
    )
    core = (lax.axis_index("fibre") % cores).astype(jnp.int32).reshape(1)
    (samples,) = call(
        gather_kernel,
        [shape((k_in + 4 * cin, cores * fibre_in), bf16)],
        [],
        1e6,
        (core, z, other_z),
        small=(0,),
    )
    grad_cols, filter_grad, samples = lax.optimization_barrier((grad_cols, filter_grad, samples))
    some = k_out // cores
    taps_part, keep, send = call(
        functools.partial(tap_kernel, dims),
        [
            shape((ks * cin + ks * cin * (cout // cores) // lanes, lanes), f32),
            shape((3, some, width), bf16),
            shape((3, some, width), bf16),
        ],
        [
            pltpu.VMEM((some, cores * width + 2 * lanes), f32),
            pltpu.VMEM((3, some, cores * width), bf16),
        ],
        1e9,
        (core, grad_cols, samples),
        small=(0,),
    )
    got = lax.ppermute(send, "fibre", partners(count, 1))
    chips = count // cores
    step = 4 if chips % 4 == 0 else 1
    total = taps_part
    if step == 4:
        total = summed_over_chips(total, "fibre", (cores, 2 * cores, 3 * cores))
    total, keep, got = lax.optimization_barrier((total, keep, got))
    (input_grad,) = call(
        functools.partial(input_kernel, dims),
        [shape((k_in, fibre_in), bf16)],
        [pltpu.VMEM((ks, k_in, k_out), bf16)],
        2e9,
        (core, keep, got, taps),
        small=(0,),
    )
    while step < chips:
        total = summed_over_chips(total, "fibre", (cores * step,))
        step *= 2
    total, input_grad = lax.optimization_barrier((total, input_grad))
    other = lax.ppermute(total, "fibre", partners(count, 1))
    total = jnp.where(core[0] == 0, jnp.concatenate([total, other]), jnp.concatenate([other, total]))
    (tap_grad,) = call(
        functools.partial(unpack_kernel, dims, 1.0 / math.sqrt(tout * waves)),
        [shape((ks, ks, cin, cout), f32)],
        [],
        1e6,
        (total,),
    )
    return (input_grad.reshape(signal.shape), jnp.swapaxes(tap_grad, 2, 3), filter_grad)


def solution(mesh):
    in_specs = (P("parts", None, "fibre"), P(), P(None, "fibre", None), P("parts", None, "fibre"))
    out_specs = (P("parts", None, "fibre"), P("parts", None, None, None), P("parts", "fibre", None))
    return jax.shard_map(
        per_device, mesh=mesh, in_specs=in_specs, out_specs=out_specs, check_vma=False
    )
```

```python
import functools
import math

import jax
import jax.numpy as jnp
import numpy as np
from jax import lax
from jax.experimental import pallas as pl
from jax.experimental.pallas import tpu as pltpu
from jax.sharding import PartitionSpec as P

bf16 = jnp.bfloat16
f32 = jnp.float32
inv_root_two = 1.0 / math.sqrt(2.0)
inv_root_tau = 1.0 / math.sqrt(2.0 * math.pi)
lanes = 128
edge_rows = 8
cores = 2


def dot(a, b):
    return jnp.dot(a, b, preferred_element_type=f32)


def dot_nt(a, b):
    return lax.dot_general(a, b, (((1,), (1,)), ((), ())), preferred_element_type=f32)


def dot_tn(a, b):
    return lax.dot_general(a, b, (((0,), (0,)), ((), ())), preferred_element_type=f32)


def iota(shape, dim):
    return lax.broadcasted_iota(jnp.int32, shape, dim)


def split_index(x, size):
    if size & (size - 1):
        return x // size, x % size
    return lax.shift_right_logical(x, jnp.full_like(x, size.bit_length() - 1)), x & (size - 1)


def swapped(x, outer, inner):
    a, b = split_index(x, inner)
    return b * outer + a


def one_hot(shape, column_of_row):
    return (iota(shape, 1) == column_of_row(iota((shape[0], 1), 0))).astype(f32).astype(bf16)


def one_hot_columns(shape, row_of_column):
    return (iota(shape, 0) == row_of_column(iota((1, shape[1]), 1))).astype(f32).astype(bf16)


def call(kernel, outs, scratch, flops, args, left=(), left_out=(), small=(), room=24):
    moved = sum(a.size * a.dtype.itemsize for a in list(args) + list(outs))
    return pl.pallas_call(
        kernel,
        out_shape=outs,
        in_specs=[
            pl.BlockSpec(
                memory_space=pltpu.HBM if a in left else pltpu.SMEM if a in small else pltpu.VMEM
            )
            for a in range(len(args))
        ],
        out_specs=[
            pl.BlockSpec(memory_space=pltpu.HBM if a in left_out else pltpu.VMEM) for a in range(len(outs))
        ],
        scratch_shapes=scratch,
        compiler_params=pltpu.CompilerParams(vmem_limit_bytes=room << 20),
        cost_estimate=pl.CostEstimate(flops=int(flops), bytes_accessed=moved, transcendentals=0),
    )(*args)


def conv_kernel(
    dims, sig_hbm, cot_hbm, taps_hbm, out_hbm, z_hbm,
    w_ref, sig_ref, taps_ref, out_ref, z_ref, sem,
):
    cin, tin, cout, tout, ks, count, rows = dims
    k_in, k_out = cin * tin, cout * tout
    half = sig_ref.shape[1] // 2
    tiles_wide = half // lanes
    conv_rows = rows * tiles_wide
    taps_copy = pltpu.make_async_copy(taps_hbm, taps_ref, sem.at[0])
    sig_copy = pltpu.make_async_copy(sig_hbm, sig_ref, sem.at[1])
    cot_copies = [
        pltpu.make_async_copy(
            cot_hbm.at[:, :, pl.ds(lanes * b, lanes)],
            out_ref.at[:, pl.ds(conv_rows + rows * b, rows)],
            sem.at[6 + b],
        )
        for b in range(tiles_wide)
    ]
    at_conv, at_edge = pl.ds(0, conv_rows), pl.ds(2 * conv_rows, edge_rows)
    at_cot = pl.ds(conv_rows, conv_rows)
    cot_out = pltpu.make_async_copy(out_ref.at[:, at_cot], out_hbm.at[:, at_cot], sem.at[5])
    z_out = pltpu.make_async_copy(z_ref, z_hbm, sem.at[2])
    conv_out = pltpu.make_async_copy(out_ref.at[:, at_conv], out_hbm.at[:, at_conv], sem.at[3])
    edge_out = pltpu.make_async_copy(out_ref.at[:, at_edge], out_hbm.at[:, at_edge], sem.at[4])
    taps_copy.start()
    sig_copy.start()
    for copy in cot_copies:
        copy.start()
    taps_copy.wait()
    blank = jnp.zeros((2 * cin, cout), bf16)
    stacked = []
    for j in range(ks):
        column = jnp.concatenate([blank] + [taps_ref[i, j] for i in range(ks)] + [blank, blank], axis=0)
        for v in range(4):
            stacked.append(column[2 * cin * v : 2 * cin * v + lanes])
    eye = one_hot((cout, cout), lambda r: r)
    tiles = dot_nt(eye, jnp.concatenate(stacked, axis=0)).astype(bf16)
    empty = jnp.zeros((cout, lanes), bf16)
    for j in range(ks):
        for t in range(tout):
            for q in range(k_in // lanes):
                v = 2 * q - t + 2
                at = (j * 4 + v) * lanes
                tile = tiles[:, at : at + lanes] if 0 <= v < 4 else empty
                w_ref[j, cout * t : cout * (t + 1), lanes * q : lanes * (q + 1)] = tile
    sig_copy.wait()
    split = one_hot_columns((2 * lanes, 2 * lanes), lambda q: swapped(q, 2, lanes))
    parts = [dot(sig_ref[:, b : b + 2 * lanes], split) for b in range(0, 2 * half, 2 * lanes)]
    apart = jnp.concatenate([p[:, :lanes] for p in parts] + [p[:, lanes:] for p in parts], axis=1)
    to_time = one_hot((k_in, k_in), lambda r: swapped(r, tin, cin))
    z = dot(to_time, apart.astype(bf16)).astype(bf16)
    z_ref[...] = z
    z_out.start()
    for copy in cot_copies:
        copy.wait()
    cot_out.start()
    even, odd = z[:, :half], z[:, half:]
    left = dot(w_ref[0], even) + dot(w_ref[1], odd)
    right = dot(w_ref[4], even)
    lane = iota((k_out, half), 1)
    own = (
        dot(w_ref[2], even)
        + dot(w_ref[3], odd)
        + jnp.where(lane == 0, 0.0, pltpu.roll(left, 1, 1))
        + jnp.where(lane == half - 1, 0.0, pltpu.roll(right, half - 1, 1))
    )
    high = own.astype(bf16)
    first = iota((k_out, lanes), 1) == 0

    def parts_of(v):
        top = v.astype(bf16)
        return top, (v - top.astype(f32)).astype(bf16)

    _, own_rest = parts_of(jnp.where(first, own[:, :lanes], own[:, half - lanes :]))
    next_high, next_rest = parts_of(jnp.where(first, right[:, :lanes], left[:, half - lanes :]))
    row, col = iota((edge_rows, 3 * lanes), 0), iota((edge_rows, 3 * lanes), 1)
    pick = jnp.zeros((edge_rows, 3 * lanes), f32)
    for at, column in enumerate((0, lanes - 1, 2 * lanes - 1, 3 * lanes - 1, lanes, 2 * lanes)):
        pick = jnp.where((row == at) & (col == column), 1.0, pick)
    edges = dot_nt(pick.astype(bf16), jnp.concatenate([own_rest, next_high, next_rest], axis=1))
    from_time = one_hot((k_out, k_out), lambda r: swapped(r, cout, tout))
    edges = dot_nt(edges.astype(bf16), from_time)
    main = dot(from_time, high).astype(bf16)
    for d in range(count):
        for b in range(tiles_wide):
            at = slice(lanes * b, lanes * (b + 1))
            out_ref[d, rows * b : rows * (b + 1)] = main[rows * d : rows * (d + 1), at]
        out_ref[d, 2 * conv_rows :] = jnp.zeros((edge_rows, lanes), bf16)
        out_ref[d, 2 * conv_rows :, :rows] = edges[:, rows * d : rows * (d + 1)].astype(bf16)
    conv_out.start()
    edge_out.start()
    cot_out.wait()
    z_out.wait()
    conv_out.wait()
    edge_out.wait()


def transform(real, imag, sign):
    size = len(real)
    if size == 1:
        return (list(real), [None] if imag is None else list(imag))
    even_re, even_im = transform(real[0::2], None if imag is None else imag[0::2], sign)
    odd_re, odd_im = transform(real[1::2], None if imag is None else imag[1::2], sign)
    out_re, out_im = [None] * size, [None] * size

    def plus(a, b):
        return b if a is None else (a if b is None else a + b)

    def minus(a, b):
        return a if b is None else (-b if a is None else a - b)

    for k in range(size // 2):
        re, im = odd_re[k], odd_im[k]
        if k == 0:
            tr, ti = re, im
        elif 4 * k == size:
            tr = None if im is None else (im if sign < 0 else -im)
            ti = -re if sign < 0 else re
        else:
            c, s = math.cos(2 * math.pi * k / size), sign * math.sin(2 * math.pi * k / size)
            if im is None:
                tr, ti = c * re, s * re
            elif 8 * k == size:
                tr, ti = (c * (re - im), c * (re + im)) if sign > 0 else (c * (re + im), c * (im - re))
            elif 8 * k == 3 * size:
                tr, ti = (c * (re + im), c * (im - re)) if sign > 0 else (c * (re - im), c * (re + im))
            else:
                tr, ti = c * re - s * im, s * re + c * im
        out_re[k], out_im[k] = plus(even_re[k], tr), plus(even_im[k], ti)
        out_re[k + size // 2], out_im[k + size // 2] = minus(even_re[k], tr), minus(even_im[k], ti)
    return out_re, out_im


def gelu_slope(v):
    return 0.5 * (1.0 + lax.erf(v * inv_root_two)) + v * jnp.exp(-0.5 * v * v) * inv_root_tau


def filter_kernel(
    dims, cols_ref, own_ref, twist_ref, wave_ref,
    out_ref, cross_ref, x_ref, y_ref, spec_ref, grad_ref, prod_ref, resp_ref, high_ref, rest_ref,
):
    count, channels, tout, width = dims
    rows, pair = channels * tout, tout // 2
    wide, groups = width // lanes, count * channels
    for at, table_ref in ((0, high_ref), (width, rest_ref)):
        cosine, sine = wave_ref[at : at + width, :width], wave_ref[at : at + width, width:]
        table_ref[:width, :width], table_ref[:width, width:] = cosine, -sine
        table_ref[width:, :width], table_ref[width:, width:] = sine, cosine
    for b in range(2 * wide):
        own = own_ref[b // wide, :, lanes * (b % wide) : lanes * (b % wide + 1)]
        for step in range(pair):
            resp_ref[b, pl.ds(step, groups, stride=pair), :] = own
    packed = rows // 2
    group = min(2, channels)
    chunk = group * pair
    edge_row, edge_col = iota((edge_rows, width), 0), iota((edge_rows, width), 1)
    to_low = (edge_col == 0) & ((edge_row == 0) | (edge_row == 2) | (edge_row == 3))
    to_high = (edge_col == width - 1) & ((edge_row == 1) | (edge_row == 4) | (edge_row == 5))
    spread = (to_low | to_high).astype(f32).astype(bf16)
    low = 2 * rows * (width // lanes)
    edges = [cols_ref[d, low:, :rows].astype(f32) for d in range(count)]
    none = jnp.zeros((edge_rows, rows), f32)
    kind = iota((edge_rows, rows), 0)
    for d in range(count):
        before = edges[d - 1] if d > 0 else none
        after = edges[d + 1] if d < count - 1 else none
        joined = jnp.where(kind < 2, edges[d], jnp.where(kind < 4, before, after))
        blocks = [cols_ref[d, rows * b : rows * (b + 1)] for b in range(width // lanes)]
        whole = jnp.concatenate(blocks, axis=1).astype(f32) + dot_tn(joined.astype(bf16), spread)
        x_ref[d] = whole.astype(bf16).astype(f32)

    def forward_planes(real, imag, r, h):
        re, im = transform(real, imag, -1)
        for k in range(count):
            c = twist_ref[0, k : k + 1, h : h + lanes]
            s = twist_ref[1, k : k + 1, h : h + lanes]
            at = slice(k * packed + r, k * packed + r + chunk)
            y_ref[at, h : h + lanes] = re[k] * c + im[k] * s if k else re[k]
            y_ref[at, width + h : width + h + lanes] = im[k] * c - re[k] * s if k else im[k]

    def backward_planes(r, h):
        re, im = [], []
        for k in range(count):
            c = twist_ref[0, k : k + 1, h : h + lanes]
            s = twist_ref[1, k : k + 1, h : h + lanes]
            at = slice(k * packed + r, k * packed + r + chunk)
            a, b = y_ref[at, h : h + lanes], y_ref[at, width + h : width + h + lanes]
            re.append(a * c - b * s if k else a)
            im.append(b * c + a * s if k else b)
        return transform(re, im, 1)

    def inner(product):
        v = y_ref[...]
        high = v.astype(bf16)
        rest = (v - high.astype(f32)).astype(bf16)
        both = product(jnp.concatenate([high, rest], axis=0), high_ref[...])
        size = v.shape[0]
        return both[:size] + both[size:] + product(high, rest_ref[...])

    def paired(tiles):
        return (
            jnp.concatenate([tile[:pair] for tile in tiles], axis=0),
            jnp.concatenate([tile[pair:] for tile in tiles], axis=0),
        )

    chunks = [(r, h) for r in range(0, packed, chunk) for h in range(0, width, lanes)]
    for r, h in chunks:
        planes = [
            paired([x_ref[d, 2 * r + tout * g : 2 * r + tout * (g + 1), h : h + lanes] for g in range(group)])
            for d in range(count)
        ]
        forward_planes([re for re, im in planes], [im for re, im in planes], r, h)
    spec_ref[...] = inner(dot)
    sr, si = spec_ref[:, :width], spec_ref[:, width:]
    rr, ri = (jnp.concatenate([resp_ref[p * wide + b] for b in range(wide)], axis=1) for p in range(2))
    y_ref[:, :width] = rr * sr - ri * si
    y_ref[:, width:] = rr * si + ri * sr
    y_ref[...] = inner(dot_nt)
    for r, h in chunks:
        real, imag = backward_planes(r, h)
        at = rows * (width + h) // lanes + 2 * r
        for d in range(count):
            cot = cols_ref[d, at : at + tout * group].astype(f32)
            re, im = paired([cot[tout * g : tout * (g + 1)] for g in range(group)])
            real[d], imag[d] = re * gelu_slope(real[d]), im * gelu_slope(imag[d])
        forward_planes(real, imag, r, h)
    grad_ref[...] = inner(dot)
    sr, si = spec_ref[:, :width], spec_ref[:, width:]
    gr, gi = grad_ref[:, :width], grad_ref[:, width:]
    rr, ri = (jnp.concatenate([resp_ref[p * wide + b] for b in range(wide)], axis=1) for p in range(2))
    y_ref[:, :width] = rr * gr + ri * gi
    y_ref[:, width:] = rr * gi - ri * gr
    scale = 1.0 / (count * width)
    crossed = ((sr * gr + si * gi) * scale, (sr * gi - si * gr) * scale)
    for b in range(2 * wide):
        prod_ref[b] = crossed[b // wide][:, lanes * (b % wide) : lanes * (b % wide + 1)]
    for b in range(2 * wide):
        summed = prod_ref[b, pl.ds(0, groups, stride=pair), :]
        for step in range(1, pair):
            summed = summed + prod_ref[b, pl.ds(step, groups, stride=pair), :]
        cross_ref[:, lanes * b : lanes * (b + 1)] = summed
    y_ref[...] = inner(dot_nt)
    for r, h in chunks:
        real, imag = backward_planes(r, h)
        for d in range(count):
            for g in range(group):
                at = slice(pair * g, pair * (g + 1))
                tile = jnp.concatenate([real[d][at], imag[d][at]], axis=0)
                x_ref[d, 2 * r + tout * g : 2 * r + tout * (g + 1), h : h + lanes] = tile
    last = ((iota((edge_rows, lanes), 0) == 0) & (iota((edge_rows, lanes), 1) == lanes - 1)).astype(f32).astype(bf16)
    first = ((iota((edge_rows, lanes), 0) == 1) & (iota((edge_rows, lanes), 1) == 0)).astype(f32).astype(bf16)
    for chip in range(count // cores):
        at = 0
        for d in range(cores * chip, cores * (chip + 1)):
            for b in range(0, width, lanes):
                out_ref[chip, at : at + rows] = x_ref[d, :, b : b + lanes].astype(bf16)
                at += rows
        out_ref[chip, at:] = jnp.zeros((edge_rows, lanes), bf16)
        edge = none
        if chip > 0:
            edge = edge + dot_nt(last, x_ref[cores * chip - 1, :, width - lanes :].astype(bf16))
        if chip < count // cores - 1:
            edge = edge + dot_nt(first, x_ref[cores * (chip + 1), :, :lanes].astype(bf16))
        out_ref[chip, at:, :rows] = edge.astype(bf16)


def hermitian_kernel(cross_ref, out_ref):
    _, channels, count, width = out_ref.shape
    row, col = iota((width, width), 0), iota((width, width), 1)
    flip = (row + col == width - 1).astype(f32).astype(bf16)
    flip_first = ((row + col == width) | ((row == 0) & (col == 0))).astype(f32).astype(bf16)

    def moved(v, by):
        total = None
        for _ in range(3):
            part = v.astype(bf16)
            v = v - part.astype(f32)
            term = dot(part, by)
            total = term if total is None else total + term
        return total

    for k in range(count):
        from_k = channels * ((count - k) % count)
        own = cross_ref[channels * k : channels * (k + 1)]
        other = cross_ref[from_k : from_k + channels]
        by = flip if k else flip_first
        out_ref[0, :, k] = 0.5 * (own[:, :width] + moved(other[:, :width], by))
        out_ref[1, :, k] = 0.5 * (own[:, width:] - moved(other[:, width:], by))


def gather_kernel(core_ref, own_ref, other_ref, out_ref):
    k_in, wide = own_ref.shape
    width = wide // 2
    pad = (out_ref.shape[0] - k_in) // 2
    core = core_ref[0]
    out_ref[:pad] = jnp.zeros((pad, cores * wide), bf16)
    out_ref[pad + k_in :] = jnp.zeros((pad, cores * wide), bf16)
    for phase in range(2):
        at = slice(width * phase, width * (phase + 1))
        own_at = pl.multiple_of(wide * phase + width * core, lanes)
        other_at = pl.multiple_of(wide * phase + width * (1 - core), lanes)
        out_ref[pad : pad + k_in, pl.ds(own_at, width)] = own_ref[:, at]
        out_ref[pad : pad + k_in, pl.ds(other_at, width)] = other_ref[:, at]


def tap_kernel(
    dims, core_ref, grad_ref, z_ref, tap_ref, keep_ref, send_ref, g_ref, exact_ref, shifted_ref
):
    cin, tin, cout, tout, ks, count, rows = dims
    some = cout // cores
    width = keep_ref.shape[1] - lanes
    wide = cores * width
    core = core_ref[0]
    row, col = iota((edge_rows, 2 * lanes), 0), iota((edge_rows, 2 * lanes), 1)
    spread = (((row == 0) & (col == lanes - 1)) | ((row == 1) & (col == lanes))).astype(f32).astype(bf16)
    for chip in range(count // cores):
        at = slice(rows * chip, rows * (chip + 1))
        low = 0
        for b in range(0, wide, lanes):
            g_ref[at, lanes + b : 2 * lanes + b] = grad_ref[chip, low : low + rows].astype(f32)
            low += rows
        edge = dot_tn(grad_ref[chip, low:, :rows], spread)
        g_ref[at, :lanes] = edge[:, :lanes]
        g_ref[at, lanes + wide :] = edge[:, lanes:]
    to_time = one_hot((some * tout, some * tout), lambda r: swapped(r, tout, some))
    g = dot(to_time, g_ref[...].astype(bf16))
    inside = slice(lanes, lanes + wide)
    shifted_ref[0] = pltpu.roll(g, wide + 2 * lanes - 1, 1)[:, inside].astype(bf16)
    shifted_ref[1] = g[:, inside].astype(bf16)
    shifted_ref[2] = pltpu.roll(g, 1, 1)[:, inside].astype(bf16)
    exact_ref[...] = g.astype(bf16)
    lane = iota((some * tout, lanes), 1)
    for block, block_ref in ((core, keep_ref), (1 - core, send_ref)):
        at = width * block
        before, inner, after = (
            exact_ref[:, pl.ds(pl.multiple_of(at + low, lanes), size)]
            for low, size in ((0, lanes), (lanes, width), (lanes + width, lanes))
        )
        edge = jnp.where(lane == 0, after.astype(f32), before.astype(f32))
        block_ref[:, :width] = inner
        block_ref[:, width:] = jnp.where((lane == 0) | (lane == lanes - 1), edge, 0.0).astype(bf16)
    blank = jnp.zeros((lanes - 3 * some, wide), bf16)
    total = None
    for t in range(tout):
        at = slice(some * t, some * (t + 1))
        band = slice(2 * cin * t, 2 * cin * t + ks * cin)
        taken = jnp.concatenate([shifted_ref[shift, at] for shift in range(3)] + [blank], axis=0)
        samples = jnp.concatenate([z_ref[band, :wide], z_ref[band, wide:]], axis=0)
        term = dot_nt(samples, taken)
        total = term if total is None else total + term
    size = ks * cin
    even, odd = total[:size], total[size:]
    tap_ref[:size] = jnp.where(iota((size, lanes), 1) < 3 * some, even, pltpu.roll(odd, 3 * some, 1))
    fold = size * some // lanes
    folded = jnp.zeros((fold, lanes), f32)
    for part in range(lanes // some):
        moved = pltpu.roll(odd[fold * part : fold * (part + 1)], (some * (part - 1)) % lanes, 1)
        here = split_index(iota((fold, lanes), 1), some)[0] == part
        folded = jnp.where(here, moved, folded)
    tap_ref[size:] = folded


def input_kernel(dims, core_ref, own_ref, other_ref, taps_ref, out_ref, w_ref):
    cin, tin, cout, tout, ks, count, rows = dims
    k_in = cin * tin
    half = own_ref.shape[1] - lanes
    some, channels = cout // cores, cout // count
    steps = lanes // some
    kinds = ks + 2 * (steps - 1)
    blank = jnp.zeros((cin, cout), bf16)
    core = core_ref[0]
    o, lane = iota((cout, lanes), 0), iota((cout, lanes), 1)
    device, channel = split_index(o, channels)
    chip, core_of = split_index(device, cores)
    for part in range(cores):
        wanted = core if part == 0 else 1 - core
        tiles = None
        for step in range(steps):
            picked = [taps_ref[i - 2 * step, j] if 0 <= i - 2 * step < ks else blank
                      for j in range(ks) for i in range(kinds)]
            place = (core_of == wanted) & (lane == some * step + chip * channels + channel)
            term = dot(jnp.concatenate(picked, axis=0), place.astype(f32).astype(bf16))
            tiles = term if tiles is None else tiles + term
        tiles = tiles.astype(bf16)
        empty = jnp.zeros((cin, lanes), bf16)
        for j in range(ks):
            for s in range(tin):
                for q in range(some * tout // lanes):
                    i = s - 2 * steps * q + 2
                    at = (j * kinds + i) * cin
                    tile = tiles[at : at + cin] if 0 <= i < kinds else empty
                    low = some * tout * part + lanes * q
                    w_ref[j, cin * s : cin * (s + 1), low : low + lanes] = tile
    g = jnp.concatenate([own_ref[...], other_ref[...]], axis=0)
    wide = half + lanes
    same = g[:, :half]
    later = dot(g, one_hot_columns((wide, half), lambda n: n + 1)).astype(bf16)
    sooner = dot(g, one_hot_columns((wide, half), lambda n: jnp.where(n == 0, wide - 1, n - 1))).astype(bf16)
    even = dot(w_ref[0], later) + dot(w_ref[2], same) + dot(w_ref[4], sooner)
    odd = dot(w_ref[1], later) + dot(w_ref[3], same)
    both = jnp.concatenate([even.astype(bf16), odd.astype(bf16)], axis=1)
    to_channel = one_hot((k_in, k_in), lambda r: swapped(r, cin, tin))
    both = dot(to_channel, both).astype(bf16)
    merge = one_hot((2 * lanes, 2 * lanes), lambda r: swapped(r, 2, lanes))
    for b in range(half // lanes):
        part = jnp.concatenate(
            [both[:, lanes * b : lanes * (b + 1)], both[:, half + lanes * b : half + lanes * (b + 1)]], axis=1
        )
        out_ref[:, 2 * lanes * b : 2 * lanes * (b + 1)] = dot(part, merge).astype(bf16)


def unpack_kernel(dims, scale, tap_ref, out_ref):
    cin, tin, cout, tout, ks, count, rows = dims
    some, channels = cout // cores, cout // count
    size, folds = ks * cin, lanes // some
    fold = size // folds
    packed = size + fold
    both = jnp.concatenate([tap_ref[:packed], tap_ref[packed:]], axis=1)

    wide = cores * lanes
    source, target = iota((wide, folds * cout), 0), iota((wide, folds * cout), 1)
    slot, o = split_index(target, cout)
    device, channel = split_index(o, channels)
    chip, core_of = split_index(device, cores)
    place = (source == core_of * lanes + slot * some + chip * channels + channel).astype(f32).astype(bf16)
    total, rest = None, both
    for _ in range(3):
        part = rest.astype(bf16)
        rest = rest - part.astype(f32)
        term = dot(part, place)
        total = term if total is None else total + term
    total = total * scale
    for slot, j in enumerate((0, 2, 4, 1)):
        for i in range(ks):
            out_ref[i, j] = total[cin * i : cin * (i + 1), cout * slot : cout * (slot + 1)]
    for at in range(0, size, 8):
        slot, low = at // fold, size + at % fold
        out_ref[at // cin, 3, at % cin : at % cin + 8] = total[low : low + 8, cout * slot : cout * (slot + 1)]


def summed_over_chips(rows, axis, steps):
    count = lax.axis_size(axis)
    rounded = rows.astype(bf16)
    theirs = [lax.ppermute(rounded, axis, partners(count, step)).astype(f32) for step in steps]
    if len(steps) == 1:
        return rounded.astype(f32) + theirs[0]
    return (rounded.astype(f32) + theirs[0]) + (theirs[1] + theirs[2])


def partners(count, step):
    return [(i, i ^ step) for i in range(count)]


def mirrored(spectrum):
    return jnp.roll(jnp.flip(spectrum, -1), 1, -1)


def tables(count, width):
    inner = np.outer(np.arange(width), np.arange(width)) % width * (2.0 * np.pi / width)
    table = np.concatenate([np.cos(inner), np.sin(inner)], axis=1).astype(np.float32)
    high = table.astype(bf16)
    rest = (table - high.astype(np.float32)).astype(bf16)
    outer = np.outer(np.arange(count), np.arange(width)) * (2.0 * np.pi / (count * width))
    twist = np.stack([np.cos(outer), np.sin(outer)]).astype(np.float32)
    return twist, np.concatenate([high, rest])


def per_device(signal, conv_taps, response, cotangent):
    cin, tin, fibre_in = signal.shape
    cout, tout, width = cotangent.shape
    ks = conv_taps.shape[0]
    count = lax.axis_size("fibre")
    channels = cout // count
    rows = channels * tout
    waves = count * width
    tiles = width // lanes
    dims = (cin, tin, cout, tout, ks, count, rows)
    k_in, k_out = cin * tin, cout * tout
    taps = jnp.swapaxes(conv_taps, 2, 3)
    shape = jax.ShapeDtypeStruct
    conv_part, z = call(
        functools.partial(conv_kernel, dims),
        [
            shape((count, 2 * rows * tiles + edge_rows, lanes), bf16),
            shape((k_in, fibre_in), bf16),
        ],
        [
            pltpu.VMEM((ks, k_out, k_in), bf16),
            pltpu.VMEM((k_in, fibre_in), bf16),
            pltpu.VMEM(taps.shape, bf16),
            pltpu.VMEM((count, 2 * rows * tiles + edge_rows, lanes), bf16),
            pltpu.VMEM((k_in, fibre_in), bf16),
            pltpu.SemaphoreType.DMA((6 + tiles,)),
        ],
        2e9,
        (signal.reshape(k_in, fibre_in), cotangent.reshape(count, rows, width), taps),
        left=(0, 1, 2),
        left_out=(0, 1),
        room=60,
    )
    other_z = lax.ppermute(z, "fibre", partners(count, 1))
    cols = lax.all_to_all(conv_part, "fibre", split_axis=0, concat_axis=0, tiled=True)
    back = mirrored(response)
    real = jnp.stack([response[0] + back[0], response[1] - back[1]]) * (0.5 / waves)
    real = real.reshape(2, channels, width, count).transpose(0, 3, 1, 2)
    real = real.reshape(2, count * channels, width)
    twist, waves_table = tables(count, width)
    big = count * rows // 2
    grad_part, cross = call(
        functools.partial(filter_kernel, (count, channels, tout, width)),
        [
            shape((count // cores, cores * rows * tiles + edge_rows, lanes), bf16),
            shape((count * channels, 2 * width), f32),
        ],
        [
            pltpu.VMEM((count, rows, width), f32),
            pltpu.VMEM((big, 2 * width), f32),
            pltpu.VMEM((big, 2 * width), f32),
            pltpu.VMEM((big, 2 * width), f32),
            pltpu.VMEM((2 * tiles, big, lanes), f32),
            pltpu.VMEM((2 * tiles, big, lanes), f32),
            pltpu.VMEM((2 * width, 2 * width), bf16),
            pltpu.VMEM((2 * width, 2 * width), bf16),
        ],
        6e9,
        (cols, real, jnp.asarray(twist), jnp.asarray(waves_table)),
    )
    (cross,) = call(hermitian_kernel, [shape((2, channels, count, width), f32)], [], 1e6, (cross,))
    filter_grad = cross.transpose(0, 1, 3, 2).reshape(2, channels, waves)
    chips = [[core + cores * chip for chip in range(count // cores)] for core in range(cores)]
    grad_cols = lax.all_to_all(
        grad_part, "fibre", split_axis=0, concat_axis=0, tiled=True, axis_index_groups=chips
    )
    core = (lax.axis_index("fibre") % cores).astype(jnp.int32).reshape(1)
    (samples,) = call(
        gather_kernel,
        [shape((k_in + 4 * cin, cores * fibre_in), bf16)],
        [],
        1e6,
        (core, z, other_z),
        small=(0,),
    )
    grad_cols, filter_grad, samples = lax.optimization_barrier((grad_cols, filter_grad, samples))
    some = k_out // cores
    taps_part, keep, send = call(
        functools.partial(tap_kernel, dims),
        [
            shape((ks * cin + ks * cin * (cout // cores) // lanes, lanes), f32),
            shape((some, width + lanes), bf16),
            shape((some, width + lanes), bf16),
        ],
        [
            pltpu.VMEM((some, cores * width + 2 * lanes), f32),
            pltpu.VMEM((some, cores * width + 2 * lanes), bf16),
            pltpu.VMEM((3, some, cores * width), bf16),
        ],
        1e9,
        (core, grad_cols, samples),
        small=(0,),
    )
    got = lax.ppermute(send, "fibre", partners(count, 1))
    chips = count // cores
    step = 4 if chips % 4 == 0 else 1
    total = taps_part
    if step == 4:
        total = summed_over_chips(total, "fibre", (cores, 2 * cores, 3 * cores))
    total, keep, got = lax.optimization_barrier((total, keep, got))
    (input_grad,) = call(
        functools.partial(input_kernel, dims),
        [shape((k_in, fibre_in), bf16)],
        [pltpu.VMEM((ks, k_in, k_out), bf16)],
        2e9,
        (core, keep, got, taps),
        small=(0,),
    )
    while step < chips:
        total = summed_over_chips(total, "fibre", (cores * step,))
        step *= 2
    total, input_grad = lax.optimization_barrier((total, input_grad))
    other = lax.ppermute(total, "fibre", partners(count, 1))
    total = jnp.where(core[0] == 0, jnp.concatenate([total, other]), jnp.concatenate([other, total]))
    (tap_grad,) = call(
        functools.partial(unpack_kernel, dims, 1.0 / math.sqrt(tout * waves)),
        [shape((ks, ks, cin, cout), f32)],
        [],
        1e6,
        (total,),
    )
    return (input_grad.reshape(signal.shape), jnp.swapaxes(tap_grad, 2, 3), filter_grad)


def solution(mesh):
    in_specs = (P("parts", None, "fibre"), P(), P(None, "fibre", None), P("parts", None, "fibre"))
    out_specs = (P("parts", None, "fibre"), P("parts", None, None, None), P("parts", "fibre", None))
    return jax.shard_map(
        per_device, mesh=mesh, in_specs=in_specs, out_specs=out_specs, check_vma=False
    )
```

```python
import functools
import math

import jax
import jax.numpy as jnp
import numpy as np
from jax import lax
from jax.experimental import pallas as pl
from jax.experimental.pallas import tpu as pltpu
from jax.sharding import PartitionSpec as P

bf16 = jnp.bfloat16
f32 = jnp.float32
inv_root_two = 1.0 / math.sqrt(2.0)
inv_root_tau = 1.0 / math.sqrt(2.0 * math.pi)
lanes = 128
edge_rows = 8
cores = 2


def dot(a, b):
    return jnp.dot(a, b, preferred_element_type=f32)


def dot_nt(a, b):
    return lax.dot_general(a, b, (((1,), (1,)), ((), ())), preferred_element_type=f32)


def dot_tn(a, b):
    return lax.dot_general(a, b, (((0,), (0,)), ((), ())), preferred_element_type=f32)


def iota(shape, dim):
    return lax.broadcasted_iota(jnp.int32, shape, dim)


def split_index(x, size):
    if size & (size - 1):
        return x // size, x % size
    return lax.shift_right_logical(x, jnp.full_like(x, size.bit_length() - 1)), x & (size - 1)


def swapped(x, outer, inner):
    a, b = split_index(x, inner)
    return b * outer + a


def one_hot(shape, column_of_row):
    return (iota(shape, 1) == column_of_row(iota((shape[0], 1), 0))).astype(f32).astype(bf16)


def one_hot_columns(shape, row_of_column):
    return (iota(shape, 0) == row_of_column(iota((1, shape[1]), 1))).astype(f32).astype(bf16)


def call(kernel, outs, scratch, flops, args, left=(), left_out=(), small=(), room=24):
    moved = sum(a.size * a.dtype.itemsize for a in list(args) + list(outs))
    return pl.pallas_call(
        kernel,
        out_shape=outs,
        in_specs=[
            pl.BlockSpec(
                memory_space=pltpu.HBM if a in left else pltpu.SMEM if a in small else pltpu.VMEM
            )
            for a in range(len(args))
        ],
        out_specs=[
            pl.BlockSpec(memory_space=pltpu.HBM if a in left_out else pltpu.VMEM) for a in range(len(outs))
        ],
        scratch_shapes=scratch,
        compiler_params=pltpu.CompilerParams(vmem_limit_bytes=room << 20),
        cost_estimate=pl.CostEstimate(flops=int(flops), bytes_accessed=moved, transcendentals=0),
    )(*args)


def conv_kernel(
    dims, sig_hbm, cot_hbm, taps_hbm, out_hbm, z_hbm,
    w_ref, sig_ref, taps_ref, out_ref, z_ref, sem,
):
    cin, tin, cout, tout, ks, count, rows = dims
    k_in, k_out = cin * tin, cout * tout
    half = sig_ref.shape[1] // 2
    tiles_wide = half // lanes
    conv_rows = rows * tiles_wide
    taps_copy = pltpu.make_async_copy(taps_hbm, taps_ref, sem.at[0])
    sig_copy = pltpu.make_async_copy(sig_hbm, sig_ref, sem.at[1])
    cot_copies = [
        pltpu.make_async_copy(
            cot_hbm.at[:, :, pl.ds(lanes * b, lanes)],
            out_ref.at[:, pl.ds(conv_rows + rows * b, rows)],
            sem.at[6 + b],
        )
        for b in range(tiles_wide)
    ]
    at_conv, at_edge = pl.ds(0, conv_rows), pl.ds(2 * conv_rows, edge_rows)
    at_cot = pl.ds(conv_rows, conv_rows)
    cot_out = pltpu.make_async_copy(out_ref.at[:, at_cot], out_hbm.at[:, at_cot], sem.at[5])
    z_out = pltpu.make_async_copy(z_ref, z_hbm, sem.at[2])
    half_count = count // 2
    conv_outs = [
        pltpu.make_async_copy(
            out_ref.at[pl.ds(low, half_count), at_conv], out_hbm.at[pl.ds(low, half_count), at_conv], sem.at[at]
        )
        for at, low in ((3, 0), (6 + tiles_wide, half_count))
    ]
    edge_out = pltpu.make_async_copy(out_ref.at[:, at_edge], out_hbm.at[:, at_edge], sem.at[4])
    taps_copy.start()
    sig_copy.start()
    for copy in cot_copies:
        copy.start()
    taps_copy.wait()
    blank = jnp.zeros((2 * cin, cout), bf16)
    stacked = []
    for j in range(ks):
        column = jnp.concatenate([blank] + [taps_ref[i, j] for i in range(ks)] + [blank, blank], axis=0)
        for v in range(4):
            stacked.append(column[2 * cin * v : 2 * cin * v + lanes])
    eye = one_hot((cout, cout), lambda r: r)
    tiles = dot_nt(eye, jnp.concatenate(stacked, axis=0)).astype(bf16)
    empty = jnp.zeros((cout, lanes), bf16)
    for j in range(ks):
        for t in range(tout):
            for q in range(k_in // lanes):
                v = 2 * q - t + 2
                at = (j * 4 + v) * lanes
                tile = tiles[:, at : at + lanes] if 0 <= v < 4 else empty
                w_ref[j, cout * t : cout * (t + 1), lanes * q : lanes * (q + 1)] = tile
    sig_copy.wait()
    split = one_hot_columns((2 * lanes, 2 * lanes), lambda q: swapped(q, 2, lanes))
    parts = [dot(sig_ref[:, b : b + 2 * lanes], split) for b in range(0, 2 * half, 2 * lanes)]
    apart = jnp.concatenate([p[:, :lanes] for p in parts] + [p[:, lanes:] for p in parts], axis=1)
    to_time = one_hot((k_in, k_in), lambda r: swapped(r, tin, cin))
    z = dot(to_time, apart.astype(bf16)).astype(bf16)
    z_ref[...] = z
    z_out.start()
    for copy in cot_copies:
        copy.wait()
    cot_out.start()
    even, odd = z[:, :half], z[:, half:]
    left = dot(w_ref[0], even) + dot(w_ref[1], odd)
    right = dot(w_ref[4], even)
    lane = iota((k_out, half), 1)
    own = (
        dot(w_ref[2], even)
        + dot(w_ref[3], odd)
        + jnp.where(lane == 0, 0.0, pltpu.roll(left, 1, 1))
        + jnp.where(lane == half - 1, 0.0, pltpu.roll(right, half - 1, 1))
    )
    high = own.astype(bf16)
    first = iota((k_out, lanes), 1) == 0

    def parts_of(v):
        top = v.astype(bf16)
        return top, (v - top.astype(f32)).astype(bf16)

    _, own_rest = parts_of(jnp.where(first, own[:, :lanes], own[:, half - lanes :]))
    next_high, next_rest = parts_of(jnp.where(first, right[:, :lanes], left[:, half - lanes :]))
    row, col = iota((edge_rows, 3 * lanes), 0), iota((edge_rows, 3 * lanes), 1)
    pick = jnp.zeros((edge_rows, 3 * lanes), f32)
    for at, column in enumerate((0, lanes - 1, 2 * lanes - 1, 3 * lanes - 1, lanes, 2 * lanes)):
        pick = jnp.where((row == at) & (col == column), 1.0, pick)
    edges = dot_nt(pick.astype(bf16), jnp.concatenate([own_rest, next_high, next_rest], axis=1))
    from_time = one_hot((k_out, k_out), lambda r: swapped(r, cout, tout))
    edges = dot_nt(edges.astype(bf16), from_time)
    for d in range(count):
        out_ref[d, 2 * conv_rows :] = jnp.zeros((edge_rows, lanes), bf16)
        out_ref[d, 2 * conv_rows :, :rows] = edges[:, rows * d : rows * (d + 1)].astype(bf16)
    edge_out.start()
    for part, conv_out in enumerate(conv_outs):
        low = half_count * part
        main = dot(from_time[rows * low : rows * (low + half_count)], high).astype(bf16)
        for d in range(half_count):
            for b in range(tiles_wide):
                at = slice(lanes * b, lanes * (b + 1))
                out_ref[low + d, rows * b : rows * (b + 1)] = main[rows * d : rows * (d + 1), at]
        conv_out.start()
    cot_out.wait()
    z_out.wait()
    for conv_out in conv_outs:
        conv_out.wait()
    edge_out.wait()


def transform(real, imag, sign):
    size = len(real)
    if size == 1:
        return (list(real), [None] if imag is None else list(imag))
    even_re, even_im = transform(real[0::2], None if imag is None else imag[0::2], sign)
    odd_re, odd_im = transform(real[1::2], None if imag is None else imag[1::2], sign)
    out_re, out_im = [None] * size, [None] * size

    def plus(a, b):
        return b if a is None else (a if b is None else a + b)

    def minus(a, b):
        return a if b is None else (-b if a is None else a - b)

    for k in range(size // 2):
        re, im = odd_re[k], odd_im[k]
        if k == 0:
            tr, ti = re, im
        elif 4 * k == size:
            tr = None if im is None else (im if sign < 0 else -im)
            ti = -re if sign < 0 else re
        else:
            c, s = math.cos(2 * math.pi * k / size), sign * math.sin(2 * math.pi * k / size)
            if im is None:
                tr, ti = c * re, s * re
            elif 8 * k == size:
                tr, ti = (c * (re - im), c * (re + im)) if sign > 0 else (c * (re + im), c * (im - re))
            elif 8 * k == 3 * size:
                tr, ti = (c * (re + im), c * (im - re)) if sign > 0 else (c * (re - im), c * (re + im))
            else:
                tr, ti = c * re - s * im, s * re + c * im
        out_re[k], out_im[k] = plus(even_re[k], tr), plus(even_im[k], ti)
        out_re[k + size // 2], out_im[k + size // 2] = minus(even_re[k], tr), minus(even_im[k], ti)
    return out_re, out_im


def gelu_slope(v):
    return 0.5 * (1.0 + lax.erf(v * inv_root_two)) + v * jnp.exp(-0.5 * v * v) * inv_root_tau


def filter_kernel(
    dims, cols_ref, own_ref, twist_ref, wave_ref,
    out_ref, cross_ref, x_ref, y_ref, spec_ref, grad_ref, prod_ref, resp_ref, high_ref, rest_ref,
):
    count, channels, tout, width = dims
    rows, pair = channels * tout, tout // 2
    wide, groups = width // lanes, count * channels
    for at, table_ref in ((0, high_ref), (width, rest_ref)):
        cosine, sine = wave_ref[at : at + width, :width], wave_ref[at : at + width, width:]
        table_ref[:width, :width], table_ref[:width, width:] = cosine, -sine
        table_ref[width:, :width], table_ref[width:, width:] = sine, cosine
    for b in range(2 * wide):
        own = own_ref[b // wide, :, lanes * (b % wide) : lanes * (b % wide + 1)]
        for step in range(pair):
            resp_ref[b, pl.ds(step, groups, stride=pair), :] = own
    packed = rows // 2
    group = min(2, channels)
    chunk = group * pair
    edge_row, edge_col = iota((edge_rows, width), 0), iota((edge_rows, width), 1)
    to_low = (edge_col == 0) & ((edge_row == 0) | (edge_row == 2) | (edge_row == 3))
    to_high = (edge_col == width - 1) & ((edge_row == 1) | (edge_row == 4) | (edge_row == 5))
    spread = (to_low | to_high).astype(f32).astype(bf16)
    low = 2 * rows * (width // lanes)
    edges = [cols_ref[d, low:, :rows].astype(f32) for d in range(count)]
    none = jnp.zeros((edge_rows, rows), f32)
    kind = iota((edge_rows, rows), 0)
    for d in range(count):
        before = edges[d - 1] if d > 0 else none
        after = edges[d + 1] if d < count - 1 else none
        joined = jnp.where(kind < 2, edges[d], jnp.where(kind < 4, before, after))
        blocks = [cols_ref[d, rows * b : rows * (b + 1)] for b in range(width // lanes)]
        whole = jnp.concatenate(blocks, axis=1).astype(f32) + dot_tn(joined.astype(bf16), spread)
        x_ref[d] = whole.astype(bf16).astype(f32)

    def forward_planes(real, imag, r, h):
        re, im = transform(real, imag, -1)
        for k in range(count):
            c = twist_ref[0, k : k + 1, h : h + lanes]
            s = twist_ref[1, k : k + 1, h : h + lanes]
            at = slice(k * packed + r, k * packed + r + chunk)
            y_ref[at, h : h + lanes] = re[k] * c + im[k] * s if k else re[k]
            y_ref[at, width + h : width + h + lanes] = im[k] * c - re[k] * s if k else im[k]

    def backward_planes(r, h):
        re, im = [], []
        for k in range(count):
            c = twist_ref[0, k : k + 1, h : h + lanes]
            s = twist_ref[1, k : k + 1, h : h + lanes]
            at = slice(k * packed + r, k * packed + r + chunk)
            a, b = y_ref[at, h : h + lanes], y_ref[at, width + h : width + h + lanes]
            re.append(a * c - b * s if k else a)
            im.append(b * c + a * s if k else b)
        return transform(re, im, 1)

    def inner(product):
        v = y_ref[...]
        high = v.astype(bf16)
        rest = (v - high.astype(f32)).astype(bf16)
        both = product(jnp.concatenate([high, rest], axis=0), high_ref[...])
        size = v.shape[0]
        return both[:size] + both[size:] + product(high, rest_ref[...])

    def paired(tiles):
        return (
            jnp.concatenate([tile[:pair] for tile in tiles], axis=0),
            jnp.concatenate([tile[pair:] for tile in tiles], axis=0),
        )

    chunks = [(r, h) for r in range(0, packed, chunk) for h in range(0, width, lanes)]
    for r, h in chunks:
        planes = [
            paired([x_ref[d, 2 * r + tout * g : 2 * r + tout * (g + 1), h : h + lanes] for g in range(group)])
            for d in range(count)
        ]
        forward_planes([re for re, im in planes], [im for re, im in planes], r, h)
    spec_ref[...] = inner(dot)
    sr, si = spec_ref[:, :width], spec_ref[:, width:]
    rr, ri = (jnp.concatenate([resp_ref[p * wide + b] for b in range(wide)], axis=1) for p in range(2))
    y_ref[:, :width] = rr * sr - ri * si
    y_ref[:, width:] = rr * si + ri * sr
    y_ref[...] = inner(dot_nt)
    for r, h in chunks:
        real, imag = backward_planes(r, h)
        at = rows * (width + h) // lanes + 2 * r
        for d in range(count):
            cot = cols_ref[d, at : at + tout * group].astype(f32)
            re, im = paired([cot[tout * g : tout * (g + 1)] for g in range(group)])
            real[d], imag[d] = re * gelu_slope(real[d]), im * gelu_slope(imag[d])
        forward_planes(real, imag, r, h)
    grad_ref[...] = inner(dot)
    sr, si = spec_ref[:, :width], spec_ref[:, width:]
    gr, gi = grad_ref[:, :width], grad_ref[:, width:]
    rr, ri = (jnp.concatenate([resp_ref[p * wide + b] for b in range(wide)], axis=1) for p in range(2))
    y_ref[:, :width] = rr * gr + ri * gi
    y_ref[:, width:] = rr * gi - ri * gr
    scale = 1.0 / (count * width)
    crossed = ((sr * gr + si * gi) * scale, (sr * gi - si * gr) * scale)
    for b in range(2 * wide):
        prod_ref[b] = crossed[b // wide][:, lanes * (b % wide) : lanes * (b % wide + 1)]
    for b in range(2 * wide):
        summed = prod_ref[b, pl.ds(0, groups, stride=pair), :]
        for step in range(1, pair):
            summed = summed + prod_ref[b, pl.ds(step, groups, stride=pair), :]
        cross_ref[:, lanes * b : lanes * (b + 1)] = summed
    y_ref[...] = inner(dot_nt)
    for r, h in chunks:
        real, imag = backward_planes(r, h)
        for d in range(count):
            for g in range(group):
                at = slice(pair * g, pair * (g + 1))
                tile = jnp.concatenate([real[d][at], imag[d][at]], axis=0)
                x_ref[d, 2 * r + tout * g : 2 * r + tout * (g + 1), h : h + lanes] = tile
    last = ((iota((edge_rows, lanes), 0) == 0) & (iota((edge_rows, lanes), 1) == lanes - 1)).astype(f32).astype(bf16)
    first = ((iota((edge_rows, lanes), 0) == 1) & (iota((edge_rows, lanes), 1) == 0)).astype(f32).astype(bf16)
    for chip in range(count // cores):
        at = 0
        for d in range(cores * chip, cores * (chip + 1)):
            for b in range(0, width, lanes):
                out_ref[chip, at : at + rows] = x_ref[d, :, b : b + lanes].astype(bf16)
                at += rows
        out_ref[chip, at:] = jnp.zeros((edge_rows, lanes), bf16)
        edge = none
        if chip > 0:
            edge = edge + dot_nt(last, x_ref[cores * chip - 1, :, width - lanes :].astype(bf16))
        if chip < count // cores - 1:
            edge = edge + dot_nt(first, x_ref[cores * (chip + 1), :, :lanes].astype(bf16))
        out_ref[chip, at:, :rows] = edge.astype(bf16)


def hermitian_kernel(cross_ref, out_ref):
    _, channels, count, width = out_ref.shape
    row, col = iota((width, width), 0), iota((width, width), 1)
    flip = (row + col == width - 1).astype(f32).astype(bf16)
    flip_first = ((row + col == width) | ((row == 0) & (col == 0))).astype(f32).astype(bf16)

    def moved(v, by):
        total = None
        for _ in range(3):
            part = v.astype(bf16)
            v = v - part.astype(f32)
            term = dot(part, by)
            total = term if total is None else total + term
        return total

    for k in range(count):
        from_k = channels * ((count - k) % count)
        own = cross_ref[channels * k : channels * (k + 1)]
        other = cross_ref[from_k : from_k + channels]
        by = flip if k else flip_first
        out_ref[0, :, k] = 0.5 * (own[:, :width] + moved(other[:, :width], by))
        out_ref[1, :, k] = 0.5 * (own[:, width:] - moved(other[:, width:], by))


def gather_kernel(core_ref, own_ref, other_ref, out_ref):
    k_in, wide = own_ref.shape
    width = wide // 2
    pad = (out_ref.shape[0] - k_in) // 2
    core = core_ref[0]
    out_ref[:pad] = jnp.zeros((pad, cores * wide), bf16)
    out_ref[pad + k_in :] = jnp.zeros((pad, cores * wide), bf16)
    for phase in range(2):
        at = slice(width * phase, width * (phase + 1))
        own_at = pl.multiple_of(wide * phase + width * core, lanes)
        other_at = pl.multiple_of(wide * phase + width * (1 - core), lanes)
        out_ref[pad : pad + k_in, pl.ds(own_at, width)] = own_ref[:, at]
        out_ref[pad : pad + k_in, pl.ds(other_at, width)] = other_ref[:, at]


def tap_kernel(
    dims, core_ref, grad_ref, z_ref, tap_ref, keep_ref, send_ref, g_ref, exact_ref, shifted_ref
):
    cin, tin, cout, tout, ks, count, rows = dims
    some = cout // cores
    width = keep_ref.shape[1] - lanes
    wide = cores * width
    core = core_ref[0]
    row, col = iota((edge_rows, 2 * lanes), 0), iota((edge_rows, 2 * lanes), 1)
    spread = (((row == 0) & (col == lanes - 1)) | ((row == 1) & (col == lanes))).astype(f32).astype(bf16)
    for chip in range(count // cores):
        at = slice(rows * chip, rows * (chip + 1))
        low = 0
        for b in range(0, wide, lanes):
            g_ref[at, lanes + b : 2 * lanes + b] = grad_ref[chip, low : low + rows].astype(f32)
            low += rows
        edge = dot_tn(grad_ref[chip, low:, :rows], spread)
        g_ref[at, :lanes] = edge[:, :lanes]
        g_ref[at, lanes + wide :] = edge[:, lanes:]
    to_time = one_hot((some * tout, some * tout), lambda r: swapped(r, tout, some))
    g = dot(to_time, g_ref[...].astype(bf16))
    inside = slice(lanes, lanes + wide)
    shifted_ref[0] = pltpu.roll(g, wide + 2 * lanes - 1, 1)[:, inside].astype(bf16)
    shifted_ref[1] = g[:, inside].astype(bf16)
    shifted_ref[2] = pltpu.roll(g, 1, 1)[:, inside].astype(bf16)
    exact_ref[...] = g.astype(bf16)
    lane = iota((some * tout, lanes), 1)
    for block, block_ref in ((core, keep_ref), (1 - core, send_ref)):
        at = width * block
        before, inner, after = (
            exact_ref[:, pl.ds(pl.multiple_of(at + low, lanes), size)]
            for low, size in ((0, lanes), (lanes, width), (lanes + width, lanes))
        )
        edge = jnp.where(lane == 0, after.astype(f32), before.astype(f32))
        block_ref[:, :width] = inner
        block_ref[:, width:] = jnp.where((lane == 0) | (lane == lanes - 1), edge, 0.0).astype(bf16)
    blank = jnp.zeros((lanes - 3 * some, wide), bf16)
    size, reach = ks * cin, (ks + 2) * cin
    even, odd = None, None
    for t in range(0, tout, 2):
        band = slice(2 * cin * t, 2 * cin * t + reach)
        taken = []
        for at in (slice(some * t, some * (t + 1)), slice(some * (t + 1), some * (t + 2))):
            taken += [shifted_ref[shift, at] for shift in range(3)] + [blank]
        samples = jnp.concatenate([z_ref[band, :wide], z_ref[band, wide:]], axis=0)
        both = dot_nt(samples, jnp.concatenate(taken, axis=0))
        first = both[:size, :lanes] + both[reach - size : reach, lanes:]
        second = both[reach : reach + size, :lanes] + both[2 * reach - size :, lanes:]
        even = first if even is None else even + first
        odd = second if odd is None else odd + second
    tap_ref[:size] = jnp.where(iota((size, lanes), 1) < 3 * some, even, pltpu.roll(odd, 3 * some, 1))
    fold = size * some // lanes
    folded = jnp.zeros((fold, lanes), f32)
    for part in range(lanes // some):
        moved = pltpu.roll(odd[fold * part : fold * (part + 1)], (some * (part - 1)) % lanes, 1)
        here = split_index(iota((fold, lanes), 1), some)[0] == part
        folded = jnp.where(here, moved, folded)
    tap_ref[size:] = folded


def input_kernel(dims, core_ref, own_ref, other_ref, taps_ref, out_ref, w_ref):
    cin, tin, cout, tout, ks, count, rows = dims
    k_in = cin * tin
    half = own_ref.shape[1] - lanes
    some, channels = cout // cores, cout // count
    steps = lanes // some
    kinds = ks + 2 * (steps - 1)
    blank = jnp.zeros((cin, cout), bf16)
    core = core_ref[0]
    o, lane = iota((cout, lanes), 0), iota((cout, lanes), 1)
    device, channel = split_index(o, channels)
    chip, core_of = split_index(device, cores)
    for part in range(cores):
        wanted = core if part == 0 else 1 - core
        tiles = None
        for step in range(steps):
            picked = [taps_ref[i - 2 * step, j] if 0 <= i - 2 * step < ks else blank
                      for j in range(ks) for i in range(kinds)]
            place = (core_of == wanted) & (lane == some * step + chip * channels + channel)
            term = dot(jnp.concatenate(picked, axis=0), place.astype(f32).astype(bf16))
            tiles = term if tiles is None else tiles + term
        tiles = tiles.astype(bf16)
        empty = jnp.zeros((cin, lanes), bf16)
        for j in range(ks):
            for s in range(tin):
                for q in range(some * tout // lanes):
                    i = s - 2 * steps * q + 2
                    at = (j * kinds + i) * cin
                    tile = tiles[at : at + cin] if 0 <= i < kinds else empty
                    low = some * tout * part + lanes * q
                    w_ref[j, cin * s : cin * (s + 1), low : low + lanes] = tile
    g = jnp.concatenate([own_ref[...], other_ref[...]], axis=0)
    wide = half + lanes
    same = g[:, :half]
    later = dot(g, one_hot_columns((wide, half), lambda n: n + 1)).astype(bf16)
    sooner = dot(g, one_hot_columns((wide, half), lambda n: jnp.where(n == 0, wide - 1, n - 1))).astype(bf16)
    even = dot(w_ref[0], later) + dot(w_ref[2], same) + dot(w_ref[4], sooner)
    odd = dot(w_ref[1], later) + dot(w_ref[3], same)
    both = jnp.concatenate([even.astype(bf16), odd.astype(bf16)], axis=1)
    to_channel = one_hot((k_in, k_in), lambda r: swapped(r, cin, tin))
    both = dot(to_channel, both).astype(bf16)
    merge = one_hot((2 * lanes, 2 * lanes), lambda r: swapped(r, 2, lanes))
    for b in range(half // lanes):
        part = jnp.concatenate(
            [both[:, lanes * b : lanes * (b + 1)], both[:, half + lanes * b : half + lanes * (b + 1)]], axis=1
        )
        out_ref[:, 2 * lanes * b : 2 * lanes * (b + 1)] = dot(part, merge).astype(bf16)


def unpack_kernel(dims, scale, tap_ref, out_ref):
    cin, tin, cout, tout, ks, count, rows = dims
    some, channels = cout // cores, cout // count
    size, folds = ks * cin, lanes // some
    fold = size // folds
    packed = size + fold
    both = jnp.concatenate([tap_ref[:packed], tap_ref[packed:]], axis=1)

    wide = cores * lanes
    source, target = iota((wide, folds * cout), 0), iota((wide, folds * cout), 1)
    slot, o = split_index(target, cout)
    device, channel = split_index(o, channels)
    chip, core_of = split_index(device, cores)
    place = (source == core_of * lanes + slot * some + chip * channels + channel).astype(f32).astype(bf16)
    total, rest = None, both
    for _ in range(3):
        part = rest.astype(bf16)
        rest = rest - part.astype(f32)
        term = dot(part, place)
        total = term if total is None else total + term
    total = total * scale
    for slot, j in enumerate((0, 2, 4, 1)):
        for i in range(ks):
            out_ref[i, j] = total[cin * i : cin * (i + 1), cout * slot : cout * (slot + 1)]
    for at in range(0, size, 8):
        slot, low = at // fold, size + at % fold
        out_ref[at // cin, 3, at % cin : at % cin + 8] = total[low : low + 8, cout * slot : cout * (slot + 1)]


def summed_over_chips(rows, axis, steps):
    count = lax.axis_size(axis)
    rounded = rows.astype(bf16)
    theirs = [lax.ppermute(rounded, axis, partners(count, step)).astype(f32) for step in steps]
    if len(steps) == 1:
        return rounded.astype(f32) + theirs[0]
    return (rounded.astype(f32) + theirs[0]) + (theirs[1] + theirs[2])


def partners(count, step):
    return [(i, i ^ step) for i in range(count)]


def mirrored(spectrum):
    return jnp.roll(jnp.flip(spectrum, -1), 1, -1)


def tables(count, width):
    inner = np.outer(np.arange(width), np.arange(width)) % width * (2.0 * np.pi / width)
    table = np.concatenate([np.cos(inner), np.sin(inner)], axis=1).astype(np.float32)
    high = table.astype(bf16)
    rest = (table - high.astype(np.float32)).astype(bf16)
    outer = np.outer(np.arange(count), np.arange(width)) * (2.0 * np.pi / (count * width))
    twist = np.stack([np.cos(outer), np.sin(outer)]).astype(np.float32)
    return twist, np.concatenate([high, rest])


def per_device(signal, conv_taps, response, cotangent):
    cin, tin, fibre_in = signal.shape
    cout, tout, width = cotangent.shape
    ks = conv_taps.shape[0]
    count = lax.axis_size("fibre")
    channels = cout // count
    rows = channels * tout
    waves = count * width
    tiles = width // lanes
    dims = (cin, tin, cout, tout, ks, count, rows)
    k_in, k_out = cin * tin, cout * tout
    taps = jnp.swapaxes(conv_taps, 2, 3)
    shape = jax.ShapeDtypeStruct
    conv_part, z = call(
        functools.partial(conv_kernel, dims),
        [
            shape((count, 2 * rows * tiles + edge_rows, lanes), bf16),
            shape((k_in, fibre_in), bf16),
        ],
        [
            pltpu.VMEM((ks, k_out, k_in), bf16),
            pltpu.VMEM((k_in, fibre_in), bf16),
            pltpu.VMEM(taps.shape, bf16),
            pltpu.VMEM((count, 2 * rows * tiles + edge_rows, lanes), bf16),
            pltpu.VMEM((k_in, fibre_in), bf16),
            pltpu.SemaphoreType.DMA((7 + tiles,)),
        ],
        2e9,
        (signal.reshape(k_in, fibre_in), cotangent.reshape(count, rows, width), taps),
        left=(0, 1, 2),
        left_out=(0, 1),
        room=60,
    )
    other_z = lax.ppermute(z, "fibre", partners(count, 1))
    cols = lax.all_to_all(conv_part, "fibre", split_axis=0, concat_axis=0, tiled=True)
    back = mirrored(response)
    real = jnp.stack([response[0] + back[0], response[1] - back[1]]) * (0.5 / waves)
    real = real.reshape(2, channels, width, count).transpose(0, 3, 1, 2)
    real = real.reshape(2, count * channels, width)
    twist, waves_table = tables(count, width)
    big = count * rows // 2
    grad_part, cross = call(
        functools.partial(filter_kernel, (count, channels, tout, width)),
        [
            shape((count // cores, cores * rows * tiles + edge_rows, lanes), bf16),
            shape((count * channels, 2 * width), f32),
        ],
        [
            pltpu.VMEM((count, rows, width), f32),
            pltpu.VMEM((big, 2 * width), f32),
            pltpu.VMEM((big, 2 * width), f32),
            pltpu.VMEM((big, 2 * width), f32),
            pltpu.VMEM((2 * tiles, big, lanes), f32),
            pltpu.VMEM((2 * tiles, big, lanes), f32),
            pltpu.VMEM((2 * width, 2 * width), bf16),
            pltpu.VMEM((2 * width, 2 * width), bf16),
        ],
        6e9,
        (cols, real, jnp.asarray(twist), jnp.asarray(waves_table)),
    )
    (cross,) = call(hermitian_kernel, [shape((2, channels, count, width), f32)], [], 1e6, (cross,))
    filter_grad = cross.transpose(0, 1, 3, 2).reshape(2, channels, waves)
    chips = [[core + cores * chip for chip in range(count // cores)] for core in range(cores)]
    grad_cols = lax.all_to_all(
        grad_part, "fibre", split_axis=0, concat_axis=0, tiled=True, axis_index_groups=chips
    )
    core = (lax.axis_index("fibre") % cores).astype(jnp.int32).reshape(1)
    (samples,) = call(
        gather_kernel,
        [shape((k_in + 4 * cin, cores * fibre_in), bf16)],
        [],
        1e6,
        (core, z, other_z),
        small=(0,),
    )
    grad_cols, filter_grad, samples = lax.optimization_barrier((grad_cols, filter_grad, samples))
    some = k_out // cores
    taps_part, keep, send = call(
        functools.partial(tap_kernel, dims),
        [
            shape((ks * cin + ks * cin * (cout // cores) // lanes, lanes), f32),
            shape((some, width + lanes), bf16),
            shape((some, width + lanes), bf16),
        ],
        [
            pltpu.VMEM((some, cores * width + 2 * lanes), f32),
            pltpu.VMEM((some, cores * width + 2 * lanes), bf16),
            pltpu.VMEM((3, some, cores * width), bf16),
        ],
        1e9,
        (core, grad_cols, samples),
        small=(0,),
    )
    got = lax.ppermute(send, "fibre", partners(count, 1))
    chips = count // cores
    step = 4 if chips % 4 == 0 else 1
    total = taps_part
    if step == 4:
        total = summed_over_chips(total, "fibre", (cores, 2 * cores, 3 * cores))
    total, keep, got = lax.optimization_barrier((total, keep, got))
    (input_grad,) = call(
        functools.partial(input_kernel, dims),
        [shape((k_in, fibre_in), bf16)],
        [pltpu.VMEM((ks, k_in, k_out), bf16)],
        2e9,
        (core, keep, got, taps),
        small=(0,),
    )
    while step < chips:
        total = summed_over_chips(total, "fibre", (cores * step,))
        step *= 2
    total, input_grad = lax.optimization_barrier((total, input_grad))
    other = lax.ppermute(total, "fibre", partners(count, 1))
    total = jnp.where(core[0] == 0, jnp.concatenate([total, other]), jnp.concatenate([other, total]))
    (tap_grad,) = call(
        functools.partial(unpack_kernel, dims, 1.0 / math.sqrt(tout * waves)),
        [shape((ks, ks, cin, cout), f32)],
        [],
        1e6,
        (total,),
    )
    return (input_grad.reshape(signal.shape), jnp.swapaxes(tap_grad, 2, 3), filter_grad)


def solution(mesh):
    in_specs = (P("parts", None, "fibre"), P(), P(None, "fibre", None), P("parts", None, "fibre"))
    out_specs = (P("parts", None, "fibre"), P("parts", None, None, None), P("parts", "fibre", None))
    return jax.shard_map(
        per_device, mesh=mesh, in_specs=in_specs, out_specs=out_specs, check_vma=False
    )
```

```python
import functools
import math

import jax
import jax.numpy as jnp
import numpy as np
from jax import lax
from jax.experimental import pallas as pl
from jax.experimental.pallas import tpu as pltpu
from jax.sharding import PartitionSpec as P

bf16 = jnp.bfloat16
f32 = jnp.float32
inv_root_two = 1.0 / math.sqrt(2.0)
inv_root_tau = 1.0 / math.sqrt(2.0 * math.pi)
lanes = 128
edge_rows = 8
cores = 2


def dot(a, b):
    return jnp.dot(a, b, preferred_element_type=f32)


def dot_nt(a, b):
    return lax.dot_general(a, b, (((1,), (1,)), ((), ())), preferred_element_type=f32)


def dot_tn(a, b):
    return lax.dot_general(a, b, (((0,), (0,)), ((), ())), preferred_element_type=f32)


def iota(shape, dim):
    return lax.broadcasted_iota(jnp.int32, shape, dim)


def split_index(x, size):
    if size & (size - 1):
        return x // size, x % size
    return lax.shift_right_logical(x, jnp.full_like(x, size.bit_length() - 1)), x & (size - 1)


def swapped(x, outer, inner):
    a, b = split_index(x, inner)
    return b * outer + a


def one_hot(shape, column_of_row):
    return (iota(shape, 1) == column_of_row(iota((shape[0], 1), 0))).astype(f32).astype(bf16)


def one_hot_columns(shape, row_of_column):
    return (iota(shape, 0) == row_of_column(iota((1, shape[1]), 1))).astype(f32).astype(bf16)


def call(kernel, outs, scratch, flops, args, left=(), left_out=(), small=(), room=24):
    moved = sum(a.size * a.dtype.itemsize for a in list(args) + list(outs))
    return pl.pallas_call(
        kernel,
        out_shape=outs,
        in_specs=[
            pl.BlockSpec(
                memory_space=pltpu.HBM if a in left else pltpu.SMEM if a in small else pltpu.VMEM
            )
            for a in range(len(args))
        ],
        out_specs=[
            pl.BlockSpec(memory_space=pltpu.HBM if a in left_out else pltpu.VMEM) for a in range(len(outs))
        ],
        scratch_shapes=scratch,
        compiler_params=pltpu.CompilerParams(vmem_limit_bytes=room << 20),
        cost_estimate=pl.CostEstimate(flops=int(flops), bytes_accessed=moved, transcendentals=0),
    )(*args)


def conv_kernel(
    dims, sig_hbm, cot_hbm, taps_hbm, out_hbm, z_hbm,
    w_ref, sig_ref, taps_ref, out_ref, z_ref, sem,
):
    cin, tin, cout, tout, ks, count, rows = dims
    k_in, k_out = cin * tin, cout * tout
    half = sig_ref.shape[1] // 2
    tiles_wide = half // lanes
    conv_rows = rows * tiles_wide
    taps_copy = pltpu.make_async_copy(taps_hbm, taps_ref, sem.at[0])
    sig_copy = pltpu.make_async_copy(sig_hbm, sig_ref, sem.at[1])
    cot_copies = [
        pltpu.make_async_copy(
            cot_hbm.at[:, :, pl.ds(lanes * b, lanes)],
            out_ref.at[:, pl.ds(conv_rows + rows * b, rows)],
            sem.at[6 + b],
        )
        for b in range(tiles_wide)
    ]
    at_conv, at_edge = pl.ds(0, conv_rows), pl.ds(2 * conv_rows, edge_rows)
    at_cot = pl.ds(conv_rows, conv_rows)
    cot_out = pltpu.make_async_copy(out_ref.at[:, at_cot], out_hbm.at[:, at_cot], sem.at[5])
    z_out = pltpu.make_async_copy(z_ref, z_hbm, sem.at[2])
    half_count = count // 2
    conv_outs = [
        pltpu.make_async_copy(
            out_ref.at[pl.ds(low, half_count), at_conv], out_hbm.at[pl.ds(low, half_count), at_conv], sem.at[at]
        )
        for at, low in ((3, 0), (6 + tiles_wide, half_count))
    ]
    edge_out = pltpu.make_async_copy(out_ref.at[:, at_edge], out_hbm.at[:, at_edge], sem.at[4])
    taps_copy.start()
    sig_copy.start()
    for copy in cot_copies:
        copy.start()
    taps_copy.wait()
    blank = jnp.zeros((2 * cin, cout), bf16)
    stacked = []
    for j in range(ks):
        column = jnp.concatenate([blank] + [taps_ref[i, j] for i in range(ks)] + [blank, blank], axis=0)
        for v in range(4):
            stacked.append(column[2 * cin * v : 2 * cin * v + lanes])
    eye = one_hot((cout, cout), lambda r: r)
    tiles = dot_nt(eye, jnp.concatenate(stacked, axis=0)).astype(bf16)
    empty = jnp.zeros((cout, lanes), bf16)
    for j in range(ks):
        for t in range(tout):
            for q in range(k_in // lanes):
                v = 2 * q - t + 2
                at = (j * 4 + v) * lanes
                tile = tiles[:, at : at + lanes] if 0 <= v < 4 else empty
                w_ref[j, cout * t : cout * (t + 1), lanes * q : lanes * (q + 1)] = tile
    sig_copy.wait()
    split = one_hot_columns((2 * lanes, 2 * lanes), lambda q: swapped(q, 2, lanes))
    parts = [dot(sig_ref[:, b : b + 2 * lanes], split) for b in range(0, 2 * half, 2 * lanes)]
    apart = jnp.concatenate([p[:, :lanes] for p in parts] + [p[:, lanes:] for p in parts], axis=1)
    to_time = one_hot((k_in, k_in), lambda r: swapped(r, tin, cin))
    z = dot(to_time, apart.astype(bf16)).astype(bf16)
    z_ref[...] = z
    z_out.start()
    for copy in cot_copies:
        copy.wait()
    cot_out.start()
    even, odd = z[:, :half], z[:, half:]
    left = dot(w_ref[0], even) + dot(w_ref[1], odd)
    right = dot(w_ref[4], even)
    lane = iota((k_out, half), 1)
    own = (
        dot(w_ref[2], even)
        + dot(w_ref[3], odd)
        + jnp.where(lane == 0, 0.0, pltpu.roll(left, 1, 1))
        + jnp.where(lane == half - 1, 0.0, pltpu.roll(right, half - 1, 1))
    )
    high = own.astype(bf16)
    first = iota((k_out, lanes), 1) == 0

    def parts_of(v):
        top = v.astype(bf16)
        return top, (v - top.astype(f32)).astype(bf16)

    _, own_rest = parts_of(jnp.where(first, own[:, :lanes], own[:, half - lanes :]))
    next_high, next_rest = parts_of(jnp.where(first, right[:, :lanes], left[:, half - lanes :]))
    row, col = iota((edge_rows, 3 * lanes), 0), iota((edge_rows, 3 * lanes), 1)
    pick = jnp.zeros((edge_rows, 3 * lanes), f32)
    for at, column in enumerate((0, lanes - 1, 2 * lanes - 1, 3 * lanes - 1, lanes, 2 * lanes)):
        pick = jnp.where((row == at) & (col == column), 1.0, pick)
    edges = dot_nt(pick.astype(bf16), jnp.concatenate([own_rest, next_high, next_rest], axis=1))
    from_time = one_hot((k_out, k_out), lambda r: swapped(r, cout, tout))
    edges = dot_nt(edges.astype(bf16), from_time)
    for d in range(count):
        out_ref[d, 2 * conv_rows :] = jnp.zeros((edge_rows, lanes), bf16)
        out_ref[d, 2 * conv_rows :, :rows] = edges[:, rows * d : rows * (d + 1)].astype(bf16)
    edge_out.start()
    for part, conv_out in enumerate(conv_outs):
        low = half_count * part
        main = dot(from_time[rows * low : rows * (low + half_count)], high).astype(bf16)
        for d in range(half_count):
            for b in range(tiles_wide):
                at = slice(lanes * b, lanes * (b + 1))
                out_ref[low + d, rows * b : rows * (b + 1)] = main[rows * d : rows * (d + 1), at]
        conv_out.start()
    cot_out.wait()
    z_out.wait()
    for conv_out in conv_outs:
        conv_out.wait()
    edge_out.wait()


def transform(real, imag, sign):
    size = len(real)
    if size == 1:
        return (list(real), [None] if imag is None else list(imag))
    even_re, even_im = transform(real[0::2], None if imag is None else imag[0::2], sign)
    odd_re, odd_im = transform(real[1::2], None if imag is None else imag[1::2], sign)
    out_re, out_im = [None] * size, [None] * size

    def plus(a, b):
        return b if a is None else (a if b is None else a + b)

    def minus(a, b):
        return a if b is None else (-b if a is None else a - b)

    for k in range(size // 2):
        re, im = odd_re[k], odd_im[k]
        if k == 0:
            tr, ti = re, im
        elif 4 * k == size:
            tr = None if im is None else (im if sign < 0 else -im)
            ti = -re if sign < 0 else re
        else:
            c, s = math.cos(2 * math.pi * k / size), sign * math.sin(2 * math.pi * k / size)
            if im is None:
                tr, ti = c * re, s * re
            elif 8 * k == size:
                tr, ti = (c * (re - im), c * (re + im)) if sign > 0 else (c * (re + im), c * (im - re))
            elif 8 * k == 3 * size:
                tr, ti = (c * (re + im), c * (im - re)) if sign > 0 else (c * (re - im), c * (re + im))
            else:
                tr, ti = c * re - s * im, s * re + c * im
        out_re[k], out_im[k] = plus(even_re[k], tr), plus(even_im[k], ti)
        out_re[k + size // 2], out_im[k + size // 2] = minus(even_re[k], tr), minus(even_im[k], ti)
    return out_re, out_im


def gelu_slope(v):
    return 0.5 * (1.0 + lax.erf(v * inv_root_two)) + v * jnp.exp(-0.5 * v * v) * inv_root_tau


def filter_kernel(
    dims, cols_ref, own_ref, twist_ref, wave_ref,
    out_ref, cross_ref, x_ref, y_ref, spec_ref, grad_ref, prod_ref, resp_ref, high_ref, rest_ref,
):
    count, channels, tout, width = dims
    rows, pair = channels * tout, tout // 2
    wide, groups = width // lanes, count * channels
    for at, table_ref in ((0, high_ref), (width, rest_ref)):
        cosine, sine = wave_ref[at : at + width, :width], wave_ref[at : at + width, width:]
        table_ref[:width, :width], table_ref[:width, width:] = cosine, -sine
        table_ref[width:, :width], table_ref[width:, width:] = sine, cosine
    for b in range(2 * wide):
        own = own_ref[b // wide, :, lanes * (b % wide) : lanes * (b % wide + 1)]
        for step in range(pair):
            resp_ref[b, pl.ds(step, groups, stride=pair), :] = own
    packed = rows // 2
    group = min(2, channels)
    chunk = group * pair
    edge_row, edge_col = iota((edge_rows, width), 0), iota((edge_rows, width), 1)
    to_low = (edge_col == 0) & ((edge_row == 0) | (edge_row == 2) | (edge_row == 3))
    to_high = (edge_col == width - 1) & ((edge_row == 1) | (edge_row == 4) | (edge_row == 5))
    spread = (to_low | to_high).astype(f32).astype(bf16)
    low = 2 * rows * (width // lanes)
    edges = [cols_ref[d, low:, :rows].astype(f32) for d in range(count)]
    none = jnp.zeros((edge_rows, rows), f32)
    kind = iota((edge_rows, rows), 0)
    for d in range(count):
        before = edges[d - 1] if d > 0 else none
        after = edges[d + 1] if d < count - 1 else none
        joined = jnp.where(kind < 2, edges[d], jnp.where(kind < 4, before, after))
        blocks = [cols_ref[d, rows * b : rows * (b + 1)] for b in range(width // lanes)]
        whole = jnp.concatenate(blocks, axis=1).astype(f32) + dot_tn(joined.astype(bf16), spread)
        x_ref[d] = whole.astype(bf16).astype(f32)

    def forward_planes(real, imag, r, h):
        re, im = transform(real, imag, -1)
        for k in range(count):
            c = twist_ref[0, k : k + 1, h : h + lanes]
            s = twist_ref[1, k : k + 1, h : h + lanes]
            at = slice(k * packed + r, k * packed + r + chunk)
            y_ref[at, h : h + lanes] = re[k] * c + im[k] * s if k else re[k]
            y_ref[at, width + h : width + h + lanes] = im[k] * c - re[k] * s if k else im[k]

    def backward_planes(r, h):
        re, im = [], []
        for k in range(count):
            c = twist_ref[0, k : k + 1, h : h + lanes]
            s = twist_ref[1, k : k + 1, h : h + lanes]
            at = slice(k * packed + r, k * packed + r + chunk)
            a, b = y_ref[at, h : h + lanes], y_ref[at, width + h : width + h + lanes]
            re.append(a * c - b * s if k else a)
            im.append(b * c + a * s if k else b)
        return transform(re, im, 1)

    def inner(product):
        v = y_ref[...]
        high = v.astype(bf16)
        rest = (v - high.astype(f32)).astype(bf16)
        both = product(jnp.concatenate([high, rest], axis=0), high_ref[...])
        size = v.shape[0]
        return both[:size] + both[size:] + product(high, rest_ref[...])

    def paired(tiles):
        return (
            jnp.concatenate([tile[:pair] for tile in tiles], axis=0),
            jnp.concatenate([tile[pair:] for tile in tiles], axis=0),
        )

    chunks = [(r, h) for r in range(0, packed, chunk) for h in range(0, width, lanes)]
    for r, h in chunks:
        planes = [
            paired([x_ref[d, 2 * r + tout * g : 2 * r + tout * (g + 1), h : h + lanes] for g in range(group)])
            for d in range(count)
        ]
        forward_planes([re for re, im in planes], [im for re, im in planes], r, h)
    spec_ref[...] = inner(dot)
    sr, si = spec_ref[:, :width], spec_ref[:, width:]
    rr, ri = (jnp.concatenate([resp_ref[p * wide + b] for b in range(wide)], axis=1) for p in range(2))
    y_ref[:, :width] = rr * sr - ri * si
    y_ref[:, width:] = rr * si + ri * sr
    y_ref[...] = inner(dot_nt)
    for r, h in chunks:
        real, imag = backward_planes(r, h)
        at = rows * (width + h) // lanes + 2 * r
        for d in range(count):
            cot = cols_ref[d, at : at + tout * group].astype(f32)
            re, im = paired([cot[tout * g : tout * (g + 1)] for g in range(group)])
            real[d], imag[d] = re * gelu_slope(real[d]), im * gelu_slope(imag[d])
        forward_planes(real, imag, r, h)
    grad_ref[...] = inner(dot)
    sr, si = spec_ref[:, :width], spec_ref[:, width:]
    gr, gi = grad_ref[:, :width], grad_ref[:, width:]
    rr, ri = (jnp.concatenate([resp_ref[p * wide + b] for b in range(wide)], axis=1) for p in range(2))
    y_ref[:, :width] = rr * gr + ri * gi
    y_ref[:, width:] = rr * gi - ri * gr
    scale = 1.0 / (count * width)
    crossed = ((sr * gr + si * gi) * scale, (sr * gi - si * gr) * scale)
    for b in range(2 * wide):
        prod_ref[b] = crossed[b // wide][:, lanes * (b % wide) : lanes * (b % wide + 1)]
    for b in range(2 * wide):
        summed = prod_ref[b, pl.ds(0, groups, stride=pair), :]
        for step in range(1, pair):
            summed = summed + prod_ref[b, pl.ds(step, groups, stride=pair), :]
        cross_ref[:, lanes * b : lanes * (b + 1)] = summed
    y_ref[...] = inner(dot_nt)
    for r, h in chunks:
        real, imag = backward_planes(r, h)
        for d in range(count):
            for g in range(group):
                at = slice(pair * g, pair * (g + 1))
                tile = jnp.concatenate([real[d][at], imag[d][at]], axis=0)
                x_ref[d, 2 * r + tout * g : 2 * r + tout * (g + 1), h : h + lanes] = tile
    last = ((iota((edge_rows, lanes), 0) == 0) & (iota((edge_rows, lanes), 1) == lanes - 1)).astype(f32).astype(bf16)
    first = ((iota((edge_rows, lanes), 0) == 1) & (iota((edge_rows, lanes), 1) == 0)).astype(f32).astype(bf16)
    for chip in range(count // cores):
        at = 0
        for d in range(cores * chip, cores * (chip + 1)):
            for b in range(0, width, lanes):
                out_ref[chip, at : at + rows] = x_ref[d, :, b : b + lanes].astype(bf16)
                at += rows
        out_ref[chip, at:] = jnp.zeros((edge_rows, lanes), bf16)
        edge = none
        if chip > 0:
            edge = edge + dot_nt(last, x_ref[cores * chip - 1, :, width - lanes :].astype(bf16))
        if chip < count // cores - 1:
            edge = edge + dot_nt(first, x_ref[cores * (chip + 1), :, :lanes].astype(bf16))
        out_ref[chip, at:, :rows] = edge.astype(bf16)


def hermitian_kernel(cross_ref, out_ref):
    _, channels, count, width = out_ref.shape
    row, col = iota((width, width), 0), iota((width, width), 1)
    flip = (row + col == width - 1).astype(f32).astype(bf16)
    flip_first = ((row + col == width) | ((row == 0) & (col == 0))).astype(f32).astype(bf16)

    def moved(v, by):
        total = None
        for _ in range(3):
            part = v.astype(bf16)
            v = v - part.astype(f32)
            term = dot(part, by)
            total = term if total is None else total + term
        return total

    for k in range(count):
        from_k = channels * ((count - k) % count)
        own = cross_ref[channels * k : channels * (k + 1)]
        other = cross_ref[from_k : from_k + channels]
        by = flip if k else flip_first
        out_ref[0, :, k] = 0.5 * (own[:, :width] + moved(other[:, :width], by))
        out_ref[1, :, k] = 0.5 * (own[:, width:] - moved(other[:, width:], by))


def gather_kernel(core_ref, own_ref, other_ref, out_ref):
    k_in, wide = own_ref.shape
    width = wide // 2
    pad = (out_ref.shape[0] - k_in) // 2
    core = core_ref[0]
    out_ref[:pad] = jnp.zeros((pad, cores * wide), bf16)
    out_ref[pad + k_in :] = jnp.zeros((pad, cores * wide), bf16)
    for phase in range(2):
        at = slice(width * phase, width * (phase + 1))
        own_at = pl.multiple_of(wide * phase + width * core, lanes)
        other_at = pl.multiple_of(wide * phase + width * (1 - core), lanes)
        out_ref[pad : pad + k_in, pl.ds(own_at, width)] = own_ref[:, at]
        out_ref[pad : pad + k_in, pl.ds(other_at, width)] = other_ref[:, at]


def tap_kernel(
    dims, core_ref, grad_ref, z_ref, tap_ref, keep_ref, send_ref, g_ref, exact_ref, shifted_ref
):
    cin, tin, cout, tout, ks, count, rows = dims
    some = cout // cores
    width = keep_ref.shape[1] - lanes
    wide = cores * width
    core = core_ref[0]
    row, col = iota((edge_rows, 2 * lanes), 0), iota((edge_rows, 2 * lanes), 1)
    spread = (((row == 0) & (col == lanes - 1)) | ((row == 1) & (col == lanes))).astype(f32).astype(bf16)
    for chip in range(count // cores):
        at = slice(rows * chip, rows * (chip + 1))
        low = 0
        for b in range(0, wide, lanes):
            g_ref[at, lanes + b : 2 * lanes + b] = grad_ref[chip, low : low + rows].astype(f32)
            low += rows
        edge = dot_tn(grad_ref[chip, low:, :rows], spread)
        g_ref[at, :lanes] = edge[:, :lanes]
        g_ref[at, lanes + wide :] = edge[:, lanes:]
    to_time = one_hot((some * tout, some * tout), lambda r: swapped(r, tout, some))
    g = dot(to_time, g_ref[...].astype(bf16))
    inside = slice(lanes, lanes + wide)
    shifted_ref[0] = pltpu.roll(g, wide + 2 * lanes - 1, 1)[:, inside].astype(bf16)
    shifted_ref[1] = g[:, inside].astype(bf16)
    shifted_ref[2] = pltpu.roll(g, 1, 1)[:, inside].astype(bf16)
    exact_ref[...] = g.astype(bf16)
    lane = iota((some * tout, lanes), 1)
    for block, block_ref in ((core, keep_ref), (1 - core, send_ref)):
        at = width * block
        before, inner, after = (
            exact_ref[:, pl.ds(pl.multiple_of(at + low, lanes), size)]
            for low, size in ((0, lanes), (lanes, width), (lanes + width, lanes))
        )
        edge = jnp.where(lane == 0, after.astype(f32), before.astype(f32))
        block_ref[:, :width] = inner
        block_ref[:, width:] = jnp.where((lane == 0) | (lane == lanes - 1), edge, 0.0).astype(bf16)
    blank = jnp.zeros((lanes - 3 * some, wide), bf16)
    size, reach = ks * cin, (ks + 2) * cin
    even, odd = None, None
    for t in range(0, tout, 2):
        band = slice(2 * cin * t, 2 * cin * t + reach)
        taken = []
        for at in (slice(some * t, some * (t + 1)), slice(some * (t + 1), some * (t + 2))):
            taken += [shifted_ref[shift, at] for shift in range(3)] + [blank]
        samples = jnp.concatenate([z_ref[band, :wide], z_ref[band, wide:]], axis=0)
        both = dot_nt(samples, jnp.concatenate(taken, axis=0))
        first = both[:size, :lanes] + both[reach - size : reach, lanes:]
        second = both[reach : reach + size, :lanes] + both[2 * reach - size :, lanes:]
        even = first if even is None else even + first
        odd = second if odd is None else odd + second
    tap_ref[:size] = jnp.where(iota((size, lanes), 1) < 3 * some, even, pltpu.roll(odd, 3 * some, 1))
    fold = size * some // lanes
    folded = jnp.zeros((fold, lanes), f32)
    for part in range(lanes // some):
        moved = pltpu.roll(odd[fold * part : fold * (part + 1)], (some * (part - 1)) % lanes, 1)
        here = split_index(iota((fold, lanes), 1), some)[0] == part
        folded = jnp.where(here, moved, folded)
    tap_ref[size:] = folded


def input_kernel(dims, core_ref, own_ref, other_ref, taps_ref, out_ref, w_ref):
    cin, tin, cout, tout, ks, count, rows = dims
    k_in = cin * tin
    half = own_ref.shape[1] - lanes
    some, channels = cout // cores, cout // count
    steps = lanes // some
    kinds = ks + 2 * (steps - 1)
    blank = jnp.zeros((cin, cout), bf16)
    core = core_ref[0]
    o, lane = iota((cout, lanes), 0), iota((cout, lanes), 1)
    device, channel = split_index(o, channels)
    chip, core_of = split_index(device, cores)
    for part in range(cores):
        wanted = core if part == 0 else 1 - core
        tiles = None
        for step in range(steps):
            picked = [taps_ref[i - 2 * step, j] if 0 <= i - 2 * step < ks else blank
                      for j in range(ks) for i in range(kinds)]
            place = (core_of == wanted) & (lane == some * step + chip * channels + channel)
            term = dot(jnp.concatenate(picked, axis=0), place.astype(f32).astype(bf16))
            tiles = term if tiles is None else tiles + term
        tiles = tiles.astype(bf16)
        empty = jnp.zeros((cin, lanes), bf16)
        for j in range(ks):
            for s in range(tin):
                for q in range(some * tout // lanes):
                    i = s - 2 * steps * q + 2
                    at = (j * kinds + i) * cin
                    tile = tiles[at : at + cin] if 0 <= i < kinds else empty
                    low = some * tout * part + lanes * q
                    w_ref[j, cin * s : cin * (s + 1), low : low + lanes] = tile
    g = jnp.concatenate([own_ref[...], other_ref[...]], axis=0)
    wide = half + lanes
    same = g[:, :half]
    later = dot(g, one_hot_columns((wide, half), lambda n: n + 1)).astype(bf16)
    sooner = dot(g, one_hot_columns((wide, half), lambda n: jnp.where(n == 0, wide - 1, n - 1))).astype(bf16)
    even = dot(w_ref[0], later) + dot(w_ref[2], same) + dot(w_ref[4], sooner)
    odd = dot(w_ref[1], later) + dot(w_ref[3], same)
    both = jnp.concatenate([even.astype(bf16), odd.astype(bf16)], axis=1)
    to_channel = one_hot((k_in, k_in), lambda r: swapped(r, cin, tin))
    both = dot(to_channel, both).astype(bf16)
    merge = one_hot((2 * lanes, 2 * lanes), lambda r: swapped(r, 2, lanes))
    for b in range(half // lanes):
        part = jnp.concatenate(
            [both[:, lanes * b : lanes * (b + 1)], both[:, half + lanes * b : half + lanes * (b + 1)]], axis=1
        )
        out_ref[:, 2 * lanes * b : 2 * lanes * (b + 1)] = dot(part, merge).astype(bf16)


def unpack_kernel(dims, scale, tap_ref, out_ref):
    cin, tin, cout, tout, ks, count, rows = dims
    some, channels = cout // cores, cout // count
    size, folds = ks * cin, lanes // some
    fold = size // folds
    packed = size + fold
    both = jnp.concatenate([tap_ref[:packed], tap_ref[packed:]], axis=1)

    wide = cores * lanes
    source, target = iota((wide, folds * cout), 0), iota((wide, folds * cout), 1)
    slot, o = split_index(target, cout)
    device, channel = split_index(o, channels)
    chip, core_of = split_index(device, cores)
    place = (source == core_of * lanes + slot * some + chip * channels + channel).astype(f32).astype(bf16)
    total, rest = None, both
    for _ in range(3):
        part = rest.astype(bf16)
        rest = rest - part.astype(f32)
        term = dot(part, place)
        total = term if total is None else total + term
    total = total * scale
    for slot, j in enumerate((0, 2, 4, 1)):
        for i in range(ks):
            out_ref[i, j] = total[cin * i : cin * (i + 1), cout * slot : cout * (slot + 1)]
    for at in range(0, size, 8):
        slot, low = at // fold, size + at % fold
        out_ref[at // cin, 3, at % cin : at % cin + 8] = total[low : low + 8, cout * slot : cout * (slot + 1)]


def summed_over_chips(rows, axis, steps):
    count = lax.axis_size(axis)
    rounded = rows.astype(bf16)
    theirs = [lax.ppermute(rounded, axis, partners(count, step)).astype(f32) for step in steps]
    if len(steps) == 1:
        return rounded.astype(f32) + theirs[0]
    return (rounded.astype(f32) + theirs[0]) + (theirs[1] + theirs[2])


def partners(count, step):
    return [(i, i ^ step) for i in range(count)]


def mirrored(spectrum):
    return jnp.roll(jnp.flip(spectrum, -1), 1, -1)


def tables(count, width):
    inner = np.outer(np.arange(width), np.arange(width)) % width * (2.0 * np.pi / width)
    table = np.concatenate([np.cos(inner), np.sin(inner)], axis=1).astype(np.float32)
    high = table.astype(bf16)
    rest = (table - high.astype(np.float32)).astype(bf16)
    outer = np.outer(np.arange(count), np.arange(width)) * (2.0 * np.pi / (count * width))
    twist = np.stack([np.cos(outer), np.sin(outer)]).astype(np.float32)
    return twist, np.concatenate([high, rest])


def per_device(signal, conv_taps, response, cotangent):
    cin, tin, fibre_in = signal.shape
    cout, tout, width = cotangent.shape
    ks = conv_taps.shape[0]
    count = lax.axis_size("fibre")
    channels = cout // count
    rows = channels * tout
    waves = count * width
    tiles = width // lanes
    dims = (cin, tin, cout, tout, ks, count, rows)
    k_in, k_out = cin * tin, cout * tout
    taps = jnp.swapaxes(conv_taps, 2, 3)
    shape = jax.ShapeDtypeStruct
    conv_part, z = call(
        functools.partial(conv_kernel, dims),
        [
            shape((count, 2 * rows * tiles + edge_rows, lanes), bf16),
            shape((k_in, fibre_in), bf16),
        ],
        [
            pltpu.VMEM((ks, k_out, k_in), bf16),
            pltpu.VMEM((k_in, fibre_in), bf16),
            pltpu.VMEM(taps.shape, bf16),
            pltpu.VMEM((count, 2 * rows * tiles + edge_rows, lanes), bf16),
            pltpu.VMEM((k_in, fibre_in), bf16),
            pltpu.SemaphoreType.DMA((7 + tiles,)),
        ],
        2e9,
        (signal.reshape(k_in, fibre_in), cotangent.reshape(count, rows, width), taps),
        left=(0, 1, 2),
        left_out=(0, 1),
        room=60,
    )
    other_z = lax.ppermute(z, "fibre", partners(count, 1))
    cols = lax.all_to_all(conv_part, "fibre", split_axis=0, concat_axis=0, tiled=True)
    back = mirrored(response)
    real = jnp.stack([response[0] + back[0], response[1] - back[1]]) * (0.5 / waves)
    real = real.reshape(2, channels, width, count).transpose(0, 3, 1, 2)
    real = real.reshape(2, count * channels, width)
    twist, waves_table = tables(count, width)
    big = count * rows // 2
    grad_part, cross = call(
        functools.partial(filter_kernel, (count, channels, tout, width)),
        [
            shape((count // cores, cores * rows * tiles + edge_rows, lanes), bf16),
            shape((count * channels, 2 * width), f32),
        ],
        [
            pltpu.VMEM((count, rows, width), f32),
            pltpu.VMEM((big, 2 * width), f32),
            pltpu.VMEM((big, 2 * width), f32),
            pltpu.VMEM((big, 2 * width), f32),
            pltpu.VMEM((2 * tiles, big, lanes), f32),
            pltpu.VMEM((2 * tiles, big, lanes), f32),
            pltpu.VMEM((2 * width, 2 * width), bf16),
            pltpu.VMEM((2 * width, 2 * width), bf16),
        ],
        6e9,
        (cols, real, jnp.asarray(twist), jnp.asarray(waves_table)),
    )
    (cross,) = call(hermitian_kernel, [shape((2, channels, count, width), f32)], [], 1e6, (cross,))
    filter_grad = cross.transpose(0, 1, 3, 2).reshape(2, channels, waves)
    chips = [[core + cores * chip for chip in range(count // cores)] for core in range(cores)]
    grad_cols = lax.all_to_all(
        grad_part, "fibre", split_axis=0, concat_axis=0, tiled=True, axis_index_groups=chips
    )
    core = (lax.axis_index("fibre") % cores).astype(jnp.int32).reshape(1)
    (samples,) = call(
        gather_kernel,
        [shape((k_in + 4 * cin, cores * fibre_in), bf16)],
        [],
        1e6,
        (core, z, other_z),
        small=(0,),
    )
    grad_cols, filter_grad, samples = lax.optimization_barrier((grad_cols, filter_grad, samples))
    some = k_out // cores
    taps_part, keep, send = call(
        functools.partial(tap_kernel, dims),
        [
            shape((ks * cin + ks * cin * (cout // cores) // lanes, lanes), f32),
            shape((some, width + lanes), bf16),
            shape((some, width + lanes), bf16),
        ],
        [
            pltpu.VMEM((some, cores * width + 2 * lanes), f32),
            pltpu.VMEM((some, cores * width + 2 * lanes), bf16),
            pltpu.VMEM((3, some, cores * width), bf16),
        ],
        1e9,
        (core, grad_cols, samples),
        small=(0,),
    )
    got = lax.ppermute(send, "fibre", partners(count, 1))
    chips = count // cores
    total = summed_over_chips(taps_part, "fibre", (cores,))
    step = 2
    total, keep, got = lax.optimization_barrier((total, keep, got))
    (input_grad,) = call(
        functools.partial(input_kernel, dims),
        [shape((k_in, fibre_in), bf16)],
        [pltpu.VMEM((ks, k_in, k_out), bf16)],
        2e9,
        (core, keep, got, taps),
        small=(0,),
    )
    if chips % 8 == 0:
        total = summed_over_chips(total, "fibre", (2 * cores, 4 * cores, 6 * cores))
        step = 8
    while step < chips:
        total = summed_over_chips(total, "fibre", (cores * step,))
        step *= 2
    total, input_grad = lax.optimization_barrier((total, input_grad))
    other = lax.ppermute(total, "fibre", partners(count, 1))
    total = jnp.where(core[0] == 0, jnp.concatenate([total, other]), jnp.concatenate([other, total]))
    (tap_grad,) = call(
        functools.partial(unpack_kernel, dims, 1.0 / math.sqrt(tout * waves)),
        [shape((ks, ks, cin, cout), f32)],
        [],
        1e6,
        (total,),
    )
    return (input_grad.reshape(signal.shape), jnp.swapaxes(tap_grad, 2, 3), filter_grad)


def solution(mesh):
    in_specs = (P("parts", None, "fibre"), P(), P(None, "fibre", None), P("parts", None, "fibre"))
    out_specs = (P("parts", None, "fibre"), P("parts", None, None, None), P("parts", "fibre", None))
    return jax.shard_map(
        per_device, mesh=mesh, in_specs=in_specs, out_specs=out_specs, check_vma=False
    )
```

```python
import functools
import math

import jax
import jax.numpy as jnp
import numpy as np
from jax import lax
from jax.experimental import pallas as pl
from jax.experimental.pallas import tpu as pltpu
from jax.sharding import PartitionSpec as P

bf16 = jnp.bfloat16
f32 = jnp.float32
inv_root_two = 1.0 / math.sqrt(2.0)
inv_root_tau = 1.0 / math.sqrt(2.0 * math.pi)
lanes = 128
edge_rows = 8
cores = 2


def dot(a, b):
    return jnp.dot(a, b, preferred_element_type=f32)


def dot_nt(a, b):
    return lax.dot_general(a, b, (((1,), (1,)), ((), ())), preferred_element_type=f32)


def dot_tn(a, b):
    return lax.dot_general(a, b, (((0,), (0,)), ((), ())), preferred_element_type=f32)


def iota(shape, dim):
    return lax.broadcasted_iota(jnp.int32, shape, dim)


def split_index(x, size):
    if size & (size - 1):
        return x // size, x % size
    return lax.shift_right_logical(x, jnp.full_like(x, size.bit_length() - 1)), x & (size - 1)


def swapped(x, outer, inner):
    a, b = split_index(x, inner)
    return b * outer + a


def one_hot(shape, column_of_row):
    return (iota(shape, 1) == column_of_row(iota((shape[0], 1), 0))).astype(f32).astype(bf16)


def one_hot_columns(shape, row_of_column):
    return (iota(shape, 0) == row_of_column(iota((1, shape[1]), 1))).astype(f32).astype(bf16)


def call(kernel, outs, scratch, flops, args, left=(), left_out=(), small=(), room=24):
    moved = sum(a.size * a.dtype.itemsize for a in list(args) + list(outs))
    return pl.pallas_call(
        kernel,
        out_shape=outs,
        in_specs=[
            pl.BlockSpec(
                memory_space=pltpu.HBM if a in left else pltpu.SMEM if a in small else pltpu.VMEM
            )
            for a in range(len(args))
        ],
        out_specs=[
            pl.BlockSpec(memory_space=pltpu.HBM if a in left_out else pltpu.VMEM) for a in range(len(outs))
        ],
        scratch_shapes=scratch,
        compiler_params=pltpu.CompilerParams(vmem_limit_bytes=room << 20),
        cost_estimate=pl.CostEstimate(flops=int(flops), bytes_accessed=moved, transcendentals=0),
    )(*args)


def conv_kernel(
    dims, sig_hbm, cot_hbm, taps_hbm, out_hbm, z_hbm,
    w_ref, sig_ref, taps_ref, out_ref, z_ref, sem,
):
    cin, tin, cout, tout, ks, count, rows = dims
    k_in, k_out = cin * tin, cout * tout
    half = sig_ref.shape[1] // 2
    tiles_wide = half // lanes
    conv_rows = rows * tiles_wide
    taps_copy = pltpu.make_async_copy(taps_hbm, taps_ref, sem.at[0])
    sig_copy = pltpu.make_async_copy(sig_hbm, sig_ref, sem.at[1])
    cot_copies = [
        pltpu.make_async_copy(
            cot_hbm.at[:, :, pl.ds(lanes * b, lanes)],
            out_ref.at[:, pl.ds(conv_rows + rows * b, rows)],
            sem.at[6 + b],
        )
        for b in range(tiles_wide)
    ]
    at_conv, at_edge = pl.ds(0, conv_rows), pl.ds(2 * conv_rows, edge_rows)
    at_cot = pl.ds(conv_rows, conv_rows)
    cot_out = pltpu.make_async_copy(out_ref.at[:, at_cot], out_hbm.at[:, at_cot], sem.at[5])
    z_out = pltpu.make_async_copy(z_ref, z_hbm, sem.at[2])
    half_count = count // 2
    conv_outs = [
        pltpu.make_async_copy(
            out_ref.at[pl.ds(low, half_count), at_conv], out_hbm.at[pl.ds(low, half_count), at_conv], sem.at[at]
        )
        for at, low in ((3, 0), (6 + tiles_wide, half_count))
    ]
    edge_out = pltpu.make_async_copy(out_ref.at[:, at_edge], out_hbm.at[:, at_edge], sem.at[4])
    taps_copy.start()
    sig_copy.start()
    for copy in cot_copies:
        copy.start()
    taps_copy.wait()
    blank = jnp.zeros((2 * cin, cout), bf16)
    stacked = []
    for j in range(ks):
        column = jnp.concatenate([blank] + [taps_ref[i, j] for i in range(ks)] + [blank, blank], axis=0)
        for v in range(4):
            stacked.append(column[2 * cin * v : 2 * cin * v + lanes])
    eye = one_hot((cout, cout), lambda r: r)
    tiles = dot_nt(eye, jnp.concatenate(stacked, axis=0)).astype(bf16)
    empty = jnp.zeros((cout, lanes), bf16)
    for j in range(ks):
        for t in range(tout):
            for q in range(k_in // lanes):
                v = 2 * q - t + 2
                at = (j * 4 + v) * lanes
                tile = tiles[:, at : at + lanes] if 0 <= v < 4 else empty
                w_ref[j, cout * t : cout * (t + 1), lanes * q : lanes * (q + 1)] = tile
    sig_copy.wait()
    split = one_hot_columns((2 * lanes, 2 * lanes), lambda q: swapped(q, 2, lanes))
    parts = [dot(sig_ref[:, b : b + 2 * lanes], split) for b in range(0, 2 * half, 2 * lanes)]
    apart = jnp.concatenate([p[:, :lanes] for p in parts] + [p[:, lanes:] for p in parts], axis=1)
    to_time = one_hot((k_in, k_in), lambda r: swapped(r, tin, cin))
    z = dot(to_time, apart.astype(bf16)).astype(bf16)
    z_ref[...] = z
    z_out.start()
    for copy in cot_copies:
        copy.wait()
    cot_out.start()
    even, odd = z[:, :half], z[:, half:]
    left = dot(w_ref[0], even) + dot(w_ref[1], odd)
    right = dot(w_ref[4], even)
    lane = iota((k_out, half), 1)
    own = (
        dot(w_ref[2], even)
        + dot(w_ref[3], odd)
        + jnp.where(lane == 0, 0.0, pltpu.roll(left, 1, 1))
        + jnp.where(lane == half - 1, 0.0, pltpu.roll(right, half - 1, 1))
    )
    high = own.astype(bf16)
    first = iota((k_out, lanes), 1) == 0

    def parts_of(v):
        top = v.astype(bf16)
        return top, (v - top.astype(f32)).astype(bf16)

    _, own_rest = parts_of(jnp.where(first, own[:, :lanes], own[:, half - lanes :]))
    next_high, next_rest = parts_of(jnp.where(first, right[:, :lanes], left[:, half - lanes :]))
    row, col = iota((edge_rows, 3 * lanes), 0), iota((edge_rows, 3 * lanes), 1)
    pick = jnp.zeros((edge_rows, 3 * lanes), f32)
    for at, column in enumerate((0, lanes - 1, 2 * lanes - 1, 3 * lanes - 1, lanes, 2 * lanes)):
        pick = jnp.where((row == at) & (col == column), 1.0, pick)
    edges = dot_nt(pick.astype(bf16), jnp.concatenate([own_rest, next_high, next_rest], axis=1))
    from_time = one_hot((k_out, k_out), lambda r: swapped(r, cout, tout))
    edges = dot_nt(edges.astype(bf16), from_time)
    for d in range(count):
        out_ref[d, 2 * conv_rows :] = jnp.zeros((edge_rows, lanes), bf16)
        out_ref[d, 2 * conv_rows :, :rows] = edges[:, rows * d : rows * (d + 1)].astype(bf16)
    edge_out.start()
    for part, conv_out in enumerate(conv_outs):
        low = half_count * part
        main = dot(from_time[rows * low : rows * (low + half_count)], high).astype(bf16)
        for d in range(half_count):
            for b in range(tiles_wide):
                at = slice(lanes * b, lanes * (b + 1))
                out_ref[low + d, rows * b : rows * (b + 1)] = main[rows * d : rows * (d + 1), at]
        conv_out.start()
    cot_out.wait()
    z_out.wait()
    for conv_out in conv_outs:
        conv_out.wait()
    edge_out.wait()


def transform(real, imag, sign):
    size = len(real)
    if size == 1:
        return (list(real), [None] if imag is None else list(imag))
    even_re, even_im = transform(real[0::2], None if imag is None else imag[0::2], sign)
    odd_re, odd_im = transform(real[1::2], None if imag is None else imag[1::2], sign)
    out_re, out_im = [None] * size, [None] * size

    def plus(a, b):
        return b if a is None else (a if b is None else a + b)

    def minus(a, b):
        return a if b is None else (-b if a is None else a - b)

    for k in range(size // 2):
        re, im = odd_re[k], odd_im[k]
        if k == 0:
            tr, ti = re, im
        elif 4 * k == size:
            tr = None if im is None else (im if sign < 0 else -im)
            ti = -re if sign < 0 else re
        else:
            c, s = math.cos(2 * math.pi * k / size), sign * math.sin(2 * math.pi * k / size)
            if im is None:
                tr, ti = c * re, s * re
            elif 8 * k == size:
                tr, ti = (c * (re - im), c * (re + im)) if sign > 0 else (c * (re + im), c * (im - re))
            elif 8 * k == 3 * size:
                tr, ti = (c * (re + im), c * (im - re)) if sign > 0 else (c * (re - im), c * (re + im))
            else:
                tr, ti = c * re - s * im, s * re + c * im
        out_re[k], out_im[k] = plus(even_re[k], tr), plus(even_im[k], ti)
        out_re[k + size // 2], out_im[k + size // 2] = minus(even_re[k], tr), minus(even_im[k], ti)
    return out_re, out_im


def gelu_slope(v):
    return 0.5 * (1.0 + lax.erf(v * inv_root_two)) + v * jnp.exp(-0.5 * v * v) * inv_root_tau


def filter_kernel(
    dims, cols_ref, own_ref, twist_ref, wave_ref,
    out_ref, cross_ref, x_ref, y_ref, spec_ref, grad_ref, prod_ref, resp_ref, high_ref, rest_ref,
):
    count, channels, tout, width = dims
    rows, pair = channels * tout, tout // 2
    wide, groups = width // lanes, count * channels
    for at, table_ref in ((0, high_ref), (width, rest_ref)):
        cosine, sine = wave_ref[at : at + width, :width], wave_ref[at : at + width, width:]
        table_ref[:width, :width], table_ref[:width, width:] = cosine, -sine
        table_ref[width:, :width], table_ref[width:, width:] = sine, cosine
    for b in range(2 * wide):
        own = own_ref[b // wide, :, lanes * (b % wide) : lanes * (b % wide + 1)]
        for step in range(pair):
            resp_ref[b, pl.ds(step, groups, stride=pair), :] = own
    packed = rows // 2
    group = min(2, channels)
    chunk = group * pair
    edge_row, edge_col = iota((edge_rows, width), 0), iota((edge_rows, width), 1)
    to_low = (edge_col == 0) & ((edge_row == 0) | (edge_row == 2) | (edge_row == 3))
    to_high = (edge_col == width - 1) & ((edge_row == 1) | (edge_row == 4) | (edge_row == 5))
    spread = (to_low | to_high).astype(f32).astype(bf16)
    low = 2 * rows * (width // lanes)
    edges = [cols_ref[d, low:, :rows].astype(f32) for d in range(count)]
    none = jnp.zeros((edge_rows, rows), f32)
    kind = iota((edge_rows, rows), 0)
    for d in range(count):
        before = edges[d - 1] if d > 0 else none
        after = edges[d + 1] if d < count - 1 else none
        joined = jnp.where(kind < 2, edges[d], jnp.where(kind < 4, before, after))
        blocks = [cols_ref[d, rows * b : rows * (b + 1)] for b in range(width // lanes)]
        whole = jnp.concatenate(blocks, axis=1).astype(f32) + dot_tn(joined.astype(bf16), spread)
        x_ref[d] = whole.astype(bf16).astype(f32)

    def forward_planes(real, imag, r, h):
        re, im = transform(real, imag, -1)
        for k in range(count):
            c = twist_ref[0, k : k + 1, h : h + lanes]
            s = twist_ref[1, k : k + 1, h : h + lanes]
            at = slice(k * packed + r, k * packed + r + chunk)
            y_ref[at, h : h + lanes] = re[k] * c + im[k] * s if k else re[k]
            y_ref[at, width + h : width + h + lanes] = im[k] * c - re[k] * s if k else im[k]

    def backward_planes(r, h):
        re, im = [], []
        for k in range(count):
            c = twist_ref[0, k : k + 1, h : h + lanes]
            s = twist_ref[1, k : k + 1, h : h + lanes]
            at = slice(k * packed + r, k * packed + r + chunk)
            a, b = y_ref[at, h : h + lanes], y_ref[at, width + h : width + h + lanes]
            re.append(a * c - b * s if k else a)
            im.append(b * c + a * s if k else b)
        return transform(re, im, 1)

    def inner(product):
        v = y_ref[...]
        high = v.astype(bf16)
        rest = (v - high.astype(f32)).astype(bf16)
        both = product(jnp.concatenate([high, rest], axis=0), high_ref[...])
        size = v.shape[0]
        return both[:size] + both[size:] + product(high, rest_ref[...])

    def paired(tiles):
        return (
            jnp.concatenate([tile[:pair] for tile in tiles], axis=0),
            jnp.concatenate([tile[pair:] for tile in tiles], axis=0),
        )

    chunks = [(r, h) for r in range(0, packed, chunk) for h in range(0, width, lanes)]
    for r, h in chunks:
        planes = [
            paired([x_ref[d, 2 * r + tout * g : 2 * r + tout * (g + 1), h : h + lanes] for g in range(group)])
            for d in range(count)
        ]
        forward_planes([re for re, im in planes], [im for re, im in planes], r, h)
    spec_ref[...] = inner(dot)
    sr, si = spec_ref[:, :width], spec_ref[:, width:]
    rr, ri = (jnp.concatenate([resp_ref[p * wide + b] for b in range(wide)], axis=1) for p in range(2))
    y_ref[:, :width] = rr * sr - ri * si
    y_ref[:, width:] = rr * si + ri * sr
    y_ref[...] = inner(dot_nt)
    for r, h in chunks:
        real, imag = backward_planes(r, h)
        at = rows * (width + h) // lanes + 2 * r
        for d in range(count):
            cot = cols_ref[d, at : at + tout * group].astype(f32)
            re, im = paired([cot[tout * g : tout * (g + 1)] for g in range(group)])
            real[d], imag[d] = re * gelu_slope(real[d]), im * gelu_slope(imag[d])
        forward_planes(real, imag, r, h)
    grad_ref[...] = inner(dot)
    sr, si = spec_ref[:, :width], spec_ref[:, width:]
    gr, gi = grad_ref[:, :width], grad_ref[:, width:]
    rr, ri = (jnp.concatenate([resp_ref[p * wide + b] for b in range(wide)], axis=1) for p in range(2))
    y_ref[:, :width] = rr * gr + ri * gi
    y_ref[:, width:] = rr * gi - ri * gr
    scale = 1.0 / (count * width)
    crossed = ((sr * gr + si * gi) * scale, (sr * gi - si * gr) * scale)
    for b in range(2 * wide):
        prod_ref[b] = crossed[b // wide][:, lanes * (b % wide) : lanes * (b % wide + 1)]
    for b in range(2 * wide):
        summed = prod_ref[b, pl.ds(0, groups, stride=pair), :]
        for step in range(1, pair):
            summed = summed + prod_ref[b, pl.ds(step, groups, stride=pair), :]
        cross_ref[:, lanes * b : lanes * (b + 1)] = summed
    y_ref[...] = inner(dot_nt)
    for r, h in chunks:
        real, imag = backward_planes(r, h)
        for d in range(count):
            for g in range(group):
                at = slice(pair * g, pair * (g + 1))
                tile = jnp.concatenate([real[d][at], imag[d][at]], axis=0)
                x_ref[d, 2 * r + tout * g : 2 * r + tout * (g + 1), h : h + lanes] = tile
    last = ((iota((edge_rows, lanes), 0) == 0) & (iota((edge_rows, lanes), 1) == lanes - 1)).astype(f32).astype(bf16)
    first = ((iota((edge_rows, lanes), 0) == 1) & (iota((edge_rows, lanes), 1) == 0)).astype(f32).astype(bf16)
    for chip in range(count // cores):
        at = 0
        for d in range(cores * chip, cores * (chip + 1)):
            for b in range(0, width, lanes):
                out_ref[chip, at : at + rows] = x_ref[d, :, b : b + lanes].astype(bf16)
                at += rows
        out_ref[chip, at:] = jnp.zeros((edge_rows, lanes), bf16)
        edge = none
        if chip > 0:
            edge = edge + dot_nt(last, x_ref[cores * chip - 1, :, width - lanes :].astype(bf16))
        if chip < count // cores - 1:
            edge = edge + dot_nt(first, x_ref[cores * (chip + 1), :, :lanes].astype(bf16))
        out_ref[chip, at:, :rows] = edge.astype(bf16)


def hermitian_kernel(cross_ref, out_ref):
    _, channels, count, width = out_ref.shape
    row, col = iota((width, width), 0), iota((width, width), 1)
    flip = (row + col == width - 1).astype(f32).astype(bf16)
    flip_first = ((row + col == width) | ((row == 0) & (col == 0))).astype(f32).astype(bf16)

    def moved(v, by):
        total = None
        for _ in range(3):
            part = v.astype(bf16)
            v = v - part.astype(f32)
            term = dot(part, by)
            total = term if total is None else total + term
        return total

    for k in range(count):
        from_k = channels * ((count - k) % count)
        own = cross_ref[channels * k : channels * (k + 1)]
        other = cross_ref[from_k : from_k + channels]
        by = flip if k else flip_first
        out_ref[0, :, k] = 0.5 * (own[:, :width] + moved(other[:, :width], by))
        out_ref[1, :, k] = 0.5 * (own[:, width:] - moved(other[:, width:], by))


def gather_kernel(core_ref, own_ref, other_ref, out_ref):
    k_in, wide = own_ref.shape
    width = wide // 2
    pad = (out_ref.shape[0] - k_in) // 2
    core = core_ref[0]
    out_ref[:pad] = jnp.zeros((pad, cores * wide), bf16)
    out_ref[pad + k_in :] = jnp.zeros((pad, cores * wide), bf16)
    for phase in range(2):
        at = slice(width * phase, width * (phase + 1))
        own_at = pl.multiple_of(wide * phase + width * core, lanes)
        other_at = pl.multiple_of(wide * phase + width * (1 - core), lanes)
        out_ref[pad : pad + k_in, pl.ds(own_at, width)] = own_ref[:, at]
        out_ref[pad : pad + k_in, pl.ds(other_at, width)] = other_ref[:, at]


def tap_kernel(
    dims, core_ref, grad_ref, z_ref, tap_ref, keep_ref, send_ref, g_ref, exact_ref, shifted_ref
):
    cin, tin, cout, tout, ks, count, rows = dims
    some = cout // cores
    width = keep_ref.shape[1] - lanes
    wide = cores * width
    core = core_ref[0]
    row, col = iota((edge_rows, 2 * lanes), 0), iota((edge_rows, 2 * lanes), 1)
    spread = (((row == 0) & (col == lanes - 1)) | ((row == 1) & (col == lanes))).astype(f32).astype(bf16)
    for chip in range(count // cores):
        at = slice(rows * chip, rows * (chip + 1))
        low = 0
        for b in range(0, wide, lanes):
            g_ref[at, lanes + b : 2 * lanes + b] = grad_ref[chip, low : low + rows].astype(f32)
            low += rows
        edge = dot_tn(grad_ref[chip, low:, :rows], spread)
        g_ref[at, :lanes] = edge[:, :lanes]
        g_ref[at, lanes + wide :] = edge[:, lanes:]
    to_time = one_hot((some * tout, some * tout), lambda r: swapped(r, tout, some))
    g = dot(to_time, g_ref[...].astype(bf16))
    inside = slice(lanes, lanes + wide)
    shifted_ref[0] = pltpu.roll(g, wide + 2 * lanes - 1, 1)[:, inside].astype(bf16)
    shifted_ref[1] = g[:, inside].astype(bf16)
    shifted_ref[2] = pltpu.roll(g, 1, 1)[:, inside].astype(bf16)
    exact_ref[...] = g.astype(bf16)
    lane = iota((some * tout, lanes), 1)
    for block, block_ref in ((core, keep_ref), (1 - core, send_ref)):
        at = width * block
        before, inner, after = (
            exact_ref[:, pl.ds(pl.multiple_of(at + low, lanes), size)]
            for low, size in ((0, lanes), (lanes, width), (lanes + width, lanes))
        )
        edge = jnp.where(lane == 0, after.astype(f32), before.astype(f32))
        block_ref[:, :width] = inner
        block_ref[:, width:] = jnp.where((lane == 0) | (lane == lanes - 1), edge, 0.0).astype(bf16)
    blank = jnp.zeros((lanes - 3 * some, wide), bf16)
    size, reach = ks * cin, (ks + 2) * cin
    even, odd = None, None
    for t in range(0, tout, 2):
        band = slice(2 * cin * t, 2 * cin * t + reach)
        taken = []
        for at in (slice(some * t, some * (t + 1)), slice(some * (t + 1), some * (t + 2))):
            taken += [shifted_ref[shift, at] for shift in range(3)] + [blank]
        samples = jnp.concatenate([z_ref[band, :wide], z_ref[band, wide:]], axis=0)
        both = dot_nt(samples, jnp.concatenate(taken, axis=0))
        first = both[:size, :lanes] + both[reach - size : reach, lanes:]
        second = both[reach : reach + size, :lanes] + both[2 * reach - size :, lanes:]
        even = first if even is None else even + first
        odd = second if odd is None else odd + second
    tap_ref[:size] = jnp.where(iota((size, lanes), 1) < 3 * some, even, pltpu.roll(odd, 3 * some, 1))
    fold = size * some // lanes
    folded = jnp.zeros((fold, lanes), f32)
    for part in range(lanes // some):
        moved = pltpu.roll(odd[fold * part : fold * (part + 1)], (some * (part - 1)) % lanes, 1)
        here = split_index(iota((fold, lanes), 1), some)[0] == part
        folded = jnp.where(here, moved, folded)
    tap_ref[size:] = folded


def input_kernel(dims, part, core_ref, g_ref, *refs):
    *started, taps_ref, out_ref, w_ref = refs
    cin, tin, cout, tout, ks, count, rows = dims
    k_in = cin * tin
    half = g_ref.shape[1] - lanes
    some, channels = cout // cores, cout // count
    steps = lanes // some
    kinds = ks + 2 * (steps - 1)
    blank = jnp.zeros((cin, cout), bf16)
    wanted = core_ref[0] if part == 0 else 1 - core_ref[0]
    o, lane = iota((cout, lanes), 0), iota((cout, lanes), 1)
    device, channel = split_index(o, channels)
    chip, core_of = split_index(device, cores)
    tiles = None
    for step in range(steps):
        picked = [taps_ref[i - 2 * step, j] if 0 <= i - 2 * step < ks else blank
                  for j in range(ks) for i in range(kinds)]
        place = (core_of == wanted) & (lane == some * step + chip * channels + channel)
        term = dot(jnp.concatenate(picked, axis=0), place.astype(f32).astype(bf16))
        tiles = term if tiles is None else tiles + term
    tiles = tiles.astype(bf16)
    empty = jnp.zeros((cin, lanes), bf16)
    for j in range(ks):
        for s in range(tin):
            for q in range(some * tout // lanes):
                i = s - 2 * steps * q + 2
                at = (j * kinds + i) * cin
                tile = tiles[at : at + cin] if 0 <= i < kinds else empty
                w_ref[j, cin * s : cin * (s + 1), lanes * q : lanes * (q + 1)] = tile
    g = g_ref[...]
    wide = half + lanes
    same = g[:, :half]
    later = dot(g, one_hot_columns((wide, half), lambda n: n + 1)).astype(bf16)
    sooner = dot(g, one_hot_columns((wide, half), lambda n: jnp.where(n == 0, wide - 1, n - 1))).astype(bf16)
    even = dot(w_ref[0], later) + dot(w_ref[2], same) + dot(w_ref[4], sooner)
    odd = dot(w_ref[1], later) + dot(w_ref[3], same)
    if not started:
        out_ref[:, :half], out_ref[:, half:] = even, odd
        return
    even, odd = even + started[0][:, :half], odd + started[0][:, half:]
    both = jnp.concatenate([even.astype(bf16), odd.astype(bf16)], axis=1)
    to_channel = one_hot((k_in, k_in), lambda r: swapped(r, cin, tin))
    both = dot(to_channel, both).astype(bf16)
    merge = one_hot((2 * lanes, 2 * lanes), lambda r: swapped(r, 2, lanes))
    for b in range(half // lanes):
        piece = jnp.concatenate(
            [both[:, lanes * b : lanes * (b + 1)], both[:, half + lanes * b : half + lanes * (b + 1)]], axis=1
        )
        out_ref[:, 2 * lanes * b : 2 * lanes * (b + 1)] = dot(piece, merge).astype(bf16)


def unpack_kernel(dims, scale, tap_ref, out_ref):
    cin, tin, cout, tout, ks, count, rows = dims
    some, channels = cout // cores, cout // count
    size, folds = ks * cin, lanes // some
    fold = size // folds
    packed = size + fold
    both = jnp.concatenate([tap_ref[:packed], tap_ref[packed:]], axis=1)

    wide = cores * lanes
    source, target = iota((wide, folds * cout), 0), iota((wide, folds * cout), 1)
    slot, o = split_index(target, cout)
    device, channel = split_index(o, channels)
    chip, core_of = split_index(device, cores)
    place = (source == core_of * lanes + slot * some + chip * channels + channel).astype(f32).astype(bf16)
    total, rest = None, both
    for _ in range(3):
        part = rest.astype(bf16)
        rest = rest - part.astype(f32)
        term = dot(part, place)
        total = term if total is None else total + term
    total = total * scale
    for slot, j in enumerate((0, 2, 4, 1)):
        for i in range(ks):
            out_ref[i, j] = total[cin * i : cin * (i + 1), cout * slot : cout * (slot + 1)]
    for at in range(0, size, 8):
        slot, low = at // fold, size + at % fold
        out_ref[at // cin, 3, at % cin : at % cin + 8] = total[low : low + 8, cout * slot : cout * (slot + 1)]


def summed_over_chips(rows, axis, steps):
    count = lax.axis_size(axis)
    rounded = rows.astype(bf16)
    theirs = [lax.ppermute(rounded, axis, partners(count, step)).astype(f32) for step in steps]
    if len(steps) == 1:
        return rounded.astype(f32) + theirs[0]
    return (rounded.astype(f32) + theirs[0]) + (theirs[1] + theirs[2])


def partners(count, step):
    return [(i, i ^ step) for i in range(count)]


def mirrored(spectrum):
    return jnp.roll(jnp.flip(spectrum, -1), 1, -1)


def tables(count, width):
    inner = np.outer(np.arange(width), np.arange(width)) % width * (2.0 * np.pi / width)
    table = np.concatenate([np.cos(inner), np.sin(inner)], axis=1).astype(np.float32)
    high = table.astype(bf16)
    rest = (table - high.astype(np.float32)).astype(bf16)
    outer = np.outer(np.arange(count), np.arange(width)) * (2.0 * np.pi / (count * width))
    twist = np.stack([np.cos(outer), np.sin(outer)]).astype(np.float32)
    return twist, np.concatenate([high, rest])


def per_device(signal, conv_taps, response, cotangent):
    cin, tin, fibre_in = signal.shape
    cout, tout, width = cotangent.shape
    ks = conv_taps.shape[0]
    count = lax.axis_size("fibre")
    channels = cout // count
    rows = channels * tout
    waves = count * width
    tiles = width // lanes
    dims = (cin, tin, cout, tout, ks, count, rows)
    k_in, k_out = cin * tin, cout * tout
    taps = jnp.swapaxes(conv_taps, 2, 3)
    shape = jax.ShapeDtypeStruct
    conv_part, z = call(
        functools.partial(conv_kernel, dims),
        [
            shape((count, 2 * rows * tiles + edge_rows, lanes), bf16),
            shape((k_in, fibre_in), bf16),
        ],
        [
            pltpu.VMEM((ks, k_out, k_in), bf16),
            pltpu.VMEM((k_in, fibre_in), bf16),
            pltpu.VMEM(taps.shape, bf16),
            pltpu.VMEM((count, 2 * rows * tiles + edge_rows, lanes), bf16),
            pltpu.VMEM((k_in, fibre_in), bf16),
            pltpu.SemaphoreType.DMA((7 + tiles,)),
        ],
        2e9,
        (signal.reshape(k_in, fibre_in), cotangent.reshape(count, rows, width), taps),
        left=(0, 1, 2),
        left_out=(0, 1),
        room=60,
    )
    other_z = lax.ppermute(z, "fibre", partners(count, 1))
    cols = lax.all_to_all(conv_part, "fibre", split_axis=0, concat_axis=0, tiled=True)
    back = mirrored(response)
    real = jnp.stack([response[0] + back[0], response[1] - back[1]]) * (0.5 / waves)
    real = real.reshape(2, channels, width, count).transpose(0, 3, 1, 2)
    real = real.reshape(2, count * channels, width)
    twist, waves_table = tables(count, width)
    big = count * rows // 2
    grad_part, cross = call(
        functools.partial(filter_kernel, (count, channels, tout, width)),
        [
            shape((count // cores, cores * rows * tiles + edge_rows, lanes), bf16),
            shape((count * channels, 2 * width), f32),
        ],
        [
            pltpu.VMEM((count, rows, width), f32),
            pltpu.VMEM((big, 2 * width), f32),
            pltpu.VMEM((big, 2 * width), f32),
            pltpu.VMEM((big, 2 * width), f32),
            pltpu.VMEM((2 * tiles, big, lanes), f32),
            pltpu.VMEM((2 * tiles, big, lanes), f32),
            pltpu.VMEM((2 * width, 2 * width), bf16),
            pltpu.VMEM((2 * width, 2 * width), bf16),
        ],
        6e9,
        (cols, real, jnp.asarray(twist), jnp.asarray(waves_table)),
    )
    (cross,) = call(hermitian_kernel, [shape((2, channels, count, width), f32)], [], 1e6, (cross,))
    filter_grad = cross.transpose(0, 1, 3, 2).reshape(2, channels, waves)
    chips = [[core + cores * chip for chip in range(count // cores)] for core in range(cores)]
    grad_cols = lax.all_to_all(
        grad_part, "fibre", split_axis=0, concat_axis=0, tiled=True, axis_index_groups=chips
    )
    core = (lax.axis_index("fibre") % cores).astype(jnp.int32).reshape(1)
    (samples,) = call(
        gather_kernel,
        [shape((k_in + 4 * cin, cores * fibre_in), bf16)],
        [],
        1e6,
        (core, z, other_z),
        small=(0,),
    )
    grad_cols, filter_grad, samples = lax.optimization_barrier((grad_cols, filter_grad, samples))
    some = k_out // cores
    taps_part, keep, send = call(
        functools.partial(tap_kernel, dims),
        [
            shape((ks * cin + ks * cin * (cout // cores) // lanes, lanes), f32),
            shape((some, width + lanes), bf16),
            shape((some, width + lanes), bf16),
        ],
        [
            pltpu.VMEM((some, cores * width + 2 * lanes), f32),
            pltpu.VMEM((some, cores * width + 2 * lanes), bf16),
            pltpu.VMEM((3, some, cores * width), bf16),
        ],
        1e9,
        (core, grad_cols, samples),
        small=(0,),
    )
    got = lax.ppermute(send, "fibre", partners(count, 1))
    chips = count // cores
    total = summed_over_chips(taps_part, "fibre", (cores,))
    step = 2
    (started,) = call(
        functools.partial(input_kernel, dims, 0),
        [shape((k_in, fibre_in), f32)],
        [pltpu.VMEM((ks, k_in, some), bf16)],
        1e9,
        (core, keep, taps),
        small=(0,),
    )
    total, started, got = lax.optimization_barrier((total, started, got))
    (input_grad,) = call(
        functools.partial(input_kernel, dims, 1),
        [shape((k_in, fibre_in), bf16)],
        [pltpu.VMEM((ks, k_in, some), bf16)],
        1e9,
        (core, got, started, taps),
        small=(0,),
    )
    if chips % 8 == 0:
        total = summed_over_chips(total, "fibre", (2 * cores, 4 * cores, 6 * cores))
        step = 8
    while step < chips:
        total = summed_over_chips(total, "fibre", (cores * step,))
        step *= 2
    total, input_grad = lax.optimization_barrier((total, input_grad))
    other = lax.ppermute(total, "fibre", partners(count, 1))
    total = jnp.where(core[0] == 0, jnp.concatenate([total, other]), jnp.concatenate([other, total]))
    (tap_grad,) = call(
        functools.partial(unpack_kernel, dims, 1.0 / math.sqrt(tout * waves)),
        [shape((ks, ks, cin, cout), f32)],
        [],
        1e6,
        (total,),
    )
    return (input_grad.reshape(signal.shape), jnp.swapaxes(tap_grad, 2, 3), filter_grad)


def solution(mesh):
    in_specs = (P("parts", None, "fibre"), P(), P(None, "fibre", None), P("parts", None, "fibre"))
    out_specs = (P("parts", None, "fibre"), P("parts", None, None, None), P("parts", "fibre", None))
    return jax.shard_map(
        per_device, mesh=mesh, in_specs=in_specs, out_specs=out_specs, check_vma=False
    )
```

```python
import functools
import math

import jax
import jax.numpy as jnp
import numpy as np
from jax import lax
from jax.experimental import pallas as pl
from jax.experimental.pallas import tpu as pltpu
from jax.sharding import PartitionSpec as P

bf16 = jnp.bfloat16
f32 = jnp.float32
inv_root_two = 1.0 / math.sqrt(2.0)
inv_root_tau = 1.0 / math.sqrt(2.0 * math.pi)
lanes = 128
edge_rows = 8
cores = 2


def dot(a, b):
    return jnp.dot(a, b, preferred_element_type=f32)


def dot_nt(a, b):
    return lax.dot_general(a, b, (((1,), (1,)), ((), ())), preferred_element_type=f32)


def dot_tn(a, b):
    return lax.dot_general(a, b, (((0,), (0,)), ((), ())), preferred_element_type=f32)


def iota(shape, dim):
    return lax.broadcasted_iota(jnp.int32, shape, dim)


def split_index(x, size):
    if size & (size - 1):
        return x // size, x % size
    return lax.shift_right_logical(x, jnp.full_like(x, size.bit_length() - 1)), x & (size - 1)


def swapped(x, outer, inner):
    a, b = split_index(x, inner)
    return b * outer + a


def one_hot(shape, column_of_row):
    return (iota(shape, 1) == column_of_row(iota((shape[0], 1), 0))).astype(f32).astype(bf16)


def one_hot_columns(shape, row_of_column):
    return (iota(shape, 0) == row_of_column(iota((1, shape[1]), 1))).astype(f32).astype(bf16)


def call(kernel, outs, scratch, flops, args, left=(), left_out=(), small=(), room=24):
    moved = sum(a.size * a.dtype.itemsize for a in list(args) + list(outs))
    return pl.pallas_call(
        kernel,
        out_shape=outs,
        in_specs=[
            pl.BlockSpec(
                memory_space=pltpu.HBM if a in left else pltpu.SMEM if a in small else pltpu.VMEM
            )
            for a in range(len(args))
        ],
        out_specs=[
            pl.BlockSpec(memory_space=pltpu.HBM if a in left_out else pltpu.VMEM) for a in range(len(outs))
        ],
        scratch_shapes=scratch,
        compiler_params=pltpu.CompilerParams(vmem_limit_bytes=room << 20),
        cost_estimate=pl.CostEstimate(flops=int(flops), bytes_accessed=moved, transcendentals=0),
    )(*args)


def conv_kernel(
    dims, sig_hbm, cot_hbm, taps_hbm, out_hbm, z_hbm,
    w_ref, sig_ref, taps_ref, out_ref, z_ref, sem,
):
    cin, tin, cout, tout, ks, count, rows = dims
    k_in, k_out = cin * tin, cout * tout
    half = sig_ref.shape[1] // 2
    tiles_wide = half // lanes
    conv_rows = rows * tiles_wide
    taps_copy = pltpu.make_async_copy(taps_hbm, taps_ref, sem.at[0])
    sig_copy = pltpu.make_async_copy(sig_hbm, sig_ref, sem.at[1])
    cot_copies = [
        pltpu.make_async_copy(
            cot_hbm.at[:, :, pl.ds(lanes * b, lanes)],
            out_ref.at[:, pl.ds(conv_rows + rows * b, rows)],
            sem.at[6 + b],
        )
        for b in range(tiles_wide)
    ]
    at_conv, at_edge = pl.ds(0, conv_rows), pl.ds(2 * conv_rows, edge_rows)
    at_cot = pl.ds(conv_rows, conv_rows)
    cot_out = pltpu.make_async_copy(out_ref.at[:, at_cot], out_hbm.at[:, at_cot], sem.at[5])
    z_out = pltpu.make_async_copy(z_ref, z_hbm, sem.at[2])
    half_count = count // 2
    conv_outs = [
        pltpu.make_async_copy(
            out_ref.at[pl.ds(low, half_count), at_conv], out_hbm.at[pl.ds(low, half_count), at_conv], sem.at[at]
        )
        for at, low in ((3, 0), (6 + tiles_wide, half_count))
    ]
    edge_out = pltpu.make_async_copy(out_ref.at[:, at_edge], out_hbm.at[:, at_edge], sem.at[4])
    taps_copy.start()
    sig_copy.start()
    for copy in cot_copies:
        copy.start()
    taps_copy.wait()
    blank = jnp.zeros((2 * cin, cout), bf16)
    stacked = []
    for j in range(ks):
        column = jnp.concatenate([blank] + [taps_ref[i, j] for i in range(ks)] + [blank, blank], axis=0)
        for v in range(4):
            stacked.append(column[2 * cin * v : 2 * cin * v + lanes])
    eye = one_hot((cout, cout), lambda r: r)
    tiles = dot_nt(eye, jnp.concatenate(stacked, axis=0)).astype(bf16)
    empty = jnp.zeros((cout, lanes), bf16)
    for j in range(ks):
        for t in range(tout):
            for q in range(k_in // lanes):
                v = 2 * q - t + 2
                at = (j * 4 + v) * lanes
                tile = tiles[:, at : at + lanes] if 0 <= v < 4 else empty
                w_ref[j, cout * t : cout * (t + 1), lanes * q : lanes * (q + 1)] = tile
    sig_copy.wait()
    split = one_hot_columns((2 * lanes, 2 * lanes), lambda q: swapped(q, 2, lanes))
    parts = [dot(sig_ref[:, b : b + 2 * lanes], split) for b in range(0, 2 * half, 2 * lanes)]
    apart = jnp.concatenate([p[:, :lanes] for p in parts] + [p[:, lanes:] for p in parts], axis=1)
    to_time = one_hot((k_in, k_in), lambda r: swapped(r, tin, cin))
    z = dot(to_time, apart.astype(bf16)).astype(bf16)
    z_ref[...] = z
    z_out.start()
    for copy in cot_copies:
        copy.wait()
    cot_out.start()
    even, odd = z[:, :half], z[:, half:]
    left = dot(w_ref[0], even) + dot(w_ref[1], odd)
    right = dot(w_ref[4], even)
    lane = iota((k_out, half), 1)
    own = (
        dot(w_ref[2], even)
        + dot(w_ref[3], odd)
        + jnp.where(lane == 0, 0.0, pltpu.roll(left, 1, 1))
        + jnp.where(lane == half - 1, 0.0, pltpu.roll(right, half - 1, 1))
    )
    high = own.astype(bf16)
    first = iota((k_out, lanes), 1) == 0

    def parts_of(v):
        top = v.astype(bf16)
        return top, (v - top.astype(f32)).astype(bf16)

    _, own_rest = parts_of(jnp.where(first, own[:, :lanes], own[:, half - lanes :]))
    next_high, next_rest = parts_of(jnp.where(first, right[:, :lanes], left[:, half - lanes :]))
    row, col = iota((edge_rows, 3 * lanes), 0), iota((edge_rows, 3 * lanes), 1)
    pick = jnp.zeros((edge_rows, 3 * lanes), f32)
    for at, column in enumerate((0, lanes - 1, 2 * lanes - 1, 3 * lanes - 1, lanes, 2 * lanes)):
        pick = jnp.where((row == at) & (col == column), 1.0, pick)
    edges = dot_nt(pick.astype(bf16), jnp.concatenate([own_rest, next_high, next_rest], axis=1))
    from_time = one_hot((k_out, k_out), lambda r: swapped(r, cout, tout))
    edges = dot_nt(edges.astype(bf16), from_time)
    for d in range(count):
        out_ref[d, 2 * conv_rows :] = jnp.zeros((edge_rows, lanes), bf16)
        out_ref[d, 2 * conv_rows :, :rows] = edges[:, rows * d : rows * (d + 1)].astype(bf16)
    edge_out.start()
    for part, conv_out in enumerate(conv_outs):
        low = half_count * part
        main = dot(from_time[rows * low : rows * (low + half_count)], high).astype(bf16)
        for d in range(half_count):
            for b in range(tiles_wide):
                at = slice(lanes * b, lanes * (b + 1))
                out_ref[low + d, rows * b : rows * (b + 1)] = main[rows * d : rows * (d + 1), at]
        conv_out.start()
    cot_out.wait()
    z_out.wait()
    for conv_out in conv_outs:
        conv_out.wait()
    edge_out.wait()


def transform(real, imag, sign):
    size = len(real)
    if size == 1:
        return (list(real), [None] if imag is None else list(imag))
    even_re, even_im = transform(real[0::2], None if imag is None else imag[0::2], sign)
    odd_re, odd_im = transform(real[1::2], None if imag is None else imag[1::2], sign)
    out_re, out_im = [None] * size, [None] * size

    def plus(a, b):
        return b if a is None else (a if b is None else a + b)

    def minus(a, b):
        return a if b is None else (-b if a is None else a - b)

    for k in range(size // 2):
        re, im = odd_re[k], odd_im[k]
        if k == 0:
            tr, ti = re, im
        elif 4 * k == size:
            tr = None if im is None else (im if sign < 0 else -im)
            ti = -re if sign < 0 else re
        else:
            c, s = math.cos(2 * math.pi * k / size), sign * math.sin(2 * math.pi * k / size)
            if im is None:
                tr, ti = c * re, s * re
            elif 8 * k == size:
                tr, ti = (c * (re - im), c * (re + im)) if sign > 0 else (c * (re + im), c * (im - re))
            elif 8 * k == 3 * size:
                tr, ti = (c * (re + im), c * (im - re)) if sign > 0 else (c * (re - im), c * (re + im))
            else:
                tr, ti = c * re - s * im, s * re + c * im
        out_re[k], out_im[k] = plus(even_re[k], tr), plus(even_im[k], ti)
        out_re[k + size // 2], out_im[k + size // 2] = minus(even_re[k], tr), minus(even_im[k], ti)
    return out_re, out_im


def gelu_slope(v):
    return 0.5 * (1.0 + lax.erf(v * inv_root_two)) + v * jnp.exp(-0.5 * v * v) * inv_root_tau


def filter_kernel(
    dims, cols_ref, own_ref, twist_ref, wave_ref,
    out_ref, prod_ref, x_ref, y_ref, spec_ref, grad_ref, resp_ref, high_ref, rest_ref,
):
    count, channels, tout, width = dims
    rows, pair = channels * tout, tout // 2
    wide, groups = width // lanes, count * channels
    for at, table_ref in ((0, high_ref), (width, rest_ref)):
        cosine, sine = wave_ref[at : at + width, :width], wave_ref[at : at + width, width:]
        table_ref[:width, :width], table_ref[:width, width:] = cosine, -sine
        table_ref[width:, :width], table_ref[width:, width:] = sine, cosine
    for b in range(2 * wide):
        own = own_ref[b // wide, :, lanes * (b % wide) : lanes * (b % wide + 1)]
        for step in range(pair):
            resp_ref[b, pl.ds(step, groups, stride=pair), :] = own
    packed = rows // 2
    group = min(2, channels)
    chunk = group * pair
    edge_row, edge_col = iota((edge_rows, width), 0), iota((edge_rows, width), 1)
    to_low = (edge_col == 0) & ((edge_row == 0) | (edge_row == 2) | (edge_row == 3))
    to_high = (edge_col == width - 1) & ((edge_row == 1) | (edge_row == 4) | (edge_row == 5))
    spread = (to_low | to_high).astype(f32).astype(bf16)
    low = 2 * rows * (width // lanes)
    edges = [cols_ref[d, low:, :rows].astype(f32) for d in range(count)]
    none = jnp.zeros((edge_rows, rows), f32)
    kind = iota((edge_rows, rows), 0)
    for d in range(count):
        before = edges[d - 1] if d > 0 else none
        after = edges[d + 1] if d < count - 1 else none
        joined = jnp.where(kind < 2, edges[d], jnp.where(kind < 4, before, after))
        blocks = [cols_ref[d, rows * b : rows * (b + 1)] for b in range(width // lanes)]
        whole = jnp.concatenate(blocks, axis=1).astype(f32) + dot_tn(joined.astype(bf16), spread)
        x_ref[d] = whole.astype(bf16).astype(f32)

    def forward_planes(real, imag, r, h):
        re, im = transform(real, imag, -1)
        for k in range(count):
            c = twist_ref[0, k : k + 1, h : h + lanes]
            s = twist_ref[1, k : k + 1, h : h + lanes]
            at = slice(k * packed + r, k * packed + r + chunk)
            y_ref[at, h : h + lanes] = re[k] * c + im[k] * s if k else re[k]
            y_ref[at, width + h : width + h + lanes] = im[k] * c - re[k] * s if k else im[k]

    def backward_planes(r, h):
        re, im = [], []
        for k in range(count):
            c = twist_ref[0, k : k + 1, h : h + lanes]
            s = twist_ref[1, k : k + 1, h : h + lanes]
            at = slice(k * packed + r, k * packed + r + chunk)
            a, b = y_ref[at, h : h + lanes], y_ref[at, width + h : width + h + lanes]
            re.append(a * c - b * s if k else a)
            im.append(b * c + a * s if k else b)
        return transform(re, im, 1)

    def inner(product):
        v = y_ref[...]
        high = v.astype(bf16)
        rest = (v - high.astype(f32)).astype(bf16)
        both = product(jnp.concatenate([high, rest], axis=0), high_ref[...])
        size = v.shape[0]
        return both[:size] + both[size:] + product(high, rest_ref[...])

    def paired(tiles):
        return (
            jnp.concatenate([tile[:pair] for tile in tiles], axis=0),
            jnp.concatenate([tile[pair:] for tile in tiles], axis=0),
        )

    chunks = [(r, h) for r in range(0, packed, chunk) for h in range(0, width, lanes)]
    for r, h in chunks:
        planes = [
            paired([x_ref[d, 2 * r + tout * g : 2 * r + tout * (g + 1), h : h + lanes] for g in range(group)])
            for d in range(count)
        ]
        forward_planes([re for re, im in planes], [im for re, im in planes], r, h)
    spec_ref[...] = inner(dot)
    sr, si = spec_ref[:, :width], spec_ref[:, width:]
    rr, ri = (jnp.concatenate([resp_ref[p * wide + b] for b in range(wide)], axis=1) for p in range(2))
    y_ref[:, :width] = rr * sr - ri * si
    y_ref[:, width:] = rr * si + ri * sr
    y_ref[...] = inner(dot_nt)
    for r, h in chunks:
        real, imag = backward_planes(r, h)
        at = rows * (width + h) // lanes + 2 * r
        for d in range(count):
            cot = cols_ref[d, at : at + tout * group].astype(f32)
            re, im = paired([cot[tout * g : tout * (g + 1)] for g in range(group)])
            real[d], imag[d] = re * gelu_slope(real[d]), im * gelu_slope(imag[d])
        forward_planes(real, imag, r, h)
    grad_ref[...] = inner(dot)
    sr, si = spec_ref[:, :width], spec_ref[:, width:]
    gr, gi = grad_ref[:, :width], grad_ref[:, width:]
    rr, ri = (jnp.concatenate([resp_ref[p * wide + b] for b in range(wide)], axis=1) for p in range(2))
    y_ref[:, :width] = rr * gr + ri * gi
    y_ref[:, width:] = rr * gi - ri * gr
    scale = 1.0 / (count * width)
    crossed = ((sr * gr + si * gi) * scale, (sr * gi - si * gr) * scale)
    for b in range(2 * wide):
        prod_ref[b] = crossed[b // wide][:, lanes * (b % wide) : lanes * (b % wide + 1)]
    y_ref[...] = inner(dot_nt)
    for r, h in chunks:
        real, imag = backward_planes(r, h)
        for d in range(count):
            for g in range(group):
                at = slice(pair * g, pair * (g + 1))
                tile = jnp.concatenate([real[d][at], imag[d][at]], axis=0)
                x_ref[d, 2 * r + tout * g : 2 * r + tout * (g + 1), h : h + lanes] = tile
    last = ((iota((edge_rows, lanes), 0) == 0) & (iota((edge_rows, lanes), 1) == lanes - 1)).astype(f32).astype(bf16)
    first = ((iota((edge_rows, lanes), 0) == 1) & (iota((edge_rows, lanes), 1) == 0)).astype(f32).astype(bf16)
    for chip in range(count // cores):
        at = 0
        for d in range(cores * chip, cores * (chip + 1)):
            for b in range(0, width, lanes):
                out_ref[chip, at : at + rows] = x_ref[d, :, b : b + lanes].astype(bf16)
                at += rows
        out_ref[chip, at:] = jnp.zeros((edge_rows, lanes), bf16)
        edge = none
        if chip > 0:
            edge = edge + dot_nt(last, x_ref[cores * chip - 1, :, width - lanes :].astype(bf16))
        if chip < count // cores - 1:
            edge = edge + dot_nt(first, x_ref[cores * (chip + 1), :, :lanes].astype(bf16))
        out_ref[chip, at:, :rows] = edge.astype(bf16)


def hermitian_kernel(prod_ref, out_ref, cross_ref):
    _, channels, count, width = out_ref.shape
    wide, groups = width // lanes, count * channels
    pair = prod_ref.shape[1] // groups
    for b in range(2 * wide):
        summed = prod_ref[b, pl.ds(0, groups, stride=pair), :]
        for step in range(1, pair):
            summed = summed + prod_ref[b, pl.ds(step, groups, stride=pair), :]
        cross_ref[:, lanes * b : lanes * (b + 1)] = summed
    row, col = iota((width, width), 0), iota((width, width), 1)
    flip = (row + col == width - 1).astype(f32).astype(bf16)
    flip_first = ((row + col == width) | ((row == 0) & (col == 0))).astype(f32).astype(bf16)

    def moved(v, by):
        total = None
        for _ in range(3):
            part = v.astype(bf16)
            v = v - part.astype(f32)
            term = dot(part, by)
            total = term if total is None else total + term
        return total

    for k in range(count):
        from_k = channels * ((count - k) % count)
        own = cross_ref[channels * k : channels * (k + 1)]
        other = cross_ref[from_k : from_k + channels]
        by = flip if k else flip_first
        out_ref[0, :, k] = 0.5 * (own[:, :width] + moved(other[:, :width], by))
        out_ref[1, :, k] = 0.5 * (own[:, width:] - moved(other[:, width:], by))


def gather_kernel(core_ref, own_ref, other_ref, out_ref):
    k_in, wide = own_ref.shape
    width = wide // 2
    pad = (out_ref.shape[0] - k_in) // 2
    core = core_ref[0]
    out_ref[:pad] = jnp.zeros((pad, cores * wide), bf16)
    out_ref[pad + k_in :] = jnp.zeros((pad, cores * wide), bf16)
    for phase in range(2):
        at = slice(width * phase, width * (phase + 1))
        own_at = pl.multiple_of(wide * phase + width * core, lanes)
        other_at = pl.multiple_of(wide * phase + width * (1 - core), lanes)
        out_ref[pad : pad + k_in, pl.ds(own_at, width)] = own_ref[:, at]
        out_ref[pad : pad + k_in, pl.ds(other_at, width)] = other_ref[:, at]


def tap_kernel(
    dims, core_ref, grad_ref, z_ref, tap_ref, keep_ref, send_ref, g_ref, exact_ref, shifted_ref
):
    cin, tin, cout, tout, ks, count, rows = dims
    some = cout // cores
    width = keep_ref.shape[1] - lanes
    wide = cores * width
    core = core_ref[0]
    row, col = iota((edge_rows, 2 * lanes), 0), iota((edge_rows, 2 * lanes), 1)
    spread = (((row == 0) & (col == lanes - 1)) | ((row == 1) & (col == lanes))).astype(f32).astype(bf16)
    for chip in range(count // cores):
        at = slice(rows * chip, rows * (chip + 1))
        low = 0
        for b in range(0, wide, lanes):
            g_ref[at, lanes + b : 2 * lanes + b] = grad_ref[chip, low : low + rows].astype(f32)
            low += rows
        edge = dot_tn(grad_ref[chip, low:, :rows], spread)
        g_ref[at, :lanes] = edge[:, :lanes]
        g_ref[at, lanes + wide :] = edge[:, lanes:]
    to_time = one_hot((some * tout, some * tout), lambda r: swapped(r, tout, some))
    g = dot(to_time, g_ref[...].astype(bf16))
    inside = slice(lanes, lanes + wide)
    shifted_ref[0] = pltpu.roll(g, wide + 2 * lanes - 1, 1)[:, inside].astype(bf16)
    shifted_ref[1] = g[:, inside].astype(bf16)
    shifted_ref[2] = pltpu.roll(g, 1, 1)[:, inside].astype(bf16)
    exact_ref[...] = g.astype(bf16)
    lane = iota((some * tout, lanes), 1)
    for block, block_ref in ((core, keep_ref), (1 - core, send_ref)):
        at = width * block
        before, inner, after = (
            exact_ref[:, pl.ds(pl.multiple_of(at + low, lanes), size)]
            for low, size in ((0, lanes), (lanes, width), (lanes + width, lanes))
        )
        edge = jnp.where(lane == 0, after.astype(f32), before.astype(f32))
        block_ref[:, :width] = inner
        block_ref[:, width:] = jnp.where((lane == 0) | (lane == lanes - 1), edge, 0.0).astype(bf16)
    blank = jnp.zeros((lanes - 3 * some, wide), bf16)
    size, reach = ks * cin, (ks + 2) * cin
    even, odd = None, None
    for t in range(0, tout, 2):
        band = slice(2 * cin * t, 2 * cin * t + reach)
        taken = []
        for at in (slice(some * t, some * (t + 1)), slice(some * (t + 1), some * (t + 2))):
            taken += [shifted_ref[shift, at] for shift in range(3)] + [blank]
        samples = jnp.concatenate([z_ref[band, :wide], z_ref[band, wide:]], axis=0)
        both = dot_nt(samples, jnp.concatenate(taken, axis=0))
        first = both[:size, :lanes] + both[reach - size : reach, lanes:]
        second = both[reach : reach + size, :lanes] + both[2 * reach - size :, lanes:]
        even = first if even is None else even + first
        odd = second if odd is None else odd + second
    tap_ref[:size] = jnp.where(iota((size, lanes), 1) < 3 * some, even, pltpu.roll(odd, 3 * some, 1))
    fold = size * some // lanes
    folded = jnp.zeros((fold, lanes), f32)
    for part in range(lanes // some):
        moved = pltpu.roll(odd[fold * part : fold * (part + 1)], (some * (part - 1)) % lanes, 1)
        here = split_index(iota((fold, lanes), 1), some)[0] == part
        folded = jnp.where(here, moved, folded)
    tap_ref[size:] = folded


def input_kernel(dims, part, core_ref, g_ref, *refs):
    *started, taps_ref, out_ref, w_ref = refs
    cin, tin, cout, tout, ks, count, rows = dims
    k_in = cin * tin
    half = g_ref.shape[1] - lanes
    some, channels = cout // cores, cout // count
    steps = lanes // some
    kinds = ks + 2 * (steps - 1)
    blank = jnp.zeros((cin, cout), bf16)
    wanted = core_ref[0] if part == 0 else 1 - core_ref[0]
    o, lane = iota((cout, lanes), 0), iota((cout, lanes), 1)
    device, channel = split_index(o, channels)
    chip, core_of = split_index(device, cores)
    tiles = None
    for step in range(steps):
        picked = [taps_ref[i - 2 * step, j] if 0 <= i - 2 * step < ks else blank
                  for j in range(ks) for i in range(kinds)]
        place = (core_of == wanted) & (lane == some * step + chip * channels + channel)
        term = dot(jnp.concatenate(picked, axis=0), place.astype(f32).astype(bf16))
        tiles = term if tiles is None else tiles + term
    tiles = tiles.astype(bf16)
    empty = jnp.zeros((cin, lanes), bf16)
    for j in range(ks):
        for s in range(tin):
            for q in range(some * tout // lanes):
                i = s - 2 * steps * q + 2
                at = (j * kinds + i) * cin
                tile = tiles[at : at + cin] if 0 <= i < kinds else empty
                w_ref[j, cin * s : cin * (s + 1), lanes * q : lanes * (q + 1)] = tile
    g = g_ref[...]
    wide = half + lanes
    same = g[:, :half]
    later = dot(g, one_hot_columns((wide, half), lambda n: n + 1)).astype(bf16)
    sooner = dot(g, one_hot_columns((wide, half), lambda n: jnp.where(n == 0, wide - 1, n - 1))).astype(bf16)
    even = dot(w_ref[0], later) + dot(w_ref[2], same) + dot(w_ref[4], sooner)
    odd = dot(w_ref[1], later) + dot(w_ref[3], same)
    if not started:
        out_ref[:, :half], out_ref[:, half:] = even, odd
        return
    even, odd = even + started[0][:, :half], odd + started[0][:, half:]
    both = jnp.concatenate([even.astype(bf16), odd.astype(bf16)], axis=1)
    to_channel = one_hot((k_in, k_in), lambda r: swapped(r, cin, tin))
    both = dot(to_channel, both).astype(bf16)
    merge = one_hot((2 * lanes, 2 * lanes), lambda r: swapped(r, 2, lanes))
    for b in range(half // lanes):
        piece = jnp.concatenate(
            [both[:, lanes * b : lanes * (b + 1)], both[:, half + lanes * b : half + lanes * (b + 1)]], axis=1
        )
        out_ref[:, 2 * lanes * b : 2 * lanes * (b + 1)] = dot(piece, merge).astype(bf16)


def unpack_kernel(dims, scale, tap_ref, out_ref):
    cin, tin, cout, tout, ks, count, rows = dims
    some, channels = cout // cores, cout // count
    size, folds = ks * cin, lanes // some
    fold = size // folds
    packed = size + fold
    both = jnp.concatenate([tap_ref[:packed], tap_ref[packed:]], axis=1)

    wide = cores * lanes
    source, target = iota((wide, folds * cout), 0), iota((wide, folds * cout), 1)
    slot, o = split_index(target, cout)
    device, channel = split_index(o, channels)
    chip, core_of = split_index(device, cores)
    place = (source == core_of * lanes + slot * some + chip * channels + channel).astype(f32).astype(bf16)
    total, rest = None, both
    for _ in range(3):
        part = rest.astype(bf16)
        rest = rest - part.astype(f32)
        term = dot(part, place)
        total = term if total is None else total + term
    total = total * scale
    for slot, j in enumerate((0, 2, 4, 1)):
        for i in range(ks):
            out_ref[i, j] = total[cin * i : cin * (i + 1), cout * slot : cout * (slot + 1)]
    for at in range(0, size, 8):
        slot, low = at // fold, size + at % fold
        out_ref[at // cin, 3, at % cin : at % cin + 8] = total[low : low + 8, cout * slot : cout * (slot + 1)]


def summed_over_chips(rows, axis, steps):
    count = lax.axis_size(axis)
    rounded = rows.astype(bf16)
    theirs = [lax.ppermute(rounded, axis, partners(count, step)).astype(f32) for step in steps]
    if len(steps) == 1:
        return rounded.astype(f32) + theirs[0]
    return (rounded.astype(f32) + theirs[0]) + (theirs[1] + theirs[2])


def partners(count, step):
    return [(i, i ^ step) for i in range(count)]


def mirrored(spectrum):
    return jnp.roll(jnp.flip(spectrum, -1), 1, -1)


def tables(count, width):
    inner = np.outer(np.arange(width), np.arange(width)) % width * (2.0 * np.pi / width)
    table = np.concatenate([np.cos(inner), np.sin(inner)], axis=1).astype(np.float32)
    high = table.astype(bf16)
    rest = (table - high.astype(np.float32)).astype(bf16)
    outer = np.outer(np.arange(count), np.arange(width)) * (2.0 * np.pi / (count * width))
    twist = np.stack([np.cos(outer), np.sin(outer)]).astype(np.float32)
    return twist, np.concatenate([high, rest])


def per_device(signal, conv_taps, response, cotangent):
    cin, tin, fibre_in = signal.shape
    cout, tout, width = cotangent.shape
    ks = conv_taps.shape[0]
    count = lax.axis_size("fibre")
    channels = cout // count
    rows = channels * tout
    waves = count * width
    tiles = width // lanes
    dims = (cin, tin, cout, tout, ks, count, rows)
    k_in, k_out = cin * tin, cout * tout
    taps = jnp.swapaxes(conv_taps, 2, 3)
    shape = jax.ShapeDtypeStruct
    conv_part, z = call(
        functools.partial(conv_kernel, dims),
        [
            shape((count, 2 * rows * tiles + edge_rows, lanes), bf16),
            shape((k_in, fibre_in), bf16),
        ],
        [
            pltpu.VMEM((ks, k_out, k_in), bf16),
            pltpu.VMEM((k_in, fibre_in), bf16),
            pltpu.VMEM(taps.shape, bf16),
            pltpu.VMEM((count, 2 * rows * tiles + edge_rows, lanes), bf16),
            pltpu.VMEM((k_in, fibre_in), bf16),
            pltpu.SemaphoreType.DMA((7 + tiles,)),
        ],
        2e9,
        (signal.reshape(k_in, fibre_in), cotangent.reshape(count, rows, width), taps),
        left=(0, 1, 2),
        left_out=(0, 1),
        room=60,
    )
    other_z = lax.ppermute(z, "fibre", partners(count, 1))
    cols = lax.all_to_all(conv_part, "fibre", split_axis=0, concat_axis=0, tiled=True)
    back = mirrored(response)
    real = jnp.stack([response[0] + back[0], response[1] - back[1]]) * (0.5 / waves)
    real = real.reshape(2, channels, width, count).transpose(0, 3, 1, 2)
    real = real.reshape(2, count * channels, width)
    twist, waves_table = tables(count, width)
    big = count * rows // 2
    grad_part, cross = call(
        functools.partial(filter_kernel, (count, channels, tout, width)),
        [
            shape((count // cores, cores * rows * tiles + edge_rows, lanes), bf16),
            shape((2 * tiles, count * rows // 2, lanes), f32),
        ],
        [
            pltpu.VMEM((count, rows, width), f32),
            pltpu.VMEM((big, 2 * width), f32),
            pltpu.VMEM((big, 2 * width), f32),
            pltpu.VMEM((big, 2 * width), f32),
            pltpu.VMEM((2 * tiles, big, lanes), f32),
            pltpu.VMEM((2 * width, 2 * width), bf16),
            pltpu.VMEM((2 * width, 2 * width), bf16),
        ],
        6e9,
        (cols, real, jnp.asarray(twist), jnp.asarray(waves_table)),
    )
    (cross,) = call(
        hermitian_kernel,
        [shape((2, channels, count, width), f32)],
        [pltpu.VMEM((count * channels, 2 * width), f32)],
        1e6,
        (cross,),
    )
    filter_grad = cross.transpose(0, 1, 3, 2).reshape(2, channels, waves)
    chips = [[core + cores * chip for chip in range(count // cores)] for core in range(cores)]
    grad_cols = lax.all_to_all(
        grad_part, "fibre", split_axis=0, concat_axis=0, tiled=True, axis_index_groups=chips
    )
    core = (lax.axis_index("fibre") % cores).astype(jnp.int32).reshape(1)
    (samples,) = call(
        gather_kernel,
        [shape((k_in + 4 * cin, cores * fibre_in), bf16)],
        [],
        1e6,
        (core, z, other_z),
        small=(0,),
    )
    grad_cols, filter_grad, samples = lax.optimization_barrier((grad_cols, filter_grad, samples))
    some = k_out // cores
    taps_part, keep, send = call(
        functools.partial(tap_kernel, dims),
        [
            shape((ks * cin + ks * cin * (cout // cores) // lanes, lanes), f32),
            shape((some, width + lanes), bf16),
            shape((some, width + lanes), bf16),
        ],
        [
            pltpu.VMEM((some, cores * width + 2 * lanes), f32),
            pltpu.VMEM((some, cores * width + 2 * lanes), bf16),
            pltpu.VMEM((3, some, cores * width), bf16),
        ],
        1e9,
        (core, grad_cols, samples),
        small=(0,),
    )
    got = lax.ppermute(send, "fibre", partners(count, 1))
    chips = count // cores
    total = summed_over_chips(taps_part, "fibre", (cores,))
    step = 2
    (started,) = call(
        functools.partial(input_kernel, dims, 0),
        [shape((k_in, fibre_in), f32)],
        [pltpu.VMEM((ks, k_in, some), bf16)],
        1e9,
        (core, keep, taps),
        small=(0,),
    )
    total, started, got = lax.optimization_barrier((total, started, got))
    (input_grad,) = call(
        functools.partial(input_kernel, dims, 1),
        [shape((k_in, fibre_in), bf16)],
        [pltpu.VMEM((ks, k_in, some), bf16)],
        1e9,
        (core, got, started, taps),
        small=(0,),
    )
    if chips % 8 == 0:
        total = summed_over_chips(total, "fibre", (2 * cores, 4 * cores, 6 * cores))
        step = 8
    while step < chips:
        total = summed_over_chips(total, "fibre", (cores * step,))
        step *= 2
    total, input_grad = lax.optimization_barrier((total, input_grad))
    other = lax.ppermute(total, "fibre", partners(count, 1))
    total = jnp.where(core[0] == 0, jnp.concatenate([total, other]), jnp.concatenate([other, total]))
    (tap_grad,) = call(
        functools.partial(unpack_kernel, dims, 1.0 / math.sqrt(tout * waves)),
        [shape((ks, ks, cin, cout), f32)],
        [],
        1e6,
        (total,),
    )
    return (input_grad.reshape(signal.shape), jnp.swapaxes(tap_grad, 2, 3), filter_grad)


def solution(mesh):
    in_specs = (P("parts", None, "fibre"), P(), P(None, "fibre", None), P("parts", None, "fibre"))
    out_specs = (P("parts", None, "fibre"), P("parts", None, None, None), P("parts", "fibre", None))
    return jax.shard_map(
        per_device, mesh=mesh, in_specs=in_specs, out_specs=out_specs, check_vma=False
    )
```

```python
import functools
import math

import jax
import jax.numpy as jnp
import numpy as np
from jax import lax
from jax.experimental import pallas as pl
from jax.experimental.pallas import tpu as pltpu
from jax.sharding import PartitionSpec as P

bf16 = jnp.bfloat16
f32 = jnp.float32
inv_root_two = 1.0 / math.sqrt(2.0)
inv_root_tau = 1.0 / math.sqrt(2.0 * math.pi)
lanes = 128
edge_rows = 8
cores = 2


def dot(a, b):
    return jnp.dot(a, b, preferred_element_type=f32)


def dot_nt(a, b):
    return lax.dot_general(a, b, (((1,), (1,)), ((), ())), preferred_element_type=f32)


def dot_tn(a, b):
    return lax.dot_general(a, b, (((0,), (0,)), ((), ())), preferred_element_type=f32)


def iota(shape, dim):
    return lax.broadcasted_iota(jnp.int32, shape, dim)


def split_index(x, size):
    if size & (size - 1):
        return x // size, x % size
    return lax.shift_right_logical(x, jnp.full_like(x, size.bit_length() - 1)), x & (size - 1)


def swapped(x, outer, inner):
    a, b = split_index(x, inner)
    return b * outer + a


def one_hot(shape, column_of_row):
    return (iota(shape, 1) == column_of_row(iota((shape[0], 1), 0))).astype(f32).astype(bf16)


def one_hot_columns(shape, row_of_column):
    return (iota(shape, 0) == row_of_column(iota((1, shape[1]), 1))).astype(f32).astype(bf16)


def call(kernel, outs, scratch, flops, args, left=(), left_out=(), small=(), room=24):
    moved = sum(a.size * a.dtype.itemsize for a in list(args) + list(outs))
    return pl.pallas_call(
        kernel,
        out_shape=outs,
        in_specs=[
            pl.BlockSpec(
                memory_space=pltpu.HBM if a in left else pltpu.SMEM if a in small else pltpu.VMEM
            )
            for a in range(len(args))
        ],
        out_specs=[
            pl.BlockSpec(memory_space=pltpu.HBM if a in left_out else pltpu.VMEM) for a in range(len(outs))
        ],
        scratch_shapes=scratch,
        compiler_params=pltpu.CompilerParams(vmem_limit_bytes=room << 20),
        cost_estimate=pl.CostEstimate(flops=int(flops), bytes_accessed=moved, transcendentals=0),
    )(*args)


def conv_kernel(
    dims, sig_hbm, cot_hbm, taps_hbm, out_hbm, z_hbm,
    w_ref, sig_ref, taps_ref, out_ref, z_ref, sem,
):
    cin, tin, cout, tout, ks, count, rows = dims
    k_in, k_out = cin * tin, cout * tout
    half = sig_ref.shape[1] // 2
    tiles_wide = half // lanes
    conv_rows = rows * tiles_wide
    taps_copy = pltpu.make_async_copy(taps_hbm, taps_ref, sem.at[0])
    sig_copy = pltpu.make_async_copy(sig_hbm, sig_ref, sem.at[1])
    cot_copies = [
        pltpu.make_async_copy(
            cot_hbm.at[:, :, pl.ds(lanes * b, lanes)],
            out_ref.at[:, pl.ds(conv_rows + rows * b, rows)],
            sem.at[6 + b],
        )
        for b in range(tiles_wide)
    ]
    at_conv, at_edge = pl.ds(0, conv_rows), pl.ds(2 * conv_rows, edge_rows)
    at_cot = pl.ds(conv_rows, conv_rows)
    cot_out = pltpu.make_async_copy(out_ref.at[:, at_cot], out_hbm.at[:, at_cot], sem.at[5])
    z_out = pltpu.make_async_copy(z_ref, z_hbm, sem.at[2])
    half_count = count // 2
    conv_outs = [
        pltpu.make_async_copy(
            out_ref.at[pl.ds(low, half_count), at_conv], out_hbm.at[pl.ds(low, half_count), at_conv], sem.at[at]
        )
        for at, low in ((3, 0), (6 + tiles_wide, half_count))
    ]
    edge_out = pltpu.make_async_copy(out_ref.at[:, at_edge], out_hbm.at[:, at_edge], sem.at[4])
    taps_copy.start()
    sig_copy.start()
    for copy in cot_copies:
        copy.start()
    taps_copy.wait()
    blank = jnp.zeros((2 * cin, cout), bf16)
    stacked = []
    for j in range(ks):
        column = jnp.concatenate([blank] + [taps_ref[i, j] for i in range(ks)] + [blank, blank], axis=0)
        for v in range(4):
            stacked.append(column[2 * cin * v : 2 * cin * v + lanes])
    eye = one_hot((cout, cout), lambda r: r)
    tiles = dot_nt(eye, jnp.concatenate(stacked, axis=0)).astype(bf16)
    empty = jnp.zeros((cout, lanes), bf16)
    for j in range(ks):
        for t in range(tout):
            for q in range(k_in // lanes):
                v = 2 * q - t + 2
                at = (j * 4 + v) * lanes
                tile = tiles[:, at : at + lanes] if 0 <= v < 4 else empty
                w_ref[j, cout * t : cout * (t + 1), lanes * q : lanes * (q + 1)] = tile
    sig_copy.wait()
    split = one_hot_columns((2 * lanes, 2 * lanes), lambda q: swapped(q, 2, lanes))
    parts = [dot(sig_ref[:, b : b + 2 * lanes], split) for b in range(0, 2 * half, 2 * lanes)]
    apart = jnp.concatenate([p[:, :lanes] for p in parts] + [p[:, lanes:] for p in parts], axis=1)
    to_time = one_hot((k_in, k_in), lambda r: swapped(r, tin, cin))
    z = dot(to_time, apart.astype(bf16)).astype(bf16)
    z_ref[...] = z
    z_out.start()
    for copy in cot_copies:
        copy.wait()
    cot_out.start()
    even, odd = z[:, :half], z[:, half:]
    left = dot(w_ref[0], even) + dot(w_ref[1], odd)
    right = dot(w_ref[4], even)
    lane = iota((k_out, half), 1)
    own = (
        dot(w_ref[2], even)
        + dot(w_ref[3], odd)
        + jnp.where(lane == 0, 0.0, pltpu.roll(left, 1, 1))
        + jnp.where(lane == half - 1, 0.0, pltpu.roll(right, half - 1, 1))
    )
    high = own.astype(bf16)
    first = iota((k_out, lanes), 1) == 0

    def parts_of(v):
        top = v.astype(bf16)
        return top, (v - top.astype(f32)).astype(bf16)

    _, own_rest = parts_of(jnp.where(first, own[:, :lanes], own[:, half - lanes :]))
    next_high, next_rest = parts_of(jnp.where(first, right[:, :lanes], left[:, half - lanes :]))
    row, col = iota((edge_rows, 3 * lanes), 0), iota((edge_rows, 3 * lanes), 1)
    pick = jnp.zeros((edge_rows, 3 * lanes), f32)
    for at, column in enumerate((0, lanes - 1, 2 * lanes - 1, 3 * lanes - 1, lanes, 2 * lanes)):
        pick = jnp.where((row == at) & (col == column), 1.0, pick)
    edges = dot_nt(pick.astype(bf16), jnp.concatenate([own_rest, next_high, next_rest], axis=1))
    from_time = one_hot((k_out, k_out), lambda r: swapped(r, cout, tout))
    edges = dot_nt(edges.astype(bf16), from_time)
    for d in range(count):
        out_ref[d, 2 * conv_rows :] = jnp.zeros((edge_rows, lanes), bf16)
        out_ref[d, 2 * conv_rows :, :rows] = edges[:, rows * d : rows * (d + 1)].astype(bf16)
    edge_out.start()
    for part, conv_out in enumerate(conv_outs):
        low = half_count * part
        main = dot(from_time[rows * low : rows * (low + half_count)], high).astype(bf16)
        for d in range(half_count):
            for b in range(tiles_wide):
                at = slice(lanes * b, lanes * (b + 1))
                out_ref[low + d, rows * b : rows * (b + 1)] = main[rows * d : rows * (d + 1), at]
        conv_out.start()
    cot_out.wait()
    z_out.wait()
    for conv_out in conv_outs:
        conv_out.wait()
    edge_out.wait()


def transform(real, imag, sign):
    size = len(real)
    if size == 1:
        return (list(real), [None] if imag is None else list(imag))
    even_re, even_im = transform(real[0::2], None if imag is None else imag[0::2], sign)
    odd_re, odd_im = transform(real[1::2], None if imag is None else imag[1::2], sign)
    out_re, out_im = [None] * size, [None] * size

    def plus(a, b):
        return b if a is None else (a if b is None else a + b)

    def minus(a, b):
        return a if b is None else (-b if a is None else a - b)

    for k in range(size // 2):
        re, im = odd_re[k], odd_im[k]
        if k == 0:
            tr, ti = re, im
        elif 4 * k == size:
            tr = None if im is None else (im if sign < 0 else -im)
            ti = -re if sign < 0 else re
        else:
            c, s = math.cos(2 * math.pi * k / size), sign * math.sin(2 * math.pi * k / size)
            if im is None:
                tr, ti = c * re, s * re
            elif 8 * k == size:
                tr, ti = (c * (re - im), c * (re + im)) if sign > 0 else (c * (re + im), c * (im - re))
            elif 8 * k == 3 * size:
                tr, ti = (c * (re + im), c * (im - re)) if sign > 0 else (c * (re - im), c * (re + im))
            else:
                tr, ti = c * re - s * im, s * re + c * im
        out_re[k], out_im[k] = plus(even_re[k], tr), plus(even_im[k], ti)
        out_re[k + size // 2], out_im[k + size // 2] = minus(even_re[k], tr), minus(even_im[k], ti)
    return out_re, out_im


def gelu_slope(v):
    return 0.5 * (1.0 + lax.erf(v * inv_root_two)) + v * jnp.exp(-0.5 * v * v) * inv_root_tau


def filter_kernel(
    dims, cols_ref, own_ref, twist_ref, wave_ref,
    out_ref, prod_ref, x_ref, y_ref, spec_ref, grad_ref, resp_ref, high_ref, rest_ref,
):
    count, channels, tout, width = dims
    rows, pair = channels * tout, tout // 2
    wide, groups = width // lanes, count * channels
    for at, table_ref in ((0, high_ref), (width, rest_ref)):
        cosine, sine = wave_ref[at : at + width, :width], wave_ref[at : at + width, width:]
        table_ref[:width, :width], table_ref[:width, width:] = cosine, -sine
        table_ref[width:, :width], table_ref[width:, width:] = sine, cosine
    for b in range(2 * wide):
        own = own_ref[b // wide, :, lanes * (b % wide) : lanes * (b % wide + 1)]
        for step in range(pair):
            resp_ref[b, pl.ds(step, groups, stride=pair), :] = own
    packed = rows // 2
    group = min(2, channels)
    chunk = group * pair
    edge_row, edge_col = iota((edge_rows, width), 0), iota((edge_rows, width), 1)
    to_low = (edge_col == 0) & ((edge_row == 0) | (edge_row == 2) | (edge_row == 3))
    to_high = (edge_col == width - 1) & ((edge_row == 1) | (edge_row == 4) | (edge_row == 5))
    spread = (to_low | to_high).astype(f32).astype(bf16)
    low = 2 * rows * (width // lanes)
    edges = [cols_ref[d, low:, :rows].astype(f32) for d in range(count)]
    none = jnp.zeros((edge_rows, rows), f32)
    kind = iota((edge_rows, rows), 0)
    for d in range(count):
        before = edges[d - 1] if d > 0 else none
        after = edges[d + 1] if d < count - 1 else none
        joined = jnp.where(kind < 2, edges[d], jnp.where(kind < 4, before, after))
        blocks = [cols_ref[d, rows * b : rows * (b + 1)] for b in range(width // lanes)]
        whole = jnp.concatenate(blocks, axis=1).astype(f32) + dot_tn(joined.astype(bf16), spread)
        x_ref[d] = whole.astype(bf16).astype(f32)

    def forward_planes(real, imag, r, h):
        re, im = transform(real, imag, -1)
        for k in range(count):
            c = twist_ref[0, k : k + 1, h : h + lanes]
            s = twist_ref[1, k : k + 1, h : h + lanes]
            at = slice(k * packed + r, k * packed + r + chunk)
            y_ref[at, h : h + lanes] = re[k] * c + im[k] * s if k else re[k]
            y_ref[at, width + h : width + h + lanes] = im[k] * c - re[k] * s if k else im[k]

    def backward_planes(r, h):
        re, im = [], []
        for k in range(count):
            c = twist_ref[0, k : k + 1, h : h + lanes]
            s = twist_ref[1, k : k + 1, h : h + lanes]
            at = slice(k * packed + r, k * packed + r + chunk)
            a, b = y_ref[at, h : h + lanes], y_ref[at, width + h : width + h + lanes]
            re.append(a * c - b * s if k else a)
            im.append(b * c + a * s if k else b)
        return transform(re, im, 1)

    def inner(product):
        v = y_ref[...]
        high = v.astype(bf16)
        rest = (v - high.astype(f32)).astype(bf16)
        both = product(jnp.concatenate([high, rest], axis=0), high_ref[...])
        size = v.shape[0]
        return both[:size] + both[size:] + product(high, rest_ref[...])

    def paired(tiles):
        return (
            jnp.concatenate([tile[:pair] for tile in tiles], axis=0),
            jnp.concatenate([tile[pair:] for tile in tiles], axis=0),
        )

    chunks = [(r, h) for r in range(0, packed, chunk) for h in range(0, width, lanes)]
    for r, h in chunks:
        planes = [
            paired([x_ref[d, 2 * r + tout * g : 2 * r + tout * (g + 1), h : h + lanes] for g in range(group)])
            for d in range(count)
        ]
        forward_planes([re for re, im in planes], [im for re, im in planes], r, h)
    spec_ref[...] = inner(dot)
    sr, si = spec_ref[:, :width], spec_ref[:, width:]
    rr, ri = (jnp.concatenate([resp_ref[p * wide + b] for b in range(wide)], axis=1) for p in range(2))
    y_ref[:, :width] = rr * sr - ri * si
    y_ref[:, width:] = rr * si + ri * sr
    y_ref[...] = inner(dot_nt)
    for r, h in chunks:
        real, imag = backward_planes(r, h)
        at = rows * (width + h) // lanes + 2 * r
        for d in range(count):
            cot = cols_ref[d, at : at + tout * group].astype(f32)
            re, im = paired([cot[tout * g : tout * (g + 1)] for g in range(group)])
            real[d], imag[d] = re * gelu_slope(real[d]), im * gelu_slope(imag[d])
        forward_planes(real, imag, r, h)
    grad_ref[...] = inner(dot)
    sr, si = spec_ref[:, :width], spec_ref[:, width:]
    gr, gi = grad_ref[:, :width], grad_ref[:, width:]
    rr, ri = (jnp.concatenate([resp_ref[p * wide + b] for b in range(wide)], axis=1) for p in range(2))
    y_ref[:, :width] = rr * gr + ri * gi
    y_ref[:, width:] = rr * gi - ri * gr
    scale = 1.0 / (count * width)
    crossed = ((sr * gr + si * gi) * scale, (sr * gi - si * gr) * scale)
    for b in range(2 * wide):
        prod_ref[b] = crossed[b // wide][:, lanes * (b % wide) : lanes * (b % wide + 1)]
    y_ref[...] = inner(dot_nt)
    for r, h in chunks:
        real, imag = backward_planes(r, h)
        for d in range(count):
            for g in range(group):
                at = slice(pair * g, pair * (g + 1))
                tile = jnp.concatenate([real[d][at], imag[d][at]], axis=0)
                x_ref[d, 2 * r + tout * g : 2 * r + tout * (g + 1), h : h + lanes] = tile
    last = ((iota((edge_rows, lanes), 0) == 0) & (iota((edge_rows, lanes), 1) == lanes - 1)).astype(f32).astype(bf16)
    first = ((iota((edge_rows, lanes), 0) == 1) & (iota((edge_rows, lanes), 1) == 0)).astype(f32).astype(bf16)
    for chip in range(count // cores):
        at = 0
        for d in range(cores * chip, cores * (chip + 1)):
            for b in range(0, width, lanes):
                out_ref[chip, at : at + rows] = x_ref[d, :, b : b + lanes].astype(bf16)
                at += rows
        out_ref[chip, at:] = jnp.zeros((edge_rows, lanes), bf16)
        edge = none
        if chip > 0:
            edge = edge + dot_nt(last, x_ref[cores * chip - 1, :, width - lanes :].astype(bf16))
        if chip < count // cores - 1:
            edge = edge + dot_nt(first, x_ref[cores * (chip + 1), :, :lanes].astype(bf16))
        out_ref[chip, at:, :rows] = edge.astype(bf16)


def hermitian_kernel(prod_ref, out_ref, cross_ref):
    _, channels, count, width = out_ref.shape
    wide, groups = width // lanes, count * channels
    pair = prod_ref.shape[1] // groups
    for b in range(2 * wide):
        summed = prod_ref[b, pl.ds(0, groups, stride=pair), :]
        for step in range(1, pair):
            summed = summed + prod_ref[b, pl.ds(step, groups, stride=pair), :]
        cross_ref[:, lanes * b : lanes * (b + 1)] = summed
    row, col = iota((width, width), 0), iota((width, width), 1)
    flip = (row + col == width - 1).astype(f32).astype(bf16)
    flip_first = ((row + col == width) | ((row == 0) & (col == 0))).astype(f32).astype(bf16)

    def moved(v, by):
        total = None
        for _ in range(3):
            part = v.astype(bf16)
            v = v - part.astype(f32)
            term = dot(part, by)
            total = term if total is None else total + term
        return total

    for k in range(count):
        from_k = channels * ((count - k) % count)
        own = cross_ref[channels * k : channels * (k + 1)]
        other = cross_ref[from_k : from_k + channels]
        by = flip if k else flip_first
        out_ref[0, :, k] = 0.5 * (own[:, :width] + moved(other[:, :width], by))
        out_ref[1, :, k] = 0.5 * (own[:, width:] - moved(other[:, width:], by))


def gather_kernel(core_ref, own_ref, other_ref, out_ref):
    k_in, wide = own_ref.shape
    width = wide // 2
    pad = (out_ref.shape[0] - k_in) // 2
    core = core_ref[0]
    out_ref[:pad] = jnp.zeros((pad, cores * wide), bf16)
    out_ref[pad + k_in :] = jnp.zeros((pad, cores * wide), bf16)
    for phase in range(2):
        at = slice(width * phase, width * (phase + 1))
        own_at = pl.multiple_of(wide * phase + width * core, lanes)
        other_at = pl.multiple_of(wide * phase + width * (1 - core), lanes)
        out_ref[pad : pad + k_in, pl.ds(own_at, width)] = own_ref[:, at]
        out_ref[pad : pad + k_in, pl.ds(other_at, width)] = other_ref[:, at]


def tap_kernel(
    dims, core_ref, grad_ref, z_ref, tap_ref, keep_ref, send_ref, g_ref, exact_ref, shifted_ref
):
    cin, tin, cout, tout, ks, count, rows = dims
    some = cout // cores
    width = keep_ref.shape[1] - lanes
    wide = cores * width
    core = core_ref[0]
    row, col = iota((edge_rows, 2 * lanes), 0), iota((edge_rows, 2 * lanes), 1)
    spread = (((row == 0) & (col == lanes - 1)) | ((row == 1) & (col == lanes))).astype(f32).astype(bf16)
    for chip in range(count // cores):
        at = slice(rows * chip, rows * (chip + 1))
        low = 0
        for b in range(0, wide, lanes):
            g_ref[at, lanes + b : 2 * lanes + b] = grad_ref[chip, low : low + rows]
            low += rows
        edge = dot_tn(grad_ref[chip, low:, :rows], spread).astype(bf16)
        g_ref[at, :lanes] = edge[:, :lanes]
        g_ref[at, lanes + wide :] = edge[:, lanes:]
    to_time = one_hot((some * tout, some * tout), lambda r: swapped(r, tout, some))
    g = dot(to_time, g_ref[...])
    inside = slice(lanes, lanes + wide)
    shifted_ref[0] = pltpu.roll(g, wide + 2 * lanes - 1, 1)[:, inside].astype(bf16)
    shifted_ref[1] = g[:, inside].astype(bf16)
    shifted_ref[2] = pltpu.roll(g, 1, 1)[:, inside].astype(bf16)
    exact_ref[...] = g.astype(bf16)
    lane = iota((some * tout, lanes), 1)
    for block, block_ref in ((core, keep_ref), (1 - core, send_ref)):
        at = width * block
        before, inner, after = (
            exact_ref[:, pl.ds(pl.multiple_of(at + low, lanes), size)]
            for low, size in ((0, lanes), (lanes, width), (lanes + width, lanes))
        )
        edge = jnp.where(lane == 0, after.astype(f32), before.astype(f32))
        block_ref[:, :width] = inner
        block_ref[:, width:] = jnp.where((lane == 0) | (lane == lanes - 1), edge, 0.0).astype(bf16)
    blank = jnp.zeros((lanes - 3 * some, wide), bf16)
    size, reach = ks * cin, (ks + 2) * cin
    even, odd = None, None
    for t in range(0, tout, 2):
        band = slice(2 * cin * t, 2 * cin * t + reach)
        taken = []
        for at in (slice(some * t, some * (t + 1)), slice(some * (t + 1), some * (t + 2))):
            taken += [shifted_ref[shift, at] for shift in range(3)] + [blank]
        samples = jnp.concatenate([z_ref[band, :wide], z_ref[band, wide:]], axis=0)
        both = dot_nt(samples, jnp.concatenate(taken, axis=0))
        first = both[:size, :lanes] + both[reach - size : reach, lanes:]
        second = both[reach : reach + size, :lanes] + both[2 * reach - size :, lanes:]
        even = first if even is None else even + first
        odd = second if odd is None else odd + second
    tap_ref[:size] = jnp.where(iota((size, lanes), 1) < 3 * some, even, pltpu.roll(odd, 3 * some, 1))
    fold = size * some // lanes
    folded = jnp.zeros((fold, lanes), f32)
    for part in range(lanes // some):
        moved = pltpu.roll(odd[fold * part : fold * (part + 1)], (some * (part - 1)) % lanes, 1)
        here = split_index(iota((fold, lanes), 1), some)[0] == part
        folded = jnp.where(here, moved, folded)
    tap_ref[size:] = folded


def input_kernel(dims, part, core_ref, g_ref, *refs):
    *started, taps_ref, out_ref, w_ref = refs
    cin, tin, cout, tout, ks, count, rows = dims
    k_in = cin * tin
    half = g_ref.shape[1] - lanes
    some, channels = cout // cores, cout // count
    steps = lanes // some
    kinds = ks + 2 * (steps - 1)
    blank = jnp.zeros((cin, cout), bf16)
    wanted = core_ref[0] if part == 0 else 1 - core_ref[0]
    o, lane = iota((cout, lanes), 0), iota((cout, lanes), 1)
    device, channel = split_index(o, channels)
    chip, core_of = split_index(device, cores)
    tiles = None
    for step in range(steps):
        picked = [taps_ref[i - 2 * step, j] if 0 <= i - 2 * step < ks else blank
                  for j in range(ks) for i in range(kinds)]
        place = (core_of == wanted) & (lane == some * step + chip * channels + channel)
        term = dot(jnp.concatenate(picked, axis=0), place.astype(f32).astype(bf16))
        tiles = term if tiles is None else tiles + term
    tiles = tiles.astype(bf16)
    empty = jnp.zeros((cin, lanes), bf16)
    for j in range(ks):
        for s in range(tin):
            for q in range(some * tout // lanes):
                i = s - 2 * steps * q + 2
                at = (j * kinds + i) * cin
                tile = tiles[at : at + cin] if 0 <= i < kinds else empty
                w_ref[j, cin * s : cin * (s + 1), lanes * q : lanes * (q + 1)] = tile
    g = g_ref[...]
    wide = half + lanes
    same = g[:, :half]
    later = dot(g, one_hot_columns((wide, half), lambda n: n + 1)).astype(bf16)
    sooner = dot(g, one_hot_columns((wide, half), lambda n: jnp.where(n == 0, wide - 1, n - 1))).astype(bf16)
    even = dot(w_ref[0], later) + dot(w_ref[2], same) + dot(w_ref[4], sooner)
    odd = dot(w_ref[1], later) + dot(w_ref[3], same)
    if not started:
        out_ref[:, :half], out_ref[:, half:] = even, odd
        return
    even, odd = even + started[0][:, :half], odd + started[0][:, half:]
    both = jnp.concatenate([even.astype(bf16), odd.astype(bf16)], axis=1)
    to_channel = one_hot((k_in, k_in), lambda r: swapped(r, cin, tin))
    both = dot(to_channel, both).astype(bf16)
    merge = one_hot((2 * lanes, 2 * lanes), lambda r: swapped(r, 2, lanes))
    for b in range(half // lanes):
        piece = jnp.concatenate(
            [both[:, lanes * b : lanes * (b + 1)], both[:, half + lanes * b : half + lanes * (b + 1)]], axis=1
        )
        out_ref[:, 2 * lanes * b : 2 * lanes * (b + 1)] = dot(piece, merge).astype(bf16)


def unpack_kernel(dims, scale, tap_ref, out_ref):
    cin, tin, cout, tout, ks, count, rows = dims
    some, channels = cout // cores, cout // count
    size, folds = ks * cin, lanes // some
    fold = size // folds
    packed = size + fold
    both = jnp.concatenate([tap_ref[:packed], tap_ref[packed:]], axis=1)

    wide = cores * lanes
    source, target = iota((wide, folds * cout), 0), iota((wide, folds * cout), 1)
    slot, o = split_index(target, cout)
    device, channel = split_index(o, channels)
    chip, core_of = split_index(device, cores)
    place = (source == core_of * lanes + slot * some + chip * channels + channel).astype(f32).astype(bf16)
    total, rest = None, both
    for _ in range(3):
        part = rest.astype(bf16)
        rest = rest - part.astype(f32)
        term = dot(part, place)
        total = term if total is None else total + term
    total = total * scale
    for slot, j in enumerate((0, 2, 4, 1)):
        for i in range(ks):
            out_ref[i, j] = total[cin * i : cin * (i + 1), cout * slot : cout * (slot + 1)]
    for at in range(0, size, 8):
        slot, low = at // fold, size + at % fold
        out_ref[at // cin, 3, at % cin : at % cin + 8] = total[low : low + 8, cout * slot : cout * (slot + 1)]


def summed_over_chips(rows, axis, steps):
    count = lax.axis_size(axis)
    rounded = rows.astype(bf16)
    theirs = [lax.ppermute(rounded, axis, partners(count, step)).astype(f32) for step in steps]
    if len(steps) == 1:
        return rounded.astype(f32) + theirs[0]
    return (rounded.astype(f32) + theirs[0]) + (theirs[1] + theirs[2])


def partners(count, step):
    return [(i, i ^ step) for i in range(count)]


def mirrored(spectrum):
    return jnp.roll(jnp.flip(spectrum, -1), 1, -1)


def tables(count, width):
    inner = np.outer(np.arange(width), np.arange(width)) % width * (2.0 * np.pi / width)
    table = np.concatenate([np.cos(inner), np.sin(inner)], axis=1).astype(np.float32)
    high = table.astype(bf16)
    rest = (table - high.astype(np.float32)).astype(bf16)
    outer = np.outer(np.arange(count), np.arange(width)) * (2.0 * np.pi / (count * width))
    twist = np.stack([np.cos(outer), np.sin(outer)]).astype(np.float32)
    return twist, np.concatenate([high, rest])


def per_device(signal, conv_taps, response, cotangent):
    cin, tin, fibre_in = signal.shape
    cout, tout, width = cotangent.shape
    ks = conv_taps.shape[0]
    count = lax.axis_size("fibre")
    channels = cout // count
    rows = channels * tout
    waves = count * width
    tiles = width // lanes
    dims = (cin, tin, cout, tout, ks, count, rows)
    k_in, k_out = cin * tin, cout * tout
    taps = jnp.swapaxes(conv_taps, 2, 3)
    shape = jax.ShapeDtypeStruct
    conv_part, z = call(
        functools.partial(conv_kernel, dims),
        [
            shape((count, 2 * rows * tiles + edge_rows, lanes), bf16),
            shape((k_in, fibre_in), bf16),
        ],
        [
            pltpu.VMEM((ks, k_out, k_in), bf16),
            pltpu.VMEM((k_in, fibre_in), bf16),
            pltpu.VMEM(taps.shape, bf16),
            pltpu.VMEM((count, 2 * rows * tiles + edge_rows, lanes), bf16),
            pltpu.VMEM((k_in, fibre_in), bf16),
            pltpu.SemaphoreType.DMA((7 + tiles,)),
        ],
        2e9,
        (signal.reshape(k_in, fibre_in), cotangent.reshape(count, rows, width), taps),
        left=(0, 1, 2),
        left_out=(0, 1),
        room=60,
    )
    other_z = lax.ppermute(z, "fibre", partners(count, 1))
    cols = lax.all_to_all(conv_part, "fibre", split_axis=0, concat_axis=0, tiled=True)
    back = mirrored(response)
    real = jnp.stack([response[0] + back[0], response[1] - back[1]]) * (0.5 / waves)
    real = real.reshape(2, channels, width, count).transpose(0, 3, 1, 2)
    real = real.reshape(2, count * channels, width)
    twist, waves_table = tables(count, width)
    big = count * rows // 2
    grad_part, cross = call(
        functools.partial(filter_kernel, (count, channels, tout, width)),
        [
            shape((count // cores, cores * rows * tiles + edge_rows, lanes), bf16),
            shape((2 * tiles, count * rows // 2, lanes), f32),
        ],
        [
            pltpu.VMEM((count, rows, width), f32),
            pltpu.VMEM((big, 2 * width), f32),
            pltpu.VMEM((big, 2 * width), f32),
            pltpu.VMEM((big, 2 * width), f32),
            pltpu.VMEM((2 * tiles, big, lanes), f32),
            pltpu.VMEM((2 * width, 2 * width), bf16),
            pltpu.VMEM((2 * width, 2 * width), bf16),
        ],
        6e9,
        (cols, real, jnp.asarray(twist), jnp.asarray(waves_table)),
    )
    (cross,) = call(
        hermitian_kernel,
        [shape((2, channels, count, width), f32)],
        [pltpu.VMEM((count * channels, 2 * width), f32)],
        1e6,
        (cross,),
    )
    filter_grad = cross.transpose(0, 1, 3, 2).reshape(2, channels, waves)
    chips = [[core + cores * chip for chip in range(count // cores)] for core in range(cores)]
    grad_cols = lax.all_to_all(
        grad_part, "fibre", split_axis=0, concat_axis=0, tiled=True, axis_index_groups=chips
    )
    core = (lax.axis_index("fibre") % cores).astype(jnp.int32).reshape(1)
    (samples,) = call(
        gather_kernel,
        [shape((k_in + 4 * cin, cores * fibre_in), bf16)],
        [],
        1e6,
        (core, z, other_z),
        small=(0,),
    )
    grad_cols, filter_grad, samples = lax.optimization_barrier((grad_cols, filter_grad, samples))
    some = k_out // cores
    taps_part, keep, send = call(
        functools.partial(tap_kernel, dims),
        [
            shape((ks * cin + ks * cin * (cout // cores) // lanes, lanes), f32),
            shape((some, width + lanes), bf16),
            shape((some, width + lanes), bf16),
        ],
        [
            pltpu.VMEM((some, cores * width + 2 * lanes), bf16),
            pltpu.VMEM((some, cores * width + 2 * lanes), bf16),
            pltpu.VMEM((3, some, cores * width), bf16),
        ],
        1e9,
        (core, grad_cols, samples),
        small=(0,),
    )
    got = lax.ppermute(send, "fibre", partners(count, 1))
    chips = count // cores
    total = summed_over_chips(taps_part, "fibre", (cores,))
    step = 2
    (started,) = call(
        functools.partial(input_kernel, dims, 0),
        [shape((k_in, fibre_in), f32)],
        [pltpu.VMEM((ks, k_in, some), bf16)],
        1e9,
        (core, keep, taps),
        small=(0,),
    )
    total, started, got = lax.optimization_barrier((total, started, got))
    (input_grad,) = call(
        functools.partial(input_kernel, dims, 1),
        [shape((k_in, fibre_in), bf16)],
        [pltpu.VMEM((ks, k_in, some), bf16)],
        1e9,
        (core, got, started, taps),
        small=(0,),
    )
    if chips % 8 == 0:
        total = summed_over_chips(total, "fibre", (2 * cores, 4 * cores, 6 * cores))
        step = 8
    while step < chips:
        total = summed_over_chips(total, "fibre", (cores * step,))
        step *= 2
    total, input_grad = lax.optimization_barrier((total, input_grad))
    other = lax.ppermute(total, "fibre", partners(count, 1))
    total = jnp.where(core[0] == 0, jnp.concatenate([total, other]), jnp.concatenate([other, total]))
    (tap_grad,) = call(
        functools.partial(unpack_kernel, dims, 1.0 / math.sqrt(tout * waves)),
        [shape((ks, ks, cin, cout), f32)],
        [],
        1e6,
        (total,),
    )
    return (input_grad.reshape(signal.shape), jnp.swapaxes(tap_grad, 2, 3), filter_grad)


def solution(mesh):
    in_specs = (P("parts", None, "fibre"), P(), P(None, "fibre", None), P("parts", None, "fibre"))
    out_specs = (P("parts", None, "fibre"), P("parts", None, None, None), P("parts", "fibre", None))
    return jax.shard_map(
        per_device, mesh=mesh, in_specs=in_specs, out_specs=out_specs, check_vma=False
    )
```
